32 devices in a mesh: groups: 2 (over x), tm: 8 (over z, y), space: 2 (over core).
Axes of the slice: x: 2, y: 2, z: 4, core: 2. Of those that a mesh axis runs over, the one named last changes fastest.
Arguments:
- queries: bfloat16 [16384, 256], P(('groups', 'tm', 'space')), parts along dimension 0, may hold values from -22 to 22, as said below
- key_rows: bfloat16 [16384, 256], P(('groups', 'tm', 'space')), parts along dimension 0, may hold values from -10 to 10
- value_rows: bfloat16 [16384, 256], P(('groups', 'tm', 'space')), parts along dimension 0, may hold values from -6 to 6
- out_grad: bfloat16 [16384, 256], P(('groups', 'tm', 'space')), parts along dimension 0, may hold values from -6 to 6
- block_lists: int32 [32, 8], P('groups'), parts along dimension 0, may hold values from -1 to 31, as said below
Outputs:
- attn_out: bfloat16 [16384, 256], P(('groups', 'tm', 'space')), parts along dimension 0
- grad_queries: bfloat16 [16384, 256], P(('groups', 'tm', 'space')), parts along dimension 0
- grad_keys: bfloat16 [16384, 256], P(('groups', 'tm', 'space')), parts along dimension 0
- grad_values: bfloat16 [16384, 256], P(('groups', 'tm', 'space')), parts along dimension 0
The draws below stay inside these ranges and needn't reach their ends.
There are 2 independent parts, one for each index of `groups`. The reference program is written for one: setup_inputs(seed, part) draws one part's arguments, and reference() takes and returns one part's arrays. A program takes and returns all parts, laid end to end along the dimension named above; each array names one. Nothing has to cross between parts.
Inputs may be any that keep to these rules, and one draw needn't show every extreme that they name: `block_lists`: row r belongs to query slab r. Slots 0 to 3 concern earlier frames and slots 4 to 7 later ones; in each half the first two slots name two different blocks of the frame at distance 1, and the half's slot j >= 2 names one block of the frame at distance 2 ** (j - 1). An entry is frame * 4 + block with block 0 to 3, or -1 exactly where that frame lies outside the video. `queries`: query entries.
All inputs are finite; a program needn't handle non-finite values.
Results may differ from the reference program's by a relative error of at most 0.012.
Values may be sent and summed in bfloat16 or wider, within the bound.
No kernel may reach another device: no remote copies, remote signals or barrier semaphores. Data moves between devices by JAX's collectives and lax.ppermute only.
A program may use at most 128 MiB of HBM per device.

```python
import math
import jax
import jax.numpy as jnp
from jax import lax

DH = 128
HEADS = 2
S_DEV = 512
HEAD_FEATURES = 256
FRAME_TOK = 1024
KEY_BLOCK_TOKENS = 256
LATENT_FRAMES = 8
LOGF = 3
SLOT_COUNT = 8
QUERY_SLABS = 16
VIDEO_TOKENS = 8192


def row_scales(key, count):
    return jnp.exp(jax.random.uniform(key, (count, 1), jnp.float32, jnp.log(0.4), jnp.log(2.5)))


def base_draw(key):
    noise_key, scale_key = jax.random.split(key)
    base = jnp.clip(jax.random.normal(noise_key, (VIDEO_TOKENS, HEAD_FEATURES), jnp.float32), -4.0, 4.0)
    return base * row_scales(scale_key, VIDEO_TOKENS)


def draw_queries(key, part):
    scaled = base_draw(jax.random.fold_in(key, 11))
    return scaled.astype(jnp.bfloat16)


def draw_key_rows(key, part):
    scaled = base_draw(jax.random.fold_in(key, 13))
    return scaled.astype(jnp.bfloat16)


def draw_block_lists(key, part):
    slab = jnp.arange(QUERY_SLABS, dtype=jnp.int32)[:, None]
    frame = slab // (QUERY_SLABS // LATENT_FRAMES)
    slot_position = jnp.arange(SLOT_COUNT, dtype=jnp.int32)[None, :]
    side = slot_position // (LOGF + 1)
    within = slot_position % (LOGF + 1)
    level = jnp.maximum(within - 1, 0)
    distance = jnp.left_shift(jnp.ones_like(level), level)
    target = jnp.where(side == 0, frame - distance, frame + distance)
    initial_key_block, step_random_key = jax.random.split(jax.random.fold_in(key, 3))
    initial_entry = jax.random.randint(initial_key_block, (QUERY_SLABS, SLOT_COUNT), 0, 4, dtype=jnp.int32)
    forced = (slab == (LATENT_FRAMES - 2) * (QUERY_SLABS // LATENT_FRAMES)) & (slot_position == LOGF + 1)
    initial_entry = jnp.where(forced, 3, initial_entry)
    loop_step = jax.random.randint(step_random_key, (QUERY_SLABS, SLOT_COUNT), 1, 4, dtype=jnp.int32)
    second = (jnp.roll(initial_entry, 1, axis=1) + loop_step) % 4
    chosen = jnp.where(within == 1, second, initial_entry)
    inside = (target >= 0) & (target < LATENT_FRAMES)
    return jnp.where(inside, target * 4 + chosen, -1).astype(jnp.int32)


def steps_of(key, dims, cuts, smallest, high):
    def one(position, parts):
        steps = jax.random.uniform(jax.random.fold_in(jax.random.fold_in(key, 6), position), (parts,), jnp.float32, smallest / len(cuts), high / len(cuts))
        return jnp.repeat(jnp.exp(steps), dims[position] // parts).reshape((-1,) + (1,) * (len(dims) - position - 1))

    gain = one(*cuts[0])
    for cut in cuts[1:]:
        gain = gain * one(*cut)
    return gain


def normal_values(key, dims, deviation, limit, cuts=(), kind=jnp.bfloat16):
    gain = steps_of(key, dims, cuts, -0.22, 0.18) if cuts else 1.0
    array = jax.random.normal(key, dims, jnp.float32) * deviation * gain
    return jnp.minimum(jnp.maximum(array, -limit), limit).astype(kind)


def setup_inputs(seed: int = 0, part: int = 0) -> dict:
    arg_keys = jax.random.split(jax.random.key(seed), 6)
    part_splits = jax.random.split(jax.random.fold_in(arg_keys[5], part), 6)
    queries = draw_queries(jax.random.fold_in(jax.random.fold_in(arg_keys[5], part), 71), part)
    key_rows = draw_key_rows(jax.random.fold_in(jax.random.fold_in(arg_keys[5], part), 71), part)
    value_rows = normal_values(part_splits[2], (VIDEO_TOKENS, HEAD_FEATURES), 1.0, 6.0, ((0, 16),))
    out_grad = normal_values(part_splits[3], (VIDEO_TOKENS, HEAD_FEATURES), 1.0, 6.0, ((0, 16),))
    block_lists = draw_block_lists(jax.random.fold_in(jax.random.fold_in(arg_keys[5], part), 71), part)
    return dict(queries=queries, key_rows=key_rows, value_rows=value_rows, out_grad=out_grad, block_lists=block_lists)


def forward_head(query_h, key_h, value_h, usable, inv_scale):
    scores = jnp.dot(query_h, key_h.T, preferred_element_type=jnp.float32) * inv_scale
    scores = jnp.where(usable[None, :], scores, -jnp.inf)
    row_max = lax.optimization_barrier(jnp.max(scores, axis=1, keepdims=True))
    raised = jnp.exp(scores - row_max)
    attn_prob = raised / lax.optimization_barrier(jnp.sum(raised, axis=1, keepdims=True))
    attn_bf = attn_prob.astype(jnp.bfloat16)
    out_head = jnp.dot(attn_bf, value_h, preferred_element_type=jnp.float32).astype(jnp.bfloat16)
    return (attn_prob, attn_bf, out_head)

def backward_head(query_h, key_h, value_h, grad_h, out_head, attn_prob, attn_bf, inv_scale):
    grad_prob = jnp.dot(grad_h, value_h.T, preferred_element_type=jnp.float32)
    row_dot = lax.optimization_barrier(jnp.sum(grad_h.astype(jnp.float32) * out_head.astype(jnp.float32), axis=1, keepdims=True))
    grad_score = (attn_prob * (grad_prob - row_dot)).astype(jnp.bfloat16)
    grad_q = (jnp.dot(grad_score, key_h, preferred_element_type=jnp.float32) * inv_scale).astype(jnp.bfloat16)
    grad_k = jnp.dot(grad_score.T, query_h, preferred_element_type=jnp.float32) * inv_scale
    grad_v = jnp.dot(attn_bf.T, grad_h, preferred_element_type=jnp.float32)
    return (grad_q, grad_k, grad_v)

def split_heads(matrix):
    return matrix.reshape(matrix.shape[0], HEADS, DH).transpose(1, 0, 2)

def merge_heads(stacked):
    return stacked.transpose(1, 0, 2).reshape(stacked.shape[1], HEADS * DH)

def attend_slab(query_s, key_all, value_all, grad_s, usable):
    inv_scale = 1.0 / math.sqrt(DH)

    def per_head(operands):
        query_h, key_h, value_h, grad_h = operands
        attn_prob, attn_bf, out_head = forward_head(query_h, key_h, value_h, usable, inv_scale)
        grad_q, grad_k, grad_v = backward_head(query_h, key_h, value_h, grad_h, out_head, attn_prob, attn_bf, inv_scale)
        return (out_head, grad_q, grad_k, grad_v)
    results = lax.map(per_head, (split_heads(query_s), split_heads(key_all), split_heads(value_all), split_heads(grad_s)))
    return tuple((merge_heads(stacked) for stacked in results))

def reference(queries, key_rows, value_rows, out_grad, block_lists):
    key_block_rows = key_rows.reshape(LATENT_FRAMES * 4, KEY_BLOCK_TOKENS, HEAD_FEATURES)
    value_block_rows = value_rows.reshape(LATENT_FRAMES * 4, KEY_BLOCK_TOKENS, HEAD_FEATURES)

    def one_slab(carry, slab_index):
        key_gradient_total, value_gradient_total = carry
        frame_index = slab_index // (QUERY_SLABS // LATENT_FRAMES)
        start = (slab_index * S_DEV).astype(jnp.int32)
        frame_start = (frame_index * FRAME_TOK).astype(jnp.int32)
        query_s = lax.dynamic_slice_in_dim(queries, start, S_DEV, 0)
        grad_s = lax.dynamic_slice_in_dim(out_grad, start, S_DEV, 0)
        own_k = lax.dynamic_slice_in_dim(key_rows, frame_start, FRAME_TOK, 0)
        own_v = lax.dynamic_slice_in_dim(value_rows, frame_start, FRAME_TOK, 0)
        block_ids = lax.dynamic_index_in_dim(block_lists, slab_index, 0, keepdims=False)
        present = block_ids >= 0
        bounded_index = jnp.maximum(block_ids, 0).astype(jnp.int32)
        remote_keys = key_block_rows[bounded_index].reshape(SLOT_COUNT * KEY_BLOCK_TOKENS, HEAD_FEATURES)
        remote_values = value_block_rows[bounded_index].reshape(SLOT_COUNT * KEY_BLOCK_TOKENS, HEAD_FEATURES)
        usable = jnp.concatenate([jnp.ones((FRAME_TOK,), dtype=bool), jnp.repeat(present, KEY_BLOCK_TOKENS)])
        key_all = jnp.concatenate([own_k, remote_keys], axis=0)
        value_all = jnp.concatenate([own_v, remote_values], axis=0)
        out_s, grad_q, grad_k, grad_v = attend_slab(query_s, key_all, value_all, grad_s, usable)
        near_k = lax.dynamic_slice_in_dim(key_gradient_total, frame_start, FRAME_TOK, 0) + grad_k[:FRAME_TOK]
        near_v = lax.dynamic_slice_in_dim(value_gradient_total, frame_start, FRAME_TOK, 0) + grad_v[:FRAME_TOK]
        key_gradient_total = lax.dynamic_update_slice_in_dim(key_gradient_total, near_k, frame_start, 0)
        value_gradient_total = lax.dynamic_update_slice_in_dim(value_gradient_total, near_v, frame_start, 0)
        remote_key_gradient = lax.optimization_barrier(grad_k[FRAME_TOK:].astype(jnp.bfloat16)).astype(jnp.float32)
        remote_value_gradient = lax.optimization_barrier(grad_v[FRAME_TOK:].astype(jnp.bfloat16)).astype(jnp.float32)
        key_gradient_total = key_gradient_total.reshape(LATENT_FRAMES * 4, KEY_BLOCK_TOKENS, HEAD_FEATURES).at[bounded_index].add(remote_key_gradient.reshape(SLOT_COUNT, KEY_BLOCK_TOKENS, HEAD_FEATURES)).reshape(VIDEO_TOKENS, HEAD_FEATURES)
        value_gradient_total = value_gradient_total.reshape(LATENT_FRAMES * 4, KEY_BLOCK_TOKENS, HEAD_FEATURES).at[bounded_index].add(remote_value_gradient.reshape(SLOT_COUNT, KEY_BLOCK_TOKENS, HEAD_FEATURES)).reshape(VIDEO_TOKENS, HEAD_FEATURES)
        return ((key_gradient_total, value_gradient_total), (out_s, grad_q))
    zeros_init = jnp.zeros((VIDEO_TOKENS, HEAD_FEATURES), dtype=jnp.float32)
    (key_gradient_total, value_gradient_total), (out_all, grad_q_all) = lax.scan(one_slab, (zeros_init, zeros_init), jnp.arange(QUERY_SLABS, dtype=jnp.int32))
    return (out_all.reshape(VIDEO_TOKENS, HEAD_FEATURES), grad_q_all.reshape(VIDEO_TOKENS, HEAD_FEATURES), key_gradient_total.astype(jnp.bfloat16), value_gradient_total.astype(jnp.bfloat16))
```

```python
import functools
import math

import jax
import jax.numpy as jnp
from jax import lax
from jax.experimental import pallas as pl
from jax.experimental.pallas import tpu as pltpu
from jax.sharding import PartitionSpec as P

DH = 128
HEADS = 2
F32 = jnp.float32
BF16 = jnp.bfloat16
VMEM = pl.BlockSpec(memory_space=pltpu.VMEM)
SMEM = pl.BlockSpec(memory_space=pltpu.SMEM)
NEG = -1e30


def dot_nn(a, b):
    return lax.dot_general(a, b, (((1,), (0,)), ((), ())), preferred_element_type=F32)


def dot_nt(a, b):
    return lax.dot_general(a, b, (((1,), (1,)), ((), ())), preferred_element_type=F32)


def dot_tn(a, b):
    return lax.dot_general(a, b, (((0,), (0,)), ((), ())), preferred_element_type=F32)


def partner_pairs(count, distance, second):
    pairs = []
    for frame in range(count):
        up = ((frame // distance) % 2 == 0) != second
        target = frame + distance if up else frame - distance
        pairs.append((frame, target if 0 <= target < count else frame))
    return pairs


def exchanges(count):
    levels = count.bit_length() - 1
    found = []
    for level in range(levels):
        for second in (False, True):
            pairs = partner_pairs(count, 1 << level, second)
            if all(source == target for source, target in pairs):
                continue
            found.append((level, second, 2 if level == 0 else 1, pairs))
    return found


def exchange_partner(tm_index, count, level, second):
    odd = lax.rem(lax.shift_right_logical(tm_index, level), 2)
    goes_up = odd == (1 if second else 0)
    partner = jnp.where(goes_up, tm_index + (1 << level), tm_index - (1 << level))
    exists = jnp.logical_and(partner >= 0, partner < count)
    return partner, goes_up, exists


def slot_of(goes_up, level, k, levels):
    return jnp.where(goes_up, levels + 1, 0) + (0 if level == 0 else level + 1) + k


def wanted_blocks(lists_ref, tm_index, space_index, count, n_space, level, second, k):
    levels = count.bit_length() - 1
    partner, goes_up, exists = exchange_partner(tm_index, count, level, second)
    row = jnp.where(exists, partner, tm_index) * n_space + space_index
    slot = slot_of(jnp.logical_not(goes_up), level, k, levels)
    entry = lists_ref[row, slot]
    return jnp.clip(entry - tm_index * 4, 0, 3), exists


def select_kernel(plan, count, n_space, block, lists, k_own, v_own, k_oth, v_oth, *outs):
    tm_index = lax.axis_index("tm")
    space_index = lax.axis_index("space")
    width = k_own.shape[1]
    per_half = k_own.shape[0] // block
    for (level, second, blocks, _), out in zip(plan, outs):
        for k in range(blocks):
            b, _ = wanted_blocks(lists, tm_index, space_index, count, n_space, level, second, k)
            half = b // per_half
            row = pl.multiple_of((b - half * per_half) * block, block)
            rows = pl.ds(k * block, block)

            @pl.when(half == space_index)
            def _():
                out[rows, :width] = k_own[pl.ds(row, block), :]
                out[rows, width:] = v_own[pl.ds(row, block), :]

            @pl.when(half != space_index)
            def _():
                out[rows, :width] = k_oth[pl.ds(row, block), :]
                out[rows, width:] = v_oth[pl.ds(row, block), :]


def attend_kernel(plan, count, n_space, block, *refs):
    n_far = len(plan)
    lists, q_ref, g_ref, k_own, v_own, k_oth, v_oth = refs[:7]
    far = refs[7 : 7 + n_far]
    o_ref, dq_ref, near_own, near_oth = refs[7 + n_far : 11 + n_far]
    far_out = refs[11 + n_far : 11 + 2 * n_far]
    s_ref, e_ref = refs[11 + 2 * n_far :]
    tm_index = lax.axis_index("tm")
    width = q_ref.shape[1]
    scale = 1.0 / math.sqrt(DH)
    log2e = scale * math.log2(math.e)
    half = k_own.shape[0]

    pieces = []
    for k_ref, v_ref, out in ((k_own, v_own, near_own), (k_oth, v_oth, near_oth)):
        for r in range(0, half, block):
            pieces.append((k_ref, 0, v_ref, 0, r, out, None))
    for (level, second, blocks, _), ref, out in zip(plan, far, far_out):
        _, _, exists = exchange_partner(tm_index, count, level, second)
        for k in range(blocks):
            pieces.append((ref, 0, ref, width, k * block, out, exists))

    for h in range(HEADS):
        cols = slice(h * DH, (h + 1) * DH)
        q = q_ref[:, cols]
        g = g_ref[:, cols]
        top = None
        for j, (k_ref, k_at, _, _, r, _, exists) in enumerate(pieces):
            s = dot_nt(q, k_ref[r : r + block, k_at + h * DH : k_at + (h + 1) * DH])
            if exists is not None:
                s = jnp.where(exists, s, NEG)
            s_ref[j] = s
            for c in range(0, block, DH):
                part = s[:, c : c + DH]
                top = part if top is None else jnp.maximum(top, part)
        peak = jnp.max(top, axis=1, keepdims=True)
        total = None
        acc = None
        for j, (_, _, v_ref, v_at, r, _, _) in enumerate(pieces):
            e = jnp.exp2((s_ref[j] - peak) * log2e)
            for c in range(0, block, DH):
                part = e[:, c : c + DH]
                total = part if total is None else total + part
            eb = e.astype(BF16)
            e_ref[j] = eb
            out = dot_nn(eb, v_ref[r : r + block, v_at + h * DH : v_at + (h + 1) * DH])
            acc = out if acc is None else acc + out
        inv = 1.0 / jnp.sum(total, axis=1, keepdims=True)
        o = (acc * inv).astype(BF16)
        o_ref[:, cols] = o
        gs = (g.astype(F32) * inv).astype(BF16)
        row_dot = jnp.sum(gs.astype(F32) * o.astype(F32), axis=1, keepdims=True)
        dq = None
        for j, (k_ref, k_at, v_ref, v_at, r, out, _) in enumerate(pieces):
            k_blk = k_ref[r : r + block, k_at + h * DH : k_at + (h + 1) * DH]
            v_blk = v_ref[r : r + block, v_at + h * DH : v_at + (h + 1) * DH]
            gp = dot_nt(gs, v_blk)
            eb = e_ref[j]
            ds = (eb.astype(F32) * (gp - row_dot)).astype(BF16)
            part = dot_nn(ds, k_blk)
            dq = part if dq is None else dq + part
            dk = dot_tn(ds, q) * scale
            dv = dot_tn(eb, gs)
            out[r : r + block, h * DH : (h + 1) * DH] = dk.astype(out.dtype)
            out[r : r + block, width + h * DH : width + (h + 1) * DH] = dv.astype(out.dtype)
        dq_ref[:, cols] = (dq * scale).astype(BF16)


def gather_kernel(plan, count, n_space, block, *refs):
    n_far = len(plan)
    lists, near_own, near_oth = refs[:3]
    back = refs[3 : 3 + n_far]
    keep, send = refs[3 + n_far : 5 + n_far]
    acc = refs[5 + n_far]
    tm_index = lax.axis_index("tm")
    space_index = lax.axis_index("space")
    half = near_own.shape[0]
    per_half = half // block
    own_at = pl.multiple_of(space_index * half, half)
    oth_at = pl.multiple_of((1 - space_index) * half, half)
    acc[pl.ds(own_at, half), :] = near_own[...]
    acc[pl.ds(oth_at, half), :] = near_oth[...]
    for (level, second, blocks, _), ref in zip(plan, back):
        for k in range(blocks):
            b, exists = wanted_blocks(lists, tm_index, space_index, count, n_space, level, second, k)
            rows = pl.ds(pl.multiple_of(b * block, block), block)

            @pl.when(exists)
            def _():
                acc[rows, :] += ref[k * block : (k + 1) * block, :].astype(F32)

    keep[...] = acc[pl.ds(own_at, half), :]
    send[...] = acc[pl.ds(oth_at, half), :].astype(BF16)


def finish_kernel(keep, came, dk_ref, dv_ref):
    width = dk_ref.shape[1]
    total = keep[...] + came[...].astype(F32)
    dk_ref[...] = total[:, :width].astype(BF16)
    dv_ref[...] = total[:, width:].astype(BF16)


def call(kernel, ins, out_shape, scratch=(), flops=0, traffic=4 << 20):
    return pl.pallas_call(
        kernel,
        out_shape=out_shape,
        in_specs=ins,
        out_specs=tuple(VMEM for _ in out_shape),
        scratch_shapes=list(scratch),
        compiler_params=pltpu.CompilerParams(vmem_limit_bytes=48 << 20),
        cost_estimate=pl.CostEstimate(flops=flops, bytes_accessed=traffic, transcendentals=0),
    )


def per_device(queries, key_rows, value_rows, out_grad, block_lists):
    s_dev, width = queries.shape
    n_space = lax.axis_size("space")
    count = lax.axis_size("tm")
    block = s_dev * n_space // 4
    plan = exchanges(count)
    n_far = len(plan)
    sds = jax.ShapeDtypeStruct
    common = (plan, count, n_space, block)

    def across(value):
        return lax.ppermute(value, "space", [(0, 1), (1, 0)])

    k_oth = across(key_rows)
    v_oth = across(value_rows)
    sends = call(
        functools.partial(select_kernel, *common),
        [SMEM] + [VMEM] * 4,
        [sds((p[2] * block, 2 * width), BF16) for p in plan],
    )(block_lists, key_rows, value_rows, k_oth, v_oth)
    far = [lax.ppermute(value, "tm", p[3]) for value, p in zip(sends, plan)]
    n_pieces = 2 * s_dev // block + sum(p[2] for p in plan)
    results = call(
        functools.partial(attend_kernel, *common),
        [SMEM] + [VMEM] * (6 + n_far),
        [sds((s_dev, width), BF16)] * 2
        + [sds((s_dev, 2 * width), F32)] * 2
        + [sds((p[2] * block, 2 * width), BF16) for p in plan],
        scratch=[
            pltpu.VMEM((n_pieces, s_dev, block), F32),
            pltpu.VMEM((n_pieces, s_dev, block), BF16),
        ],
        flops=12 * s_dev * n_pieces * block * width,
        traffic=12 << 20,
    )(block_lists, queries, out_grad, key_rows, value_rows, k_oth, v_oth, *far)
    attn_out, grad_q, near_own, near_oth = results[:4]
    back = [lax.ppermute(value, "tm", p[3]) for value, p in zip(results[4:], plan)]
    keep, send = call(
        functools.partial(gather_kernel, *common),
        [SMEM] + [VMEM] * (2 + n_far),
        [sds((s_dev, 2 * width), F32), sds((s_dev, 2 * width), BF16)],
        scratch=[pltpu.VMEM((2 * s_dev, 2 * width), F32)],
    )(block_lists, near_own, near_oth, *back)
    grad_k, grad_v = call(
        finish_kernel, [VMEM] * 2, [sds((s_dev, width), BF16)] * 2
    )(keep, across(send))
    return attn_out, grad_q, grad_k, grad_v


def solution(mesh):
    rows = P(("groups", "tm", "space"), None)
    return jax.shard_map(
        per_device,
        mesh=mesh,
        in_specs=(rows, rows, rows, rows, P("groups", None)),
        out_specs=(rows, rows, rows, rows),
        check_vma=False,
    )
```

```python
import functools
import math

import jax
import jax.numpy as jnp
from jax import lax
from jax.experimental import pallas as pl
from jax.experimental.pallas import tpu as pltpu
from jax.sharding import PartitionSpec as P

DH = 128
F32 = jnp.float32
BF16 = jnp.bfloat16
VMEM = pl.BlockSpec(memory_space=pltpu.VMEM)
SMEM = pl.BlockSpec(memory_space=pltpu.SMEM)
NEG = -1e30
SCALE = 1.0 / math.sqrt(DH)
EXP_SCALE = SCALE * math.log2(math.e)
KEY = slice(0, DH)
VALUE = slice(DH, 2 * DH)
sds = jax.ShapeDtypeStruct


def dot_nn(a, b):
    return lax.dot_general(a, b, (((1,), (0,)), ((), ())), preferred_element_type=F32)


def dot_nt(a, b):
    return lax.dot_general(a, b, (((1,), (1,)), ((), ())), preferred_element_type=F32)


def dot_tn(a, b):
    return lax.dot_general(a, b, (((0,), (0,)), ((), ())), preferred_element_type=F32)


def call(kernel, args, out_shape, scratch=(), flops=0):
    traffic = sum(a.size * a.dtype.itemsize for a in (*args, *out_shape))
    return pl.pallas_call(
        kernel,
        out_shape=out_shape,
        in_specs=[SMEM if a.dtype == jnp.int32 else VMEM for a in args],
        out_specs=tuple(VMEM for _ in out_shape),
        scratch_shapes=list(scratch),
        compiler_params=pltpu.CompilerParams(vmem_limit_bytes=40 << 20),
        cost_estimate=pl.CostEstimate(flops=flops, bytes_accessed=traffic, transcendentals=0),
    )(*args)


def swap_pairs(count, distance, second):
    pairs = []
    for frame in range(count):
        up = ((frame // distance) % 2 == 0) != second
        target = frame + distance if up else frame - distance
        pairs.append((frame, target if 0 <= target < count else frame))
    return pairs


class Swap:
    def __init__(self, count, level, second):
        self.count, self.level, self.second = count, level, second
        self.levels = count.bit_length() - 1
        self.pairs = swap_pairs(count, 1 << level, second)
        self.moves = any(source != target for source, target in self.pairs)

    def partner(self, frame):
        odd = lax.rem(lax.shift_right_logical(frame, self.level), 2)
        later = odd == (1 if self.second else 0)
        other = jnp.where(later, frame + (1 << self.level), frame - (1 << self.level))
        return other, later, jnp.logical_and(other >= 0, other < self.count)

    def slot(self, later, k):
        base = 0 if self.level == 0 else self.level + 1
        return jnp.where(later, self.levels + 1, 0) + base + k

    def block_of_mine(self, lists, frame, slab, k):
        other, later, exists = self.partner(frame)
        entry = lists[frame * 2 + slab, self.slot(later, k)]
        return jnp.clip(entry - other * 4, 0, 3), exists

    def block_of_theirs(self, lists, frame, slab, k):
        other, later, exists = self.partner(frame)
        row = jnp.where(exists, other, frame) * 2 + slab
        entry = lists[row, self.slot(jnp.logical_not(later), k)]
        return jnp.clip(entry - frame * 4, 0, 3), exists


def head_cols(head):
    return slice(head * DH, (head + 1) * DH)


def each_core(body):
    core = lax.axis_index("space")
    for mine in range(2):
        pl.when(core == mine)(functools.partial(body, mine))


def pack_kernel(k, v, q, g, kv_out, qg_out):
    def body(mine):
        cols = head_cols(1 - mine)
        kv_out[:, KEY] = k[:, cols]
        kv_out[:, VALUE] = v[:, cols]
        qg_out[:, KEY] = q[:, cols]
        qg_out[:, VALUE] = g[:, cols]

    each_core(body)


def join(mine, a, b, came, out):
    half = a.shape[0]
    cols = head_cols(mine)
    own = slice(mine * half, (mine + 1) * half)
    other = slice((1 - mine) * half, (2 - mine) * half)
    out[own, KEY] = a[:, cols]
    out[own, VALUE] = b[:, cols]
    out[other, :] = came[...]


def frame_kernel(far, block, lists, k, v, came, kv_out, *sends):
    each_core(lambda mine: join(mine, k, v, came, kv_out))
    frame = lax.axis_index("tm")
    for swap, send in zip(far, sends):
        for slab in range(2):
            b, _ = swap.block_of_theirs(lists, frame, slab, 0)
            row = pl.multiple_of(b * block, block)
            send[slab * block : (slab + 1) * block, :] = kv_out[pl.ds(row, block), :]


def join_kernel(q, g, came, out):
    each_core(lambda mine: join(mine, q, g, came, out))


class Piece:
    def __init__(self, kv, row, exists=None, grad=None, grad_row=None, add=False):
        self.kv, self.row, self.exists = kv, row, exists
        self.grad, self.grad_row, self.add = grad, row if grad_row is None else grad_row, add


def forward_slab(q, pieces, block, s_ref, old):
    top = None
    for j, piece in enumerate(pieces):
        s = dot_nt(q, piece.kv[pl.ds(piece.row, block), KEY])
        if piece.exists is not None:
            s = jnp.where(piece.exists, s, NEG)
        s_ref[j] = s
        for c in range(0, block, DH):
            part = s[:, c : c + DH]
            top = part if top is None else jnp.maximum(top, part)
    peak = jnp.max(top, axis=1, keepdims=True)
    if old is not None:
        peak = jnp.maximum(peak, old[0])
    total = None
    acc = None
    for j, piece in enumerate(pieces):
        e = jnp.exp2((s_ref[j] - peak) * EXP_SCALE)
        for c in range(0, block, DH):
            part = e[:, c : c + DH]
            total = part if total is None else total + part
        out = dot_nn(e.astype(BF16), piece.kv[pl.ds(piece.row, block), VALUE])
        acc = out if acc is None else acc + out
    total = jnp.sum(total, axis=1, keepdims=True)
    if old is not None:
        shrink = jnp.exp2((old[0] - peak) * EXP_SCALE)
        total = total + old[1] * shrink
        acc = acc + old[2] * shrink
    return peak, total, acc


def backward_slab(q, g, lse, row_dot, pieces, block):
    dq = None
    for piece in pieces:
        k = piece.kv[pl.ds(piece.row, block), KEY]
        v = piece.kv[pl.ds(piece.row, block), VALUE]
        s = dot_nt(k, q)
        if piece.exists is not None:
            s = jnp.where(piece.exists, s, NEG)
        p = jnp.exp2(s * EXP_SCALE - lse)
        ds = (p * (dot_nt(v, g) - row_dot)).astype(BF16)
        dk = dot_nn(ds, q) * SCALE
        dv = dot_nn(p.astype(BF16), g)
        rows = pl.ds(piece.grad_row, block)
        if piece.add:
            piece.grad[rows, KEY] += dk
            piece.grad[rows, VALUE] += dv
        else:
            piece.grad[rows, KEY] = dk.astype(piece.grad.dtype)
            piece.grad[rows, VALUE] = dv.astype(piece.grad.dtype)
        part = dot_tn(ds, k)
        dq = part if dq is None else dq + part
    return dq


def listed(swap, kv, lists, frame, slab, block, grad=None, count=1):
    pieces = []
    for k in range(count):
        b, exists = swap.block_of_mine(lists, frame, slab, k)
        row = pl.multiple_of(b * block, block)
        pieces.append(Piece(kv, row, exists, grad, add=True))
    return pieces


def arrived(swap, kv, frame, slab, block, grad=None):
    _, _, exists = swap.partner(frame)
    return Piece(kv, slab * block, exists, grad)


def rows_of(slab, half):
    return slice(slab * half, (slab + 1) * half)


def store_state(refs, rows, peak, total, acc):
    stat, acc_ref = refs
    lane = lax.broadcasted_iota(jnp.int32, acc.shape, 1)
    stat[rows, :] = jnp.where(lane == 0, peak, total)
    acc_ref[rows, :] = acc


def load_state(refs, rows):
    stat, acc_ref = refs
    return stat[rows, 0:1], stat[rows, 1:2], acc_ref[rows, :]


def near_kernel(block, qg, kv, stat, acc, s_ref):
    half = qg.shape[0] // 2
    for slab in range(2):
        rows = rows_of(slab, half)
        pieces = [Piece(kv, r) for r in range(0, 2 * half, block)]
        store_state((stat, acc), rows, *forward_slab(qg[rows, KEY], pieces, block, s_ref, None))


def middle_kernel(block, swaps, lists, qg, stat, acc, a_kv, z_kv, y_kv, stat2, acc2, s_ref):
    half = qg.shape[0] // 2
    frame = lax.axis_index("tm")
    a, z, y = swaps
    for slab in range(2):
        rows = rows_of(slab, half)
        pieces = listed(a, a_kv, lists, frame, slab, block, count=2)
        pieces += listed(z, z_kv, lists, frame, slab, block)
        pieces += listed(y, y_kv, lists, frame, slab, block)
        old = load_state((stat, acc), rows)
        new = forward_slab(qg[rows, KEY], pieces, block, s_ref, old)
        store_state((stat2, acc2), rows, *new)


def last_kernel(block, relayed, far, *refs):
    n = len(far)
    lists, qg, stat, acc, c_kv = refs[:5]
    far_kv = refs[5 : 5 + n]
    o_ref, row_ref, dc_ref, dq_ref = refs[5 + n : 9 + n]
    s_ref, grad = refs[9 + n :]
    half = qg.shape[0] // 2
    frame = lax.axis_index("tm")
    grad[...] = jnp.zeros_like(grad)
    for slab in range(2):
        rows = rows_of(slab, half)
        q, g = qg[rows, KEY], qg[rows, VALUE]
        pieces = listed(relayed, c_kv, lists, frame, slab, block, grad, count=2)
        more = [arrived(swap, kv, frame, slab, block) for swap, kv in zip(far, far_kv)]
        old = load_state((stat, acc), rows)
        peak, total, out = forward_slab(q, pieces + more, block, s_ref, old)
        o = (out / total).astype(BF16)
        o_ref[rows, :] = o
        row_dot = jnp.sum(g.astype(F32) * o.astype(F32), axis=1, keepdims=True)
        lse = peak * EXP_SCALE + jnp.log2(total)
        lane = lax.broadcasted_iota(jnp.int32, out.shape, 1)
        turned = jnp.where(lane == 0, lse, row_dot).T[:8, :]
        row_ref[:, rows] = turned
        dq_ref[rows, :] = backward_slab(q, g, turned[0:1, :], turned[1:2, :], pieces, block)
    dc_ref[...] = grad[...].astype(BF16)


def far_kernel(block, far, *refs):
    n = len(far)
    qg, row_ref, dq_old = refs[:3]
    far_kv = refs[3 : 3 + n]
    grads = refs[3 + n : 3 + 2 * n]
    dq_ref = refs[3 + 2 * n]
    half = qg.shape[0] // 2
    frame = lax.axis_index("tm")
    for slab in range(2):
        rows = rows_of(slab, half)
        q, g = qg[rows, KEY], qg[rows, VALUE]
        pieces = [
            arrived(swap, kv, frame, slab, block, out)
            for swap, kv, out in zip(far, far_kv, grads)
        ]
        lse, row_dot = row_ref[0:1, rows], row_ref[1:2, rows]
        dq_ref[rows, :] = dq_old[rows, :] + backward_slab(q, g, lse, row_dot, pieces, block)


def rest_kernel(block, swaps, lists, o, qg, row_ref, dq_old, kv, a_kv, z_kv, y_kv, *refs):
    near, da, dz, dy, keep, send, grad_a = refs
    half = qg.shape[0] // 2
    frame = lax.axis_index("tm")
    a, z, y = swaps
    near[...] = jnp.zeros_like(near)
    grad_a[...] = jnp.zeros_like(grad_a)
    dz[...] = jnp.zeros_like(dz)
    dy[...] = jnp.zeros_like(dy)
    whole = []
    for slab in range(2):
        rows = rows_of(slab, half)
        q, g = qg[rows, KEY], qg[rows, VALUE]
        pieces = listed(z, z_kv, lists, frame, slab, block, dz)
        pieces += listed(y, y_kv, lists, frame, slab, block, dy)
        pieces += listed(a, a_kv, lists, frame, slab, block, grad_a, count=2)
        pieces += [Piece(kv, r, grad=near, add=True) for r in range(0, 2 * half, block)]
        lse, row_dot = row_ref[0:1, rows], row_ref[1:2, rows]
        dq = dq_old[rows, :] + backward_slab(q, g, lse, row_dot, pieces, block)
        whole.append((dq * SCALE).astype(BF16))
    da[...] = grad_a[...].astype(BF16)

    def body(mine):
        for slab in range(2):
            out = keep if slab == mine else send
            out[:, KEY] = o[rows_of(slab, half), :]
            out[:, VALUE] = whole[slab]

    each_core(body)


def forwards_first(frame):
    return lax.rem(frame, 2) == lax.rem(lax.shift_right_logical(frame, 1), 2)


def relay_kernel(z_kv, y_kv, out):
    first = forwards_first(lax.axis_index("tm"))

    @pl.when(first)
    def _():
        out[...] = z_kv[...]

    @pl.when(jnp.logical_not(first))
    def _():
        out[...] = y_kv[...]


def merge_kernel(dz, dy, came, z_out, y_out):
    first = forwards_first(lax.axis_index("tm"))
    more = came[...].astype(F32)
    z_out[...] = (dz[...] + jnp.where(first, more, 0.0)).astype(BF16)
    y_out[...] = (dy[...] + jnp.where(first, 0.0, more)).astype(BF16)


def gather_kernel(block, swaps, far, *refs):
    n = len(far)
    lists, near, da, dz, dy = refs[:5]
    far_back = refs[5 : 5 + n]
    keep, send, total = refs[5 + n :]
    frame = lax.axis_index("tm")
    half = near.shape[0] // 2
    sums = near[...]
    for swap, came in zip(swaps, (da, dz, dy)):
        _, _, exists = swap.partner(frame)
        sums = sums + jnp.where(exists, came[...].astype(F32), 0.0)
    total[...] = sums
    for swap, came in zip(far, far_back):
        for slab in range(2):
            b, exists = swap.block_of_theirs(lists, frame, slab, 0)
            rows = pl.ds(pl.multiple_of(b * block, block), block)
            part = came[slab * block : (slab + 1) * block, :].astype(F32)
            total[rows, :] += jnp.where(exists, part, 0.0)

    def body(mine):
        keep[...] = total[rows_of(mine, half), :].astype(BF16)
        send[...] = total[rows_of(1 - mine, half), :].astype(BF16)

    each_core(body)


def split_kernel(keep, came, first, second):
    def body(mine):
        for head, source in ((mine, keep), (1 - mine, came)):
            first[:, head_cols(head)] = source[:, KEY]
            second[:, head_cols(head)] = source[:, VALUE]

    each_core(body)


def per_device(queries, key_rows, value_rows, out_grad, block_lists):
    s_dev, width = queries.shape
    count = lax.axis_size("tm")
    block = s_dev // 2
    pair = sds((s_dev, 2 * DH), BF16)
    frame_bf = sds((2 * s_dev, 2 * DH), BF16)
    frame_f32 = sds((2 * s_dev, 2 * DH), F32)
    row_f32 = sds((2 * s_dev, DH), F32)
    levels = count.bit_length() - 1
    near_swap, relayed = Swap(count, 0, False), Swap(count, 0, True)
    z_swap, y_swap = Swap(count, 1, False), Swap(count, 1, True)
    swaps = (near_swap, z_swap, y_swap)
    far = [Swap(count, level, second) for level in range(2, levels) for second in (False, True)]
    far = [swap for swap in far if swap.moves]
    product = 2 * 2 * s_dev * block * DH

    def across(value):
        return lax.ppermute(value, "space", [(0, 1), (1, 0)])

    def swapped(value, swap):
        return lax.ppermute(value, "tm", swap.pairs)

    def scores(n):
        return pltpu.VMEM((n, s_dev, block), F32)

    kv_send, qg_send = call(pack_kernel, (key_rows, value_rows, queries, out_grad), [pair, pair])
    kv_came = across(kv_send)
    kv, *far_send = call(
        functools.partial(frame_kernel, far, block),
        (block_lists, key_rows, value_rows, kv_came),
        [frame_bf] + [pair] * len(far),
    )
    a_kv = swapped(kv, near_swap)
    z_kv = swapped(kv, z_swap)
    y_kv = swapped(kv, y_swap)
    (qg,) = call(join_kernel, (queries, out_grad, across(qg_send)), [frame_bf])
    stat, acc = call(
        functools.partial(near_kernel, block),
        (qg, kv),
        [row_f32, row_f32],
        scratch=[scores(4)],
        flops=2 * 4 * 2 * product,
    )
    z_kv, y_kv, stat = lax.optimization_barrier((z_kv, y_kv, stat))
    (relay,) = call(relay_kernel, (z_kv, y_kv), [frame_bf])
    relay, far_send = lax.optimization_barrier((relay, far_send))
    c_kv = swapped(relay, near_swap)
    far_kv = [swapped(value, swap) for value, swap in zip(far_send, far)]
    stat, acc = call(
        functools.partial(middle_kernel, block, swaps),
        (block_lists, qg, stat, acc, a_kv, z_kv, y_kv),
        [row_f32, row_f32],
        scratch=[scores(4)],
        flops=2 * 4 * 2 * product,
    )
    o, row_stat, dc, dq = call(
        functools.partial(last_kernel, block, relayed, far),
        (block_lists, qg, stat, acc, c_kv, *far_kv),
        [sds((2 * s_dev, DH), BF16), sds((8, 2 * s_dev), F32), frame_bf, row_f32],
        scratch=[scores(2 + len(far)), pltpu.VMEM((2 * s_dev, 2 * DH), F32)],
        flops=2 * ((2 + len(far)) * 2 + 10) * product,
    )
    dc_came = swapped(dc, near_swap)
    *far_grad, dq = call(
        functools.partial(far_kernel, block, far),
        (qg, row_stat, dq, *far_kv),
        [pair] * len(far) + [row_f32],
        flops=2 * 5 * len(far) * product,
    )
    far_back = [swapped(value, swap) for value, swap in zip(far_grad, far)]
    near, da, dz, dy, keep, send = call(
        functools.partial(rest_kernel, block, swaps),
        (block_lists, o, qg, row_stat, dq, kv, a_kv, z_kv, y_kv),
        [frame_f32, frame_bf, frame_f32, frame_f32, pair, pair],
        scratch=[pltpu.VMEM((2 * s_dev, 2 * DH), F32)],
        flops=2 * 8 * 5 * product,
    )
    dc_came, far_back = lax.optimization_barrier((dc_came, far_back))
    dz, dy = call(merge_kernel, (dz, dy, dc_came), [frame_bf, frame_bf])
    dz, dy, da = lax.optimization_barrier((dz, dy, da))
    dz_came = swapped(dz, z_swap)
    dy_came = swapped(dy, y_swap)
    da_came = swapped(da, near_swap)
    half_rows = sds((s_dev, width), BF16)
    attn_out, grad_q = call(split_kernel, (keep, across(send)), [half_rows, half_rows])
    keep, send = call(
        functools.partial(gather_kernel, block, swaps, far),
        (block_lists, near, da_came, dz_came, dy_came, *far_back),
        [pair, pair],
        scratch=[pltpu.VMEM((2 * s_dev, 2 * DH), F32)],
    )
    grad_k, grad_v = call(split_kernel, (keep, across(send)), [half_rows, half_rows])
    return attn_out, grad_q, grad_k, grad_v


def solution(mesh):
    rows = P(("groups", "tm", "space"), None)
    return jax.shard_map(
        per_device,
        mesh=mesh,
        in_specs=(rows, rows, rows, rows, P("groups", None)),
        out_specs=(rows, rows, rows, rows),
        check_vma=False,
    )
```

```python
import functools
import math

import jax
import jax.numpy as jnp
from jax import lax
from jax.experimental import pallas as pl
from jax.experimental.pallas import tpu as pltpu
from jax.sharding import PartitionSpec as P

DH = 128
F32 = jnp.float32
BF16 = jnp.bfloat16
VMEM = pl.BlockSpec(memory_space=pltpu.VMEM)
SMEM = pl.BlockSpec(memory_space=pltpu.SMEM)
HBM = pl.BlockSpec(memory_space=pltpu.HBM)
NEG = -1e30
SCALE = 1.0 / math.sqrt(DH)
EXP_SCALE = SCALE * math.log2(math.e)
KEY = slice(0, DH)
VALUE = slice(DH, 2 * DH)
sds = jax.ShapeDtypeStruct


def dot_nn(a, b):
    return lax.dot_general(a, b, (((1,), (0,)), ((), ())), preferred_element_type=F32)


def dot_nt(a, b):
    return lax.dot_general(a, b, (((1,), (1,)), ((), ())), preferred_element_type=F32)


def dot_tn(a, b):
    return lax.dot_general(a, b, (((0,), (0,)), ((), ())), preferred_element_type=F32)


def call(kernel, args, out_shape, scratch=(), flops=0, source=VMEM):
    return pl.pallas_call(
        kernel,
        out_shape=out_shape,
        in_specs=[SMEM if a.dtype == jnp.int32 else source for a in args],
        out_specs=tuple(VMEM for _ in out_shape),
        scratch_shapes=list(scratch),
        compiler_params=pltpu.CompilerParams(vmem_limit_bytes=40 << 20),
        cost_estimate=pl.CostEstimate(flops=flops // 1000, bytes_accessed=1024, transcendentals=0),
    )(*args)


def swap_pairs(count, distance, second):
    pairs = []
    for frame in range(count):
        up = ((frame // distance) % 2 == 0) != second
        target = frame + distance if up else frame - distance
        pairs.append((frame, target if 0 <= target < count else frame))
    return pairs


class Swap:
    def __init__(self, count, level, second):
        self.count, self.level, self.second = count, level, second
        self.levels = count.bit_length() - 1
        self.pairs = swap_pairs(count, 1 << level, second)
        self.moves = any(source != target for source, target in self.pairs)

    def partner(self, frame):
        odd = lax.rem(lax.shift_right_logical(frame, self.level), 2)
        later = odd == (1 if self.second else 0)
        other = jnp.where(later, frame + (1 << self.level), frame - (1 << self.level))
        return other, later, jnp.logical_and(other >= 0, other < self.count)

    def slot(self, later, k):
        base = 0 if self.level == 0 else self.level + 1
        return jnp.where(later, self.levels + 1, 0) + base + k

    def block_of_mine(self, lists, frame, slab, k):
        other, later, exists = self.partner(frame)
        entry = lists[frame * 2 + slab, self.slot(later, k)]
        return jnp.clip(entry - other * 4, 0, 3), exists

    def block_of_theirs(self, lists, frame, slab, k):
        other, later, exists = self.partner(frame)
        row = jnp.where(exists, other, frame) * 2 + slab
        entry = lists[row, self.slot(jnp.logical_not(later), k)]
        return jnp.clip(entry - frame * 4, 0, 3), exists


def head_cols(head):
    return slice(head * DH, (head + 1) * DH)


def rows_of(slab, half):
    return slice(slab * half, (slab + 1) * half)


def each_core(body):
    core = lax.axis_index("space")
    for mine in range(2):
        pl.when(core == mine)(functools.partial(body, mine))


def pack_kernel(k, v, q, g, kv_send, kv_own, qg_send, qg_own, sems):
    def body(mine):
        copies = []
        for a, b, send, own in ((k, v, kv_send, kv_own), (q, g, qg_send, qg_own)):
            for head, out in ((1 - mine, send), (mine, own)):
                for source, cols in ((a, KEY), (b, VALUE)):
                    sem = sems.at[len(copies)]
                    copies.append(
                        pltpu.make_async_copy(source.at[:, head_cols(head)], out.at[:, cols], sem)
                    )
        for copy in copies:
            copy.start()
        for copy in copies:
            copy.wait()

    each_core(body)


def frame_kernel(own, came, kv, keys, values):
    half = own.shape[0]

    def body(mine):
        for slab, source in ((mine, own), (1 - mine, came)):
            rows = rows_of(slab, half)
            part = source[...]
            kv[rows, :] = part
            keys[rows, :] = part[:, KEY]
            values[rows, :] = part[:, VALUE]

    each_core(body)


def join_kernel(own, came, out):
    half = own.shape[0]

    def body(mine):
        out[rows_of(mine, half), :] = own[...]
        out[rows_of(1 - mine, half), :] = came[...]

    each_core(body)


def select_kernel(far, block, lists, kv, *sends):
    frame = lax.axis_index("tm")
    for swap, send in zip(far, sends):
        for slab in range(2):
            b, _ = swap.block_of_theirs(lists, frame, slab, 0)
            row = pl.multiple_of(b * block, block)
            send[slab * block : (slab + 1) * block, :] = kv[pl.ds(row, block), :]


def forwards_first(frame):
    return lax.rem(frame, 2) == lax.rem(lax.shift_right_logical(frame, 1), 2)


def relay_kernel(z, y, out):
    first = forwards_first(lax.axis_index("tm"))

    @pl.when(first)
    def _():
        out[...] = z[...]

    @pl.when(jnp.logical_not(first))
    def _():
        out[...] = y[...]


class Piece:
    def __init__(self, k, v, row, exists=None, dk=None, dv=None, add=True):
        self.k_at, self.v_at, self.row, self.exists = k, v, row, exists
        self.dk, self.dv, self.add = dk, dv, add

    def load(self, at, block):
        ref, cols = at
        return ref[pl.ds(self.row, block), cols]

    def k(self, block):
        return self.load(self.k_at, block)

    def v(self, block):
        return self.load(self.v_at, block)

    def store(self, at, block, value):
        ref, cols = at
        rows = pl.ds(self.row, block)
        if self.add:
            ref[rows, cols] += value
        else:
            ref[rows, cols] = value.astype(ref.dtype)


def listed(swap, lists, frame, slab, block, k, v, count=1, **grads):
    pieces = []
    for n in range(count):
        b, exists = swap.block_of_mine(lists, frame, slab, n)
        pieces.append(Piece(k, v, pl.multiple_of(b * block, block), exists, **grads))
    return pieces


def arrived(swap, frame, slab, block, kv, **grads):
    _, _, exists = swap.partner(frame)
    return Piece((kv, KEY), (kv, VALUE), slab * block, exists, add=False, **grads)


def score_pieces(q, pieces, block, s_ref, peak):
    top = None
    for j, piece in enumerate(pieces):
        s = dot_nt(q, piece.k(block))
        s_ref[j] = s
        part = s[:, :DH]
        for c in range(DH, block, DH):
            part = jnp.maximum(part, s[:, c : c + DH])
        if piece.exists is not None:
            part = jnp.where(piece.exists, part, NEG)
        top = part if top is None else jnp.maximum(top, part)
    top = jnp.max(top, axis=1, keepdims=True)
    return top if peak is None else jnp.maximum(peak, top)


def raise_pieces(pieces, block, s_ref, peak, with_values):
    total = None
    acc = None
    for j, piece in enumerate(pieces):
        base = peak * EXP_SCALE
        if piece.exists is not None:
            base = jnp.where(piece.exists, base, -NEG)
        e = jnp.exp2(s_ref[j] * EXP_SCALE - base)
        for c in range(0, block, DH):
            part = e[:, c : c + DH]
            total = part if total is None else total + part
        if j < with_values:
            out = dot_nn(e.astype(BF16), piece.v(block))
            acc = out if acc is None else acc + out
    return jnp.sum(total, axis=1, keepdims=True), acc


def merge_state(old, peak, total, acc):
    shrink = jnp.exp2((old[0] - peak) * EXP_SCALE)
    total = total + old[1] * shrink
    return total, old[2] * shrink + acc


def probs(piece, q, lse, block):
    if piece.exists is not None:
        lse = jnp.where(piece.exists, lse, -NEG)
    return jnp.exp2(dot_nt(piece.k(block), q) * EXP_SCALE - lse)


def backward_slab(q, g, lse, row_dot, pieces, block, with_dq=True):
    dq = None
    for piece in pieces:
        p = probs(piece, q, lse, block)
        if piece.dv is not None:
            piece.store(piece.dv, block, dot_nn(p.astype(BF16), g))
        ds = (p * (dot_nt(piece.v(block), g) - row_dot)).astype(BF16)
        if piece.dk is not None:
            piece.store(piece.dk, block, dot_nn(ds, q) * SCALE)
        if with_dq:
            part = dot_tn(ds, piece.k(block))
            dq = part if dq is None else dq + part
    return dq


def store_state(refs, rows, peak, total, acc):
    stat, acc_ref = refs
    lane = lax.broadcasted_iota(jnp.int32, acc.shape, 1)
    stat[rows, :] = jnp.where(lane == 0, peak, total)
    acc_ref[rows, :] = acc


def load_state(refs, rows):
    stat, acc_ref = refs
    return stat[rows, 0:1], stat[rows, 1:2], acc_ref[rows, :]


ALL = slice(None)


def near_kernel(block, qg, kv, stat, acc, s_ref):
    half = qg.shape[0] // 2
    for slab in range(2):
        rows = rows_of(slab, half)
        pieces = [Piece((kv, KEY), (kv, VALUE), r) for r in range(0, 2 * half, block)]
        peak = score_pieces(qg[rows, KEY], pieces, block, s_ref, None)
        total, out = raise_pieces(pieces, block, s_ref, peak, len(pieces))
        store_state((stat, acc), rows, peak, total, out)


def middle_kernel(
    block, swaps, lists, qg, stat, acc, a_kv, z_k, y_k, z_v, y_v, stat2, acc2, s_ref
):
    half = qg.shape[0] // 2
    frame = lax.axis_index("tm")
    a, z, y = swaps
    for slab in range(2):
        rows = rows_of(slab, half)
        pieces = listed(a, lists, frame, slab, block, (a_kv, KEY), (a_kv, VALUE), 2)
        pieces += listed(z, lists, frame, slab, block, (z_k, ALL), (z_v, ALL))
        pieces += listed(y, lists, frame, slab, block, (y_k, ALL), (y_v, ALL))
        old = load_state((stat, acc), rows)
        peak = score_pieces(qg[rows, KEY], pieces, block, s_ref, old[0])
        new = raise_pieces(pieces, block, s_ref, peak, len(pieces))
        store_state((stat2, acc2), rows, peak, *merge_state(old, peak, *new))


def close_kernel(block, relayed, far, *refs):
    n = len(far)
    lists, qg, stat, acc, c_k = refs[:5]
    far_kv = refs[5 : 5 + n]
    lse_ref, part_ref, dc_v = refs[5 + n : 8 + n]
    far_dv = refs[8 + n : 8 + 2 * n]
    s_ref, grad = refs[8 + 2 * n :]
    half = qg.shape[0] // 2
    frame = lax.axis_index("tm")
    grad[...] = jnp.zeros_like(grad)
    for slab in range(2):
        rows = rows_of(slab, half)
        q, g = qg[rows, KEY], qg[rows, VALUE]
        pieces = [
            arrived(swap, frame, slab, block, kv, dv=(out, ALL))
            for swap, kv, out in zip(far, far_kv, far_dv)
        ]
        late = listed(
            relayed, lists, frame, slab, block, (c_k, ALL), None, 2, dv=(grad, ALL)
        )
        old = load_state((stat, acc), rows)
        peak = score_pieces(q, pieces + late, block, s_ref, old[0])
        new = raise_pieces(pieces + late, block, s_ref, peak, n)
        total, out = merge_state(old, peak, *new)
        part_ref[rows, :] = out / total
        lse = jnp.broadcast_to(peak * EXP_SCALE + jnp.log2(total), out.shape).T[:8, :]
        lse_ref[:, rows] = lse
        for piece in late + pieces:
            p = probs(piece, q, lse[0:1, :], block).astype(BF16)
            piece.store(piece.dv, block, dot_nn(p, g))
    dc_v[...] = grad[...].astype(BF16)


def late_kernel(block, relayed, lists, qg, lse_ref, part_ref, c_k, c_v, o_ref, dot_ref, dc_k, grad):
    half = qg.shape[0] // 2
    frame = lax.axis_index("tm")
    grad[...] = jnp.zeros_like(grad)
    for slab in range(2):
        rows = rows_of(slab, half)
        q, g = qg[rows, KEY], qg[rows, VALUE]
        lse = lse_ref[0:1, rows]
        late = listed(
            relayed, lists, frame, slab, block, (c_k, ALL), (c_v, ALL), 2, dk=(grad, ALL)
        )
        out = part_ref[rows, :]
        kept = []
        for piece in late:
            p = probs(piece, q, lse, block)
            kept.append(p)
            out = out + dot_tn(p.astype(BF16), piece.v(block))
        o = out.astype(BF16)
        o_ref[rows, :] = o
        row_dot = jnp.sum(g.astype(F32) * o.astype(F32), axis=1, keepdims=True)
        turned = jnp.broadcast_to(row_dot, out.shape).T[:8, :]
        dot_ref[:, rows] = turned
        for piece, p in zip(late, kept):
            ds = (p * (dot_nt(piece.v(block), g) - turned[0:1, :])).astype(BF16)
            piece.store(piece.dk, block, dot_nn(ds, q) * SCALE)
    dc_k[...] = grad[...].astype(BF16)


def far_kernel(block, far, *refs):
    n = len(far)
    qg, lse_ref, dot_ref = refs[:3]
    far_kv = refs[3 : 3 + n]
    far_dk = refs[3 + n : 3 + 2 * n]
    half = qg.shape[0] // 2
    frame = lax.axis_index("tm")
    for slab in range(2):
        rows = rows_of(slab, half)
        pieces = [
            arrived(swap, frame, slab, block, kv, dk=(out, ALL))
            for swap, kv, out in zip(far, far_kv, far_dk)
        ]
        backward_slab(
            qg[rows, KEY], qg[rows, VALUE], lse_ref[0:1, rows], dot_ref[0:1, rows], pieces, block, False
        )


def second_kernel(
    block, swaps, lists, qg, lse_ref, dot_ref, z_k, y_k, z_v, y_v, dz_k, dy_k, dz_v, dy_v, dq_ref
):
    half = qg.shape[0] // 2
    frame = lax.axis_index("tm")
    _, z, y = swaps
    for ref in (dz_k, dy_k, dz_v, dy_v):
        ref[...] = jnp.zeros_like(ref)
    for slab in range(2):
        rows = rows_of(slab, half)
        pieces = listed(
            z, lists, frame, slab, block, (z_k, ALL), (z_v, ALL), dk=(dz_k, ALL), dv=(dz_v, ALL)
        )
        pieces += listed(
            y, lists, frame, slab, block, (y_k, ALL), (y_v, ALL), dk=(dy_k, ALL), dv=(dy_v, ALL)
        )
        dq_ref[rows, :] = backward_slab(
            qg[rows, KEY], qg[rows, VALUE], lse_ref[0:1, rows], dot_ref[0:1, rows], pieces, block
        )


def first_kernel(block, swaps, lists, qg, lse_ref, dot_ref, dq_old, a_kv, da, dq_ref, grad):
    half = qg.shape[0] // 2
    frame = lax.axis_index("tm")
    grad[...] = jnp.zeros_like(grad)
    for slab in range(2):
        rows = rows_of(slab, half)
        pieces = listed(
            swaps[0], lists, frame, slab, block, (a_kv, KEY), (a_kv, VALUE), 2,
            dk=(grad, KEY), dv=(grad, VALUE),
        )
        dq_ref[rows, :] = dq_old[rows, :] + backward_slab(
            qg[rows, KEY], qg[rows, VALUE], lse_ref[0:1, rows], dot_ref[0:1, rows], pieces, block
        )
    da[...] = grad[...].astype(BF16)


def own_kernel(block, relayed, far, *refs):
    n = len(far)
    lists, qg, lse_ref, dot_ref, dq_old, o, kv, c_k, c_v = refs[:9]
    far_kv = refs[9 : 9 + n]
    near, keep, send = refs[9 + n :]
    half = qg.shape[0] // 2
    frame = lax.axis_index("tm")
    near[...] = jnp.zeros_like(near)
    whole = []
    for slab in range(2):
        rows = rows_of(slab, half)
        pieces = [
            Piece((kv, KEY), (kv, VALUE), r, dk=(near, KEY), dv=(near, VALUE))
            for r in range(0, 2 * half, block)
        ]
        pieces += listed(relayed, lists, frame, slab, block, (c_k, ALL), (c_v, ALL), 2)
        pieces += [arrived(swap, frame, slab, block, ref) for swap, ref in zip(far, far_kv)]
        dq = dq_old[rows, :] + backward_slab(
            qg[rows, KEY], qg[rows, VALUE], lse_ref[0:1, rows], dot_ref[0:1, rows], pieces, block
        )
        whole.append((dq * SCALE).astype(BF16))

    def body(mine):
        for slab in range(2):
            out = keep if slab == mine else send
            out[:, KEY] = o[rows_of(slab, half), :]
            out[:, VALUE] = whole[slab]

    each_core(body)


def merge_kernel(dz, dy, came, z_out, y_out):
    first = forwards_first(lax.axis_index("tm"))
    more = came[...].astype(F32)
    z_out[...] = (dz[...] + jnp.where(first, more, 0.0)).astype(BF16)
    y_out[...] = (dy[...] + jnp.where(first, 0.0, more)).astype(BF16)


def place_kernel(block, far, *refs):
    n = len(far)
    lists, near = refs[:2]
    far_dk, far_dv = refs[2 : 2 + n], refs[2 + n : 2 + 2 * n]
    sum_k, sum_v = refs[2 + 2 * n :]
    frame = lax.axis_index("tm")
    sum_k[...] = near[:, KEY]
    sum_v[...] = near[:, VALUE]
    for j, swap in enumerate(far):
        for slab in range(2):
            b, exists = swap.block_of_theirs(lists, frame, slab, 0)
            rows = pl.ds(pl.multiple_of(b * block, block), block)
            for came, out in ((far_dk[j], sum_k), (far_dv[j], sum_v)):
                part = came[slab * block : (slab + 1) * block, :].astype(F32)
                out[rows, :] += jnp.where(exists, part, 0.0)


def gather_kernel(swaps, cols, near, da, dz, dy, keep, send):
    frame = lax.axis_index("tm")
    half = near.shape[0] // 2
    there = [swap.partner(frame)[2] for swap in swaps]

    def body(mine):
        for slab, out in ((mine, keep), (1 - mine, send)):
            rows = rows_of(slab, half)
            total = near[rows, :]
            for exists, part in zip(there, (da[rows, cols], dz[rows, :], dy[rows, :])):
                total = total + jnp.where(exists, part.astype(F32), 0.0)
            out[...] = total.astype(BF16)

    each_core(body)


def heads_kernel(keep, came, out):
    def body(mine):
        out[:, head_cols(mine)] = keep[...]
        out[:, head_cols(1 - mine)] = came[...]

    each_core(body)


def split_kernel(keep, came, first, second):
    def body(mine):
        for head, source in ((mine, keep), (1 - mine, came)):
            first[:, head_cols(head)] = source[:, KEY]
            second[:, head_cols(head)] = source[:, VALUE]

    each_core(body)


def per_device(queries, key_rows, value_rows, out_grad, block_lists):
    s_dev, width = queries.shape
    count = lax.axis_size("tm")
    block = s_dev // 2
    pair = sds((s_dev, 2 * DH), BF16)
    single = sds((s_dev, DH), BF16)
    frame_two = sds((2 * s_dev, 2 * DH), BF16)
    frame_one = sds((2 * s_dev, DH), BF16)
    frame_sum = sds((2 * s_dev, DH), F32)
    stat_row = sds((8, 2 * s_dev), F32)
    levels = count.bit_length() - 1
    near_swap, relayed = Swap(count, 0, False), Swap(count, 0, True)
    z_swap, y_swap = Swap(count, 1, False), Swap(count, 1, True)
    swaps = (near_swap, z_swap, y_swap)
    far = [Swap(count, level, second) for level in range(2, levels) for second in (False, True)]
    far = [swap for swap in far if swap.moves]
    n = len(far)
    product = 2 * 2 * s_dev * block * DH
    grad_one = pltpu.VMEM((2 * s_dev, DH), F32)

    def across(value):
        return lax.ppermute(value, "space", [(0, 1), (1, 0)])

    def swapped(value, swap):
        return lax.ppermute(value, "tm", swap.pairs)

    def scores(pieces):
        return pltpu.VMEM((pieces, s_dev, block), F32)

    kv_send, kv_own, qg_send, qg_own = call(
        pack_kernel,
        (key_rows, value_rows, queries, out_grad),
        [pair] * 4,
        scratch=[pltpu.SemaphoreType.DMA((8,))],
        source=HBM,
    )
    kv, keys, values = call(
        frame_kernel, (kv_own, across(kv_send)), [frame_two, frame_one, frame_one]
    )
    z_k = swapped(keys, z_swap)
    y_k = swapped(keys, y_swap)
    a_kv = swapped(kv, near_swap)
    z_v = swapped(values, z_swap)
    y_v = swapped(values, y_swap)
    far_send = call(functools.partial(select_kernel, far, block), (block_lists, kv), [pair] * n)
    (qg,) = call(join_kernel, (qg_own, across(qg_send)), [frame_two])
    stat, acc = call(
        functools.partial(near_kernel, block),
        (qg, kv),
        [frame_sum, frame_sum],
        scratch=[scores(4)],
        flops=2 * 4 * 2 * product,
    )
    z_k, y_k, stat = lax.optimization_barrier((z_k, y_k, stat))
    (relay_k,) = call(relay_kernel, (z_k, y_k), [frame_one])
    relay_k, far_send = lax.optimization_barrier((relay_k, far_send))
    c_k = swapped(relay_k, near_swap)
    far_kv = [swapped(value, swap) for value, swap in zip(far_send, far)]
    (relay_v,) = call(relay_kernel, (z_v, y_v), [frame_one])
    c_v = swapped(relay_v, near_swap)
    relay_v, stat = lax.optimization_barrier((relay_v, stat))
    stat, acc = call(
        functools.partial(middle_kernel, block, swaps),
        (block_lists, qg, stat, acc, a_kv, z_k, y_k, z_v, y_v),
        [frame_sum, frame_sum],
        scratch=[scores(4)],
        flops=2 * 4 * 2 * product,
    )
    lse, part, dc_v, *far_dv = call(
        functools.partial(close_kernel, block, relayed, far),
        (block_lists, qg, stat, acc, c_k, *far_kv),
        [stat_row, frame_sum, frame_one] + [single] * n,
        scratch=[scores(2 + n), grad_one],
        flops=2 * (2 + n) * 4 * product,
    )
    dc_v_came = swapped(dc_v, near_swap)
    far_dv_came = [swapped(value, swap) for value, swap in zip(far_dv, far)]
    o, row_dot, dc_k = call(
        functools.partial(late_kernel, block, relayed),
        (block_lists, qg, lse, part, c_k, c_v),
        [frame_one, stat_row, frame_one],
        scratch=[grad_one],
        flops=2 * 2 * 4 * product,
    )
    dc_k_came = swapped(dc_k, near_swap)
    far_dk = call(
        functools.partial(far_kernel, block, far),
        (qg, lse, row_dot, *far_kv),
        [single] * n,
        flops=2 * n * 3 * product,
    )
    far_dk_came = [swapped(value, swap) for value, swap in zip(far_dk, far)]
    far_dk, row_dot = lax.optimization_barrier((far_dk, row_dot))
    dz_k, dy_k, dz_v, dy_v, dq = call(
        functools.partial(second_kernel, block, swaps),
        (block_lists, qg, lse, row_dot, z_k, y_k, z_v, y_v),
        [frame_sum] * 5,
        flops=2 * 2 * 5 * product,
    )
    dc_v_came, far_dv_came = lax.optimization_barrier((dc_v_came, far_dv_came))
    dz_v, dy_v = call(merge_kernel, (dz_v, dy_v, dc_v_came), [frame_one, frame_one])
    dz_v_came = swapped(dz_v, z_swap)
    dy_v_came = swapped(dy_v, y_swap)
    dq, dz_v, dy_v = lax.optimization_barrier((dq, dz_v, dy_v))
    da, dq = call(
        functools.partial(first_kernel, block, swaps),
        (block_lists, qg, lse, row_dot, dq, a_kv),
        [frame_two, frame_sum],
        scratch=[pltpu.VMEM((2 * s_dev, 2 * DH), F32)],
        flops=2 * 2 * 5 * product,
    )
    da_came = swapped(da, near_swap)
    dc_k_came, far_dk_came = lax.optimization_barrier((dc_k_came, far_dk_came))
    dz_k, dy_k = call(merge_kernel, (dz_k, dy_k, dc_k_came), [frame_one, frame_one])
    dz_k_came = swapped(dz_k, z_swap)
    dy_k_came = swapped(dy_k, y_swap)
    dq, dz_k, dy_k = lax.optimization_barrier((dq, dz_k, dy_k))
    near, keep, send = call(
        functools.partial(own_kernel, block, relayed, far),
        (block_lists, qg, lse, row_dot, dq, o, kv, c_k, c_v, *far_kv),
        [frame_two_sum(s_dev), pair, pair],
        flops=2 * (4 * 5 + (2 + n) * 3) * product,
    )
    half_rows = sds((s_dev, width), BF16)
    attn_out, grad_q = call(split_kernel, (keep, across(send)), [half_rows, half_rows])
    sum_k, sum_v = call(
        functools.partial(place_kernel, block, far),
        (block_lists, near, *far_dk_came, *far_dv_came),
        [frame_sum, frame_sum],
    )
    outs = []
    for total, cols, dz, dy in (
        (sum_v, VALUE, dz_v_came, dy_v_came),
        (sum_k, KEY, dz_k_came, dy_k_came),
    ):
        keep, send = call(
            functools.partial(gather_kernel, swaps, cols),
            (total, da_came, dz, dy),
            [single, single],
        )
        outs += call(heads_kernel, (keep, across(send)), [half_rows])
    grad_v, grad_k = outs
    return attn_out, grad_q, grad_k, grad_v


def frame_two_sum(s_dev):
    return sds((2 * s_dev, 2 * DH), F32)


def solution(mesh):
    rows = P(("groups", "tm", "space"), None)
    return jax.shard_map(
        per_device,
        mesh=mesh,
        in_specs=(rows, rows, rows, rows, P("groups", None)),
        out_specs=(rows, rows, rows, rows),
        check_vma=False,
    )
```

```python
import functools
import math

import jax
import jax.numpy as jnp
from jax import lax
from jax.experimental import pallas as pl
from jax.experimental.pallas import tpu as pltpu
from jax.sharding import PartitionSpec as P

DH = 128
F32 = jnp.float32
BF16 = jnp.bfloat16
VMEM = pl.BlockSpec(memory_space=pltpu.VMEM)
SMEM = pl.BlockSpec(memory_space=pltpu.SMEM)
HBM = pl.BlockSpec(memory_space=pltpu.HBM)
NEG = -1e30
SCALE = 1.0 / math.sqrt(DH)
EXP_SCALE = SCALE * math.log2(math.e)
KEY = slice(0, DH)
VALUE = slice(DH, 2 * DH)
sds = jax.ShapeDtypeStruct


def dot_nn(a, b):
    return lax.dot_general(a, b, (((1,), (0,)), ((), ())), preferred_element_type=F32)


def dot_nt(a, b):
    return lax.dot_general(a, b, (((1,), (1,)), ((), ())), preferred_element_type=F32)


def dot_tn(a, b):
    return lax.dot_general(a, b, (((0,), (0,)), ((), ())), preferred_element_type=F32)


def call(kernel, args, out_shape, scratch=(), flops=0, source=VMEM):
    return pl.pallas_call(
        kernel,
        out_shape=out_shape,
        in_specs=[SMEM if a.dtype == jnp.int32 else source for a in args],
        out_specs=tuple(VMEM for _ in out_shape),
        scratch_shapes=list(scratch),
        compiler_params=pltpu.CompilerParams(vmem_limit_bytes=40 << 20),
        cost_estimate=pl.CostEstimate(flops=flops // 1000, bytes_accessed=1024, transcendentals=0),
    )(*args)


def swap_pairs(count, distance, second):
    pairs = []
    for frame in range(count):
        up = ((frame // distance) % 2 == 0) != second
        target = frame + distance if up else frame - distance
        pairs.append((frame, target if 0 <= target < count else frame))
    return pairs


class Swap:
    def __init__(self, count, level, second):
        self.count, self.level, self.second = count, level, second
        self.levels = count.bit_length() - 1
        self.pairs = swap_pairs(count, 1 << level, second)
        self.moves = any(source != target for source, target in self.pairs)

    def partner(self, frame):
        odd = lax.rem(lax.shift_right_logical(frame, self.level), 2)
        later = odd == (1 if self.second else 0)
        other = jnp.where(later, frame + (1 << self.level), frame - (1 << self.level))
        return other, later, jnp.logical_and(other >= 0, other < self.count)

    def slot(self, later, k):
        base = 0 if self.level == 0 else self.level + 1
        return jnp.where(later, self.levels + 1, 0) + base + k

    def block_of_mine(self, lists, frame, slab, k):
        other, later, exists = self.partner(frame)
        entry = lists[frame * 2 + slab, self.slot(later, k)]
        return jnp.clip(entry - other * 4, 0, 3), exists

    def block_of_theirs(self, lists, frame, slab, k):
        other, later, exists = self.partner(frame)
        row = jnp.where(exists, other, frame) * 2 + slab
        entry = lists[row, self.slot(jnp.logical_not(later), k)]
        return jnp.clip(entry - frame * 4, 0, 3), exists


def head_cols(head):
    return slice(head * DH, (head + 1) * DH)


def rows_of(slab, half):
    return slice(slab * half, (slab + 1) * half)


def each_core(body):
    core = lax.axis_index("space")
    for mine in range(2):
        pl.when(core == mine)(functools.partial(body, mine))


def pack_kernel(k, v, q, g, kv_send, kv_own, qg_send, qg_own, sems):
    def body(mine):
        copies = []
        for a, b, send, own in ((k, v, kv_send, kv_own), (q, g, qg_send, qg_own)):
            for head, out in ((1 - mine, send), (mine, own)):
                for source, cols in ((a, KEY), (b, VALUE)):
                    sem = sems.at[len(copies)]
                    copies.append(
                        pltpu.make_async_copy(source.at[:, head_cols(head)], out.at[:, cols], sem)
                    )
        for copy in copies:
            copy.start()
        for copy in copies:
            copy.wait()

    each_core(body)


def frame_kernel(own, came, kv, keys, values):
    half = own.shape[0]

    def body(mine):
        for slab, source in ((mine, own), (1 - mine, came)):
            rows = rows_of(slab, half)
            part = source[...]
            kv[rows, :] = part
            keys[rows, :] = part[:, KEY]
            values[rows, :] = part[:, VALUE]

    each_core(body)


def select_kernel(far, block, lists, kv, *sends):
    frame = lax.axis_index("tm")
    for swap, send in zip(far, sends):
        for slab in range(2):
            b, _ = swap.block_of_theirs(lists, frame, slab, 0)
            row = pl.multiple_of(b * block, block)
            send[slab * block : (slab + 1) * block, :] = kv[pl.ds(row, block), :]


def forwards_first(frame):
    return lax.rem(frame, 2) == lax.rem(lax.shift_right_logical(frame, 1), 2)


def relay_kernel(z, y, out):
    first = forwards_first(lax.axis_index("tm"))

    @pl.when(first)
    def _():
        out[...] = z[...]

    @pl.when(jnp.logical_not(first))
    def _():
        out[...] = y[...]


class Piece:
    def __init__(self, k, v, row, size, exists=None, dk=None, dv=None, add=True):
        self.k_at, self.v_at, self.exists = k, v, exists
        self.rows, self.size = pl.ds(row, size), size
        self.dk, self.dv, self.add = dk, dv, add

    def store(self, at, value):
        ref, cols = at
        if self.add:
            ref[self.rows, cols] += value
        else:
            ref[self.rows, cols] = value.astype(ref.dtype)


def stack(parts):
    return parts[0] if len(parts) == 1 else jnp.concatenate(parts, axis=0)


def keys_of(group):
    return stack([p.k_at[0][p.rows, p.k_at[1]] for p in group])


def values_of(group):
    return stack([p.v_at[0][p.rows, p.v_at[1]] for p in group])


def by_piece(group, value):
    at = 0
    for piece in group:
        yield piece, value[at : at + piece.size, :]
        at += piece.size


def store_grads(group, value, name):
    for piece, part in by_piece(group, value):
        piece.store(getattr(piece, name), part)


def listed(swap, lists, frame, slab, block, k, v, count=1, **grads):
    pieces = []
    for n in range(count):
        b, exists = swap.block_of_mine(lists, frame, slab, n)
        pieces.append(Piece(k, v, pl.multiple_of(b * block, block), block, exists, **grads))
    return pieces


def arrived(swap, frame, slab, block, kv, **grads):
    _, _, exists = swap.partner(frame)
    return Piece((kv, KEY), (kv, VALUE), slab * block, block, exists, add=False, **grads)


def raised(group, s, base):
    parts = []
    for piece, part in by_piece(group, s):
        low = base if piece.exists is None else jnp.where(piece.exists, base, -NEG)
        parts.append(jnp.exp2(part * EXP_SCALE - low))
    return stack(parts)


def score_groups(q, groups, s_ref, peak):
    at = 0
    for group in groups:
        s = dot_nt(keys_of(group), q)
        s_ref[at : at + s.shape[0], :] = s
        at += s.shape[0]
        for piece, part in by_piece(group, s):
            top = jnp.max(part, axis=0, keepdims=True)
            if piece.exists is not None:
                top = jnp.where(piece.exists, top, NEG)
            peak = top if peak is None else jnp.maximum(peak, top)
    return peak


def group_scores(groups, s_ref):
    at = 0
    for group in groups:
        size = sum(piece.size for piece in group)
        yield group, s_ref[at : at + size, :]
        at += size


def forward_slab(q, groups, with_values, s_ref, old):
    peak = score_groups(q, groups, s_ref, None if old is None else old[0])
    total, acc = 0.0, 0.0
    if old is not None:
        shrink = jnp.exp2((old[0] - peak) * EXP_SCALE)
        total, acc = old[1] * shrink, old[2] * shrink
    for j, (group, s) in enumerate(group_scores(groups, s_ref)):
        e = raised(group, s, peak * EXP_SCALE)
        total = total + jnp.sum(e, axis=0, keepdims=True)
        if j < with_values:
            acc = acc + dot_tn(values_of(group), e.astype(BF16))
    return peak, total, acc


def backward_group(q, g, lse, row_dot, group, p=None):
    k = keys_of(group)
    if p is None:
        p = raised(group, dot_nt(k, q), lse)
    if group[0].dv is not None:
        store_grads(group, dot_nn(p.astype(BF16), g), "dv")
    ds = (p * (dot_nt(values_of(group), g) - row_dot)).astype(BF16)
    if group[0].dk is not None:
        store_grads(group, dot_nn(ds, q) * SCALE, "dk")
    return dot_tn(k, ds)


def join_kernel(own, came, out, turned):
    half = own.shape[0]

    def body(mine):
        for slab, source in ((mine, own), (1 - mine, came)):
            rows = rows_of(slab, half)
            out[rows, :] = source[...]
            turned[:, rows] = source[:, VALUE].T

    each_core(body)


ALL = slice(None)


def store_state(refs, rows, peak, total, acc):
    stat, acc_ref = refs
    stat[0:1, rows] = peak
    stat[1:2, rows] = total
    acc_ref[:, rows] = acc


def load_state(refs, rows):
    stat, acc_ref = refs
    return stat[0:1, rows], stat[1:2, rows], acc_ref[:, rows]


def own_groups(kv, half, **grads):
    return [
        [Piece((kv, KEY), (kv, VALUE), r, half, **grads)] for r in range(0, kv.shape[0], half)
    ]


def near_kernel(qg, kv, stat, acc, s_ref):
    half = qg.shape[0] // 2
    for slab in range(2):
        rows = rows_of(slab, half)
        groups = own_groups(kv, half)
        store_state((stat, acc), rows, *forward_slab(qg[rows, KEY], groups, 2, s_ref, None))


def middle_kernel(
    block, swaps, lists, qg, stat, acc, a_kv, z_k, y_k, z_v, y_v, stat2, acc2, s_ref
):
    half = qg.shape[0] // 2
    frame = lax.axis_index("tm")
    a, z, y = swaps
    for slab in range(2):
        rows = rows_of(slab, half)
        at = (lists, frame, slab, block)
        groups = [
            listed(z, *at, (z_k, ALL), (z_v, ALL)) + listed(y, *at, (y_k, ALL), (y_v, ALL)),
            listed(a, *at, (a_kv, KEY), (a_kv, VALUE), 2),
        ]
        old = load_state((stat, acc), rows)
        store_state((stat2, acc2), rows, *forward_slab(qg[rows, KEY], groups, 2, s_ref, old))


def close_kernel(block, relayed, far, *refs):
    n = len(far)
    lists, qg, stat, acc, c_k = refs[:5]
    far_kv = refs[5 : 5 + n]
    lse_ref, part_ref, dc_v, p_ref = refs[5 + n : 9 + n]
    far_dv = refs[9 + n : 9 + 2 * n]
    s_ref, grad = refs[9 + 2 * n :]
    half = qg.shape[0] // 2
    frame = lax.axis_index("tm")
    grad[...] = jnp.zeros_like(grad)
    for slab in range(2):
        rows = rows_of(slab, half)
        q, g = qg[rows, KEY], qg[rows, VALUE]
        groups = [
            [arrived(swap, frame, slab, block, kv, dv=(out, ALL))]
            for swap, kv, out in zip(far, far_kv, far_dv)
        ]
        groups.append(
            listed(relayed, lists, frame, slab, block, (c_k, ALL), None, 2, dv=(grad, ALL))
        )
        old = load_state((stat, acc), rows)
        peak, total, out = forward_slab(q, groups, n, s_ref, old)
        part_ref[:, rows] = out / total
        lse = peak * EXP_SCALE + jnp.log2(total)
        lse_ref[0:1, rows] = lse
        for j, (group, s) in enumerate(group_scores(groups, s_ref)):
            p = raised(group, s, lse)
            store_grads(group, dot_nn(p.astype(BF16), g), "dv")
            if j == n:
                p_ref[slab] = p
    dc_v[...] = grad[...].astype(BF16)


def late_kernel(
    block, relayed, lists, qg, turned, lse_ref, part_ref, p_ref, c_k, c_v,
    o_ref, dot_ref, dc_k, dq_ref, grad,
):
    half = qg.shape[0] // 2
    frame = lax.axis_index("tm")
    grad[...] = jnp.zeros_like(grad)
    for slab in range(2):
        rows = rows_of(slab, half)
        q, g = qg[rows, KEY], qg[rows, VALUE]
        group = listed(
            relayed, lists, frame, slab, block, (c_k, ALL), (c_v, ALL), 2, dk=(grad, ALL)
        )
        p = p_ref[slab]
        o = (part_ref[:, rows] + dot_tn(values_of(group), p.astype(BF16))).astype(BF16)
        o_ref[:, rows] = o
        products = turned[:, rows].astype(F32) * o.astype(F32)
        row_dot = jnp.sum(products, axis=0, keepdims=True)
        dot_ref[0:1, rows] = row_dot
        dq_ref[:, rows] = backward_group(q, g, None, row_dot, group, p)
    dc_k[...] = grad[...].astype(BF16)


def far_kernel(block, far, *refs):
    n = len(far)
    qg, lse_ref, dot_ref, dq_old = refs[:4]
    far_kv = refs[4 : 4 + n]
    far_dk = refs[4 + n : 4 + 2 * n]
    dq_ref = refs[4 + 2 * n]
    half = qg.shape[0] // 2
    frame = lax.axis_index("tm")
    for slab in range(2):
        rows = rows_of(slab, half)
        q, g, lse, row_dot = qg[rows, KEY], qg[rows, VALUE], lse_ref[0:1, rows], dot_ref[0:1, rows]
        dq = dq_old[:, rows]
        for swap, kv, out in zip(far, far_kv, far_dk):
            group = [arrived(swap, frame, slab, block, kv, dk=(out, ALL))]
            dq = dq + backward_group(q, g, lse, row_dot, group)
        dq_ref[:, rows] = dq


def second_kernel(
    block, swaps, lists, qg, lse_ref, dot_ref, dq_old, z_k, y_k, z_v, y_v, dz_k, dy_k, dz_v, dy_v, dq_ref
):
    half = qg.shape[0] // 2
    frame = lax.axis_index("tm")
    _, z, y = swaps
    for ref in (dz_k, dy_k, dz_v, dy_v):
        ref[...] = jnp.zeros_like(ref)
    for slab in range(2):
        rows = rows_of(slab, half)
        q, g, lse, row_dot = qg[rows, KEY], qg[rows, VALUE], lse_ref[0:1, rows], dot_ref[0:1, rows]
        at = (lists, frame, slab, block)
        group = listed(z, *at, (z_k, ALL), (z_v, ALL), dk=(dz_k, ALL), dv=(dz_v, ALL))
        group += listed(y, *at, (y_k, ALL), (y_v, ALL), dk=(dy_k, ALL), dv=(dy_v, ALL))
        dq_ref[:, rows] = dq_old[:, rows] + backward_group(q, g, lse, row_dot, group)


def first_kernel(block, swaps, lists, qg, lse_ref, dot_ref, dq_old, a_kv, da, dq_ref, grad):
    half = qg.shape[0] // 2
    frame = lax.axis_index("tm")
    grad[...] = jnp.zeros_like(grad)
    for slab in range(2):
        rows = rows_of(slab, half)
        q, g, lse, row_dot = qg[rows, KEY], qg[rows, VALUE], lse_ref[0:1, rows], dot_ref[0:1, rows]
        group = listed(
            swaps[0], lists, frame, slab, block, (a_kv, KEY), (a_kv, VALUE), 2,
            dk=(grad, KEY), dv=(grad, VALUE),
        )
        dq_ref[:, rows] = dq_old[:, rows] + backward_group(q, g, lse, row_dot, group)
    da[...] = grad[...].astype(BF16)


def own_kernel(qg, lse_ref, dot_ref, dq_old, o, kv, near, keep, send):
    half = qg.shape[0] // 2
    whole = []
    for slab in range(2):
        rows = rows_of(slab, half)
        q, g, lse, row_dot = qg[rows, KEY], qg[rows, VALUE], lse_ref[0:1, rows], dot_ref[0:1, rows]
        dq = dq_old[:, rows]
        for group in own_groups(kv, half, dk=(near, KEY), dv=(near, VALUE), add=slab > 0):
            dq = dq + backward_group(q, g, lse, row_dot, group)
        whole.append((dq.T * SCALE).astype(BF16))

    def body(mine):
        for slab in range(2):
            out = keep if slab == mine else send
            out[:, KEY] = o[:, rows_of(slab, half)].T
            out[:, VALUE] = whole[slab]

    each_core(body)


def merge_kernel(dz, dy, came, z_out, y_out):
    first = forwards_first(lax.axis_index("tm"))
    more = came[...].astype(F32)
    z_out[...] = (dz[...] + jnp.where(first, more, 0.0)).astype(BF16)
    y_out[...] = (dy[...] + jnp.where(first, 0.0, more)).astype(BF16)


def place_kernel(block, far, *refs):
    n = len(far)
    lists, near = refs[:2]
    far_dk, far_dv = refs[2 : 2 + n], refs[2 + n : 2 + 2 * n]
    sum_k, sum_v = refs[2 + 2 * n :]
    frame = lax.axis_index("tm")
    sum_k[...] = near[:, KEY]
    sum_v[...] = near[:, VALUE]
    for j, swap in enumerate(far):
        for slab in range(2):
            b, exists = swap.block_of_theirs(lists, frame, slab, 0)
            rows = pl.ds(pl.multiple_of(b * block, block), block)
            for came, out in ((far_dk[j], sum_k), (far_dv[j], sum_v)):
                part = came[slab * block : (slab + 1) * block, :].astype(F32)
                out[rows, :] += jnp.where(exists, part, 0.0)


def gather_kernel(swaps, cols, near, da, dz, dy, keep, send):
    frame = lax.axis_index("tm")
    half = near.shape[0] // 2
    there = [swap.partner(frame)[2] for swap in swaps]

    def body(mine):
        for slab, out in ((mine, keep), (1 - mine, send)):
            rows = rows_of(slab, half)
            total = near[rows, :]
            for exists, part in zip(there, (da[rows, cols], dz[rows, :], dy[rows, :])):
                total = total + jnp.where(exists, part.astype(F32), 0.0)
            out[...] = total.astype(BF16)

    each_core(body)


def heads_kernel(keep, came, out):
    def body(mine):
        out[:, head_cols(mine)] = keep[...]
        out[:, head_cols(1 - mine)] = came[...]

    each_core(body)


def split_kernel(keep, came, first, second):
    def body(mine):
        for head, source in ((mine, keep), (1 - mine, came)):
            first[:, head_cols(head)] = source[:, KEY]
            second[:, head_cols(head)] = source[:, VALUE]

    each_core(body)


def per_device(queries, key_rows, value_rows, out_grad, block_lists):
    s_dev, width = queries.shape
    count = lax.axis_size("tm")
    block = s_dev // 2
    pair = sds((s_dev, 2 * DH), BF16)
    single = sds((s_dev, DH), BF16)
    frame_two = sds((2 * s_dev, 2 * DH), BF16)
    frame_one = sds((2 * s_dev, DH), BF16)
    frame_sum = sds((2 * s_dev, DH), F32)
    stat_row = sds((8, 2 * s_dev), F32)
    turned_sum = sds((DH, 2 * s_dev), F32)
    turned_bf = sds((DH, 2 * s_dev), BF16)
    levels = count.bit_length() - 1
    near_swap, relayed = Swap(count, 0, False), Swap(count, 0, True)
    z_swap, y_swap = Swap(count, 1, False), Swap(count, 1, True)
    swaps = (near_swap, z_swap, y_swap)
    far = [Swap(count, level, second) for level in range(2, levels) for second in (False, True)]
    far = [swap for swap in far if swap.moves]
    n = len(far)
    product = 2 * 2 * s_dev * block * DH
    grad_one = pltpu.VMEM((2 * s_dev, DH), F32)

    def across(value):
        return lax.ppermute(value, "space", [(0, 1), (1, 0)])

    def swapped(value, swap):
        return lax.ppermute(value, "tm", swap.pairs)

    def scores(pieces):
        return pltpu.VMEM((pieces * block, s_dev), F32)

    kv_send, kv_own, qg_send, qg_own = call(
        pack_kernel,
        tuple(pltpu.with_memory_space_constraint(a, pltpu.HBM) for a in (key_rows, value_rows, queries, out_grad)),
        [pair] * 4,
        scratch=[pltpu.SemaphoreType.DMA((8,))],
        source=HBM,
    )
    kv, keys, values = call(
        frame_kernel, (kv_own, across(kv_send)), [frame_two, frame_one, frame_one]
    )
    z_k = swapped(keys, z_swap)
    y_k = swapped(keys, y_swap)
    a_kv = swapped(kv, near_swap)
    z_v = swapped(values, z_swap)
    y_v = swapped(values, y_swap)
    far_send = call(functools.partial(select_kernel, far, block), (block_lists, kv), [pair] * n)
    qg, turned = call(join_kernel, (qg_own, across(qg_send)), [frame_two, turned_bf])
    stat, acc = call(
        near_kernel,
        (qg, kv),
        [stat_row, turned_sum],
        scratch=[scores(4)],
        flops=2 * 4 * 2 * product,
    )
    z_k, y_k, stat = lax.optimization_barrier((z_k, y_k, stat))
    (relay_k,) = call(relay_kernel, (z_k, y_k), [frame_one])
    relay_k, far_send = lax.optimization_barrier((relay_k, far_send))
    c_k = swapped(relay_k, near_swap)
    far_kv = [swapped(value, swap) for value, swap in zip(far_send, far)]
    (relay_v,) = call(relay_kernel, (z_v, y_v), [frame_one])
    c_v = swapped(relay_v, near_swap)
    relay_v, stat = lax.optimization_barrier((relay_v, stat))
    stat, acc = call(
        functools.partial(middle_kernel, block, swaps),
        (block_lists, qg, stat, acc, a_kv, z_k, y_k, z_v, y_v),
        [stat_row, turned_sum],
        scratch=[scores(4)],
        flops=2 * 4 * 2 * product,
    )
    lse, part, dc_v, probs, *far_dv = call(
        functools.partial(close_kernel, block, relayed, far),
        (block_lists, qg, stat, acc, c_k, *far_kv),
        [stat_row, turned_sum, frame_one, sds((2, s_dev, s_dev), F32)] + [single] * n,
        scratch=[scores(2 + n), grad_one],
        flops=2 * (2 + n) * 4 * product,
    )
    dc_v_came = swapped(dc_v, near_swap)
    far_dv_came = [swapped(value, swap) for value, swap in zip(far_dv, far)]
    o, row_dot, dc_k, dq = call(
        functools.partial(late_kernel, block, relayed),
        (block_lists, qg, turned, lse, part, probs, c_k, c_v),
        [turned_bf, stat_row, frame_one, turned_sum],
        scratch=[grad_one],
        flops=2 * 2 * 4 * product,
    )
    dc_k_came = swapped(dc_k, near_swap)
    *far_dk, dq = call(
        functools.partial(far_kernel, block, far),
        (qg, lse, row_dot, dq, *far_kv),
        [single] * n + [turned_sum],
        flops=2 * n * 3 * product,
    )
    far_dk_came = [swapped(value, swap) for value, swap in zip(far_dk, far)]
    dz_k, dy_k, dz_v, dy_v, dq = call(
        functools.partial(second_kernel, block, swaps),
        (block_lists, qg, lse, row_dot, dq, z_k, y_k, z_v, y_v),
        [frame_sum] * 4 + [turned_sum],
        flops=2 * 2 * 5 * product,
    )
    dc_v_came, far_dv_came = lax.optimization_barrier((dc_v_came, far_dv_came))
    dz_v, dy_v = call(merge_kernel, (dz_v, dy_v, dc_v_came), [frame_one, frame_one])
    dz_v_came = swapped(dz_v, z_swap)
    dy_v_came = swapped(dy_v, y_swap)
    dq, dz_v, dy_v = lax.optimization_barrier((dq, dz_v, dy_v))
    da, dq = call(
        functools.partial(first_kernel, block, swaps),
        (block_lists, qg, lse, row_dot, dq, a_kv),
        [frame_two, turned_sum],
        scratch=[pltpu.VMEM((2 * s_dev, 2 * DH), F32)],
        flops=2 * 2 * 5 * product,
    )
    da_came = swapped(da, near_swap)
    dc_k_came, far_dk_came = lax.optimization_barrier((dc_k_came, far_dk_came))
    dz_k, dy_k = call(merge_kernel, (dz_k, dy_k, dc_k_came), [frame_one, frame_one])
    dz_k_came = swapped(dz_k, z_swap)
    dy_k_came = swapped(dy_k, y_swap)
    dq, dz_k, dy_k = lax.optimization_barrier((dq, dz_k, dy_k))
    near, keep, send = call(
        own_kernel,
        (qg, lse, row_dot, dq, o, kv),
        [sds((2 * s_dev, 2 * DH), F32), pair, pair],
        flops=2 * 4 * 5 * product,
    )
    half_rows = sds((s_dev, width), BF16)
    attn_out, grad_q = call(split_kernel, (keep, across(send)), [half_rows, half_rows])
    sum_k, sum_v = call(
        functools.partial(place_kernel, block, far),
        (block_lists, near, *far_dk_came, *far_dv_came),
        [frame_sum, frame_sum],
    )
    outs = []
    for total, cols, dz, dy in (
        (sum_v, VALUE, dz_v_came, dy_v_came),
        (sum_k, KEY, dz_k_came, dy_k_came),
    ):
        keep, send = call(
            functools.partial(gather_kernel, swaps, cols),
            (total, da_came, dz, dy),
            [single, single],
        )
        outs += call(heads_kernel, (keep, across(send)), [half_rows])
    grad_v, grad_k = outs
    return attn_out, grad_q, grad_k, grad_v


def solution(mesh):
    rows = P(("groups", "tm", "space"), None)
    return jax.shard_map(
        per_device,
        mesh=mesh,
        in_specs=(rows, rows, rows, rows, P("groups", None)),
        out_specs=(rows, rows, rows, rows),
        check_vma=False,
    )
```

```python
import functools
import math

import jax
import jax.numpy as jnp
from jax import lax
from jax.experimental import pallas as pl
from jax.experimental.pallas import tpu as pltpu
from jax.sharding import PartitionSpec as P

DH = 128
F32 = jnp.float32
BF16 = jnp.bfloat16
VMEM = pl.BlockSpec(memory_space=pltpu.VMEM)
SMEM = pl.BlockSpec(memory_space=pltpu.SMEM)
HBM = pl.BlockSpec(memory_space=pltpu.HBM)
NEG = -1e30
SCALE = 1.0 / math.sqrt(DH)
EXP_SCALE = SCALE * math.log2(math.e)
KEY = slice(0, DH)
VALUE = slice(DH, 2 * DH)
sds = jax.ShapeDtypeStruct


def dot_nn(a, b):
    return lax.dot_general(a, b, (((1,), (0,)), ((), ())), preferred_element_type=F32)


def dot_nt(a, b):
    return lax.dot_general(a, b, (((1,), (1,)), ((), ())), preferred_element_type=F32)


def dot_tn(a, b):
    return lax.dot_general(a, b, (((0,), (0,)), ((), ())), preferred_element_type=F32)


def call(kernel, args, out_shape, scratch=(), source=VMEM, flops=1024):
    return pl.pallas_call(
        kernel,
        out_shape=out_shape,
        in_specs=[SMEM if a.dtype == jnp.int32 else source for a in args],
        out_specs=tuple(VMEM for _ in out_shape),
        scratch_shapes=list(scratch),
        compiler_params=pltpu.CompilerParams(vmem_limit_bytes=40 << 20),
        cost_estimate=pl.CostEstimate(flops=flops, bytes_accessed=1024, transcendentals=0),
    )(*args)


def swap_pairs(count, distance, second):
    pairs = []
    for frame in range(count):
        up = ((frame // distance) % 2 == 0) != second
        target = frame + distance if up else frame - distance
        pairs.append((frame, target if 0 <= target < count else frame))
    return pairs


class Swap:
    def __init__(self, count, level, second):
        self.count, self.level, self.second = count, level, second
        self.levels = count.bit_length() - 1
        self.pairs = swap_pairs(count, 1 << level, second)
        self.moves = any(source != target for source, target in self.pairs)

    def partner(self, frame):
        odd = lax.rem(lax.shift_right_logical(frame, self.level), 2)
        later = odd == (1 if self.second else 0)
        other = jnp.where(later, frame + (1 << self.level), frame - (1 << self.level))
        return other, later, jnp.logical_and(other >= 0, other < self.count)

    def slot(self, later, k):
        base = 0 if self.level == 0 else self.level + 1
        return jnp.where(later, self.levels + 1, 0) + base + k

    def block_of_mine(self, lists, frame, slab, k):
        other, later, exists = self.partner(frame)
        entry = lists[self.slot(later, k), frame * 2 + slab]
        return jnp.clip(entry - other * 4, 0, 3), exists

    def block_of_theirs(self, lists, frame, slab, k):
        other, later, exists = self.partner(frame)
        row = jnp.where(exists, other, frame) * 2 + slab
        entry = lists[self.slot(jnp.logical_not(later), k), row]
        return jnp.clip(entry - frame * 4, 0, 3), exists


def head_cols(head):
    return slice(head * DH, (head + 1) * DH)


def rows_of(slab, half):
    return slice(slab * half, (slab + 1) * half)


def each_core(body):
    core = lax.axis_index("space")
    for mine in range(2):
        pl.when(core == mine)(functools.partial(body, mine))


def pack_kernel(a, b, send, own, sems):
    def body(mine):
        copies = []
        for head, out in ((1 - mine, send), (mine, own)):
            for source, cols in ((a, KEY), (b, VALUE)):
                sem = sems.at[len(copies)]
                copies.append(
                    pltpu.make_async_copy(source.at[:, head_cols(head)], out.at[:, cols], sem)
                )
        for copy in copies:
            copy.start()
        for copy in copies:
            copy.wait()

    each_core(body)


def frame_kernel(own, came, kv, keys, values):
    half = own.shape[0]

    def body(mine):
        for slab, source in ((mine, own), (1 - mine, came)):
            rows = rows_of(slab, half)
            part = source[...]
            kv[rows, :] = part
            keys[rows, :] = part[:, KEY]
            values[rows, :] = part[:, VALUE]

    each_core(body)


def select_kernel(far, block, lists, kv, *sends):
    frame = lax.axis_index("tm")
    for swap, send in zip(far, sends):
        for slab in range(2):
            b, _ = swap.block_of_theirs(lists, frame, slab, 0)
            row = pl.multiple_of(b * block, block)
            send[slab * block : (slab + 1) * block, :] = kv[pl.ds(row, block), :]


def forwards_first(frame):
    return lax.rem(frame, 2) == lax.rem(lax.shift_right_logical(frame, 1), 2)


def relay_kernel(y, z, out):
    first = forwards_first(lax.axis_index("tm"))

    @pl.when(first)
    def _():
        out[...] = z[...]

    @pl.when(jnp.logical_not(first))
    def _():
        out[...] = y[...]


class Piece:
    def __init__(self, k, v, row, size, exists=None, dk=None, dv=None, add=True):
        self.k_at, self.v_at, self.exists = k, v, exists
        self.rows, self.size = pl.ds(row, size), size
        self.dk, self.dv, self.add = dk, dv, add

    def store(self, at, value):
        ref, cols = at
        if self.add:
            ref[self.rows, cols] += value
        else:
            ref[self.rows, cols] = value.astype(ref.dtype)


def stack(parts):
    return parts[0] if len(parts) == 1 else jnp.concatenate(parts, axis=0)


def keys_of(group):
    return stack([p.k_at[0][p.rows, p.k_at[1]] for p in group])


def values_of(group):
    return stack([p.v_at[0][p.rows, p.v_at[1]] for p in group])


def by_piece(group, value):
    at = 0
    for piece in group:
        yield piece, value[at : at + piece.size, :]
        at += piece.size


def store_grads(group, value, name):
    for piece, part in by_piece(group, value):
        piece.store(getattr(piece, name), part)


def listed(swap, lists, frame, slab, block, k, v, count=1, **grads):
    pieces = []
    for n in range(count):
        b, exists = swap.block_of_mine(lists, frame, slab, n)
        pieces.append(Piece(k, v, pl.multiple_of(b * block, block), block, exists, **grads))
    return pieces


def arrived(swap, frame, slab, block, kv, **grads):
    _, _, exists = swap.partner(frame)
    return Piece((kv, KEY), (kv, VALUE), slab * block, block, exists, add=False, **grads)


def raised(group, s, base):
    parts = []
    for piece, part in by_piece(group, s):
        low = base if piece.exists is None else jnp.where(piece.exists, base, -NEG)
        parts.append(jnp.exp2(part * EXP_SCALE - low))
    return stack(parts)


def score_groups(q, groups, s_ref, peak):
    at = 0
    for group in groups:
        s = dot_nt(keys_of(group), q)
        s_ref[at : at + s.shape[0], :] = s
        at += s.shape[0]
        for piece, part in by_piece(group, s):
            top = jnp.max(part, axis=0, keepdims=True)
            if piece.exists is not None:
                top = jnp.where(piece.exists, top, NEG)
            peak = top if peak is None else jnp.maximum(peak, top)
    return peak


def group_scores(groups, s_ref):
    at = 0
    for group in groups:
        size = sum(piece.size for piece in group)
        yield group, s_ref[at : at + size, :]
        at += size


def forward_slab(q, groups, with_values, s_ref, old):
    peak = score_groups(q, groups, s_ref, None if old is None else old[0])
    total, acc = 0.0, 0.0
    if old is not None:
        shrink = jnp.exp2((old[0] - peak) * EXP_SCALE)
        total, acc = old[1] * shrink, old[2] * shrink
    for j, (group, s) in enumerate(group_scores(groups, s_ref)):
        e = raised(group, s, peak * EXP_SCALE)
        total = total + jnp.sum(e, axis=0, keepdims=True)
        if j < with_values:
            acc = acc + dot_tn(values_of(group), e.astype(BF16))
    return peak, total, acc


def backward_group(q, g, lse, row_dot, group, p=None):
    k = keys_of(group)
    if p is None:
        p = raised(group, dot_nt(k, q), lse)
    if group[0].dv is not None:
        store_grads(group, dot_nn(p.astype(BF16), g), "dv")
    ds = (p * (dot_nt(values_of(group), g) - row_dot)).astype(BF16)
    if group[0].dk is not None:
        store_grads(group, dot_nn(ds, q) * SCALE, "dk")
    return dot_tn(k, ds)


def join_kernel(own, came, out, turned):
    half = own.shape[0]

    def body(mine):
        for slab, source in ((mine, own), (1 - mine, came)):
            rows = rows_of(slab, half)
            out[rows, :] = source[...]
            turned[:, rows] = source[:, VALUE].T

    each_core(body)


ALL = slice(None)


def store_state(refs, rows, peak, total, acc):
    stat, acc_ref = refs
    stat[0:1, rows] = peak
    stat[1:2, rows] = total
    acc_ref[:, rows] = acc


def load_state(refs, rows):
    stat, acc_ref = refs
    return stat[0:1, rows], stat[1:2, rows], acc_ref[:, rows]


def own_groups(kv, half, **grads):
    return [
        [Piece((kv, KEY), (kv, VALUE), r, half, **grads)] for r in range(0, kv.shape[0], half)
    ]


def near_kernel(block, swap, lists, qg, kv, a_kv, stat, acc, s_ref):
    half = qg.shape[0] // 2
    frame = lax.axis_index("tm")
    for slab in range(2):
        rows = rows_of(slab, half)
        groups = own_groups(kv, half)
        groups.append(
            listed(swap, lists, frame, slab, block, (a_kv, KEY), (a_kv, VALUE), 2)
        )
        store_state((stat, acc), rows, *forward_slab(qg[rows, KEY], groups, 3, s_ref, None))


def middle_kernel(block, swaps, lists, qg, stat, acc, y_k, z_k, y_v, z_v, stat2, acc2, s_ref):
    half = qg.shape[0] // 2
    frame = lax.axis_index("tm")
    z, y = swaps
    for slab in range(2):
        rows = rows_of(slab, half)
        at = (lists, frame, slab, block)
        group = listed(z, *at, (z_k, ALL), (z_v, ALL)) + listed(y, *at, (y_k, ALL), (y_v, ALL))
        old = load_state((stat, acc), rows)
        store_state((stat2, acc2), rows, *forward_slab(qg[rows, KEY], [group], 1, s_ref, old))


def close_kernel(block, relayed, far, *refs):
    n = len(far)
    lists, qg, stat, acc, c_k = refs[:5]
    far_kv = refs[5 : 5 + n]
    lse_ref, part_ref, dc_v, p_ref, s_ref, grad = refs[5 + n :]
    half = qg.shape[0] // 2
    frame = lax.axis_index("tm")
    grad[...] = jnp.zeros_like(grad)
    for slab in range(2):
        rows = rows_of(slab, half)
        q, g = qg[rows, KEY], qg[rows, VALUE]
        groups = [[arrived(swap, frame, slab, block, kv)] for swap, kv in zip(far, far_kv)]
        groups.append(
            listed(relayed, lists, frame, slab, block, (c_k, ALL), None, 2, dv=(grad, ALL))
        )
        old = load_state((stat, acc), rows)
        peak, total, out = forward_slab(q, groups, n, s_ref, old)
        part_ref[:, rows] = out / total
        lse = peak * EXP_SCALE + jnp.log2(total)
        lse_ref[0:1, rows] = lse
        late, s = list(group_scores(groups, s_ref))[-1]
        p = raised(late, s, lse)
        p_ref[slab] = p
        store_grads(late, dot_nn(p.astype(BF16), g), "dv")
    dc_v[...] = grad[...].astype(BF16)


def late_kernel(block, relayed, far, *refs):
    n = len(far)
    lists, qg, turned, lse_ref, part_ref, p_ref, c_k, c_v = refs[:8]
    far_kv = refs[8 : 8 + n]
    o_ref, dot_ref, dc_k, dq_ref = refs[8 + n : 12 + n]
    far_grad = refs[12 + n : 12 + 2 * n]
    grad = refs[12 + 2 * n]
    half = qg.shape[0] // 2
    frame = lax.axis_index("tm")
    grad[...] = jnp.zeros_like(grad)
    for slab in range(2):
        rows = rows_of(slab, half)
        q, g, lse = qg[rows, KEY], qg[rows, VALUE], lse_ref[0:1, rows]
        group = listed(
            relayed, lists, frame, slab, block, (c_k, ALL), (c_v, ALL), 2, dk=(grad, ALL)
        )
        p = p_ref[slab]
        o = (part_ref[:, rows] + dot_tn(values_of(group), p.astype(BF16))).astype(BF16)
        o_ref[:, rows] = o
        products = turned[:, rows].astype(F32) * o.astype(F32)
        row_dot = jnp.sum(products, axis=0, keepdims=True)
        dot_ref[0:1, rows] = row_dot
        dq = backward_group(q, g, lse, row_dot, group, p)
        for swap, kv, out in zip(far, far_kv, far_grad):
            group = [arrived(swap, frame, slab, block, kv, dk=(out, KEY), dv=(out, VALUE))]
            dq = dq + backward_group(q, g, lse, row_dot, group)
        dq_ref[:, rows] = dq
    dc_k[...] = grad[...].astype(BF16)


def first_kernel(block, swap, lists, qg, lse_ref, dot_ref, dq_old, a_kv, da, dq_ref, grad):
    half = qg.shape[0] // 2
    frame = lax.axis_index("tm")
    grad[...] = jnp.zeros_like(grad)
    for slab in range(2):
        rows = rows_of(slab, half)
        q, g, lse, row_dot = qg[rows, KEY], qg[rows, VALUE], lse_ref[0:1, rows], dot_ref[0:1, rows]
        group = listed(
            swap, lists, frame, slab, block, (a_kv, KEY), (a_kv, VALUE), 2,
            dk=(grad, KEY), dv=(grad, VALUE),
        )
        dq_ref[:, rows] = dq_old[:, rows] + backward_group(q, g, lse, row_dot, group)
    da[...] = grad[...].astype(BF16)


def second_kernel(
    block, swaps, lists, qg, lse_ref, dot_ref, dq_old, came, y_k, z_k, y_v, z_v, dz, dy, dq_ref
):
    half = qg.shape[0] // 2
    frame = lax.axis_index("tm")
    z, y = swaps
    relays = forwards_first(frame)
    more = came[...].astype(F32)
    for ref, takes in ((dz, relays), (dy, jnp.logical_not(relays))):
        ref[:, KEY] = jnp.zeros_like(more)
        ref[:, VALUE] = jnp.where(takes, more, 0.0)
    for slab in range(2):
        rows = rows_of(slab, half)
        q, g, lse, row_dot = qg[rows, KEY], qg[rows, VALUE], lse_ref[0:1, rows], dot_ref[0:1, rows]
        at = (lists, frame, slab, block)
        group = listed(z, *at, (z_k, ALL), (z_v, ALL), dk=(dz, KEY), dv=(dz, VALUE))
        group += listed(y, *at, (y_k, ALL), (y_v, ALL), dk=(dy, KEY), dv=(dy, VALUE))
        dq_ref[:, rows] = dq_old[:, rows] + backward_group(q, g, lse, row_dot, group)


def own_kernel(qg, lse_ref, dot_ref, dq_old, o, kv, placed, near, keep, send):
    half = qg.shape[0] // 2
    near[...] = placed[...]
    whole = []
    for slab in range(2):
        rows = rows_of(slab, half)
        q, g, lse, row_dot = qg[rows, KEY], qg[rows, VALUE], lse_ref[0:1, rows], dot_ref[0:1, rows]
        dq = dq_old[:, rows]
        for group in own_groups(kv, half, dk=(near, KEY), dv=(near, VALUE)):
            dq = dq + backward_group(q, g, lse, row_dot, group)
        whole.append((dq.T * SCALE).astype(BF16))

    def body(mine):
        for slab in range(2):
            out = keep if slab == mine else send
            out[:, KEY] = o[:, rows_of(slab, half)].T
            out[:, VALUE] = whole[slab]

    each_core(body)


def merge_kernel(dz, dy, came, z_out, y_out):
    first = forwards_first(lax.axis_index("tm"))
    more = came[...].astype(F32)
    z_out[:, KEY] = (dz[:, KEY] + jnp.where(first, more, 0.0)).astype(BF16)
    y_out[:, KEY] = (dy[:, KEY] + jnp.where(first, 0.0, more)).astype(BF16)
    z_out[:, VALUE] = dz[:, VALUE].astype(BF16)
    y_out[:, VALUE] = dy[:, VALUE].astype(BF16)


def place_kernel(block, far, *refs):
    lists, total = refs[0], refs[-1]
    frame = lax.axis_index("tm")
    total[...] = jnp.zeros_like(total)
    for swap, came in zip(far, refs[1:-1]):
        for slab in range(2):
            b, exists = swap.block_of_theirs(lists, frame, slab, 0)
            rows = pl.ds(pl.multiple_of(b * block, block), block)
            part = came[slab * block : (slab + 1) * block, :].astype(F32)
            total[rows, :] += jnp.where(exists, part, 0.0)


def gather_kernel(swaps, near, da, dz, dy, keep, send):
    frame = lax.axis_index("tm")
    half = near.shape[0] // 2
    there = [swap.partner(frame)[2] for swap in swaps]

    def body(mine):
        for slab, out in ((1 - mine, send), (mine, keep)):
            rows = rows_of(slab, half)
            total = near[rows, :]
            for exists, part in zip(there, (da, dz, dy)):
                total = total + jnp.where(exists, part[rows, :].astype(F32), 0.0)
            out[...] = total.astype(BF16)

    each_core(body)


def finish_kernel(q_keep, q_came, k_keep, k_came, *outs):
    def body(mine):
        for head, sources in ((mine, (q_keep, k_keep)), (1 - mine, (q_came, k_came))):
            for source, first, second in zip(sources, outs[::2], outs[1::2]):
                first[:, head_cols(head)] = source[:, KEY]
                second[:, head_cols(head)] = source[:, VALUE]

    each_core(body)


def per_device(queries, key_rows, value_rows, out_grad, block_lists):
    s_dev, width = queries.shape
    count = lax.axis_size("tm")
    block = s_dev // 2
    pair = sds((s_dev, 2 * DH), BF16)
    frame_two = sds((2 * s_dev, 2 * DH), BF16)
    frame_one = sds((2 * s_dev, DH), BF16)
    frame_sum = sds((2 * s_dev, 2 * DH), F32)
    stat_row = sds((8, 2 * s_dev), F32)
    turned_sum = sds((DH, 2 * s_dev), F32)
    turned_bf = sds((DH, 2 * s_dev), BF16)
    levels = count.bit_length() - 1
    near_swap, relayed = Swap(count, 0, False), Swap(count, 0, True)
    z_swap, y_swap = Swap(count, 1, False), Swap(count, 1, True)
    swaps = (near_swap, z_swap, y_swap)
    far = [Swap(count, level, second) for level in range(2, levels) for second in (False, True)]
    far = [swap for swap in far if swap.moves]
    n = len(far)
    grad_one = pltpu.VMEM((2 * s_dev, DH), F32)

    def across(value):
        return lax.ppermute(value, "space", [(0, 1), (1, 0)])

    def swapped(value, swap):
        return lax.ppermute(value, "tm", swap.pairs)

    def scores(pieces):
        return pltpu.VMEM((pieces * block, s_dev), F32)

    lists = block_lists.T

    def packed(*pair_in):
        return call(
            pack_kernel,
            tuple(pltpu.with_memory_space_constraint(a, pltpu.HBM) for a in pair_in),
            [pair] * 2,
            scratch=[pltpu.SemaphoreType.DMA((4,))],
            source=HBM,
        )

    kv_send, kv_own = packed(key_rows, value_rows)
    kv_came = across(kv_send)
    qg_send, qg_own = packed(queries, out_grad)
    kv_came, qg_own = lax.optimization_barrier((kv_came, qg_own))
    kv, keys, values = call(
        frame_kernel, (kv_own, kv_came), [frame_two, frame_one, frame_one]
    )
    y_k = swapped(keys, y_swap)
    z_k = swapped(keys, z_swap)
    a_kv = swapped(kv, near_swap)
    y_v = swapped(values, y_swap)
    z_v = swapped(values, z_swap)
    far_send = call(functools.partial(select_kernel, far, block), (lists, kv), [pair] * n)
    qg_came, y_k = lax.optimization_barrier((across(qg_send), y_k))
    work = 4 * s_dev * s_dev * DH
    qg, turned = call(join_kernel, (qg_own, qg_came), [frame_two, turned_bf], flops=20 * work)
    y_k, z_k, turned = lax.optimization_barrier((y_k, z_k, turned))
    (relay_k,) = call(relay_kernel, (y_k, z_k), [frame_one])
    relay_k, far_send = lax.optimization_barrier((relay_k, far_send))
    a_kv, _ = lax.optimization_barrier((a_kv, relay_k))
    c_k = swapped(relay_k, near_swap)
    far_kv = [swapped(value, swap) for value, swap in zip(far_send, far)]
    stat, acc = call(
        functools.partial(near_kernel, block, near_swap),
        (lists, qg, kv, a_kv),
        [stat_row, turned_sum],
        scratch=[scores(6)],
    )
    y_v, z_v, stat = lax.optimization_barrier((y_v, z_v, stat))
    (relay_v,) = call(relay_kernel, (y_v, z_v), [frame_one])
    relay_v, stat = lax.optimization_barrier((relay_v, stat))
    c_v = swapped(relay_v, near_swap)
    stat, acc = call(
        functools.partial(middle_kernel, block, (z_swap, y_swap)),
        (lists, qg, stat, acc, y_k, z_k, y_v, z_v),
        [stat_row, turned_sum],
        scratch=[scores(2)],
    )
    lse, part, dc_v, probs = call(
        functools.partial(close_kernel, block, relayed, far),
        (lists, qg, stat, acc, c_k, *far_kv),
        [stat_row, turned_sum, frame_one, sds((2, s_dev, s_dev), F32)],
        scratch=[scores(2 + n), grad_one],
    )
    dc_v_came = swapped(dc_v, near_swap)
    o, row_dot, dc_k, dq, *far_grad = call(
        functools.partial(late_kernel, block, relayed, far),
        (lists, qg, turned, lse, part, probs, c_k, c_v, *far_kv),
        [turned_bf, stat_row, frame_one, turned_sum] + [pair] * n,
        scratch=[grad_one],
    )
    far_came = [swapped(value, swap) for value, swap in zip(far_grad, far)]
    dc_k_came = swapped(dc_k, near_swap)
    da, dq = call(
        functools.partial(first_kernel, block, near_swap),
        (lists, qg, lse, row_dot, dq, a_kv),
        [frame_two, turned_sum],
        scratch=[pltpu.VMEM((2 * s_dev, 2 * DH), F32)],
    )
    da_came = swapped(da, near_swap)
    dz, dy, dq = call(
        functools.partial(second_kernel, block, (z_swap, y_swap)),
        (lists, qg, lse, row_dot, dq, dc_v_came, y_k, z_k, y_v, z_v),
        [frame_sum, frame_sum, turned_sum],
    )
    dz, dy = call(merge_kernel, (dz, dy, dc_k_came), [frame_two, frame_two])
    dy_came = swapped(dy, y_swap)
    dz_came = swapped(dz, z_swap)
    dq, dz, dy = lax.optimization_barrier((dq, dz, dy))
    (placed,) = call(functools.partial(place_kernel, block, far), (lists, *far_came), [frame_sum])
    near, q_keep, q_send = call(
        own_kernel,
        (qg, lse, row_dot, dq, o, kv, placed),
        [frame_sum, pair, pair],
        flops=40 * work,
    )
    k_keep, k_send = call(
        functools.partial(gather_kernel, swaps),
        (near, da_came, dz_came, dy_came),
        [pair, pair],
    )
    return call(
        finish_kernel,
        (q_keep, across(q_send), k_keep, across(k_send)),
        [sds((s_dev, width), BF16)] * 4,
    )


def solution(mesh):
    rows = P(("groups", "tm", "space"), None)
    return jax.shard_map(
        per_device,
        mesh=mesh,
        in_specs=(rows, rows, rows, rows, P("groups", None)),
        out_specs=(rows, rows, rows, rows),
        check_vma=False,
    )
```

```python
import functools
import math

import jax
import jax.numpy as jnp
from jax import lax
from jax.experimental import pallas as pl
from jax.experimental.pallas import tpu as pltpu
from jax.sharding import PartitionSpec as P

DH = 128
F32 = jnp.float32
BF16 = jnp.bfloat16
VMEM = pl.BlockSpec(memory_space=pltpu.VMEM)
SMEM = pl.BlockSpec(memory_space=pltpu.SMEM)
HBM = pl.BlockSpec(memory_space=pltpu.HBM)
NEG = -1e30
SCALE = 1.0 / math.sqrt(DH)
EXP_SCALE = SCALE * math.log2(math.e)
KEY = slice(0, DH)
VALUE = slice(DH, 2 * DH)
sds = jax.ShapeDtypeStruct


def dot_nn(a, b):
    return lax.dot_general(a, b, (((1,), (0,)), ((), ())), preferred_element_type=F32)


def dot_nt(a, b):
    return lax.dot_general(a, b, (((1,), (1,)), ((), ())), preferred_element_type=F32)


def dot_tn(a, b):
    return lax.dot_general(a, b, (((0,), (0,)), ((), ())), preferred_element_type=F32)


def call(kernel, args, out_shape, scratch=(), source=VMEM, flops=1024):
    return pl.pallas_call(
        kernel,
        out_shape=out_shape,
        in_specs=[SMEM if a.dtype == jnp.int32 else source for a in args],
        out_specs=tuple(VMEM for _ in out_shape),
        scratch_shapes=list(scratch),
        compiler_params=pltpu.CompilerParams(vmem_limit_bytes=40 << 20),
        cost_estimate=pl.CostEstimate(flops=flops, bytes_accessed=1024, transcendentals=0),
    )(*args)


def swap_pairs(count, distance, second):
    pairs = []
    for frame in range(count):
        up = ((frame // distance) % 2 == 0) != second
        target = frame + distance if up else frame - distance
        pairs.append((frame, target if 0 <= target < count else frame))
    return pairs


class Swap:
    def __init__(self, count, level, second):
        self.count, self.level, self.second = count, level, second
        self.levels = count.bit_length() - 1
        self.pairs = swap_pairs(count, 1 << level, second)
        self.moves = any(source != target for source, target in self.pairs)

    def partner(self, frame):
        odd = lax.rem(lax.shift_right_logical(frame, self.level), 2)
        later = odd == (1 if self.second else 0)
        other = jnp.where(later, frame + (1 << self.level), frame - (1 << self.level))
        return other, later, jnp.logical_and(other >= 0, other < self.count)

    def slot(self, later, k):
        base = 0 if self.level == 0 else self.level + 1
        return jnp.where(later, self.levels + 1, 0) + base + k

    def block_of_mine(self, lists, frame, slab, k):
        other, later, exists = self.partner(frame)
        entry = lists[self.slot(later, k), frame * 2 + slab]
        return jnp.clip(entry - other * 4, 0, 3), exists

    def block_of_theirs(self, lists, frame, slab, k):
        other, later, exists = self.partner(frame)
        row = jnp.where(exists, other, frame) * 2 + slab
        entry = lists[self.slot(jnp.logical_not(later), k), row]
        return jnp.clip(entry - frame * 4, 0, 3), exists


def head_cols(head):
    return slice(head * DH, (head + 1) * DH)


def rows_of(slab, half):
    return slice(slab * half, (slab + 1) * half)


def each_core(body):
    core = lax.axis_index("space")
    for mine in range(2):
        pl.when(core == mine)(functools.partial(body, mine))


def pack_kernel(a, b, send, own, sems):
    def body(mine):
        copies = []
        for head, out in ((1 - mine, send), (mine, own)):
            for source, cols in ((a, KEY), (b, VALUE)):
                sem = sems.at[len(copies)]
                copies.append(
                    pltpu.make_async_copy(source.at[:, head_cols(head)], out.at[:, cols], sem)
                )
        for copy in copies:
            copy.start()
        for copy in copies:
            copy.wait()

    each_core(body)


def frame_kernel(own, came, kv, keys, values):
    half = own.shape[0]

    def body(mine):
        for slab, source in ((mine, own), (1 - mine, came)):
            rows = rows_of(slab, half)
            part = source[...]
            kv[rows, :] = part
            keys[rows, :] = part[:, KEY]
            values[rows, :] = part[:, VALUE]

    each_core(body)


def select_kernel(far, block, lists, kv, *sends):
    frame = lax.axis_index("tm")
    for swap, send in zip(far, sends):
        for slab in range(2):
            b, _ = swap.block_of_theirs(lists, frame, slab, 0)
            row = pl.multiple_of(b * block, block)
            send[slab * block : (slab + 1) * block, :] = kv[pl.ds(row, block), :]


def forwards_first(frame):
    return lax.rem(frame, 2) == lax.rem(lax.shift_right_logical(frame, 1), 2)


def relay_kernel(y, z, out):
    first = forwards_first(lax.axis_index("tm"))

    @pl.when(first)
    def _():
        out[...] = z[...]

    @pl.when(jnp.logical_not(first))
    def _():
        out[...] = y[...]


class Piece:
    def __init__(self, k, v, row, size, exists=None, dk=None, dv=None, add=True):
        self.k_at, self.v_at, self.exists = k, v, exists
        self.rows, self.size = pl.ds(row, size), size
        self.dk, self.dv, self.add = dk, dv, add

    def store(self, at, value):
        ref, cols = at
        if self.add:
            ref[self.rows, cols] += value
        else:
            ref[self.rows, cols] = value.astype(ref.dtype)


def stack(parts):
    return parts[0] if len(parts) == 1 else jnp.concatenate(parts, axis=0)


def keys_of(group):
    return stack([p.k_at[0][p.rows, p.k_at[1]] for p in group])


def values_of(group):
    return stack([p.v_at[0][p.rows, p.v_at[1]] for p in group])


def by_piece(group, value):
    at = 0
    for piece in group:
        yield piece, value[at : at + piece.size, :]
        at += piece.size


def store_grads(group, value, name):
    for piece, part in by_piece(group, value):
        piece.store(getattr(piece, name), part)


def listed(swap, lists, frame, slab, block, k, v, count=1, **grads):
    pieces = []
    for n in range(count):
        b, exists = swap.block_of_mine(lists, frame, slab, n)
        pieces.append(Piece(k, v, pl.multiple_of(b * block, block), block, exists, **grads))
    return pieces


def arrived(swap, frame, slab, block, kv, **grads):
    _, _, exists = swap.partner(frame)
    return Piece((kv, KEY), (kv, VALUE), slab * block, block, exists, add=False, **grads)


def raised(group, s, base):
    parts = []
    for piece, part in by_piece(group, s):
        low = base if piece.exists is None else jnp.where(piece.exists, base, -NEG)
        parts.append(jnp.exp2(part * EXP_SCALE - low))
    return stack(parts)


def score_groups(q, groups, s_ref, peak):
    at = 0
    for group in groups:
        s = dot_nt(keys_of(group), q)
        s_ref[at : at + s.shape[0], :] = s
        at += s.shape[0]
        for piece, part in by_piece(group, s):
            top = jnp.max(part, axis=0, keepdims=True)
            if piece.exists is not None:
                top = jnp.where(piece.exists, top, NEG)
            peak = top if peak is None else jnp.maximum(peak, top)
    return peak


def group_scores(groups, s_ref):
    at = 0
    for group in groups:
        size = sum(piece.size for piece in group)
        yield group, s_ref[at : at + size, :]
        at += size


def forward_slab(q, groups, with_values, s_ref, old):
    peak = score_groups(q, groups, s_ref, None if old is None else old[0])
    total, acc = 0.0, 0.0
    if old is not None:
        shrink = jnp.exp2((old[0] - peak) * EXP_SCALE)
        total, acc = old[1] * shrink, old[2] * shrink
    for j, (group, s) in enumerate(group_scores(groups, s_ref)):
        e = raised(group, s, peak * EXP_SCALE)
        total = total + jnp.sum(e, axis=0, keepdims=True)
        if j < with_values:
            acc = acc + dot_tn(values_of(group), e.astype(BF16))
    return peak, total, acc


def backward_group(q, g, lse, row_dot, group, p=None):
    k = keys_of(group)
    if p is None:
        p = raised(group, dot_nt(k, q), lse)
    if group[0].dv is not None:
        store_grads(group, dot_nn(p.astype(BF16), g), "dv")
    ds = (p * (dot_nt(values_of(group), g) - row_dot)).astype(BF16)
    if group[0].dk is not None:
        store_grads(group, dot_nn(ds, q) * SCALE, "dk")
    return dot_tn(k, ds)


def join_kernel(own, came, out, turned):
    half = own.shape[0]

    def body(mine):
        for slab, source in ((mine, own), (1 - mine, came)):
            rows = rows_of(slab, half)
            out[rows, :] = source[...]
            turned[:, rows] = source[:, VALUE].T

    each_core(body)


ALL = slice(None)


def store_state(refs, rows, peak, total, acc):
    stat, acc_ref = refs
    stat[0:1, rows] = peak
    stat[1:2, rows] = total
    acc_ref[:, rows] = acc


def load_state(refs, rows):
    stat, acc_ref = refs
    return stat[0:1, rows], stat[1:2, rows], acc_ref[:, rows]


def own_groups(kv, half, **grads):
    return [
        [Piece((kv, KEY), (kv, VALUE), r, half, **grads)] for r in range(0, kv.shape[0], half)
    ]


def near_kernel(block, swap, lists, qg, kv, a_kv, stat, acc, s_ref):
    half = qg.shape[0] // 2
    frame = lax.axis_index("tm")
    for slab in range(2):
        rows = rows_of(slab, half)
        groups = own_groups(kv, half)
        groups.append(
            listed(swap, lists, frame, slab, block, (a_kv, KEY), (a_kv, VALUE), 2)
        )
        store_state((stat, acc), rows, *forward_slab(qg[rows, KEY], groups, 3, s_ref, None))


def middle_kernel(block, swaps, lists, qg, stat, acc, y_k, z_k, y_v, z_v, stat2, acc2, s_ref):
    half = qg.shape[0] // 2
    frame = lax.axis_index("tm")
    z, y = swaps
    for slab in range(2):
        rows = rows_of(slab, half)
        at = (lists, frame, slab, block)
        group = listed(z, *at, (z_k, ALL), (z_v, ALL)) + listed(y, *at, (y_k, ALL), (y_v, ALL))
        old = load_state((stat, acc), rows)
        store_state((stat2, acc2), rows, *forward_slab(qg[rows, KEY], [group], 1, s_ref, old))


def relayed_kernel(block, relayed, lists, qg, stat, acc, c_k, stat2, acc2, s_ref):
    half = qg.shape[0] // 2
    frame = lax.axis_index("tm")
    for slab in range(2):
        rows = rows_of(slab, half)
        group = listed(relayed, lists, frame, slab, block, (c_k, ALL), None, 2)
        old = load_state((stat, acc), rows)
        new = forward_slab(qg[rows, KEY], [group], 0, s_ref.at[slab], old)
        store_state((stat2, acc2), rows, *new)


def close_kernel(block, far, qg, stat, acc, *refs):
    n = len(far)
    far_kv = refs[:n]
    lse_ref, part_ref = refs[n : n + 2]
    far_dv = refs[n + 2 : 2 * n + 2]
    s_ref = refs[2 * n + 2]
    half = qg.shape[0] // 2
    frame = lax.axis_index("tm")
    for slab in range(2):
        rows = rows_of(slab, half)
        q, g = qg[rows, KEY], qg[rows, VALUE]
        groups = [
            [arrived(swap, frame, slab, block, kv, dv=(out, ALL))]
            for swap, kv, out in zip(far, far_kv, far_dv)
        ]
        old = load_state((stat, acc), rows)
        peak, total, out = forward_slab(q, groups, n, s_ref, old)
        part_ref[:, rows] = out / total
        lse = peak * EXP_SCALE + jnp.log2(total)
        lse_ref[0:1, rows] = lse
        for group, s in group_scores(groups, s_ref):
            p = raised(group, s, lse)
            store_grads(group, dot_nn(p.astype(BF16), g), "dv")


def values_kernel(block, relayed, lists, qg, lse_ref, s_ref, dc_v, p_ref, grad):
    half = qg.shape[0] // 2
    frame = lax.axis_index("tm")
    grad[...] = jnp.zeros_like(grad)
    for slab in range(2):
        rows = rows_of(slab, half)
        group = listed(relayed, lists, frame, slab, block, None, None, 2, dv=(grad, ALL))
        p = raised(group, s_ref[slab], lse_ref[0:1, rows])
        p_ref[slab] = p
        store_grads(group, dot_nn(p.astype(BF16), qg[rows, VALUE]), "dv")
    dc_v[...] = grad[...].astype(BF16)


def late_kernel(block, relayed, far, *refs):
    n = len(far)
    lists, qg, turned, lse_ref, part_ref, p_ref, c_k, c_v = refs[:8]
    far_kv = refs[8 : 8 + n]
    o_ref, dot_ref, dc_k, dq_ref = refs[8 + n : 12 + n]
    far_grad = refs[12 + n : 12 + 2 * n]
    grad = refs[12 + 2 * n]
    half = qg.shape[0] // 2
    frame = lax.axis_index("tm")
    grad[...] = jnp.zeros_like(grad)
    for slab in range(2):
        rows = rows_of(slab, half)
        q, g, lse = qg[rows, KEY], qg[rows, VALUE], lse_ref[0:1, rows]
        group = listed(
            relayed, lists, frame, slab, block, (c_k, ALL), (c_v, ALL), 2, dk=(grad, ALL)
        )
        p = p_ref[slab]
        o = (part_ref[:, rows] + dot_tn(values_of(group), p.astype(BF16))).astype(BF16)
        o_ref[:, rows] = o
        products = turned[:, rows].astype(F32) * o.astype(F32)
        row_dot = jnp.sum(products, axis=0, keepdims=True)
        dot_ref[0:1, rows] = row_dot
        dq = backward_group(q, g, lse, row_dot, group, p)
        for swap, kv, out in zip(far, far_kv, far_grad):
            group = [arrived(swap, frame, slab, block, kv, dk=(out, ALL))]
            dq = dq + backward_group(q, g, lse, row_dot, group)
        dq_ref[:, rows] = dq
    dc_k[...] = grad[...].astype(BF16)


def first_kernel(block, swap, lists, qg, lse_ref, dot_ref, dq_old, a_kv, da, dq_ref, grad):
    half = qg.shape[0] // 2
    frame = lax.axis_index("tm")
    grad[...] = jnp.zeros_like(grad)
    for slab in range(2):
        rows = rows_of(slab, half)
        q, g, lse, row_dot = qg[rows, KEY], qg[rows, VALUE], lse_ref[0:1, rows], dot_ref[0:1, rows]
        group = listed(
            swap, lists, frame, slab, block, (a_kv, KEY), (a_kv, VALUE), 2,
            dk=(grad, KEY), dv=(grad, VALUE),
        )
        dq_ref[:, rows] = dq_old[:, rows] + backward_group(q, g, lse, row_dot, group)
    da[...] = grad[...].astype(BF16)


def second_kernel(
    block, swaps, lists, qg, lse_ref, dot_ref, dq_old, came, y_k, z_k, y_v, z_v, dz, dy, dq_ref
):
    half = qg.shape[0] // 2
    frame = lax.axis_index("tm")
    z, y = swaps
    relays = forwards_first(frame)
    more = came[...].astype(F32)
    for ref, takes in ((dz, relays), (dy, jnp.logical_not(relays))):
        ref[:, KEY] = jnp.zeros_like(more)
        ref[:, VALUE] = jnp.where(takes, more, 0.0)
    for slab in range(2):
        rows = rows_of(slab, half)
        q, g, lse, row_dot = qg[rows, KEY], qg[rows, VALUE], lse_ref[0:1, rows], dot_ref[0:1, rows]
        at = (lists, frame, slab, block)
        group = listed(z, *at, (z_k, ALL), (z_v, ALL), dk=(dz, KEY), dv=(dz, VALUE))
        group += listed(y, *at, (y_k, ALL), (y_v, ALL), dk=(dy, KEY), dv=(dy, VALUE))
        dq_ref[:, rows] = dq_old[:, rows] + backward_group(q, g, lse, row_dot, group)


def own_kernel(qg, lse_ref, dot_ref, dq_old, o, kv, placed, near, keep, send):
    half = qg.shape[0] // 2
    near[...] = placed[...]
    whole = []
    for slab in range(2):
        rows = rows_of(slab, half)
        q, g, lse, row_dot = qg[rows, KEY], qg[rows, VALUE], lse_ref[0:1, rows], dot_ref[0:1, rows]
        dq = dq_old[:, rows]
        for group in own_groups(kv, half, dk=(near, KEY), dv=(near, VALUE)):
            dq = dq + backward_group(q, g, lse, row_dot, group)
        whole.append((dq.T * SCALE).astype(BF16))

    def body(mine):
        for slab in range(2):
            out = keep if slab == mine else send
            out[:, KEY] = o[:, rows_of(slab, half)].T
            out[:, VALUE] = whole[slab]

    each_core(body)


def merge_kernel(dz, dy, came, z_out, y_out):
    first = forwards_first(lax.axis_index("tm"))
    more = came[...].astype(F32)
    z_out[:, KEY] = (dz[:, KEY] + jnp.where(first, more, 0.0)).astype(BF16)
    y_out[:, KEY] = (dy[:, KEY] + jnp.where(first, 0.0, more)).astype(BF16)
    z_out[:, VALUE] = dz[:, VALUE].astype(BF16)
    y_out[:, VALUE] = dy[:, VALUE].astype(BF16)


def place_kernel(block, far, *refs):
    n = len(far)
    lists, total = refs[0], refs[-1]
    frame = lax.axis_index("tm")
    total[...] = jnp.zeros_like(total)
    for swap, came_k, came_v in zip(far, refs[1 : 1 + n], refs[1 + n : -1]):
        for slab in range(2):
            b, exists = swap.block_of_theirs(lists, frame, slab, 0)
            rows = pl.ds(pl.multiple_of(b * block, block), block)
            for came, cols in ((came_k, KEY), (came_v, VALUE)):
                part = came[rows_of(slab, block), :].astype(F32)
                total[rows, cols] += jnp.where(exists, part, 0.0)


def gather_kernel(swaps, near, da, dz, dy, keep, send):
    frame = lax.axis_index("tm")
    half = near.shape[0] // 2
    there = [swap.partner(frame)[2] for swap in swaps]

    def body(mine):
        for slab, out in ((1 - mine, send), (mine, keep)):
            rows = rows_of(slab, half)
            total = near[rows, :]
            for exists, part in zip(there, (da, dz, dy)):
                total = total + jnp.where(exists, part[rows, :].astype(F32), 0.0)
            out[...] = total.astype(BF16)

    each_core(body)


def finish_kernel(q_keep, q_came, k_keep, k_came, *outs):
    def body(mine):
        for head, sources in ((mine, (q_keep, k_keep)), (1 - mine, (q_came, k_came))):
            for source, first, second in zip(sources, outs[::2], outs[1::2]):
                first[:, head_cols(head)] = source[:, KEY]
                second[:, head_cols(head)] = source[:, VALUE]

    each_core(body)


def per_device(queries, key_rows, value_rows, out_grad, block_lists):
    s_dev, width = queries.shape
    count = lax.axis_size("tm")
    block = s_dev // 2
    pair = sds((s_dev, 2 * DH), BF16)
    single = sds((s_dev, DH), BF16)
    frame_two = sds((2 * s_dev, 2 * DH), BF16)
    frame_one = sds((2 * s_dev, DH), BF16)
    frame_sum = sds((2 * s_dev, 2 * DH), F32)
    stat_row = sds((8, 2 * s_dev), F32)
    turned_sum = sds((DH, 2 * s_dev), F32)
    turned_bf = sds((DH, 2 * s_dev), BF16)
    levels = count.bit_length() - 1
    near_swap, relayed = Swap(count, 0, False), Swap(count, 0, True)
    z_swap, y_swap = Swap(count, 1, False), Swap(count, 1, True)
    swaps = (near_swap, z_swap, y_swap)
    far = [Swap(count, level, second) for level in range(2, levels) for second in (False, True)]
    far = [swap for swap in far if swap.moves]
    n = len(far)
    grad_one = pltpu.VMEM((2 * s_dev, DH), F32)

    def across(value):
        return lax.ppermute(value, "space", [(0, 1), (1, 0)])

    def swapped(value, swap):
        return lax.ppermute(value, "tm", swap.pairs)

    def scores(pieces):
        return pltpu.VMEM((pieces * block, s_dev), F32)

    lists = block_lists.T

    def packed(*pair_in):
        return call(
            pack_kernel,
            tuple(pltpu.with_memory_space_constraint(a, pltpu.HBM) for a in pair_in),
            [pair] * 2,
            scratch=[pltpu.SemaphoreType.DMA((4,))],
            source=HBM,
        )

    kv_send, kv_own = packed(key_rows, value_rows)
    kv_came = across(kv_send)
    qg_send, qg_own = packed(queries, out_grad)
    kv_came, qg_own = lax.optimization_barrier((kv_came, qg_own))
    kv, keys, values = call(
        frame_kernel, (kv_own, kv_came), [frame_two, frame_one, frame_one]
    )
    y_k = swapped(keys, y_swap)
    z_k = swapped(keys, z_swap)
    a_kv = swapped(kv, near_swap)
    y_v = swapped(values, y_swap)
    z_v = swapped(values, z_swap)
    far_send = call(functools.partial(select_kernel, far, block), (lists, kv), [pair] * n)
    qg_came, y_k = lax.optimization_barrier((across(qg_send), y_k))
    work = 4 * s_dev * s_dev * DH
    qg, turned = call(join_kernel, (qg_own, qg_came), [frame_two, turned_bf], flops=15 * work)
    y_k, z_k, turned = lax.optimization_barrier((y_k, z_k, turned))
    (relay_k,) = call(relay_kernel, (y_k, z_k), [frame_one])
    relay_k, far_send = lax.optimization_barrier((relay_k, far_send))
    a_kv, _ = lax.optimization_barrier((a_kv, relay_k))
    c_k = swapped(relay_k, near_swap)
    far_kv = [swapped(value, swap) for value, swap in zip(far_send, far)]
    stat, acc = call(
        functools.partial(near_kernel, block, near_swap),
        (lists, qg, kv, a_kv),
        [stat_row, turned_sum],
        scratch=[scores(6)],
    )
    y_v, z_v, stat = lax.optimization_barrier((y_v, z_v, stat))
    (relay_v,) = call(relay_kernel, (y_v, z_v), [frame_one])
    relay_v, stat = lax.optimization_barrier((relay_v, stat))
    c_v = swapped(relay_v, near_swap)
    stat, acc = call(
        functools.partial(middle_kernel, block, (z_swap, y_swap)),
        (lists, qg, stat, acc, y_k, z_k, y_v, z_v),
        [stat_row, turned_sum],
        scratch=[scores(2)],
    )
    score_two = sds((2, s_dev, s_dev), F32)
    stat, acc, late_scores = call(
        functools.partial(relayed_kernel, block, relayed),
        (lists, qg, stat, acc, c_k),
        [stat_row, turned_sum, score_two],
    )
    acc, far_kv = lax.optimization_barrier((acc, far_kv))
    lse, part, *far_dv = call(
        functools.partial(close_kernel, block, far),
        (qg, stat, acc, *far_kv),
        [stat_row, turned_sum] + [single] * n,
        scratch=[scores(n)],
    )
    dc_v, probs = call(
        functools.partial(values_kernel, block, relayed),
        (lists, qg, lse, late_scores),
        [frame_one, score_two],
        scratch=[grad_one],
    )
    dc_v_came = swapped(dc_v, near_swap)
    far_dv_came = [swapped(value, swap) for value, swap in zip(far_dv, far)]
    o, row_dot, dc_k, dq, *far_grad = call(
        functools.partial(late_kernel, block, relayed, far),
        (lists, qg, turned, lse, part, probs, c_k, c_v, *far_kv),
        [turned_bf, stat_row, frame_one, turned_sum] + [single] * n,
        scratch=[grad_one],
    )
    far_dk_came = [swapped(value, swap) for value, swap in zip(far_grad, far)]
    dc_k_came = swapped(dc_k, near_swap)
    da, dq = call(
        functools.partial(first_kernel, block, near_swap),
        (lists, qg, lse, row_dot, dq, a_kv),
        [frame_two, turned_sum],
        scratch=[pltpu.VMEM((2 * s_dev, 2 * DH), F32)],
    )
    da_came = swapped(da, near_swap)
    dc_v_came, far_dv_came = lax.optimization_barrier((dc_v_came, far_dv_came))
    dz, dy, dq = call(
        functools.partial(second_kernel, block, (z_swap, y_swap)),
        (lists, qg, lse, row_dot, dq, dc_v_came, y_k, z_k, y_v, z_v),
        [frame_sum, frame_sum, turned_sum],
        flops=20 * work,
    )
    dz, dy = call(merge_kernel, (dz, dy, dc_k_came), [frame_two, frame_two])
    dy_came = swapped(dy, y_swap)
    dz_came = swapped(dz, z_swap)
    dq, dz, dy = lax.optimization_barrier((dq, dz, dy))
    (placed,) = call(functools.partial(place_kernel, block, far), (lists, *far_dk_came, *far_dv_came), [frame_sum])
    near, q_keep, q_send = call(
        own_kernel,
        (qg, lse, row_dot, dq, o, kv, placed),
        [frame_sum, pair, pair],
        flops=40 * work,
    )
    k_keep, k_send = call(
        functools.partial(gather_kernel, swaps),
        (near, da_came, dz_came, dy_came),
        [pair, pair],
    )
    return call(
        finish_kernel,
        (q_keep, across(q_send), k_keep, across(k_send)),
        [sds((s_dev, width), BF16)] * 4,
    )


def solution(mesh):
    rows = P(("groups", "tm", "space"), None)
    return jax.shard_map(
        per_device,
        mesh=mesh,
        in_specs=(rows, rows, rows, rows, P("groups", None)),
        out_specs=(rows, rows, rows, rows),
        check_vma=False,
    )
```

```python
import functools
import math

import jax
import jax.numpy as jnp
from jax import lax
from jax.experimental import pallas as pl
from jax.experimental.pallas import tpu as pltpu
from jax.sharding import PartitionSpec as P

DH = 128
F32 = jnp.float32
BF16 = jnp.bfloat16
VMEM = pl.BlockSpec(memory_space=pltpu.VMEM)
SMEM = pl.BlockSpec(memory_space=pltpu.SMEM)
HBM = pl.BlockSpec(memory_space=pltpu.HBM)
NEG = -1e30
SCALE = 1.0 / math.sqrt(DH)
EXP_SCALE = SCALE * math.log2(math.e)
KEY = slice(0, DH)
VALUE = slice(DH, 2 * DH)
sds = jax.ShapeDtypeStruct


def dot_nn(a, b):
    return lax.dot_general(a, b, (((1,), (0,)), ((), ())), preferred_element_type=F32)


def dot_nt(a, b):
    return lax.dot_general(a, b, (((1,), (1,)), ((), ())), preferred_element_type=F32)


def dot_tn(a, b):
    return lax.dot_general(a, b, (((0,), (0,)), ((), ())), preferred_element_type=F32)


def call(kernel, args, out_shape, scratch=(), source=VMEM, scalars=SMEM, flops=1024):
    return pl.pallas_call(
        kernel,
        out_shape=out_shape,
        in_specs=[scalars if a.dtype == jnp.int32 else source for a in args],
        out_specs=tuple(VMEM for _ in out_shape),
        scratch_shapes=list(scratch),
        compiler_params=pltpu.CompilerParams(vmem_limit_bytes=40 << 20),
        cost_estimate=pl.CostEstimate(flops=flops, bytes_accessed=1024, transcendentals=0),
    )(*args)


def swap_pairs(count, distance, second):
    pairs = []
    for frame in range(count):
        up = ((frame // distance) % 2 == 0) != second
        target = frame + distance if up else frame - distance
        pairs.append((frame, target if 0 <= target < count else frame))
    return pairs


class Swap:
    def __init__(self, count, level, second):
        self.count, self.level, self.second = count, level, second
        self.levels = count.bit_length() - 1
        self.pairs = swap_pairs(count, 1 << level, second)
        self.moves = any(source != target for source, target in self.pairs)

    def partner(self, frame):
        odd = lax.rem(lax.shift_right_logical(frame, self.level), 2)
        later = odd == (1 if self.second else 0)
        other = jnp.where(later, frame + (1 << self.level), frame - (1 << self.level))
        return other, later, jnp.logical_and(other >= 0, other < self.count)

    def slot(self, later, k):
        base = 0 if self.level == 0 else self.level + 1
        return jnp.where(later, self.levels + 1, 0) + base + k

    def block_of_mine(self, lists, frame, slab, k):
        other, later, exists = self.partner(frame)
        entry = lists[self.slot(later, k), frame * 2 + slab]
        return jnp.clip(entry - other * 4, 0, 3), exists

    def block_of_theirs(self, lists, frame, slab, k):
        other, later, exists = self.partner(frame)
        row = jnp.where(exists, other, frame) * 2 + slab
        entry = lists[self.slot(jnp.logical_not(later), k), row]
        return jnp.clip(entry - frame * 4, 0, 3), exists


def head_cols(head):
    return slice(head * DH, (head + 1) * DH)


def rows_of(slab, half):
    return slice(slab * half, (slab + 1) * half)


def each_core(body):
    core = lax.axis_index("space")
    for mine in range(2):
        pl.when(core == mine)(functools.partial(body, mine))


def pack_kernel(a, b, *refs):
    *extra, sems = refs
    n = (len(extra) - 2) // 2
    send, own = extra[n : n + 2]

    def body(mine):
        copies = []
        for source, out in zip(extra[:n], extra[n + 2 :]):
            copies.append(pltpu.make_async_copy(source, out, sems.at[len(copies)]))
        for head, out in ((1 - mine, send), (mine, own)):
            for source, cols in ((a, KEY), (b, VALUE)):
                sem = sems.at[len(copies)]
                copies.append(
                    pltpu.make_async_copy(source.at[:, head_cols(head)], out.at[:, cols], sem)
                )
        for copy in copies:
            copy.start()
        for copy in copies:
            copy.wait()

    each_core(body)


def frame_kernel(own, came, kv, keys, values):
    half = own.shape[0]

    def body(mine):
        for slab, source in ((mine, own), (1 - mine, came)):
            rows = rows_of(slab, half)
            part = source[...]
            kv[rows, :] = part
            keys[rows, :] = part[:, KEY]
            values[rows, :] = part[:, VALUE]

    each_core(body)


def select_kernel(far, block, lists, kv, *sends):
    frame = lax.axis_index("tm")
    for swap, send in zip(far, sends):
        for slab in range(2):
            b, _ = swap.block_of_theirs(lists, frame, slab, 0)
            row = pl.multiple_of(b * block, block)
            send[slab * block : (slab + 1) * block, :] = kv[pl.ds(row, block), :]


def forwards_first(frame):
    return lax.rem(frame, 2) == lax.rem(lax.shift_right_logical(frame, 1), 2)


def relay_kernel(y, z, out):
    first = forwards_first(lax.axis_index("tm"))

    @pl.when(first)
    def _():
        out[...] = z[...]

    @pl.when(jnp.logical_not(first))
    def _():
        out[...] = y[...]


class Piece:
    def __init__(self, k, v, row, size, exists=None, dk=None, dv=None, add=True):
        self.k_at, self.v_at, self.exists = k, v, exists
        self.rows, self.size = pl.ds(row, size), size
        self.dk, self.dv, self.add = dk, dv, add

    def store(self, at, value):
        ref, cols = at
        if self.add:
            ref[self.rows, cols] += value
        else:
            ref[self.rows, cols] = value.astype(ref.dtype)


def stack(parts):
    return parts[0] if len(parts) == 1 else jnp.concatenate(parts, axis=0)


def keys_of(group):
    return stack([p.k_at[0][p.rows, p.k_at[1]] for p in group])


def values_of(group):
    return stack([p.v_at[0][p.rows, p.v_at[1]] for p in group])


def by_piece(group, value):
    at = 0
    for piece in group:
        yield piece, value[at : at + piece.size, :]
        at += piece.size


def store_grads(group, value, name):
    for piece, part in by_piece(group, value):
        piece.store(getattr(piece, name), part)


def listed(swap, lists, frame, slab, block, k, v, count=1, **grads):
    pieces = []
    for n in range(count):
        b, exists = swap.block_of_mine(lists, frame, slab, n)
        pieces.append(Piece(k, v, pl.multiple_of(b * block, block), block, exists, **grads))
    return pieces


def arrived(swap, frame, slab, block, kv, **grads):
    _, _, exists = swap.partner(frame)
    return Piece((kv, KEY), (kv, VALUE), slab * block, block, exists, add=False, **grads)


def raised(group, s, base):
    parts = []
    for piece, part in by_piece(group, s):
        low = base if piece.exists is None else jnp.where(piece.exists, base, -NEG)
        parts.append(jnp.exp2(part * EXP_SCALE - low))
    return stack(parts)


def score_groups(q, groups, s_ref, peak):
    at = 0
    for group in groups:
        s = dot_nt(keys_of(group), q)
        s_ref[at : at + s.shape[0], :] = s
        at += s.shape[0]
        for piece, part in by_piece(group, s):
            top = jnp.max(part, axis=0, keepdims=True)
            if piece.exists is not None:
                top = jnp.where(piece.exists, top, NEG)
            peak = top if peak is None else jnp.maximum(peak, top)
    return peak


def group_scores(groups, s_ref):
    at = 0
    for group in groups:
        size = sum(piece.size for piece in group)
        yield group, s_ref[at : at + size, :]
        at += size


def forward_slab(q, groups, with_values, s_ref, old):
    peak = score_groups(q, groups, s_ref, None if old is None else old[0])
    total, acc = 0.0, 0.0
    if old is not None:
        shrink = jnp.exp2((old[0] - peak) * EXP_SCALE)
        total, acc = old[1] * shrink, old[2] * shrink
    for j, (group, s) in enumerate(group_scores(groups, s_ref)):
        e = raised(group, s, peak * EXP_SCALE)
        total = total + jnp.sum(e, axis=0, keepdims=True)
        if j < with_values:
            acc = acc + dot_tn(values_of(group), e.astype(BF16))
    return peak, total, acc


def backward_group(q, g, lse, row_dot, group, p=None):
    k = keys_of(group)
    if p is None:
        p = raised(group, dot_nt(k, q), lse)
    if group[0].dv is not None:
        store_grads(group, dot_nn(p.astype(BF16), g), "dv")
    ds = (p * (dot_nt(values_of(group), g) - row_dot)).astype(BF16)
    if group[0].dk is not None:
        store_grads(group, dot_nn(ds, q) * SCALE, "dk")
    return dot_tn(k, ds)


def join_kernel(own, came, out, turned):
    half = own.shape[0]

    def body(mine):
        for slab, source in ((mine, own), (1 - mine, came)):
            rows = rows_of(slab, half)
            out[rows, :] = source[...]
            turned[:, rows] = source[:, VALUE].T

    each_core(body)


ALL = slice(None)


def store_state(refs, rows, peak, total, acc):
    stat, acc_ref = refs
    stat[0:1, rows] = peak
    stat[1:2, rows] = total
    acc_ref[:, rows] = acc


def load_state(refs, rows):
    stat, acc_ref = refs
    return stat[0:1, rows], stat[1:2, rows], acc_ref[:, rows]


def own_groups(kv, half, **grads):
    return [
        [Piece((kv, KEY), (kv, VALUE), r, half, **grads)] for r in range(0, kv.shape[0], half)
    ]


def near_kernel(block, swap, lists, qg, kv, a_kv, stat, acc, s_ref):
    half = qg.shape[0] // 2
    frame = lax.axis_index("tm")
    for slab in range(2):
        rows = rows_of(slab, half)
        groups = own_groups(kv, half)
        groups.append(
            listed(swap, lists, frame, slab, block, (a_kv, KEY), (a_kv, VALUE), 2)
        )
        store_state((stat, acc), rows, *forward_slab(qg[rows, KEY], groups, 3, s_ref, None))


def middle_kernel(
    block, swaps, lists, qg, stat, acc, y_k, z_k, y_v, z_v, c_k, stat2, acc2, late, s_ref
):
    half = qg.shape[0] // 2
    frame = lax.axis_index("tm")
    z, y, relayed = swaps
    for slab in range(2):
        rows = rows_of(slab, half)
        at = (lists, frame, slab, block)
        group = listed(z, *at, (z_k, ALL), (z_v, ALL)) + listed(y, *at, (y_k, ALL), (y_v, ALL))
        more = listed(relayed, *at, (c_k, ALL), None, 2)
        old = load_state((stat, acc), rows)
        new = forward_slab(qg[rows, KEY], [group, more], 1, s_ref, old)
        store_state((stat2, acc2), rows, *new)
        late[slab] = s_ref[2 * block :, :]


def close_kernel(block, far, qg, stat, acc, *refs):
    n = len(far)
    far_kv = refs[:n]
    lse_ref, part_ref = refs[n : n + 2]
    far_dv = refs[n + 2 : 2 * n + 2]
    s_ref = refs[2 * n + 2]
    half = qg.shape[0] // 2
    frame = lax.axis_index("tm")
    for slab in range(2):
        rows = rows_of(slab, half)
        q, g = qg[rows, KEY], qg[rows, VALUE]
        groups = [
            [arrived(swap, frame, slab, block, kv, dv=(out, ALL))]
            for swap, kv, out in zip(far, far_kv, far_dv)
        ]
        old = load_state((stat, acc), rows)
        peak, total, out = forward_slab(q, groups, n, s_ref, old)
        part_ref[:, rows] = out / total
        lse = peak * EXP_SCALE + jnp.log2(total)
        lse_ref[0:1, rows] = lse
        for group, s in group_scores(groups, s_ref):
            p = raised(group, s, lse)
            store_grads(group, dot_nn(p.astype(BF16), g), "dv")


def values_kernel(block, relayed, lists, qg, lse_ref, s_ref, dc_v, p_ref, grad):
    half = qg.shape[0] // 2
    frame = lax.axis_index("tm")
    grad[...] = jnp.zeros_like(grad)
    for slab in range(2):
        rows = rows_of(slab, half)
        group = listed(relayed, lists, frame, slab, block, None, None, 2, dv=(grad, ALL))
        p = raised(group, s_ref[slab], lse_ref[0:1, rows])
        p_ref[slab] = p
        store_grads(group, dot_nn(p.astype(BF16), qg[rows, VALUE]), "dv")
    dc_v[...] = grad[...].astype(BF16)


def late_kernel(block, relayed, far, *refs):
    n = len(far)
    lists, qg, turned, lse_ref, part_ref, p_ref, c_k, c_v = refs[:8]
    far_kv = refs[8 : 8 + n]
    o_ref, dot_ref, dc_k, dq_ref = refs[8 + n : 12 + n]
    far_grad = refs[12 + n : 12 + 2 * n]
    grad = refs[12 + 2 * n]
    half = qg.shape[0] // 2
    frame = lax.axis_index("tm")
    grad[...] = jnp.zeros_like(grad)
    for slab in range(2):
        rows = rows_of(slab, half)
        q, g, lse = qg[rows, KEY], qg[rows, VALUE], lse_ref[0:1, rows]
        group = listed(
            relayed, lists, frame, slab, block, (c_k, ALL), (c_v, ALL), 2, dk=(grad, ALL)
        )
        p = p_ref[slab]
        o = (part_ref[:, rows] + dot_tn(values_of(group), p.astype(BF16))).astype(BF16)
        o_ref[:, rows] = o
        products = turned[:, rows].astype(F32) * o.astype(F32)
        row_dot = jnp.sum(products, axis=0, keepdims=True)
        dot_ref[0:1, rows] = row_dot
        dq = backward_group(q, g, lse, row_dot, group, p)
        for swap, kv, out in zip(far, far_kv, far_grad):
            group = [arrived(swap, frame, slab, block, kv, dk=(out, ALL))]
            dq = dq + backward_group(q, g, lse, row_dot, group)
        dq_ref[:, rows] = dq
    dc_k[...] = grad[...].astype(BF16)


def first_kernel(block, swap, lists, qg, lse_ref, dot_ref, dq_old, a_kv, da, dq_ref, grad):
    half = qg.shape[0] // 2
    frame = lax.axis_index("tm")
    grad[...] = jnp.zeros_like(grad)
    for slab in range(2):
        rows = rows_of(slab, half)
        q, g, lse, row_dot = qg[rows, KEY], qg[rows, VALUE], lse_ref[0:1, rows], dot_ref[0:1, rows]
        group = listed(
            swap, lists, frame, slab, block, (a_kv, KEY), (a_kv, VALUE), 2,
            dk=(grad, KEY), dv=(grad, VALUE),
        )
        dq_ref[:, rows] = dq_old[:, rows] + backward_group(q, g, lse, row_dot, group)
    da[...] = grad[...].astype(BF16)


def second_kernel(
    block, swaps, lists, qg, lse_ref, dot_ref, dq_old, came, y_k, z_k, y_v, z_v, dz, dy, dq_ref
):
    half = qg.shape[0] // 2
    frame = lax.axis_index("tm")
    z, y = swaps
    relays = forwards_first(frame)
    more = came[...].astype(F32)
    for ref, takes in ((dz, relays), (dy, jnp.logical_not(relays))):
        ref[:, KEY] = jnp.zeros_like(more)
        ref[:, VALUE] = jnp.where(takes, more, 0.0)
    for slab in range(2):
        rows = rows_of(slab, half)
        q, g, lse, row_dot = qg[rows, KEY], qg[rows, VALUE], lse_ref[0:1, rows], dot_ref[0:1, rows]
        at = (lists, frame, slab, block)
        group = listed(z, *at, (z_k, ALL), (z_v, ALL), dk=(dz, KEY), dv=(dz, VALUE))
        group += listed(y, *at, (y_k, ALL), (y_v, ALL), dk=(dy, KEY), dv=(dy, VALUE))
        dq_ref[:, rows] = dq_old[:, rows] + backward_group(q, g, lse, row_dot, group)


def own_kernel(qg, lse_ref, dot_ref, dq_old, o, kv, placed, near, keep, send):
    half = qg.shape[0] // 2
    near[...] = placed[...]
    whole = []
    for slab in range(2):
        rows = rows_of(slab, half)
        q, g, lse, row_dot = qg[rows, KEY], qg[rows, VALUE], lse_ref[0:1, rows], dot_ref[0:1, rows]
        dq = dq_old[:, rows]
        for group in own_groups(kv, half, dk=(near, KEY), dv=(near, VALUE)):
            dq = dq + backward_group(q, g, lse, row_dot, group)
        whole.append((dq.T * SCALE).astype(BF16))

    def body(mine):
        for slab in range(2):
            out = keep if slab == mine else send
            out[:, KEY] = o[:, rows_of(slab, half)].T
            out[:, VALUE] = whole[slab]

    each_core(body)


def merge_kernel(dz, dy, came, z_out, y_out):
    first = forwards_first(lax.axis_index("tm"))
    more = came[...].astype(F32)
    z_out[:, KEY] = (dz[:, KEY] + jnp.where(first, more, 0.0)).astype(BF16)
    y_out[:, KEY] = (dy[:, KEY] + jnp.where(first, 0.0, more)).astype(BF16)
    z_out[:, VALUE] = dz[:, VALUE].astype(BF16)
    y_out[:, VALUE] = dy[:, VALUE].astype(BF16)


def place_kernel(block, far, *refs):
    n = len(far)
    lists, total = refs[0], refs[-1]
    frame = lax.axis_index("tm")
    total[...] = jnp.zeros_like(total)
    for swap, came_k, came_v in zip(far, refs[1 : 1 + n], refs[1 + n : -1]):
        for slab in range(2):
            b, exists = swap.block_of_theirs(lists, frame, slab, 0)
            rows = pl.ds(pl.multiple_of(b * block, block), block)
            for came, cols in ((came_k, KEY), (came_v, VALUE)):
                part = came[rows_of(slab, block), :].astype(F32)
                total[rows, cols] += jnp.where(exists, part, 0.0)


def add_kernel(swaps, near, *refs):
    frame = lax.axis_index("tm")
    total = near[...]
    for swap, came in zip(swaps, refs[:-1]):
        _, _, exists = swap.partner(frame)
        total = total + jnp.where(exists, came[...].astype(F32), 0.0)
    refs[-1][...] = total


def gather_kernel(swap, near, came, keep, send):
    _, _, exists = swap.partner(lax.axis_index("tm"))
    half = near.shape[0] // 2

    def body(mine):
        for slab, out in ((1 - mine, send), (mine, keep)):
            rows = rows_of(slab, half)
            part = jnp.where(exists, came[rows, :].astype(F32), 0.0)
            out[...] = (near[rows, :] + part).astype(BF16)

    each_core(body)


def finish_kernel(keep, came, first, second):
    def body(mine):
        for head, source in ((mine, keep), (1 - mine, came)):
            first[:, head_cols(head)] = source[:, KEY]
            second[:, head_cols(head)] = source[:, VALUE]

    each_core(body)


def per_device(queries, key_rows, value_rows, out_grad, block_lists):
    s_dev, width = queries.shape
    count = lax.axis_size("tm")
    block = s_dev // 2
    pair = sds((s_dev, 2 * DH), BF16)
    single = sds((s_dev, DH), BF16)
    frame_two = sds((2 * s_dev, 2 * DH), BF16)
    frame_one = sds((2 * s_dev, DH), BF16)
    frame_sum = sds((2 * s_dev, 2 * DH), F32)
    stat_row = sds((8, 2 * s_dev), F32)
    turned_sum = sds((DH, 2 * s_dev), F32)
    turned_bf = sds((DH, 2 * s_dev), BF16)
    levels = count.bit_length() - 1
    near_swap, relayed = Swap(count, 0, False), Swap(count, 0, True)
    z_swap, y_swap = Swap(count, 1, False), Swap(count, 1, True)
    far = [Swap(count, level, second) for level in range(2, levels) for second in (False, True)]
    far = [swap for swap in far if swap.moves]
    n = len(far)
    grad_one = pltpu.VMEM((2 * s_dev, DH), F32)

    def across(value):
        return lax.ppermute(value, "space", [(0, 1), (1, 0)])

    def swapped(value, swap):
        return lax.ppermute(value, "tm", swap.pairs)

    def scores(pieces):
        return pltpu.VMEM((pieces * block, s_dev), F32)


    def packed(*arrays):
        return call(
            pack_kernel,
            tuple(pltpu.with_memory_space_constraint(a, pltpu.HBM) for a in arrays),
            [pair] * 2 + [sds(a.shape, a.dtype) for a in arrays[2:]],
            scratch=[pltpu.SemaphoreType.DMA((2 + len(arrays),))],
            source=HBM,
            scalars=HBM,
        )

    kv_send, kv_own = packed(key_rows, value_rows)
    kv_came = across(kv_send)
    qg_send, qg_own, lists = packed(queries, out_grad, block_lists.T)
    kv_came, qg_own = lax.optimization_barrier((kv_came, qg_own))
    kv, keys, values = call(
        frame_kernel, (kv_own, kv_came), [frame_two, frame_one, frame_one]
    )
    qg_send, keys = lax.optimization_barrier((qg_send, keys))
    y_k = swapped(keys, y_swap)
    z_k = swapped(keys, z_swap)
    a_kv = swapped(kv, near_swap)
    y_v = swapped(values, y_swap)
    z_v = swapped(values, z_swap)
    y_k, qg_came = lax.optimization_barrier((y_k, across(qg_send)))
    work = 4 * s_dev * s_dev * DH
    qg, turned = call(join_kernel, (qg_own, qg_came), [frame_two, turned_bf], flops=15 * work)
    y_k, z_k, turned = lax.optimization_barrier((y_k, z_k, turned))
    kv, _ = lax.optimization_barrier((kv, turned))
    far_send = call(functools.partial(select_kernel, far, block), (lists, kv), [pair] * n)
    (relay_k,) = call(relay_kernel, (y_k, z_k), [frame_one])
    relay_k, far_send = lax.optimization_barrier((relay_k, far_send))
    a_kv, _ = lax.optimization_barrier((a_kv, relay_k))
    c_k = swapped(relay_k, near_swap)
    far_kv = [swapped(value, swap) for value, swap in zip(far_send, far)]
    stat, acc = call(
        functools.partial(near_kernel, block, near_swap),
        (lists, qg, kv, a_kv),
        [stat_row, turned_sum],
        scratch=[scores(6)],
    )
    score_two = sds((2, s_dev, s_dev), F32)
    y_v, z_v, stat = lax.optimization_barrier((y_v, z_v, stat))
    (relay_v,) = call(relay_kernel, (y_v, z_v), [frame_one])
    relay_v, stat = lax.optimization_barrier((relay_v, stat))
    c_v = swapped(relay_v, near_swap)
    stat, acc, late_scores = call(
        functools.partial(middle_kernel, block, (z_swap, y_swap, relayed)),
        (lists, qg, stat, acc, y_k, z_k, y_v, z_v, c_k),
        [stat_row, turned_sum, score_two],
        scratch=[scores(4)],
    )
    acc, far_kv = lax.optimization_barrier((acc, far_kv))
    lse, part, *far_dv = call(
        functools.partial(close_kernel, block, far),
        (qg, stat, acc, *far_kv),
        [stat_row, turned_sum] + [single] * n,
        scratch=[scores(n)],
    )
    dc_v, probs = call(
        functools.partial(values_kernel, block, relayed),
        (lists, qg, lse, late_scores),
        [frame_one, score_two],
        scratch=[grad_one],
    )
    dc_v_came = swapped(dc_v, near_swap)
    far_dv_came = [swapped(value, swap) for value, swap in zip(far_dv, far)]
    o, row_dot, dc_k, dq, *far_grad = call(
        functools.partial(late_kernel, block, relayed, far),
        (lists, qg, turned, lse, part, probs, c_k, c_v, *far_kv),
        [turned_bf, stat_row, frame_one, turned_sum] + [single] * n,
        scratch=[grad_one],
    )
    far_dk_came = [swapped(value, swap) for value, swap in zip(far_grad, far)]
    dc_k_came = swapped(dc_k, near_swap)
    da, dq = call(
        functools.partial(first_kernel, block, near_swap),
        (lists, qg, lse, row_dot, dq, a_kv),
        [frame_two, turned_sum],
        scratch=[pltpu.VMEM((2 * s_dev, 2 * DH), F32)],
    )
    da_came = swapped(da, near_swap)
    dc_v_came, far_dv_came = lax.optimization_barrier((dc_v_came, far_dv_came))
    dz, dy, dq = call(
        functools.partial(second_kernel, block, (z_swap, y_swap)),
        (lists, qg, lse, row_dot, dq, dc_v_came, y_k, z_k, y_v, z_v),
        [frame_sum, frame_sum, turned_sum],
        flops=20 * work,
    )
    dz, dy = call(merge_kernel, (dz, dy, dc_k_came), [frame_two, frame_two])
    dy_came = swapped(dy, y_swap)
    dz_came = swapped(dz, z_swap)
    dq, dz, dy = lax.optimization_barrier((dq, dz, dy))
    far_dk_came, dq = lax.optimization_barrier((far_dk_came, dq))
    (placed,) = call(functools.partial(place_kernel, block, far), (lists, *far_dk_came, *far_dv_came), [frame_sum])
    near, q_keep, q_send = call(
        own_kernel,
        (qg, lse, row_dot, dq, o, kv, placed),
        [frame_sum, pair, pair],
        flops=20 * work,
    )
    outputs = [sds((s_dev, width), BF16)] * 2
    attn_out, grad_q = call(finish_kernel, (q_keep, across(q_send)), outputs)
    near, attn_out, grad_q = lax.optimization_barrier((near, attn_out, grad_q))
    (near,) = call(
        functools.partial(add_kernel, (near_swap, y_swap)),
        (near, da_came, dy_came),
        [frame_sum],
        flops=20 * work,
    )
    k_keep, k_send = call(
        functools.partial(gather_kernel, z_swap), (near, dz_came), [pair, pair]
    )
    grad_k, grad_v = call(finish_kernel, (k_keep, across(k_send)), outputs)
    return attn_out, grad_q, grad_k, grad_v


def solution(mesh):
    rows = P(("groups", "tm", "space"), None)
    return jax.shard_map(
        per_device,
        mesh=mesh,
        in_specs=(rows, rows, rows, rows, P("groups", None)),
        out_specs=(rows, rows, rows, rows),
        check_vma=False,
    )
```

```python
import functools
import math

import jax
import jax.numpy as jnp
from jax import lax
from jax.experimental import pallas as pl
from jax.experimental.pallas import tpu as pltpu
from jax.sharding import PartitionSpec as P

DH = 128
F32 = jnp.float32
BF16 = jnp.bfloat16
VMEM = pl.BlockSpec(memory_space=pltpu.VMEM)
SMEM = pl.BlockSpec(memory_space=pltpu.SMEM)
HBM = pl.BlockSpec(memory_space=pltpu.HBM)
NEG = -1e30
SCALE = 1.0 / math.sqrt(DH)
EXP_SCALE = SCALE * math.log2(math.e)
KEY = slice(0, DH)
VALUE = slice(DH, 2 * DH)
sds = jax.ShapeDtypeStruct


def dot_nn(a, b):
    return lax.dot_general(a, b, (((1,), (0,)), ((), ())), preferred_element_type=F32)


def dot_nt(a, b):
    return lax.dot_general(a, b, (((1,), (1,)), ((), ())), preferred_element_type=F32)


def dot_tn(a, b):
    return lax.dot_general(a, b, (((0,), (0,)), ((), ())), preferred_element_type=F32)


def call(kernel, args, out_shape, scratch=(), source=VMEM, scalars=SMEM, flops=1024):
    return pl.pallas_call(
        kernel,
        out_shape=out_shape,
        in_specs=[scalars if a.dtype == jnp.int32 else source for a in args],
        out_specs=tuple(VMEM for _ in out_shape),
        scratch_shapes=list(scratch),
        compiler_params=pltpu.CompilerParams(vmem_limit_bytes=40 << 20),
        cost_estimate=pl.CostEstimate(flops=flops, bytes_accessed=1024, transcendentals=0),
    )(*args)


def swap_pairs(count, distance, second):
    pairs = []
    for frame in range(count):
        up = ((frame // distance) % 2 == 0) != second
        target = frame + distance if up else frame - distance
        pairs.append((frame, target if 0 <= target < count else frame))
    return pairs


class Swap:
    def __init__(self, count, level, second):
        self.count, self.level, self.second = count, level, second
        self.levels = count.bit_length() - 1
        self.pairs = swap_pairs(count, 1 << level, second)
        self.moves = any(source != target for source, target in self.pairs)

    def partner(self, frame):
        odd = lax.rem(lax.shift_right_logical(frame, self.level), 2)
        later = odd == (1 if self.second else 0)
        other = jnp.where(later, frame + (1 << self.level), frame - (1 << self.level))
        return other, later, jnp.logical_and(other >= 0, other < self.count)

    def slot(self, later, k):
        base = 0 if self.level == 0 else self.level + 1
        return jnp.where(later, self.levels + 1, 0) + base + k

    def block_of_mine(self, lists, frame, slab, k):
        other, later, exists = self.partner(frame)
        entry = lists[self.slot(later, k), frame * 2 + slab]
        return jnp.clip(entry - other * 4, 0, 3), exists

    def block_of_theirs(self, lists, frame, slab, k):
        other, later, exists = self.partner(frame)
        row = jnp.where(exists, other, frame) * 2 + slab
        entry = lists[self.slot(jnp.logical_not(later), k), row]
        return jnp.clip(entry - frame * 4, 0, 3), exists


def head_cols(head):
    return slice(head * DH, (head + 1) * DH)


def rows_of(slab, half):
    return slice(slab * half, (slab + 1) * half)


def each_core(body):
    core = lax.axis_index("space")
    for mine in range(2):
        pl.when(core == mine)(functools.partial(body, mine))


def pack_kernel(k, v, q, g, lists, k_own, v_own, qg_own, qg_send, lists_out, sems):
    def body(mine):
        moves = [(lists, lists_out)]
        for source, out in ((k, k_own), (v, v_own)):
            moves.append((source.at[:, head_cols(mine)], out))
        for head, out in ((mine, qg_own), (1 - mine, qg_send)):
            for source, cols in ((q, KEY), (g, VALUE)):
                moves.append((source.at[:, head_cols(head)], out.at[:, cols]))
        copies = [
            pltpu.make_async_copy(source, out, sems.at[n]) for n, (source, out) in enumerate(moves)
        ]
        for copy in copies:
            copy.start()
        for copy in copies:
            copy.wait()

    each_core(body)


def keys_kernel(own, came, keys):
    half = own.shape[0]

    def body(mine):
        keys[rows_of(mine, half), :] = own[...]
        keys[rows_of(1 - mine, half), :] = came[:, head_cols(mine)]

    each_core(body)


def values_kernel(keys, own, came, values, kv):
    half = own.shape[0]

    def body(mine):
        for slab, part in ((mine, own[...]), (1 - mine, came[:, head_cols(mine)])):
            rows = rows_of(slab, half)
            values[rows, :] = part
            kv[rows, VALUE] = part
            kv[rows, KEY] = keys[rows, :]

    each_core(body)


def select_kernel(far, block, lists, kv, *sends):
    frame = lax.axis_index("tm")
    for swap, send in zip(far, sends):
        for slab in range(2):
            b, _ = swap.block_of_theirs(lists, frame, slab, 0)
            row = pl.multiple_of(b * block, block)
            send[slab * block : (slab + 1) * block, :] = kv[pl.ds(row, block), :]


def forwards_first(frame):
    return lax.rem(frame, 2) == lax.rem(lax.shift_right_logical(frame, 1), 2)


def relay_kernel(y, z, out):
    first = forwards_first(lax.axis_index("tm"))

    @pl.when(first)
    def _():
        out[...] = z[...]

    @pl.when(jnp.logical_not(first))
    def _():
        out[...] = y[...]


class Piece:
    def __init__(self, k, v, row, size, exists=None, dk=None, dv=None, add=True):
        self.k_at, self.v_at, self.exists = k, v, exists
        self.rows, self.size = pl.ds(row, size), size
        self.dk, self.dv, self.add = dk, dv, add

    def store(self, at, value):
        ref, cols = at
        if self.add:
            ref[self.rows, cols] += value
        else:
            ref[self.rows, cols] = value.astype(ref.dtype)


def stack(parts):
    return parts[0] if len(parts) == 1 else jnp.concatenate(parts, axis=0)


def keys_of(group):
    return stack([p.k_at[0][p.rows, p.k_at[1]] for p in group])


def values_of(group):
    return stack([p.v_at[0][p.rows, p.v_at[1]] for p in group])


def by_piece(group, value):
    at = 0
    for piece in group:
        yield piece, value[at : at + piece.size, :]
        at += piece.size


def store_grads(group, value, name):
    for piece, part in by_piece(group, value):
        piece.store(getattr(piece, name), part)


def listed(swap, lists, frame, slab, block, k, v, count=1, **grads):
    pieces = []
    for n in range(count):
        b, exists = swap.block_of_mine(lists, frame, slab, n)
        pieces.append(Piece(k, v, pl.multiple_of(b * block, block), block, exists, **grads))
    return pieces


def arrived(swap, frame, slab, block, kv, **grads):
    _, _, exists = swap.partner(frame)
    return Piece((kv, KEY), (kv, VALUE), slab * block, block, exists, add=False, **grads)


def raised(group, s, base):
    parts = []
    for piece, part in by_piece(group, s):
        low = base if piece.exists is None else jnp.where(piece.exists, base, -NEG)
        parts.append(jnp.exp2(part * EXP_SCALE - low))
    return stack(parts)


def score_groups(q, groups, s_ref, peak):
    at = 0
    for group in groups:
        s = dot_nt(keys_of(group), q)
        s_ref[at : at + s.shape[0], :] = s
        at += s.shape[0]
        for piece, part in by_piece(group, s):
            top = jnp.max(part, axis=0, keepdims=True)
            if piece.exists is not None:
                top = jnp.where(piece.exists, top, NEG)
            peak = top if peak is None else jnp.maximum(peak, top)
    return peak


def group_scores(groups, s_ref):
    at = 0
    for group in groups:
        size = sum(piece.size for piece in group)
        yield group, s_ref[at : at + size, :]
        at += size


def forward_slab(q, groups, with_values, s_ref, old):
    peak = score_groups(q, groups, s_ref, None if old is None else old[0])
    total, acc = 0.0, 0.0
    if old is not None:
        shrink = jnp.exp2((old[0] - peak) * EXP_SCALE)
        total, acc = old[1] * shrink, old[2] * shrink
    for j, (group, s) in enumerate(group_scores(groups, s_ref)):
        e = raised(group, s, peak * EXP_SCALE)
        total = total + jnp.sum(e, axis=0, keepdims=True)
        if j < with_values:
            acc = acc + dot_tn(values_of(group), e.astype(BF16))
    return peak, total, acc


def backward_group(q, g, lse, row_dot, group, p=None):
    k = keys_of(group)
    if p is None:
        p = raised(group, dot_nt(k, q), lse)
    if group[0].dv is not None:
        store_grads(group, dot_nn(p.astype(BF16), g), "dv")
    ds = (p * (dot_nt(values_of(group), g) - row_dot)).astype(BF16)
    if group[0].dk is not None:
        store_grads(group, dot_nn(ds, q) * SCALE, "dk")
    return dot_tn(k, ds)


def join_kernel(own, came, out, turned):
    half = own.shape[0]

    def body(mine):
        for slab, source in ((mine, own), (1 - mine, came)):
            rows = rows_of(slab, half)
            out[rows, :] = source[...]
            turned[:, rows] = source[:, VALUE].T

    each_core(body)


ALL = slice(None)


def store_state(refs, rows, peak, total, acc):
    stat, acc_ref = refs
    stat[0:1, rows] = peak
    stat[1:2, rows] = total
    acc_ref[:, rows] = acc


def load_state(refs, rows):
    stat, acc_ref = refs
    return stat[0:1, rows], stat[1:2, rows], acc_ref[:, rows]


def own_groups(kv, half, **grads):
    return [
        [Piece((kv, KEY), (kv, VALUE), r, half, **grads)] for r in range(0, kv.shape[0], half)
    ]


def near_kernel(block, swap, lists, qg, kv, a_kv, stat, acc, s_ref):
    half = qg.shape[0] // 2
    frame = lax.axis_index("tm")
    for slab in range(2):
        rows = rows_of(slab, half)
        groups = own_groups(kv, half)
        groups.append(
            listed(swap, lists, frame, slab, block, (a_kv, KEY), (a_kv, VALUE), 2)
        )
        store_state((stat, acc), rows, *forward_slab(qg[rows, KEY], groups, 3, s_ref, None))


def middle_kernel(
    block, swaps, lists, qg, stat, acc, y_k, z_k, y_v, z_v, c_k, stat2, acc2, late, s_ref
):
    half = qg.shape[0] // 2
    frame = lax.axis_index("tm")
    z, y, relayed = swaps
    for slab in range(2):
        rows = rows_of(slab, half)
        at = (lists, frame, slab, block)
        group = listed(z, *at, (z_k, ALL), (z_v, ALL)) + listed(y, *at, (y_k, ALL), (y_v, ALL))
        more = listed(relayed, *at, (c_k, ALL), None, 2)
        old = load_state((stat, acc), rows)
        new = forward_slab(qg[rows, KEY], [group, more], 1, s_ref, old)
        store_state((stat2, acc2), rows, *new)
        late[slab] = s_ref[2 * block :, :]


def close_kernel(block, far, qg, stat, acc, *refs):
    n = len(far)
    far_kv = refs[:n]
    lse_ref, part_ref = refs[n : n + 2]
    far_dv = refs[n + 2 : 2 * n + 2]
    s_ref = refs[2 * n + 2]
    half = qg.shape[0] // 2
    frame = lax.axis_index("tm")
    for slab in range(2):
        rows = rows_of(slab, half)
        q, g = qg[rows, KEY], qg[rows, VALUE]
        groups = [
            [arrived(swap, frame, slab, block, kv, dv=(out, ALL))]
            for swap, kv, out in zip(far, far_kv, far_dv)
        ]
        old = load_state((stat, acc), rows)
        peak, total, out = forward_slab(q, groups, n, s_ref, old)
        part_ref[:, rows] = out / total
        lse = peak * EXP_SCALE + jnp.log2(total)
        lse_ref[0:1, rows] = lse
        for group, s in group_scores(groups, s_ref):
            p = raised(group, s, lse)
            store_grads(group, dot_nn(p.astype(BF16), g), "dv")


def shares_kernel(block, relayed, lists, qg, lse_ref, s_ref, dc_v, p_ref, grad):
    half = qg.shape[0] // 2
    frame = lax.axis_index("tm")
    grad[...] = jnp.zeros_like(grad)
    for slab in range(2):
        rows = rows_of(slab, half)
        group = listed(relayed, lists, frame, slab, block, None, None, 2, dv=(grad, ALL))
        p = raised(group, s_ref[slab], lse_ref[0:1, rows])
        p_ref[slab] = p
        store_grads(group, dot_nn(p.astype(BF16), qg[rows, VALUE]), "dv")
    dc_v[...] = grad[...].astype(BF16)


def late_kernel(block, relayed, far, *refs):
    n = len(far)
    lists, qg, turned, lse_ref, part_ref, p_ref, c_k, c_v = refs[:8]
    far_kv = refs[8 : 8 + n]
    o_ref, dot_ref, dc_k, dq_ref = refs[8 + n : 12 + n]
    far_grad = refs[12 + n : 12 + 2 * n]
    grad = refs[12 + 2 * n]
    half = qg.shape[0] // 2
    frame = lax.axis_index("tm")
    grad[...] = jnp.zeros_like(grad)
    for slab in range(2):
        rows = rows_of(slab, half)
        q, g, lse = qg[rows, KEY], qg[rows, VALUE], lse_ref[0:1, rows]
        group = listed(
            relayed, lists, frame, slab, block, (c_k, ALL), (c_v, ALL), 2, dk=(grad, ALL)
        )
        p = p_ref[slab]
        o = (part_ref[:, rows] + dot_tn(values_of(group), p.astype(BF16))).astype(BF16)
        o_ref[:, rows] = o
        products = turned[:, rows].astype(F32) * o.astype(F32)
        row_dot = jnp.sum(products, axis=0, keepdims=True)
        dot_ref[0:1, rows] = row_dot
        dq = backward_group(q, g, lse, row_dot, group, p)
        for swap, kv, out in zip(far, far_kv, far_grad):
            group = [arrived(swap, frame, slab, block, kv, dk=(out, ALL))]
            dq = dq + backward_group(q, g, lse, row_dot, group)
        dq_ref[:, rows] = dq
    dc_k[...] = grad[...].astype(BF16)


def first_kernel(block, swap, lists, qg, lse_ref, dot_ref, dq_old, a_kv, da, dq_ref, grad):
    half = qg.shape[0] // 2
    frame = lax.axis_index("tm")
    grad[...] = jnp.zeros_like(grad)
    for slab in range(2):
        rows = rows_of(slab, half)
        q, g, lse, row_dot = qg[rows, KEY], qg[rows, VALUE], lse_ref[0:1, rows], dot_ref[0:1, rows]
        group = listed(
            swap, lists, frame, slab, block, (a_kv, KEY), (a_kv, VALUE), 2,
            dk=(grad, KEY), dv=(grad, VALUE),
        )
        dq_ref[:, rows] = dq_old[:, rows] + backward_group(q, g, lse, row_dot, group)
    da[...] = grad[...].astype(BF16)


def second_kernel(
    block, swaps, lists, qg, lse_ref, dot_ref, dq_old, came, y_k, z_k, y_v, z_v, dz, dy, dq_ref
):
    half = qg.shape[0] // 2
    frame = lax.axis_index("tm")
    z, y = swaps
    relays = forwards_first(frame)
    more = came[...].astype(F32)
    for ref, takes in ((dz, relays), (dy, jnp.logical_not(relays))):
        ref[:, KEY] = jnp.zeros_like(more)
        ref[:, VALUE] = jnp.where(takes, more, 0.0)
    for slab in range(2):
        rows = rows_of(slab, half)
        q, g, lse, row_dot = qg[rows, KEY], qg[rows, VALUE], lse_ref[0:1, rows], dot_ref[0:1, rows]
        at = (lists, frame, slab, block)
        group = listed(z, *at, (z_k, ALL), (z_v, ALL), dk=(dz, KEY), dv=(dz, VALUE))
        group += listed(y, *at, (y_k, ALL), (y_v, ALL), dk=(dy, KEY), dv=(dy, VALUE))
        dq_ref[:, rows] = dq_old[:, rows] + backward_group(q, g, lse, row_dot, group)


def own_kernel(qg, lse_ref, dot_ref, dq_old, o, kv, placed, near, keep, send):
    half = qg.shape[0] // 2
    near[...] = placed[...]
    whole = []
    for slab in range(2):
        rows = rows_of(slab, half)
        q, g, lse, row_dot = qg[rows, KEY], qg[rows, VALUE], lse_ref[0:1, rows], dot_ref[0:1, rows]
        dq = dq_old[:, rows]
        for group in own_groups(kv, half, dk=(near, KEY), dv=(near, VALUE)):
            dq = dq + backward_group(q, g, lse, row_dot, group)
        whole.append((dq.T * SCALE).astype(BF16))

    def body(mine):
        for slab in range(2):
            out = keep if slab == mine else send
            out[:, KEY] = o[:, rows_of(slab, half)].T
            out[:, VALUE] = whole[slab]

    each_core(body)


def merge_kernel(dz, dy, came, z_out, y_out):
    first = forwards_first(lax.axis_index("tm"))
    more = came[...].astype(F32)
    z_out[:, KEY] = (dz[:, KEY] + jnp.where(first, more, 0.0)).astype(BF16)
    y_out[:, KEY] = (dy[:, KEY] + jnp.where(first, 0.0, more)).astype(BF16)
    z_out[:, VALUE] = dz[:, VALUE].astype(BF16)
    y_out[:, VALUE] = dy[:, VALUE].astype(BF16)


def place_kernel(block, far, *refs):
    n = len(far)
    lists, total = refs[0], refs[-1]
    frame = lax.axis_index("tm")
    total[...] = jnp.zeros_like(total)
    for swap, came_k, came_v in zip(far, refs[1 : 1 + n], refs[1 + n : -1]):
        for slab in range(2):
            b, exists = swap.block_of_theirs(lists, frame, slab, 0)
            rows = pl.ds(pl.multiple_of(b * block, block), block)
            for came, cols in ((came_k, KEY), (came_v, VALUE)):
                part = came[rows_of(slab, block), :].astype(F32)
                total[rows, cols] += jnp.where(exists, part, 0.0)


def add_kernel(swaps, near, *refs):
    frame = lax.axis_index("tm")
    total = near[...]
    for swap, came in zip(swaps, refs[:-1]):
        _, _, exists = swap.partner(frame)
        total = total + jnp.where(exists, came[...].astype(F32), 0.0)
    refs[-1][...] = total


def gather_kernel(swap, near, came, keep, send):
    _, _, exists = swap.partner(lax.axis_index("tm"))
    half = near.shape[0] // 2

    def body(mine):
        for slab, out in ((1 - mine, send), (mine, keep)):
            rows = rows_of(slab, half)
            part = jnp.where(exists, came[rows, :].astype(F32), 0.0)
            out[...] = (near[rows, :] + part).astype(BF16)

    each_core(body)


def finish_kernel(keep, came, first, second):
    def body(mine):
        for head, source in ((mine, keep), (1 - mine, came)):
            first[:, head_cols(head)] = source[:, KEY]
            second[:, head_cols(head)] = source[:, VALUE]

    each_core(body)


def per_device(queries, key_rows, value_rows, out_grad, block_lists):
    s_dev, width = queries.shape
    count = lax.axis_size("tm")
    block = s_dev // 2
    pair = sds((s_dev, 2 * DH), BF16)
    single = sds((s_dev, DH), BF16)
    frame_two = sds((2 * s_dev, 2 * DH), BF16)
    frame_one = sds((2 * s_dev, DH), BF16)
    frame_sum = sds((2 * s_dev, 2 * DH), F32)
    stat_row = sds((8, 2 * s_dev), F32)
    turned_sum = sds((DH, 2 * s_dev), F32)
    turned_bf = sds((DH, 2 * s_dev), BF16)
    levels = count.bit_length() - 1
    near_swap, relayed = Swap(count, 0, False), Swap(count, 0, True)
    z_swap, y_swap = Swap(count, 1, False), Swap(count, 1, True)
    far = [Swap(count, level, second) for level in range(2, levels) for second in (False, True)]
    far = [swap for swap in far if swap.moves]
    n = len(far)
    grad_one = pltpu.VMEM((2 * s_dev, DH), F32)

    def across(value):
        return lax.ppermute(value, "space", [(0, 1), (1, 0)])

    def swapped(value, swap):
        return lax.ppermute(value, "tm", swap.pairs)

    def scores(pieces):
        return pltpu.VMEM((pieces * block, s_dev), F32)


    k_came, v_came = across(key_rows), across(value_rows)
    sources = (key_rows, value_rows, queries, out_grad, block_lists.T)
    k_own, v_own, qg_own, qg_send, lists = call(
        pack_kernel,
        tuple(pltpu.with_memory_space_constraint(a, pltpu.HBM) for a in sources),
        [single, single, pair, pair, sds(sources[4].shape, jnp.int32)],
        scratch=[pltpu.SemaphoreType.DMA((7,))],
        source=HBM,
        scalars=HBM,
    )
    (keys,) = call(keys_kernel, (k_own, k_came), [frame_one])
    values, kv = call(values_kernel, (keys, v_own, v_came), [frame_one, frame_two])
    qg_send, _ = lax.optimization_barrier((qg_send, kv))
    y_k = swapped(keys, y_swap)
    z_k = swapped(keys, z_swap)
    a_kv = swapped(kv, near_swap)
    y_v = swapped(values, y_swap)
    z_v = swapped(values, z_swap)
    y_k, qg_came = lax.optimization_barrier((y_k, across(qg_send)))
    work = 4 * s_dev * s_dev * DH
    qg, turned = call(join_kernel, (qg_own, qg_came), [frame_two, turned_bf], flops=15 * work)
    y_k, z_k, turned = lax.optimization_barrier((y_k, z_k, turned))
    kv, _ = lax.optimization_barrier((kv, turned))
    far_send = call(functools.partial(select_kernel, far, block), (lists, kv), [pair] * n)
    (relay_k,) = call(relay_kernel, (y_k, z_k), [frame_one])
    relay_k, far_send = lax.optimization_barrier((relay_k, far_send))
    a_kv, _ = lax.optimization_barrier((a_kv, relay_k))
    c_k = swapped(relay_k, near_swap)
    far_kv = [swapped(value, swap) for value, swap in zip(far_send, far)]
    stat, acc = call(
        functools.partial(near_kernel, block, near_swap),
        (lists, qg, kv, a_kv),
        [stat_row, turned_sum],
        scratch=[scores(6)],
    )
    score_two = sds((2, s_dev, s_dev), F32)
    y_v, z_v, stat = lax.optimization_barrier((y_v, z_v, stat))
    (relay_v,) = call(relay_kernel, (y_v, z_v), [frame_one])
    relay_v, stat = lax.optimization_barrier((relay_v, stat))
    c_v = swapped(relay_v, near_swap)
    stat, acc, late_scores = call(
        functools.partial(middle_kernel, block, (z_swap, y_swap, relayed)),
        (lists, qg, stat, acc, y_k, z_k, y_v, z_v, c_k),
        [stat_row, turned_sum, score_two],
        scratch=[scores(4)],
    )
    acc, far_kv = lax.optimization_barrier((acc, far_kv))
    lse, part, *far_dv = call(
        functools.partial(close_kernel, block, far),
        (qg, stat, acc, *far_kv),
        [stat_row, turned_sum] + [single] * n,
        scratch=[scores(n)],
    )
    dc_v, probs = call(
        functools.partial(shares_kernel, block, relayed),
        (lists, qg, lse, late_scores),
        [frame_one, score_two],
        scratch=[grad_one],
    )
    dc_v_came = swapped(dc_v, near_swap)
    far_dv_came = [swapped(value, swap) for value, swap in zip(far_dv, far)]
    o, row_dot, dc_k, dq, *far_grad = call(
        functools.partial(late_kernel, block, relayed, far),
        (lists, qg, turned, lse, part, probs, c_k, c_v, *far_kv),
        [turned_bf, stat_row, frame_one, turned_sum] + [single] * n,
        scratch=[grad_one],
    )
    far_dk_came = [swapped(value, swap) for value, swap in zip(far_grad, far)]
    dc_k_came = swapped(dc_k, near_swap)
    da, dq = call(
        functools.partial(first_kernel, block, near_swap),
        (lists, qg, lse, row_dot, dq, a_kv),
        [frame_two, turned_sum],
        scratch=[pltpu.VMEM((2 * s_dev, 2 * DH), F32)],
    )
    da, dc_k_came = lax.optimization_barrier((da, dc_k_came))
    da_came = swapped(da, near_swap)
    dc_v_came, far_dv_came = lax.optimization_barrier((dc_v_came, far_dv_came))
    dz, dy, dq = call(
        functools.partial(second_kernel, block, (z_swap, y_swap)),
        (lists, qg, lse, row_dot, dq, dc_v_came, y_k, z_k, y_v, z_v),
        [frame_sum, frame_sum, turned_sum],
        flops=20 * work,
    )
    dz, dy = call(merge_kernel, (dz, dy, dc_k_came), [frame_two, frame_two])
    dy_came = swapped(dy, y_swap)
    dz_came = swapped(dz, z_swap)
    dq, dz, dy = lax.optimization_barrier((dq, dz, dy))
    far_dk_came, dq = lax.optimization_barrier((far_dk_came, dq))
    (placed,) = call(functools.partial(place_kernel, block, far), (lists, *far_dk_came, *far_dv_came), [frame_sum])
    near, q_keep, q_send = call(
        own_kernel,
        (qg, lse, row_dot, dq, o, kv, placed),
        [frame_sum, pair, pair],
        flops=20 * work,
    )
    outputs = [sds((s_dev, width), BF16)] * 2
    attn_out, grad_q = call(finish_kernel, (q_keep, across(q_send)), outputs)
    near, attn_out, grad_q = lax.optimization_barrier((near, attn_out, grad_q))
    (near,) = call(
        functools.partial(add_kernel, (near_swap, y_swap)),
        (near, da_came, dy_came),
        [frame_sum],
        flops=20 * work,
    )
    k_keep, k_send = call(
        functools.partial(gather_kernel, z_swap), (near, dz_came), [pair, pair]
    )
    grad_k, grad_v = call(finish_kernel, (k_keep, across(k_send)), outputs)
    return attn_out, grad_q, grad_k, grad_v


def solution(mesh):
    rows = P(("groups", "tm", "space"), None)
    return jax.shard_map(
        per_device,
        mesh=mesh,
        in_specs=(rows, rows, rows, rows, P("groups", None)),
        out_specs=(rows, rows, rows, rows),
        check_vma=False,
    )
```

```python
import functools
import math

import jax
import jax.numpy as jnp
from jax import lax
from jax.experimental import pallas as pl
from jax.experimental.pallas import tpu as pltpu
from jax.sharding import PartitionSpec as P

DH = 128
F32 = jnp.float32
BF16 = jnp.bfloat16
VMEM = pl.BlockSpec(memory_space=pltpu.VMEM)
SMEM = pl.BlockSpec(memory_space=pltpu.SMEM)
HBM = pl.BlockSpec(memory_space=pltpu.HBM)
NEG = -1e30
SCALE = 1.0 / math.sqrt(DH)
EXP_SCALE = SCALE * math.log2(math.e)
KEY = slice(0, DH)
VALUE = slice(DH, 2 * DH)
sds = jax.ShapeDtypeStruct


def dot_nn(a, b):
    return lax.dot_general(a, b, (((1,), (0,)), ((), ())), preferred_element_type=F32)


def dot_nt(a, b):
    return lax.dot_general(a, b, (((1,), (1,)), ((), ())), preferred_element_type=F32)


def dot_tn(a, b):
    return lax.dot_general(a, b, (((0,), (0,)), ((), ())), preferred_element_type=F32)


def call(kernel, args, out_shape, scratch=(), source=VMEM, scalars=SMEM, flops=1024):
    return pl.pallas_call(
        kernel,
        out_shape=out_shape,
        in_specs=[scalars if a.dtype == jnp.int32 else source for a in args],
        out_specs=tuple(VMEM for _ in out_shape),
        scratch_shapes=list(scratch),
        compiler_params=pltpu.CompilerParams(vmem_limit_bytes=40 << 20),
        cost_estimate=pl.CostEstimate(flops=flops, bytes_accessed=1024, transcendentals=0),
    )(*args)


def swap_pairs(count, distance, second):
    pairs = []
    for frame in range(count):
        up = ((frame // distance) % 2 == 0) != second
        target = frame + distance if up else frame - distance
        pairs.append((frame, target if 0 <= target < count else frame))
    return pairs


class Swap:
    def __init__(self, count, level, second):
        self.count, self.level, self.second = count, level, second
        self.levels = count.bit_length() - 1
        self.pairs = swap_pairs(count, 1 << level, second)
        self.moves = any(source != target for source, target in self.pairs)

    def partner(self, frame):
        odd = lax.rem(lax.shift_right_logical(frame, self.level), 2)
        later = odd == (1 if self.second else 0)
        other = jnp.where(later, frame + (1 << self.level), frame - (1 << self.level))
        return other, later, jnp.logical_and(other >= 0, other < self.count)

    def slot(self, later, k):
        base = 0 if self.level == 0 else self.level + 1
        return jnp.where(later, self.levels + 1, 0) + base + k

    def block_of_mine(self, lists, frame, slab, k):
        other, later, exists = self.partner(frame)
        entry = lists[self.slot(later, k), frame * 2 + slab]
        return jnp.clip(entry - other * 4, 0, 3), exists

    def block_of_theirs(self, lists, frame, slab, k):
        other, later, exists = self.partner(frame)
        row = jnp.where(exists, other, frame) * 2 + slab
        entry = lists[self.slot(jnp.logical_not(later), k), row]
        return jnp.clip(entry - frame * 4, 0, 3), exists


def head_cols(head):
    return slice(head * DH, (head + 1) * DH)


def rows_of(slab, half):
    return slice(slab * half, (slab + 1) * half)


def each_core(body):
    core = lax.axis_index("space")
    for mine in range(2):
        pl.when(core == mine)(functools.partial(body, mine))


def pack_kernel(k, v, q, g, lists, k_own, v_own, qg_own, qg_send, lists_out, sems):
    def body(mine):
        moves = [(lists, lists_out)]
        for source, out in ((k, k_own), (v, v_own)):
            moves.append((source.at[:, head_cols(mine)], out))
        for head, out in ((mine, qg_own), (1 - mine, qg_send)):
            for source, cols in ((q, KEY), (g, VALUE)):
                moves.append((source.at[:, head_cols(head)], out.at[:, cols]))
        copies = [
            pltpu.make_async_copy(source, out, sems.at[n]) for n, (source, out) in enumerate(moves)
        ]
        for copy in copies:
            copy.start()
        for copy in copies:
            copy.wait()

    each_core(body)


def keys_kernel(own, came, keys):
    half = own.shape[0]

    def body(mine):
        keys[rows_of(mine, half), :] = own[...]
        keys[rows_of(1 - mine, half), :] = came[:, head_cols(mine)]

    each_core(body)


def values_kernel(keys, own, came, values, kv):
    half = own.shape[0]

    def body(mine):
        for slab, part in ((mine, own[...]), (1 - mine, came[:, head_cols(mine)])):
            rows = rows_of(slab, half)
            values[rows, :] = part
            kv[rows, VALUE] = part
            kv[rows, KEY] = keys[rows, :]

    each_core(body)


def select_kernel(far, block, lists, kv, *sends):
    frame = lax.axis_index("tm")
    for swap, send in zip(far, sends):
        for slab in range(2):
            b, _ = swap.block_of_theirs(lists, frame, slab, 0)
            row = pl.multiple_of(b * block, block)
            send[slab * block : (slab + 1) * block, :] = kv[pl.ds(row, block), :]


def forwards_first(frame):
    return lax.rem(frame, 2) == lax.rem(lax.shift_right_logical(frame, 1), 2)


def relay_kernel(y, z, out):
    first = forwards_first(lax.axis_index("tm"))

    @pl.when(first)
    def _():
        out[...] = z[...]

    @pl.when(jnp.logical_not(first))
    def _():
        out[...] = y[...]


class Piece:
    def __init__(self, k, v, row, size, exists=None, dk=None, dv=None, add=True):
        self.k_at, self.v_at, self.exists = k, v, exists
        self.rows, self.size = pl.ds(row, size), size
        self.dk, self.dv, self.add = dk, dv, add

    def store(self, at, value):
        ref, cols = at
        if self.add:
            ref[self.rows, cols] += value
        else:
            ref[self.rows, cols] = value.astype(ref.dtype)


def stack(parts):
    return parts[0] if len(parts) == 1 else jnp.concatenate(parts, axis=0)


def keys_of(group):
    return stack([p.k_at[0][p.rows, p.k_at[1]] for p in group])


def values_of(group):
    return stack([p.v_at[0][p.rows, p.v_at[1]] for p in group])


def by_piece(group, value):
    at = 0
    for piece in group:
        yield piece, value[at : at + piece.size, :]
        at += piece.size


def store_grads(group, value, name):
    for piece, part in by_piece(group, value):
        piece.store(getattr(piece, name), part)


def listed(swap, lists, frame, slab, block, k, v, count=1, **grads):
    pieces = []
    for n in range(count):
        b, exists = swap.block_of_mine(lists, frame, slab, n)
        pieces.append(Piece(k, v, pl.multiple_of(b * block, block), block, exists, **grads))
    return pieces


def arrived(swap, frame, slab, block, kv, **grads):
    _, _, exists = swap.partner(frame)
    return Piece((kv, KEY), (kv, VALUE), slab * block, block, exists, add=False, **grads)


def raised(group, s, base):
    parts = []
    for piece, part in by_piece(group, s):
        low = base if piece.exists is None else jnp.where(piece.exists, base, -NEG)
        parts.append(jnp.exp2(part * EXP_SCALE - low))
    return stack(parts)


def score_groups(q, groups, s_ref, peak):
    at = 0
    for group in groups:
        s = dot_nt(keys_of(group), q)
        s_ref[at : at + s.shape[0], :] = s
        at += s.shape[0]
        for piece, part in by_piece(group, s):
            top = jnp.max(part, axis=0, keepdims=True)
            if piece.exists is not None:
                top = jnp.where(piece.exists, top, NEG)
            peak = top if peak is None else jnp.maximum(peak, top)
    return peak


def group_scores(groups, s_ref):
    at = 0
    for group in groups:
        size = sum(piece.size for piece in group)
        yield group, s_ref[at : at + size, :]
        at += size


def forward_slab(q, groups, with_values, s_ref, old):
    peak = score_groups(q, groups, s_ref, None if old is None else old[0])
    total, acc = 0.0, 0.0
    if old is not None:
        shrink = jnp.exp2((old[0] - peak) * EXP_SCALE)
        total, acc = old[1] * shrink, old[2] * shrink
    for j, (group, s) in enumerate(group_scores(groups, s_ref)):
        e = raised(group, s, peak * EXP_SCALE)
        total = total + jnp.sum(e, axis=0, keepdims=True)
        if j < with_values:
            acc = acc + dot_tn(values_of(group), e.astype(BF16))
    return peak, total, acc


def backward_group(q, g, lse, row_dot, group, p=None):
    k = keys_of(group)
    if p is None:
        p = raised(group, dot_nt(k, q), lse)
    if group[0].dv is not None:
        store_grads(group, dot_nn(p.astype(BF16), g), "dv")
    ds = (p * (dot_nt(values_of(group), g) - row_dot)).astype(BF16)
    if group[0].dk is not None:
        store_grads(group, dot_nn(ds, q) * SCALE, "dk")
    return dot_tn(k, ds)


def join_kernel(own, came, out, turned):
    half = own.shape[0]

    def body(mine):
        for slab, source in ((mine, own), (1 - mine, came)):
            rows = rows_of(slab, half)
            out[rows, :] = source[...]
            turned[:, rows] = source[:, VALUE].T

    each_core(body)


ALL = slice(None)


def store_state(refs, rows, peak, total, acc):
    stat, acc_ref = refs
    stat[0:1, rows] = peak
    stat[1:2, rows] = total
    acc_ref[:, rows] = acc


def load_state(refs, rows):
    stat, acc_ref = refs
    return stat[0:1, rows], stat[1:2, rows], acc_ref[:, rows]


def own_groups(kv, half, **grads):
    return [
        [Piece((kv, KEY), (kv, VALUE), r, half, **grads)] for r in range(0, kv.shape[0], half)
    ]


def near_kernel(block, swap, lists, qg, kv, a_kv, stat, acc, s_ref):
    half = qg.shape[0] // 2
    frame = lax.axis_index("tm")
    for slab in range(2):
        rows = rows_of(slab, half)
        groups = own_groups(kv, half)
        groups.append(
            listed(swap, lists, frame, slab, block, (a_kv, KEY), (a_kv, VALUE), 2)
        )
        store_state((stat, acc), rows, *forward_slab(qg[rows, KEY], groups, 3, s_ref, None))


def middle_kernel(
    block, swaps, lists, qg, stat, acc, y_k, z_k, y_v, z_v, c_k, stat2, acc2, late, s_ref
):
    half = qg.shape[0] // 2
    frame = lax.axis_index("tm")
    z, y, relayed = swaps
    for slab in range(2):
        rows = rows_of(slab, half)
        at = (lists, frame, slab, block)
        group = listed(z, *at, (z_k, ALL), (z_v, ALL)) + listed(y, *at, (y_k, ALL), (y_v, ALL))
        more = listed(relayed, *at, (c_k, ALL), None, 2)
        old = load_state((stat, acc), rows)
        new = forward_slab(qg[rows, KEY], [group, more], 1, s_ref, old)
        store_state((stat2, acc2), rows, *new)
        late[slab] = s_ref[2 * block :, :]


def close_kernel(block, far, qg, stat, acc, *refs):
    n = len(far)
    far_kv = refs[:n]
    lse_ref, part_ref = refs[n : n + 2]
    far_dv = refs[n + 2 : 2 * n + 2]
    s_ref = refs[2 * n + 2]
    half = qg.shape[0] // 2
    frame = lax.axis_index("tm")
    for slab in range(2):
        rows = rows_of(slab, half)
        q, g = qg[rows, KEY], qg[rows, VALUE]
        groups = [
            [arrived(swap, frame, slab, block, kv, dv=(out, ALL))]
            for swap, kv, out in zip(far, far_kv, far_dv)
        ]
        old = load_state((stat, acc), rows)
        peak, total, out = forward_slab(q, groups, n, s_ref, old)
        part_ref[:, rows] = out / total
        lse = peak * EXP_SCALE + jnp.log2(total)
        lse_ref[0:1, rows] = lse
        for group, s in group_scores(groups, s_ref):
            p = raised(group, s, lse)
            store_grads(group, dot_nn(p.astype(BF16), g), "dv")


def shares_kernel(block, relayed, lists, qg, lse_ref, s_ref, dc_v, p_ref, grad):
    half = qg.shape[0] // 2
    frame = lax.axis_index("tm")
    grad[...] = jnp.zeros_like(grad)
    for slab in range(2):
        rows = rows_of(slab, half)
        group = listed(relayed, lists, frame, slab, block, None, None, 2, dv=(grad, ALL))
        p = raised(group, s_ref[slab], lse_ref[0:1, rows])
        p_ref[slab] = p
        store_grads(group, dot_nn(p.astype(BF16), qg[rows, VALUE]), "dv")
    dc_v[...] = grad[...].astype(BF16)


def late_kernel(block, relayed, far, *refs):
    n = len(far)
    lists, qg, turned, lse_ref, part_ref, p_ref, c_k, c_v = refs[:8]
    far_kv = refs[8 : 8 + n]
    o_ref, dot_ref, dc_k, dq_ref = refs[8 + n : 12 + n]
    far_grad = refs[12 + n : 12 + 2 * n]
    grad = refs[12 + 2 * n]
    half = qg.shape[0] // 2
    frame = lax.axis_index("tm")
    grad[...] = jnp.zeros_like(grad)
    for slab in range(2):
        rows = rows_of(slab, half)
        q, g, lse = qg[rows, KEY], qg[rows, VALUE], lse_ref[0:1, rows]
        group = listed(
            relayed, lists, frame, slab, block, (c_k, ALL), (c_v, ALL), 2, dk=(grad, ALL)
        )
        p = p_ref[slab]
        o = (part_ref[:, rows] + dot_tn(values_of(group), p.astype(BF16))).astype(BF16)
        o_ref[:, rows] = o
        products = turned[:, rows].astype(F32) * o.astype(F32)
        row_dot = jnp.sum(products, axis=0, keepdims=True)
        dot_ref[0:1, rows] = row_dot
        dq = backward_group(q, g, lse, row_dot, group, p)
        for swap, kv, out in zip(far, far_kv, far_grad):
            group = [arrived(swap, frame, slab, block, kv, dk=(out, ALL))]
            dq = dq + backward_group(q, g, lse, row_dot, group)
        dq_ref[:, rows] = dq
    dc_k[...] = grad[...].astype(BF16)


def first_kernel(block, swap, lists, qg, lse_ref, dot_ref, dq_old, a_kv, da, dq_ref, grad):
    half = qg.shape[0] // 2
    frame = lax.axis_index("tm")
    grad[...] = jnp.zeros_like(grad)
    for slab in range(2):
        rows = rows_of(slab, half)
        q, g, lse, row_dot = qg[rows, KEY], qg[rows, VALUE], lse_ref[0:1, rows], dot_ref[0:1, rows]
        group = listed(
            swap, lists, frame, slab, block, (a_kv, KEY), (a_kv, VALUE), 2,
            dk=(grad, KEY), dv=(grad, VALUE),
        )
        dq_ref[:, rows] = dq_old[:, rows] + backward_group(q, g, lse, row_dot, group)
    da[...] = grad[...].astype(BF16)


def second_kernel(
    block, swaps, lists, qg, lse_ref, dot_ref, dq_old, came, y_k, z_k, y_v, z_v, dz, dy, dq_ref
):
    half = qg.shape[0] // 2
    frame = lax.axis_index("tm")
    z, y = swaps
    relays = forwards_first(frame)
    more = came[...].astype(F32)
    for ref, takes in ((dz, relays), (dy, jnp.logical_not(relays))):
        ref[:, KEY] = jnp.zeros_like(more)
        ref[:, VALUE] = jnp.where(takes, more, 0.0)
    for slab in range(2):
        rows = rows_of(slab, half)
        q, g, lse, row_dot = qg[rows, KEY], qg[rows, VALUE], lse_ref[0:1, rows], dot_ref[0:1, rows]
        at = (lists, frame, slab, block)
        group = listed(z, *at, (z_k, ALL), (z_v, ALL), dk=(dz, KEY), dv=(dz, VALUE))
        group += listed(y, *at, (y_k, ALL), (y_v, ALL), dk=(dy, KEY), dv=(dy, VALUE))
        dq_ref[:, rows] = dq_old[:, rows] + backward_group(q, g, lse, row_dot, group)


def own_kernel(qg, lse_ref, dot_ref, dq_old, o, kv, placed, near, keep, send):
    half = qg.shape[0] // 2
    near[...] = placed[...]
    whole = []
    for slab in range(2):
        rows = rows_of(slab, half)
        q, g, lse, row_dot = qg[rows, KEY], qg[rows, VALUE], lse_ref[0:1, rows], dot_ref[0:1, rows]
        dq = dq_old[:, rows]
        for group in own_groups(kv, half, dk=(near, KEY), dv=(near, VALUE)):
            dq = dq + backward_group(q, g, lse, row_dot, group)
        whole.append((dq.T * SCALE).astype(BF16))

    def body(mine):
        for slab in range(2):
            out = keep if slab == mine else send
            out[:, KEY] = o[:, rows_of(slab, half)].T
            out[:, VALUE] = whole[slab]

    each_core(body)


def merge_kernel(dz, dy, came, z_out, y_out):
    first = forwards_first(lax.axis_index("tm"))
    more = came[...].astype(F32)
    z_out[:, KEY] = (dz[:, KEY] + jnp.where(first, more, 0.0)).astype(BF16)
    y_out[:, KEY] = (dy[:, KEY] + jnp.where(first, 0.0, more)).astype(BF16)
    z_out[:, VALUE] = dz[:, VALUE].astype(BF16)
    y_out[:, VALUE] = dy[:, VALUE].astype(BF16)


def place_kernel(block, far, *refs):
    n = len(far)
    lists, total = refs[0], refs[-1]
    frame = lax.axis_index("tm")
    total[...] = jnp.zeros_like(total)
    for swap, came_k, came_v in zip(far, refs[1 : 1 + n], refs[1 + n : -1]):
        for slab in range(2):
            b, exists = swap.block_of_theirs(lists, frame, slab, 0)
            rows = pl.ds(pl.multiple_of(b * block, block), block)
            for came, cols in ((came_k, KEY), (came_v, VALUE)):
                part = came[rows_of(slab, block), :].astype(F32)
                total[rows, cols] += jnp.where(exists, part, 0.0)


def add_kernel(swaps, near, *refs):
    frame = lax.axis_index("tm")
    total = near[...]
    for swap, came in zip(swaps, refs[:-1]):
        _, _, exists = swap.partner(frame)
        total = total + jnp.where(exists, came[...].astype(F32), 0.0)
    refs[-1][...] = total


def gather_kernel(swap, near, came, keep, send):
    _, _, exists = swap.partner(lax.axis_index("tm"))
    half = near.shape[0] // 2

    def body(mine):
        for slab, out in ((1 - mine, send), (mine, keep)):
            rows = rows_of(slab, half)
            part = jnp.where(exists, came[rows, :].astype(F32), 0.0)
            out[...] = (near[rows, :] + part).astype(BF16)

    each_core(body)


def finish_kernel(keep, came, first, second):
    def body(mine):
        for head, source in ((mine, keep), (1 - mine, came)):
            first[:, head_cols(head)] = source[:, KEY]
            second[:, head_cols(head)] = source[:, VALUE]

    each_core(body)


def per_device(queries, key_rows, value_rows, out_grad, block_lists):
    s_dev, width = queries.shape
    count = lax.axis_size("tm")
    block = s_dev // 2
    pair = sds((s_dev, 2 * DH), BF16)
    single = sds((s_dev, DH), BF16)
    frame_two = sds((2 * s_dev, 2 * DH), BF16)
    frame_one = sds((2 * s_dev, DH), BF16)
    frame_sum = sds((2 * s_dev, 2 * DH), F32)
    stat_row = sds((8, 2 * s_dev), F32)
    turned_sum = sds((DH, 2 * s_dev), F32)
    turned_bf = sds((DH, 2 * s_dev), BF16)
    levels = count.bit_length() - 1
    near_swap, relayed = Swap(count, 0, False), Swap(count, 0, True)
    z_swap, y_swap = Swap(count, 1, False), Swap(count, 1, True)
    far = [Swap(count, level, second) for level in range(2, levels) for second in (False, True)]
    far = [swap for swap in far if swap.moves]
    n = len(far)
    grad_one = pltpu.VMEM((2 * s_dev, DH), F32)

    def across(value):
        return lax.ppermute(value, "space", [(0, 1), (1, 0)])

    def swapped(value, swap):
        return lax.ppermute(value, "tm", swap.pairs)

    def scores(pieces):
        return pltpu.VMEM((pieces * block, s_dev), F32)


    k_came, v_came = across(key_rows), across(value_rows)
    sources = (key_rows, value_rows, queries, out_grad, block_lists.T)
    k_own, v_own, qg_own, qg_send, lists = call(
        pack_kernel,
        tuple(pltpu.with_memory_space_constraint(a, pltpu.HBM) for a in sources),
        [single, single, pair, pair, sds(sources[4].shape, jnp.int32)],
        scratch=[pltpu.SemaphoreType.DMA((7,))],
        source=HBM,
        scalars=HBM,
    )
    (keys,) = call(keys_kernel, (k_own, k_came), [frame_one])
    values, kv = call(values_kernel, (keys, v_own, v_came), [frame_one, frame_two])
    qg_send, _ = lax.optimization_barrier((qg_send, keys))
    y_k = swapped(keys, y_swap)
    z_k = swapped(keys, z_swap)
    a_kv = swapped(kv, near_swap)
    y_v = swapped(values, y_swap)
    z_v = swapped(values, z_swap)
    y_k, qg_came = lax.optimization_barrier((y_k, across(qg_send)))
    work = 4 * s_dev * s_dev * DH
    qg, turned = call(join_kernel, (qg_own, qg_came), [frame_two, turned_bf], flops=15 * work)
    y_k, z_k, turned = lax.optimization_barrier((y_k, z_k, turned))
    kv, _ = lax.optimization_barrier((kv, turned))
    far_send = call(functools.partial(select_kernel, far, block), (lists, kv), [pair] * n)
    (relay_k,) = call(relay_kernel, (y_k, z_k), [frame_one])
    relay_k, far_send = lax.optimization_barrier((relay_k, far_send))
    a_kv, _ = lax.optimization_barrier((a_kv, relay_k))
    c_k = swapped(relay_k, near_swap)
    far_kv = [swapped(value, swap) for value, swap in zip(far_send, far)]
    stat, acc = call(
        functools.partial(near_kernel, block, near_swap),
        (lists, qg, kv, a_kv),
        [stat_row, turned_sum],
        scratch=[scores(6)],
    )
    score_two = sds((2, s_dev, s_dev), F32)
    y_v, z_v, stat = lax.optimization_barrier((y_v, z_v, stat))
    (relay_v,) = call(relay_kernel, (y_v, z_v), [frame_one])
    relay_v, stat = lax.optimization_barrier((relay_v, stat))
    c_v = swapped(relay_v, near_swap)
    stat, acc, late_scores = call(
        functools.partial(middle_kernel, block, (z_swap, y_swap, relayed)),
        (lists, qg, stat, acc, y_k, z_k, y_v, z_v, c_k),
        [stat_row, turned_sum, score_two],
        scratch=[scores(4)],
    )
    acc, far_kv = lax.optimization_barrier((acc, far_kv))
    lse, part, *far_dv = call(
        functools.partial(close_kernel, block, far),
        (qg, stat, acc, *far_kv),
        [stat_row, turned_sum] + [single] * n,
        scratch=[scores(n)],
    )
    dc_v, probs = call(
        functools.partial(shares_kernel, block, relayed),
        (lists, qg, lse, late_scores),
        [frame_one, score_two],
        scratch=[grad_one],
    )
    dc_v_came = swapped(dc_v, near_swap)
    far_dv_came = [swapped(value, swap) for value, swap in zip(far_dv, far)]
    o, row_dot, dc_k, dq, *far_grad = call(
        functools.partial(late_kernel, block, relayed, far),
        (lists, qg, turned, lse, part, probs, c_k, c_v, *far_kv),
        [turned_bf, stat_row, frame_one, turned_sum] + [single] * n,
        scratch=[grad_one],
    )
    far_dk_came = [swapped(value, swap) for value, swap in zip(far_grad, far)]
    dc_k_came = swapped(dc_k, near_swap)
    da, dq = call(
        functools.partial(first_kernel, block, near_swap),
        (lists, qg, lse, row_dot, dq, a_kv),
        [frame_two, turned_sum],
        scratch=[pltpu.VMEM((2 * s_dev, 2 * DH), F32)],
    )
    da, dc_k_came = lax.optimization_barrier((da, dc_k_came))
    da_came = swapped(da, near_swap)
    dc_v_came, far_dv_came = lax.optimization_barrier((dc_v_came, far_dv_came))
    dz, dy, dq = call(
        functools.partial(second_kernel, block, (z_swap, y_swap)),
        (lists, qg, lse, row_dot, dq, dc_v_came, y_k, z_k, y_v, z_v),
        [frame_sum, frame_sum, turned_sum],
        flops=20 * work,
    )
    dz, dy = call(merge_kernel, (dz, dy, dc_k_came), [frame_two, frame_two])
    dy_came = swapped(dy, y_swap)
    dz_came = swapped(dz, z_swap)
    dq, dz, dy = lax.optimization_barrier((dq, dz, dy))
    far_dk_came, dq = lax.optimization_barrier((far_dk_came, dq))
    (placed,) = call(functools.partial(place_kernel, block, far), (lists, *far_dk_came, *far_dv_came), [frame_sum])
    near, q_keep, q_send = call(
        own_kernel,
        (qg, lse, row_dot, dq, o, kv, placed),
        [frame_sum, pair, pair],
        flops=20 * work,
    )
    outputs = [sds((s_dev, width), BF16)] * 2
    attn_out, grad_q = call(finish_kernel, (q_keep, across(q_send)), outputs)
    near, attn_out, grad_q = lax.optimization_barrier((near, attn_out, grad_q))
    (near,) = call(
        functools.partial(add_kernel, (near_swap, y_swap)),
        (near, da_came, dy_came),
        [frame_sum],
        flops=20 * work,
    )
    k_keep, k_send = call(
        functools.partial(gather_kernel, z_swap), (near, dz_came), [pair, pair]
    )
    grad_k, grad_v = call(finish_kernel, (k_keep, across(k_send)), outputs)
    return attn_out, grad_q, grad_k, grad_v


def solution(mesh):
    rows = P(("groups", "tm", "space"), None)
    return jax.shard_map(
        per_device,
        mesh=mesh,
        in_specs=(rows, rows, rows, rows, P("groups", None)),
        out_specs=(rows, rows, rows, rows),
        check_vma=False,
    )
```

```python
import functools
import math

import jax
import jax.numpy as jnp
from jax import lax
from jax.experimental import pallas as pl
from jax.experimental.pallas import tpu as pltpu
from jax.sharding import PartitionSpec as P

DH = 128
F32 = jnp.float32
BF16 = jnp.bfloat16
VMEM = pl.BlockSpec(memory_space=pltpu.VMEM)
SMEM = pl.BlockSpec(memory_space=pltpu.SMEM)
HBM = pl.BlockSpec(memory_space=pltpu.HBM)
NEG = -1e30
SCALE = 1.0 / math.sqrt(DH)
EXP_SCALE = SCALE * math.log2(math.e)
KEY = slice(0, DH)
VALUE = slice(DH, 2 * DH)
sds = jax.ShapeDtypeStruct


def dot_nn(a, b):
    return lax.dot_general(a, b, (((1,), (0,)), ((), ())), preferred_element_type=F32)


def dot_nt(a, b):
    return lax.dot_general(a, b, (((1,), (1,)), ((), ())), preferred_element_type=F32)


def dot_tn(a, b):
    return lax.dot_general(a, b, (((0,), (0,)), ((), ())), preferred_element_type=F32)


def call(kernel, args, out_shape, scratch=(), source=VMEM, scalars=SMEM, flops=1024):
    return pl.pallas_call(
        kernel,
        out_shape=out_shape,
        in_specs=[scalars if a.dtype == jnp.int32 else source for a in args],
        out_specs=tuple(VMEM for _ in out_shape),
        scratch_shapes=list(scratch),
        compiler_params=pltpu.CompilerParams(vmem_limit_bytes=40 << 20),
        cost_estimate=pl.CostEstimate(flops=flops, bytes_accessed=1024, transcendentals=0),
    )(*args)


def swap_pairs(count, distance, second):
    pairs = []
    for frame in range(count):
        up = ((frame // distance) % 2 == 0) != second
        target = frame + distance if up else frame - distance
        pairs.append((frame, target if 0 <= target < count else frame))
    return pairs


class Swap:
    def __init__(self, count, level, second):
        self.count, self.level, self.second = count, level, second
        self.levels = count.bit_length() - 1
        self.pairs = swap_pairs(count, 1 << level, second)
        self.moves = any(source != target for source, target in self.pairs)

    def partner(self, frame):
        odd = lax.rem(lax.shift_right_logical(frame, self.level), 2)
        later = odd == (1 if self.second else 0)
        other = jnp.where(later, frame + (1 << self.level), frame - (1 << self.level))
        return other, later, jnp.logical_and(other >= 0, other < self.count)

    def slot(self, later, k):
        base = 0 if self.level == 0 else self.level + 1
        return jnp.where(later, self.levels + 1, 0) + base + k

    def block_of_mine(self, lists, frame, slab, k):
        other, later, exists = self.partner(frame)
        entry = lists[self.slot(later, k), frame * 2 + slab]
        return jnp.clip(entry - other * 4, 0, 3), exists

    def block_of_theirs(self, lists, frame, slab, k):
        other, later, exists = self.partner(frame)
        row = jnp.where(exists, other, frame) * 2 + slab
        entry = lists[self.slot(jnp.logical_not(later), k), row]
        return jnp.clip(entry - frame * 4, 0, 3), exists


def head_cols(head):
    return slice(head * DH, (head + 1) * DH)


def rows_of(slab, half):
    return slice(slab * half, (slab + 1) * half)


def each_core(body):
    core = lax.axis_index("space")
    for mine in range(2):
        pl.when(core == mine)(functools.partial(body, mine))


def pack_kernel(k, v, q, g, lists, k_own, v_own, qg_own, qg_send, lists_out, sems):
    def body(mine):
        moves = [(lists, lists_out)]
        for source, out in ((k, k_own), (v, v_own)):
            moves.append((source.at[:, head_cols(mine)], out))
        for head, out in ((mine, qg_own), (1 - mine, qg_send)):
            for source, cols in ((q, KEY), (g, VALUE)):
                moves.append((source.at[:, head_cols(head)], out.at[:, cols]))
        copies = [
            pltpu.make_async_copy(source, out, sems.at[n]) for n, (source, out) in enumerate(moves)
        ]
        for copy in copies:
            copy.start()
        for copy in copies:
            copy.wait()

    each_core(body)


def keys_kernel(own, came, keys):
    half = own.shape[0]

    def body(mine):
        keys[rows_of(mine, half), :] = own[...]
        keys[rows_of(1 - mine, half), :] = came[:, head_cols(mine)]

    each_core(body)


def values_kernel(keys, own, came, values, kv):
    half = own.shape[0]

    def body(mine):
        for slab, part in ((mine, own[...]), (1 - mine, came[:, head_cols(mine)])):
            rows = rows_of(slab, half)
            values[rows, :] = part
            kv[rows, VALUE] = part
            kv[rows, KEY] = keys[rows, :]

    each_core(body)


def select_kernel(far, block, lists, kv, *sends):
    frame = lax.axis_index("tm")
    for swap, send in zip(far, sends):
        for slab in range(2):
            b, _ = swap.block_of_theirs(lists, frame, slab, 0)
            row = pl.multiple_of(b * block, block)
            send[slab * block : (slab + 1) * block, :] = kv[pl.ds(row, block), :]


def forwards_first(frame):
    return lax.rem(frame, 2) == lax.rem(lax.shift_right_logical(frame, 1), 2)


def relay_kernel(y, z, out):
    first = forwards_first(lax.axis_index("tm"))

    @pl.when(first)
    def _():
        out[...] = z[...]

    @pl.when(jnp.logical_not(first))
    def _():
        out[...] = y[...]


class Piece:
    def __init__(self, k, v, row, size, exists=None, dk=None, dv=None, add=True):
        self.k_at, self.v_at, self.exists = k, v, exists
        self.rows, self.size = pl.ds(row, size), size
        self.dk, self.dv, self.add = dk, dv, add

    def store(self, at, value):
        ref, cols = at
        if self.add:
            ref[self.rows, cols] += value
        else:
            ref[self.rows, cols] = value.astype(ref.dtype)


def stack(parts):
    return parts[0] if len(parts) == 1 else jnp.concatenate(parts, axis=0)


def keys_of(group):
    return stack([p.k_at[0][p.rows, p.k_at[1]] for p in group])


def values_of(group):
    return stack([p.v_at[0][p.rows, p.v_at[1]] for p in group])


def by_piece(group, value):
    at = 0
    for piece in group:
        yield piece, value[at : at + piece.size, :]
        at += piece.size


def store_grads(group, value, name):
    for piece, part in by_piece(group, value):
        piece.store(getattr(piece, name), part)


def listed(swap, lists, frame, slab, block, k, v, count=1, **grads):
    pieces = []
    for n in range(count):
        b, exists = swap.block_of_mine(lists, frame, slab, n)
        pieces.append(Piece(k, v, pl.multiple_of(b * block, block), block, exists, **grads))
    return pieces


def arrived(swap, frame, slab, block, kv, **grads):
    _, _, exists = swap.partner(frame)
    return Piece((kv, KEY), (kv, VALUE), slab * block, block, exists, add=False, **grads)


def raised(group, s, base):
    parts = []
    for piece, part in by_piece(group, s):
        low = base if piece.exists is None else jnp.where(piece.exists, base, -NEG)
        parts.append(jnp.exp2(part * EXP_SCALE - low))
    return stack(parts)


def score_groups(q, groups, s_ref, peak):
    at = 0
    for group in groups:
        s = dot_nt(keys_of(group), q)
        s_ref[at : at + s.shape[0], :] = s
        at += s.shape[0]
        for piece, part in by_piece(group, s):
            top = jnp.max(part, axis=0, keepdims=True)
            if piece.exists is not None:
                top = jnp.where(piece.exists, top, NEG)
            peak = top if peak is None else jnp.maximum(peak, top)
    return peak


def group_scores(groups, s_ref):
    at = 0
    for group in groups:
        size = sum(piece.size for piece in group)
        yield group, s_ref[at : at + size, :]
        at += size


def forward_slab(q, groups, with_values, s_ref, old):
    peak = score_groups(q, groups, s_ref, None if old is None else old[0])
    total, acc = 0.0, 0.0
    if old is not None:
        shrink = jnp.exp2((old[0] - peak) * EXP_SCALE)
        total, acc = old[1] * shrink, old[2] * shrink
    for j, (group, s) in enumerate(group_scores(groups, s_ref)):
        e = raised(group, s, peak * EXP_SCALE)
        total = total + jnp.sum(e, axis=0, keepdims=True)
        if j < with_values:
            acc = acc + dot_tn(values_of(group), e.astype(BF16))
    return peak, total, acc


def backward_group(q, g, lse, row_dot, group, p=None):
    k = keys_of(group)
    if p is None:
        p = raised(group, dot_nt(k, q), lse)
    if group[0].dv is not None:
        store_grads(group, dot_nn(p.astype(BF16), g), "dv")
    ds = (p * (dot_nt(values_of(group), g) - row_dot)).astype(BF16)
    if group[0].dk is not None:
        store_grads(group, dot_nn(ds, q) * SCALE, "dk")
    return dot_tn(k, ds)


def join_kernel(own, came, out, turned):
    half = own.shape[0]

    def body(mine):
        for slab, source in ((mine, own), (1 - mine, came)):
            rows = rows_of(slab, half)
            out[rows, :] = source[...]
            turned[:, rows] = source[:, VALUE].T

    each_core(body)


ALL = slice(None)


def store_state(refs, rows, peak, total, acc):
    stat, acc_ref = refs
    stat[0:1, rows] = peak
    stat[1:2, rows] = total
    acc_ref[:, rows] = acc


def load_state(refs, rows):
    stat, acc_ref = refs
    return stat[0:1, rows], stat[1:2, rows], acc_ref[:, rows]


def own_groups(kv, half, **grads):
    return [
        [Piece((kv, KEY), (kv, VALUE), r, half, **grads)] for r in range(0, kv.shape[0], half)
    ]


def near_kernel(block, swap, lists, qg, kv, a_kv, stat, acc, s_ref):
    half = qg.shape[0] // 2
    frame = lax.axis_index("tm")
    for slab in range(2):
        rows = rows_of(slab, half)
        groups = own_groups(kv, half)
        groups.append(
            listed(swap, lists, frame, slab, block, (a_kv, KEY), (a_kv, VALUE), 2)
        )
        store_state((stat, acc), rows, *forward_slab(qg[rows, KEY], groups, 3, s_ref, None))


def middle_kernel(
    block, swaps, lists, qg, stat, acc, y_k, z_k, y_v, z_v, c_k, stat2, acc2, late, s_ref
):
    half = qg.shape[0] // 2
    frame = lax.axis_index("tm")
    z, y, relayed = swaps
    for slab in range(2):
        rows = rows_of(slab, half)
        at = (lists, frame, slab, block)
        group = listed(z, *at, (z_k, ALL), (z_v, ALL)) + listed(y, *at, (y_k, ALL), (y_v, ALL))
        more = listed(relayed, *at, (c_k, ALL), None, 2)
        old = load_state((stat, acc), rows)
        new = forward_slab(qg[rows, KEY], [group, more], 1, s_ref, old)
        store_state((stat2, acc2), rows, *new)
        late[slab] = s_ref[2 * block :, :]


def close_kernel(block, relayed, far, lists_any, qg, stat, acc, late_s, *refs):
    n = len(far)
    far_kv = refs[:n]
    lse_ref, part_ref, dc_v, p_ref = refs[n : n + 4]
    far_dv = refs[n + 4 : 2 * n + 4]
    s_ref, grad, lists, sem = refs[2 * n + 4 :]
    half = qg.shape[0] // 2
    frame = lax.axis_index("tm")
    copy = pltpu.make_async_copy(lists_any, lists, sem)
    copy.start()
    grad[...] = jnp.zeros_like(grad)
    for slab in range(2):
        rows = rows_of(slab, half)
        q, g = qg[rows, KEY], qg[rows, VALUE]
        groups = [
            [arrived(swap, frame, slab, block, kv, dv=(out, ALL))]
            for swap, kv, out in zip(far, far_kv, far_dv)
        ]
        old = load_state((stat, acc), rows)
        peak, total, out = forward_slab(q, groups, n, s_ref, old)
        part_ref[:, rows] = out / total
        lse = peak * EXP_SCALE + jnp.log2(total)
        lse_ref[0:1, rows] = lse
        for group, s in group_scores(groups, s_ref):
            p = raised(group, s, lse)
            store_grads(group, dot_nn(p.astype(BF16), g), "dv")
    copy.wait()
    for slab in range(2):
        rows = rows_of(slab, half)
        group = listed(relayed, lists, frame, slab, block, None, None, 2, dv=(grad, ALL))
        p = raised(group, late_s[slab], lse_ref[0:1, rows])
        p_ref[slab] = p
        store_grads(group, dot_nn(p.astype(BF16), qg[rows, VALUE]), "dv")
    dc_v[...] = grad[...].astype(BF16)


def late_kernel(block, relayed, far, *refs):
    n = len(far)
    lists, qg, turned, lse_ref, part_ref, p_ref, c_k, c_v = refs[:8]
    far_kv = refs[8 : 8 + n]
    o_ref, dot_ref, dc_k, dq_ref = refs[8 + n : 12 + n]
    far_grad = refs[12 + n : 12 + 2 * n]
    grad = refs[12 + 2 * n]
    half = qg.shape[0] // 2
    frame = lax.axis_index("tm")
    grad[...] = jnp.zeros_like(grad)
    for slab in range(2):
        rows = rows_of(slab, half)
        q, g, lse = qg[rows, KEY], qg[rows, VALUE], lse_ref[0:1, rows]
        group = listed(
            relayed, lists, frame, slab, block, (c_k, ALL), (c_v, ALL), 2, dk=(grad, ALL)
        )
        p = p_ref[slab]
        o = (part_ref[:, rows] + dot_tn(values_of(group), p.astype(BF16))).astype(BF16)
        o_ref[:, rows] = o
        products = turned[:, rows].astype(F32) * o.astype(F32)
        row_dot = jnp.sum(products, axis=0, keepdims=True)
        dot_ref[0:1, rows] = row_dot
        dq = backward_group(q, g, lse, row_dot, group, p)
        for swap, kv, out in zip(far, far_kv, far_grad):
            group = [arrived(swap, frame, slab, block, kv, dk=(out, ALL))]
            dq = dq + backward_group(q, g, lse, row_dot, group)
        dq_ref[:, rows] = dq
    dc_k[...] = grad[...].astype(BF16)


def first_kernel(block, swap, lists, qg, lse_ref, dot_ref, dq_old, a_kv, da, dq_ref, grad):
    half = qg.shape[0] // 2
    frame = lax.axis_index("tm")
    grad[...] = jnp.zeros_like(grad)
    for slab in range(2):
        rows = rows_of(slab, half)
        q, g, lse, row_dot = qg[rows, KEY], qg[rows, VALUE], lse_ref[0:1, rows], dot_ref[0:1, rows]
        group = listed(
            swap, lists, frame, slab, block, (a_kv, KEY), (a_kv, VALUE), 2,
            dk=(grad, KEY), dv=(grad, VALUE),
        )
        dq_ref[:, rows] = dq_old[:, rows] + backward_group(q, g, lse, row_dot, group)
    da[...] = grad[...].astype(BF16)


def second_kernel(
    block, swaps, lists, qg, lse_ref, dot_ref, dq_old, came, y_k, z_k, y_v, z_v, dz, dy, dq_ref
):
    half = qg.shape[0] // 2
    frame = lax.axis_index("tm")
    z, y = swaps
    relays = forwards_first(frame)
    more = came[...].astype(F32)
    for ref, takes in ((dz, relays), (dy, jnp.logical_not(relays))):
        ref[:, KEY] = jnp.zeros_like(more)
        ref[:, VALUE] = jnp.where(takes, more, 0.0)
    for slab in range(2):
        rows = rows_of(slab, half)
        q, g, lse, row_dot = qg[rows, KEY], qg[rows, VALUE], lse_ref[0:1, rows], dot_ref[0:1, rows]
        at = (lists, frame, slab, block)
        group = listed(z, *at, (z_k, ALL), (z_v, ALL), dk=(dz, KEY), dv=(dz, VALUE))
        group += listed(y, *at, (y_k, ALL), (y_v, ALL), dk=(dy, KEY), dv=(dy, VALUE))
        dq_ref[:, rows] = dq_old[:, rows] + backward_group(q, g, lse, row_dot, group)


def own_kernel(qg, lse_ref, dot_ref, dq_old, o, kv, placed, near, keep, send):
    half = qg.shape[0] // 2
    near[...] = placed[...]
    whole = []
    for slab in range(2):
        rows = rows_of(slab, half)
        q, g, lse, row_dot = qg[rows, KEY], qg[rows, VALUE], lse_ref[0:1, rows], dot_ref[0:1, rows]
        dq = dq_old[:, rows]
        for group in own_groups(kv, half, dk=(near, KEY), dv=(near, VALUE)):
            dq = dq + backward_group(q, g, lse, row_dot, group)
        whole.append((dq.T * SCALE).astype(BF16))

    def body(mine):
        for slab in range(2):
            out = keep if slab == mine else send
            out[:, KEY] = o[:, rows_of(slab, half)].T
            out[:, VALUE] = whole[slab]

    each_core(body)


def merge_kernel(dz, dy, came, z_out, y_out):
    first = forwards_first(lax.axis_index("tm"))
    more = came[...].astype(F32)
    z_out[:, KEY] = (dz[:, KEY] + jnp.where(first, more, 0.0)).astype(BF16)
    y_out[:, KEY] = (dy[:, KEY] + jnp.where(first, 0.0, more)).astype(BF16)
    z_out[:, VALUE] = dz[:, VALUE].astype(BF16)
    y_out[:, VALUE] = dy[:, VALUE].astype(BF16)


def place_kernel(block, far, *refs):
    n = len(far)
    lists, total = refs[0], refs[-1]
    frame = lax.axis_index("tm")
    total[...] = jnp.zeros_like(total)
    for swap, came_k, came_v in zip(far, refs[1 : 1 + n], refs[1 + n : -1]):
        for slab in range(2):
            b, exists = swap.block_of_theirs(lists, frame, slab, 0)
            rows = pl.ds(pl.multiple_of(b * block, block), block)
            for came, cols in ((came_k, KEY), (came_v, VALUE)):
                part = came[rows_of(slab, block), :].astype(F32)
                total[rows, cols] += jnp.where(exists, part, 0.0)


def add_kernel(swaps, near, *refs):
    frame = lax.axis_index("tm")
    total = near[...]
    for swap, came in zip(swaps, refs[:-1]):
        _, _, exists = swap.partner(frame)
        total = total + jnp.where(exists, came[...].astype(F32), 0.0)
    refs[-1][...] = total


def gather_kernel(swap, near, came, keep, send):
    _, _, exists = swap.partner(lax.axis_index("tm"))
    half = near.shape[0] // 2

    def body(mine):
        for slab, out in ((1 - mine, send), (mine, keep)):
            rows = rows_of(slab, half)
            part = jnp.where(exists, came[rows, :].astype(F32), 0.0)
            out[...] = (near[rows, :] + part).astype(BF16)

    each_core(body)


def finish_kernel(keep, came, first, second):
    def body(mine):
        for head, source in ((mine, keep), (1 - mine, came)):
            first[:, head_cols(head)] = source[:, KEY]
            second[:, head_cols(head)] = source[:, VALUE]

    each_core(body)


def per_device(queries, key_rows, value_rows, out_grad, block_lists):
    s_dev, width = queries.shape
    count = lax.axis_size("tm")
    block = s_dev // 2
    pair = sds((s_dev, 2 * DH), BF16)
    single = sds((s_dev, DH), BF16)
    frame_two = sds((2 * s_dev, 2 * DH), BF16)
    frame_one = sds((2 * s_dev, DH), BF16)
    frame_sum = sds((2 * s_dev, 2 * DH), F32)
    stat_row = sds((8, 2 * s_dev), F32)
    turned_sum = sds((DH, 2 * s_dev), F32)
    turned_bf = sds((DH, 2 * s_dev), BF16)
    levels = count.bit_length() - 1
    near_swap, relayed = Swap(count, 0, False), Swap(count, 0, True)
    z_swap, y_swap = Swap(count, 1, False), Swap(count, 1, True)
    far = [Swap(count, level, second) for level in range(2, levels) for second in (False, True)]
    far = [swap for swap in far if swap.moves]
    n = len(far)
    grad_one = pltpu.VMEM((2 * s_dev, DH), F32)

    def across(value):
        return lax.ppermute(value, "space", [(0, 1), (1, 0)])

    def swapped(value, swap):
        return lax.ppermute(value, "tm", swap.pairs)

    def scores(pieces):
        return pltpu.VMEM((pieces * block, s_dev), F32)


    k_came = across(key_rows)
    sources = (key_rows, value_rows, queries, out_grad, block_lists.T)
    k_own, v_own, qg_own, qg_send, lists = call(
        pack_kernel,
        tuple(pltpu.with_memory_space_constraint(a, pltpu.HBM) for a in sources),
        [single, single, pair, pair, sds(sources[4].shape, jnp.int32)],
        scratch=[pltpu.SemaphoreType.DMA((7,))],
        source=HBM,
        scalars=HBM,
    )
    (keys,) = call(keys_kernel, (k_own, k_came), [frame_one])
    later_rows, _ = lax.optimization_barrier((value_rows, keys))
    v_came = across(later_rows)
    values, kv = call(values_kernel, (keys, v_own, v_came), [frame_one, frame_two])
    qg_send, _ = lax.optimization_barrier((qg_send, keys))
    y_k = swapped(keys, y_swap)
    z_k = swapped(keys, z_swap)
    a_kv = swapped(kv, near_swap)
    y_v = swapped(values, y_swap)
    z_v = swapped(values, z_swap)
    y_k, qg_came = lax.optimization_barrier((y_k, across(qg_send)))
    work = 4 * s_dev * s_dev * DH
    qg, turned = call(join_kernel, (qg_own, qg_came), [frame_two, turned_bf], flops=15 * work)
    kv, _ = lax.optimization_barrier((kv, turned))
    far_send = call(functools.partial(select_kernel, far, block), (lists, kv), [pair] * n)
    y_k, z_k, far_send = lax.optimization_barrier((y_k, z_k, far_send))
    (relay_k,) = call(relay_kernel, (y_k, z_k), [frame_one])
    relay_k, far_send = lax.optimization_barrier((relay_k, far_send))
    a_kv, _ = lax.optimization_barrier((a_kv, relay_k))
    c_k = swapped(relay_k, near_swap)
    far_kv = [swapped(value, swap) for value, swap in zip(far_send, far)]
    stat, acc = call(
        functools.partial(near_kernel, block, near_swap),
        (lists, qg, kv, a_kv),
        [stat_row, turned_sum],
        scratch=[scores(6)],
    )
    score_two = sds((2, s_dev, s_dev), F32)
    y_v, z_v, stat = lax.optimization_barrier((y_v, z_v, stat))
    (relay_v,) = call(relay_kernel, (y_v, z_v), [frame_one])
    relay_v, stat = lax.optimization_barrier((relay_v, stat))
    c_v = swapped(relay_v, near_swap)
    stat, acc, late_scores = call(
        functools.partial(middle_kernel, block, (z_swap, y_swap, relayed)),
        (lists, qg, stat, acc, y_k, z_k, y_v, z_v, c_k),
        [stat_row, turned_sum, score_two],
        scratch=[scores(4)],
    )
    acc, far_kv = lax.optimization_barrier((acc, far_kv))
    lse, part, dc_v, probs, *far_dv = call(
        functools.partial(close_kernel, block, relayed, far),
        (lists, qg, stat, acc, late_scores, *far_kv),
        [stat_row, turned_sum, frame_one, score_two] + [single] * n,
        scratch=[
            scores(n),
            grad_one,
            pltpu.SMEM(lists.shape, jnp.int32),
            pltpu.SemaphoreType.DMA(()),
        ],
        scalars=pl.BlockSpec(memory_space=pl.ANY),
    )
    dc_v_came = swapped(dc_v, near_swap)
    far_dv_came = [swapped(value, swap) for value, swap in zip(far_dv, far)]
    o, row_dot, dc_k, dq, *far_grad = call(
        functools.partial(late_kernel, block, relayed, far),
        (lists, qg, turned, lse, part, probs, c_k, c_v, *far_kv),
        [turned_bf, stat_row, frame_one, turned_sum] + [single] * n,
        scratch=[grad_one],
    )
    far_dk_came = [swapped(value, swap) for value, swap in zip(far_grad, far)]
    dc_k_came = swapped(dc_k, near_swap)
    da, dq = call(
        functools.partial(first_kernel, block, near_swap),
        (lists, qg, lse, row_dot, dq, a_kv),
        [frame_two, turned_sum],
        scratch=[pltpu.VMEM((2 * s_dev, 2 * DH), F32)],
    )
    da, dc_k_came = lax.optimization_barrier((da, dc_k_came))
    da_came = swapped(da, near_swap)
    dc_v_came, far_dv_came = lax.optimization_barrier((dc_v_came, far_dv_came))
    dz, dy, dq = call(
        functools.partial(second_kernel, block, (z_swap, y_swap)),
        (lists, qg, lse, row_dot, dq, dc_v_came, y_k, z_k, y_v, z_v),
        [frame_sum, frame_sum, turned_sum],
        flops=20 * work,
    )
    dz, dy = call(merge_kernel, (dz, dy, dc_k_came), [frame_two, frame_two])
    dy_came = swapped(dy, y_swap)
    dz_came = swapped(dz, z_swap)
    dq, dz, dy = lax.optimization_barrier((dq, dz, dy))
    far_dk_came, dq = lax.optimization_barrier((far_dk_came, dq))
    (placed,) = call(functools.partial(place_kernel, block, far), (lists, *far_dk_came, *far_dv_came), [frame_sum])
    near, q_keep, q_send = call(
        own_kernel,
        (qg, lse, row_dot, dq, o, kv, placed),
        [frame_sum, pair, pair],
        flops=20 * work,
    )
    outputs = [sds((s_dev, width), BF16)] * 2
    attn_out, grad_q = call(finish_kernel, (q_keep, across(q_send)), outputs)
    near, attn_out, grad_q = lax.optimization_barrier((near, attn_out, grad_q))
    (near,) = call(
        functools.partial(add_kernel, (near_swap, y_swap)),
        (near, da_came, dy_came),
        [frame_sum],
        flops=20 * work,
    )
    k_keep, k_send = call(
        functools.partial(gather_kernel, z_swap), (near, dz_came), [pair, pair]
    )
    grad_k, grad_v = call(finish_kernel, (k_keep, across(k_send)), outputs)
    return attn_out, grad_q, grad_k, grad_v


def solution(mesh):
    rows = P(("groups", "tm", "space"), None)
    return jax.shard_map(
        per_device,
        mesh=mesh,
        in_specs=(rows, rows, rows, rows, P("groups", None)),
        out_specs=(rows, rows, rows, rows),
        check_vma=False,
    )
```

```python
import functools
import math

import jax
import jax.numpy as jnp
from jax import lax
from jax.experimental import pallas as pl
from jax.experimental.pallas import tpu as pltpu
from jax.sharding import PartitionSpec as P

DH = 128
F32 = jnp.float32
BF16 = jnp.bfloat16
VMEM = pl.BlockSpec(memory_space=pltpu.VMEM)
SMEM = pl.BlockSpec(memory_space=pltpu.SMEM)
HBM = pl.BlockSpec(memory_space=pltpu.HBM)
NEG = -1e30
SCALE = 1.0 / math.sqrt(DH)
EXP_SCALE = SCALE * math.log2(math.e)
KEY = slice(0, DH)
VALUE = slice(DH, 2 * DH)
sds = jax.ShapeDtypeStruct


def dot_nn(a, b):
    return lax.dot_general(a, b, (((1,), (0,)), ((), ())), preferred_element_type=F32)


def dot_nt(a, b):
    return lax.dot_general(a, b, (((1,), (1,)), ((), ())), preferred_element_type=F32)


def dot_tn(a, b):
    return lax.dot_general(a, b, (((0,), (0,)), ((), ())), preferred_element_type=F32)


def call(kernel, args, out_shape, scratch=(), source=VMEM, scalars=SMEM, flops=1024):
    return pl.pallas_call(
        kernel,
        out_shape=out_shape,
        in_specs=[scalars if a.dtype == jnp.int32 else source for a in args],
        out_specs=tuple(VMEM for _ in out_shape),
        scratch_shapes=list(scratch),
        compiler_params=pltpu.CompilerParams(vmem_limit_bytes=40 << 20),
        cost_estimate=pl.CostEstimate(flops=flops, bytes_accessed=1024, transcendentals=0),
    )(*args)


def swap_pairs(count, distance, second):
    pairs = []
    for frame in range(count):
        up = ((frame // distance) % 2 == 0) != second
        target = frame + distance if up else frame - distance
        for core in range(2):
            if 0 <= target < count:
                pairs.append((frame * 2 + core, target * 2 + core))
            else:
                pairs.append((frame * 2 + core, frame * 2 + 1 - core))
    return pairs


class Swap:
    def __init__(self, count, level, second):
        self.count, self.level, self.second = count, level, second
        self.levels = count.bit_length() - 1
        self.pairs = swap_pairs(count, 1 << level, second)
        self.moves = any(source // 2 != target // 2 for source, target in self.pairs)

    def partner(self, frame):
        odd = lax.rem(lax.shift_right_logical(frame, self.level), 2)
        later = odd == (1 if self.second else 0)
        other = jnp.where(later, frame + (1 << self.level), frame - (1 << self.level))
        return other, later, jnp.logical_and(other >= 0, other < self.count)

    def slot(self, later, k):
        base = 0 if self.level == 0 else self.level + 1
        return jnp.where(later, self.levels + 1, 0) + base + k

    def block_of_mine(self, lists, frame, slab, k):
        other, later, exists = self.partner(frame)
        entry = lists[self.slot(later, k), frame * 2 + slab]
        return jnp.clip(entry - other * 4, 0, 3), exists

    def block_of_theirs(self, lists, frame, slab, k):
        other, later, exists = self.partner(frame)
        row = jnp.where(exists, other, frame) * 2 + slab
        entry = lists[self.slot(jnp.logical_not(later), k), row]
        return jnp.clip(entry - frame * 4, 0, 3), exists


def head_cols(head):
    return slice(head * DH, (head + 1) * DH)


def rows_of(slab, half):
    return slice(slab * half, (slab + 1) * half)


def each_core(body):
    core = lax.axis_index("space")
    for mine in range(2):
        pl.when(core == mine)(functools.partial(body, mine))


def pack_kernel(k, v, q, g, lists, k_own, v_own, qg_own, qg_send, lists_out, sems):
    def body(mine):
        moves = [(lists, lists_out)]
        for source, out in ((k, k_own), (v, v_own)):
            moves.append((source.at[:, head_cols(mine)], out))
        for head, out in ((mine, qg_own), (1 - mine, qg_send)):
            for source, cols in ((q, KEY), (g, VALUE)):
                moves.append((source.at[:, head_cols(head)], out.at[:, cols]))
        copies = [
            pltpu.make_async_copy(source, out, sems.at[n]) for n, (source, out) in enumerate(moves)
        ]
        for copy in copies:
            copy.start()
        for copy in copies:
            copy.wait()

    each_core(body)


def keys_kernel(own, came, keys):
    half = own.shape[0]

    def body(mine):
        keys[rows_of(mine, half), :] = own[...]
        keys[rows_of(1 - mine, half), :] = came[:, head_cols(mine)]

    each_core(body)


def values_kernel(keys, own, came, values, kv):
    half = own.shape[0]

    def body(mine):
        for slab, part in ((mine, own[...]), (1 - mine, came[:, head_cols(mine)])):
            rows = rows_of(slab, half)
            values[rows, :] = part
            kv[rows, VALUE] = part
            kv[rows, KEY] = keys[rows, :]

    each_core(body)


def select_kernel(far, block, lists, kv, *sends):
    frame = lax.axis_index("tm")
    for swap, send in zip(far, sends):
        for slab in range(2):
            b, _ = swap.block_of_theirs(lists, frame, slab, 0)
            row = pl.multiple_of(b * block, block)
            send[slab * block : (slab + 1) * block, :] = kv[pl.ds(row, block), :]


def forwards_first(frame):
    return lax.rem(frame, 2) == lax.rem(lax.shift_right_logical(frame, 1), 2)


def relay_kernel(y, z, out):
    first = forwards_first(lax.axis_index("tm"))

    @pl.when(first)
    def _():
        out[...] = z[...]

    @pl.when(jnp.logical_not(first))
    def _():
        out[...] = y[...]


class Piece:
    def __init__(self, k, v, row, size, exists=None, dk=None, dv=None, add=True):
        self.k_at, self.v_at, self.exists = k, v, exists
        self.rows, self.size = pl.ds(row, size), size
        self.dk, self.dv, self.add = dk, dv, add

    def store(self, at, value):
        ref, cols = at
        if self.add:
            ref[self.rows, cols] += value
        else:
            ref[self.rows, cols] = value.astype(ref.dtype)


def stack(parts):
    return parts[0] if len(parts) == 1 else jnp.concatenate(parts, axis=0)


def keys_of(group):
    return stack([p.k_at[0][p.rows, p.k_at[1]] for p in group])


def values_of(group):
    return stack([p.v_at[0][p.rows, p.v_at[1]] for p in group])


def by_piece(group, value):
    at = 0
    for piece in group:
        yield piece, value[at : at + piece.size, :]
        at += piece.size


def store_grads(group, value, name):
    for piece, part in by_piece(group, value):
        piece.store(getattr(piece, name), part)


def listed(swap, lists, frame, slab, block, k, v, count=1, **grads):
    pieces = []
    for n in range(count):
        b, exists = swap.block_of_mine(lists, frame, slab, n)
        pieces.append(Piece(k, v, pl.multiple_of(b * block, block), block, exists, **grads))
    return pieces


def arrived(swap, frame, slab, block, kv, **grads):
    _, _, exists = swap.partner(frame)
    return Piece((kv, KEY), (kv, VALUE), slab * block, block, exists, add=False, **grads)


def raised(group, s, base):
    parts = []
    for piece, part in by_piece(group, s):
        low = base if piece.exists is None else jnp.where(piece.exists, base, -NEG)
        parts.append(jnp.exp2(part * EXP_SCALE - low))
    return stack(parts)


def score_groups(q, groups, s_ref, peak):
    at = 0
    for group in groups:
        s = dot_nt(keys_of(group), q)
        s_ref[at : at + s.shape[0], :] = s
        at += s.shape[0]
        for piece, part in by_piece(group, s):
            top = jnp.max(part, axis=0, keepdims=True)
            if piece.exists is not None:
                top = jnp.where(piece.exists, top, NEG)
            peak = top if peak is None else jnp.maximum(peak, top)
    return peak


def group_scores(groups, s_ref):
    at = 0
    for group in groups:
        size = sum(piece.size for piece in group)
        yield group, s_ref[at : at + size, :]
        at += size


def forward_slab(q, groups, with_values, s_ref, old):
    peak = score_groups(q, groups, s_ref, None if old is None else old[0])
    total, acc = 0.0, 0.0
    if old is not None:
        shrink = jnp.exp2((old[0] - peak) * EXP_SCALE)
        total, acc = old[1] * shrink, old[2] * shrink
    for j, (group, s) in enumerate(group_scores(groups, s_ref)):
        e = raised(group, s, peak * EXP_SCALE)
        total = total + jnp.sum(e, axis=0, keepdims=True)
        if j < with_values:
            acc = acc + dot_tn(values_of(group), e.astype(BF16))
    return peak, total, acc


def backward_group(q, g, lse, row_dot, group, p=None):
    k = keys_of(group)
    if p is None:
        p = raised(group, dot_nt(k, q), lse)
    if group[0].dv is not None:
        store_grads(group, dot_nn(p.astype(BF16), g), "dv")
    ds = (p * (dot_nt(values_of(group), g) - row_dot)).astype(BF16)
    if group[0].dk is not None:
        store_grads(group, dot_nn(ds, q) * SCALE, "dk")
    return dot_tn(k, ds)


def join_kernel(own, came, out, turned):
    half = own.shape[0]

    def body(mine):
        for slab, source in ((mine, own), (1 - mine, came)):
            rows = rows_of(slab, half)
            out[rows, :] = source[...]
            turned[:, rows] = source[:, VALUE].T

    each_core(body)


ALL = slice(None)


def store_state(refs, rows, peak, total, acc):
    stat, acc_ref = refs
    stat[0:1, rows] = peak
    stat[1:2, rows] = total
    acc_ref[:, rows] = acc


def load_state(refs, rows):
    stat, acc_ref = refs
    return stat[0:1, rows], stat[1:2, rows], acc_ref[:, rows]


def own_groups(kv, half, **grads):
    return [
        [Piece((kv, KEY), (kv, VALUE), r, half, **grads)] for r in range(0, kv.shape[0], half)
    ]


def near_kernel(block, swap, lists, qg, kv, a_kv, stat, acc, s_ref):
    half = qg.shape[0] // 2
    frame = lax.axis_index("tm")
    for slab in range(2):
        rows = rows_of(slab, half)
        groups = own_groups(kv, half)
        groups.append(
            listed(swap, lists, frame, slab, block, (a_kv, KEY), (a_kv, VALUE), 2)
        )
        store_state((stat, acc), rows, *forward_slab(qg[rows, KEY], groups, 3, s_ref, None))


def middle_kernel(
    block, swaps, lists, qg, stat, acc, y_k, z_k, y_v, z_v, c_k, stat2, acc2, late, s_ref
):
    half = qg.shape[0] // 2
    frame = lax.axis_index("tm")
    z, y, relayed = swaps
    for slab in range(2):
        rows = rows_of(slab, half)
        at = (lists, frame, slab, block)
        group = listed(z, *at, (z_k, ALL), (z_v, ALL)) + listed(y, *at, (y_k, ALL), (y_v, ALL))
        more = listed(relayed, *at, (c_k, ALL), None, 2)
        old = load_state((stat, acc), rows)
        new = forward_slab(qg[rows, KEY], [group, more], 1, s_ref, old)
        store_state((stat2, acc2), rows, *new)
        late[slab] = s_ref[2 * block :, :]


def close_kernel(block, relayed, far, lists_any, qg, stat, acc, late_s, *refs):
    n = len(far)
    far_kv = refs[:n]
    lse_ref, part_ref, dc_v, p_ref = refs[n : n + 4]
    far_dv = refs[n + 4 : 2 * n + 4]
    s_ref, grad, lists, sem = refs[2 * n + 4 :]
    half = qg.shape[0] // 2
    frame = lax.axis_index("tm")
    copy = pltpu.make_async_copy(lists_any, lists, sem)
    copy.start()
    grad[...] = jnp.zeros_like(grad)
    for slab in range(2):
        rows = rows_of(slab, half)
        q, g = qg[rows, KEY], qg[rows, VALUE]
        groups = [
            [arrived(swap, frame, slab, block, kv, dv=(out, ALL))]
            for swap, kv, out in zip(far, far_kv, far_dv)
        ]
        old = load_state((stat, acc), rows)
        peak, total, out = forward_slab(q, groups, n, s_ref, old)
        part_ref[:, rows] = out / total
        lse = peak * EXP_SCALE + jnp.log2(total)
        lse_ref[0:1, rows] = lse
        for group, s in group_scores(groups, s_ref):
            p = raised(group, s, lse)
            store_grads(group, dot_nn(p.astype(BF16), g), "dv")
    copy.wait()
    for slab in range(2):
        rows = rows_of(slab, half)
        group = listed(relayed, lists, frame, slab, block, None, None, 2, dv=(grad, ALL))
        p = raised(group, late_s[slab], lse_ref[0:1, rows])
        p_ref[slab] = p
        store_grads(group, dot_nn(p.astype(BF16), qg[rows, VALUE]), "dv")
    dc_v[...] = grad[...].astype(BF16)


def late_kernel(block, relayed, far, *refs):
    n = len(far)
    lists, qg, turned, lse_ref, part_ref, p_ref, c_k, c_v = refs[:8]
    far_kv = refs[8 : 8 + n]
    o_ref, dot_ref, dc_k, dq_ref = refs[8 + n : 12 + n]
    far_grad = refs[12 + n : 12 + 2 * n]
    grad = refs[12 + 2 * n]
    half = qg.shape[0] // 2
    frame = lax.axis_index("tm")
    grad[...] = jnp.zeros_like(grad)
    for slab in range(2):
        rows = rows_of(slab, half)
        q, g, lse = qg[rows, KEY], qg[rows, VALUE], lse_ref[0:1, rows]
        group = listed(
            relayed, lists, frame, slab, block, (c_k, ALL), (c_v, ALL), 2, dk=(grad, ALL)
        )
        p = p_ref[slab]
        o = (part_ref[:, rows] + dot_tn(values_of(group), p.astype(BF16))).astype(BF16)
        o_ref[:, rows] = o
        products = turned[:, rows].astype(F32) * o.astype(F32)
        row_dot = jnp.sum(products, axis=0, keepdims=True)
        dot_ref[0:1, rows] = row_dot
        dq = backward_group(q, g, lse, row_dot, group, p)
        for swap, kv, out in zip(far, far_kv, far_grad):
            group = [arrived(swap, frame, slab, block, kv, dk=(out, ALL))]
            dq = dq + backward_group(q, g, lse, row_dot, group)
        dq_ref[:, rows] = dq
    dc_k[...] = grad[...].astype(BF16)


def first_kernel(block, swap, lists, qg, lse_ref, dot_ref, dq_old, a_kv, da, dq_ref, grad):
    half = qg.shape[0] // 2
    frame = lax.axis_index("tm")
    grad[...] = jnp.zeros_like(grad)
    for slab in range(2):
        rows = rows_of(slab, half)
        q, g, lse, row_dot = qg[rows, KEY], qg[rows, VALUE], lse_ref[0:1, rows], dot_ref[0:1, rows]
        group = listed(
            swap, lists, frame, slab, block, (a_kv, KEY), (a_kv, VALUE), 2,
            dk=(grad, KEY), dv=(grad, VALUE),
        )
        dq_ref[:, rows] = dq_old[:, rows] + backward_group(q, g, lse, row_dot, group)
    da[...] = grad[...].astype(BF16)


def second_kernel(
    block, swaps, lists, qg, lse_ref, dot_ref, dq_old, came, y_k, z_k, y_v, z_v, dz, dy, dq_ref
):
    half = qg.shape[0] // 2
    frame = lax.axis_index("tm")
    z, y = swaps
    relays = forwards_first(frame)
    more = came[...].astype(F32)
    for ref, takes in ((dz, relays), (dy, jnp.logical_not(relays))):
        ref[:, KEY] = jnp.zeros_like(more)
        ref[:, VALUE] = jnp.where(takes, more, 0.0)
    for slab in range(2):
        rows = rows_of(slab, half)
        q, g, lse, row_dot = qg[rows, KEY], qg[rows, VALUE], lse_ref[0:1, rows], dot_ref[0:1, rows]
        at = (lists, frame, slab, block)
        group = listed(z, *at, (z_k, ALL), (z_v, ALL), dk=(dz, KEY), dv=(dz, VALUE))
        group += listed(y, *at, (y_k, ALL), (y_v, ALL), dk=(dy, KEY), dv=(dy, VALUE))
        dq_ref[:, rows] = dq_old[:, rows] + backward_group(q, g, lse, row_dot, group)


def own_kernel(qg, lse_ref, dot_ref, dq_old, o, kv, placed, near, keep, send):
    half = qg.shape[0] // 2
    near[...] = placed[...]
    whole = []
    for slab in range(2):
        rows = rows_of(slab, half)
        q, g, lse, row_dot = qg[rows, KEY], qg[rows, VALUE], lse_ref[0:1, rows], dot_ref[0:1, rows]
        dq = dq_old[:, rows]
        for group in own_groups(kv, half, dk=(near, KEY), dv=(near, VALUE)):
            dq = dq + backward_group(q, g, lse, row_dot, group)
        whole.append((dq.T * SCALE).astype(BF16))

    def body(mine):
        for slab in range(2):
            out = keep if slab == mine else send
            out[:, KEY] = o[:, rows_of(slab, half)].T
            out[:, VALUE] = whole[slab]

    each_core(body)


def merge_kernel(dz, dy, came, z_out, y_out):
    first = forwards_first(lax.axis_index("tm"))
    more = came[...].astype(F32)
    z_out[:, KEY] = (dz[:, KEY] + jnp.where(first, more, 0.0)).astype(BF16)
    y_out[:, KEY] = (dy[:, KEY] + jnp.where(first, 0.0, more)).astype(BF16)
    z_out[:, VALUE] = dz[:, VALUE].astype(BF16)
    y_out[:, VALUE] = dy[:, VALUE].astype(BF16)


def place_kernel(block, far, *refs):
    n = len(far)
    lists, total = refs[0], refs[-1]
    frame = lax.axis_index("tm")
    total[...] = jnp.zeros_like(total)
    for swap, came_k, came_v in zip(far, refs[1 : 1 + n], refs[1 + n : -1]):
        for slab in range(2):
            b, exists = swap.block_of_theirs(lists, frame, slab, 0)
            rows = pl.ds(pl.multiple_of(b * block, block), block)
            for came, cols in ((came_k, KEY), (came_v, VALUE)):
                part = came[rows_of(slab, block), :].astype(F32)
                total[rows, cols] += jnp.where(exists, part, 0.0)


def add_kernel(swaps, near, *refs):
    frame = lax.axis_index("tm")
    total = near[...]
    for swap, came in zip(swaps, refs[:-1]):
        _, _, exists = swap.partner(frame)
        total = total + jnp.where(exists, came[...].astype(F32), 0.0)
    refs[-1][...] = total


def gather_kernel(swap, near, came, keep, send):
    _, _, exists = swap.partner(lax.axis_index("tm"))
    half = near.shape[0] // 2

    def body(mine):
        for slab, out in ((1 - mine, send), (mine, keep)):
            rows = rows_of(slab, half)
            part = jnp.where(exists, came[rows, :].astype(F32), 0.0)
            out[...] = (near[rows, :] + part).astype(BF16)

    each_core(body)


def finish_kernel(keep, came, first, second):
    def body(mine):
        for head, source in ((mine, keep), (1 - mine, came)):
            first[:, head_cols(head)] = source[:, KEY]
            second[:, head_cols(head)] = source[:, VALUE]

    each_core(body)


def per_device(queries, key_rows, value_rows, out_grad, block_lists):
    s_dev, width = queries.shape
    count = lax.axis_size("tm")
    block = s_dev // 2
    pair = sds((s_dev, 2 * DH), BF16)
    single = sds((s_dev, DH), BF16)
    frame_two = sds((2 * s_dev, 2 * DH), BF16)
    frame_one = sds((2 * s_dev, DH), BF16)
    frame_sum = sds((2 * s_dev, 2 * DH), F32)
    stat_row = sds((8, 2 * s_dev), F32)
    turned_sum = sds((DH, 2 * s_dev), F32)
    turned_bf = sds((DH, 2 * s_dev), BF16)
    levels = count.bit_length() - 1
    near_swap, relayed = Swap(count, 0, False), Swap(count, 0, True)
    z_swap, y_swap = Swap(count, 1, False), Swap(count, 1, True)
    far = [Swap(count, level, second) for level in range(2, levels) for second in (False, True)]
    far = [swap for swap in far if swap.moves]
    n = len(far)
    grad_one = pltpu.VMEM((2 * s_dev, DH), F32)

    def across(value):
        return lax.ppermute(value, "space", [(0, 1), (1, 0)])

    def swapped(value, swap):
        return lax.ppermute(value, ("tm", "space"), swap.pairs)

    def scores(pieces):
        return pltpu.VMEM((pieces * block, s_dev), F32)


    k_came, v_came = across(key_rows), across(value_rows)
    sources = (key_rows, value_rows, queries, out_grad, block_lists.T)
    k_own, v_own, qg_own, qg_send, lists = call(
        pack_kernel,
        tuple(pltpu.with_memory_space_constraint(a, pltpu.HBM) for a in sources),
        [single, single, pair, pair, sds(sources[4].shape, jnp.int32)],
        scratch=[pltpu.SemaphoreType.DMA((7,))],
        source=HBM,
        scalars=HBM,
    )
    (keys,) = call(keys_kernel, (k_own, k_came), [frame_one])
    values, kv = call(values_kernel, (keys, v_own, v_came), [frame_one, frame_two])
    qg_send, _ = lax.optimization_barrier((qg_send, keys))
    y_k = swapped(keys, y_swap)
    z_k = swapped(keys, z_swap)
    a_kv = swapped(kv, near_swap)
    y_v = swapped(values, y_swap)
    z_v = swapped(values, z_swap)
    y_k, qg_came = lax.optimization_barrier((y_k, across(qg_send)))
    work = 4 * s_dev * s_dev * DH
    qg, turned = call(join_kernel, (qg_own, qg_came), [frame_two, turned_bf], flops=15 * work)
    kv, _ = lax.optimization_barrier((kv, turned))
    far_send = call(functools.partial(select_kernel, far, block), (lists, kv), [pair] * n)
    y_k, z_k, far_send = lax.optimization_barrier((y_k, z_k, far_send))
    (relay_k,) = call(relay_kernel, (y_k, z_k), [frame_one])
    relay_k, far_send = lax.optimization_barrier((relay_k, far_send))
    a_kv, _ = lax.optimization_barrier((a_kv, relay_k))
    c_k = swapped(relay_k, near_swap)
    far_kv = [swapped(value, swap) for value, swap in zip(far_send, far)]
    stat, acc = call(
        functools.partial(near_kernel, block, near_swap),
        (lists, qg, kv, a_kv),
        [stat_row, turned_sum],
        scratch=[scores(6)],
    )
    score_two = sds((2, s_dev, s_dev), F32)
    y_v, z_v, stat = lax.optimization_barrier((y_v, z_v, stat))
    (relay_v,) = call(relay_kernel, (y_v, z_v), [frame_one])
    relay_v, stat = lax.optimization_barrier((relay_v, stat))
    c_v = swapped(relay_v, near_swap)
    stat, acc, late_scores = call(
        functools.partial(middle_kernel, block, (z_swap, y_swap, relayed)),
        (lists, qg, stat, acc, y_k, z_k, y_v, z_v, c_k),
        [stat_row, turned_sum, score_two],
        scratch=[scores(4)],
    )
    acc, far_kv = lax.optimization_barrier((acc, far_kv))
    lse, part, dc_v, probs, *far_dv = call(
        functools.partial(close_kernel, block, relayed, far),
        (lists, qg, stat, acc, late_scores, *far_kv),
        [stat_row, turned_sum, frame_one, score_two] + [single] * n,
        scratch=[
            scores(n),
            grad_one,
            pltpu.SMEM(lists.shape, jnp.int32),
            pltpu.SemaphoreType.DMA(()),
        ],
        scalars=pl.BlockSpec(memory_space=pl.ANY),
    )
    dc_v_came = swapped(dc_v, near_swap)
    far_dv_came = [swapped(value, swap) for value, swap in zip(far_dv, far)]
    o, row_dot, dc_k, dq, *far_grad = call(
        functools.partial(late_kernel, block, relayed, far),
        (lists, qg, turned, lse, part, probs, c_k, c_v, *far_kv),
        [turned_bf, stat_row, frame_one, turned_sum] + [single] * n,
        scratch=[grad_one],
    )
    far_dk_came = [swapped(value, swap) for value, swap in zip(far_grad, far)]
    dc_k_came = swapped(dc_k, near_swap)
    da, dq = call(
        functools.partial(first_kernel, block, near_swap),
        (lists, qg, lse, row_dot, dq, a_kv),
        [frame_two, turned_sum],
        scratch=[pltpu.VMEM((2 * s_dev, 2 * DH), F32)],
    )
    da, dc_k_came = lax.optimization_barrier((da, dc_k_came))
    da_came = swapped(da, near_swap)
    dc_v_came, far_dv_came = lax.optimization_barrier((dc_v_came, far_dv_came))
    dz, dy, dq = call(
        functools.partial(second_kernel, block, (z_swap, y_swap)),
        (lists, qg, lse, row_dot, dq, dc_v_came, y_k, z_k, y_v, z_v),
        [frame_sum, frame_sum, turned_sum],
        flops=20 * work,
    )
    dz, dy = call(merge_kernel, (dz, dy, dc_k_came), [frame_two, frame_two])
    dy_came = swapped(dy, y_swap)
    dz_came = swapped(dz, z_swap)
    dq, dz, dy = lax.optimization_barrier((dq, dz, dy))
    far_dk_came, dq = lax.optimization_barrier((far_dk_came, dq))
    (placed,) = call(functools.partial(place_kernel, block, far), (lists, *far_dk_came, *far_dv_came), [frame_sum])
    near, q_keep, q_send = call(
        own_kernel,
        (qg, lse, row_dot, dq, o, kv, placed),
        [frame_sum, pair, pair],
        flops=20 * work,
    )
    outputs = [sds((s_dev, width), BF16)] * 2
    attn_out, grad_q = call(finish_kernel, (q_keep, across(q_send)), outputs)
    near, attn_out, grad_q = lax.optimization_barrier((near, attn_out, grad_q))
    (near,) = call(
        functools.partial(add_kernel, (near_swap, y_swap)),
        (near, da_came, dy_came),
        [frame_sum],
        flops=20 * work,
    )
    k_keep, k_send = call(
        functools.partial(gather_kernel, z_swap), (near, dz_came), [pair, pair]
    )
    grad_k, grad_v = call(finish_kernel, (k_keep, across(k_send)), outputs)
    return attn_out, grad_q, grad_k, grad_v


def solution(mesh):
    rows = P(("groups", "tm", "space"), None)
    return jax.shard_map(
        per_device,
        mesh=mesh,
        in_specs=(rows, rows, rows, rows, P("groups", None)),
        out_specs=(rows, rows, rows, rows),
        check_vma=False,
    )
```

```python
import functools
import math

import jax
import jax.numpy as jnp
from jax import lax
from jax.experimental import pallas as pl
from jax.experimental.pallas import tpu as pltpu
from jax.sharding import PartitionSpec as P

DH = 128
F32 = jnp.float32
BF16 = jnp.bfloat16
VMEM = pl.BlockSpec(memory_space=pltpu.VMEM)
SMEM = pl.BlockSpec(memory_space=pltpu.SMEM)
HBM = pl.BlockSpec(memory_space=pltpu.HBM)
NEG = -1e30
SCALE = 1.0 / math.sqrt(DH)
EXP_SCALE = SCALE * math.log2(math.e)
KEY = slice(0, DH)
VALUE = slice(DH, 2 * DH)
sds = jax.ShapeDtypeStruct


def dot_nn(a, b):
    return lax.dot_general(a, b, (((1,), (0,)), ((), ())), preferred_element_type=F32)


def dot_nt(a, b):
    return lax.dot_general(a, b, (((1,), (1,)), ((), ())), preferred_element_type=F32)


def dot_tn(a, b):
    return lax.dot_general(a, b, (((0,), (0,)), ((), ())), preferred_element_type=F32)


def call(kernel, args, out_shape, scratch=(), source=VMEM, scalars=SMEM, flops=1024):
    return pl.pallas_call(
        kernel,
        out_shape=out_shape,
        in_specs=[scalars if a.dtype == jnp.int32 else source for a in args],
        out_specs=tuple(VMEM for _ in out_shape),
        scratch_shapes=list(scratch),
        compiler_params=pltpu.CompilerParams(vmem_limit_bytes=40 << 20),
        cost_estimate=pl.CostEstimate(flops=flops, bytes_accessed=1024, transcendentals=0),
    )(*args)


def swap_pairs(count, distance, second):
    pairs = []
    for frame in range(count):
        up = ((frame // distance) % 2 == 0) != second
        target = frame + distance if up else frame - distance
        for core in range(2):
            if 0 <= target < count:
                pairs.append((frame * 2 + core, target * 2 + core))
            else:
                pairs.append((frame * 2 + core, frame * 2 + 1 - core))
    return pairs


class Swap:
    def __init__(self, count, level, second):
        self.count, self.level, self.second = count, level, second
        self.levels = count.bit_length() - 1
        self.pairs = swap_pairs(count, 1 << level, second)
        self.moves = any(source // 2 != target // 2 for source, target in self.pairs)

    def partner(self, frame):
        odd = lax.rem(lax.shift_right_logical(frame, self.level), 2)
        later = odd == (1 if self.second else 0)
        other = jnp.where(later, frame + (1 << self.level), frame - (1 << self.level))
        return other, later, jnp.logical_and(other >= 0, other < self.count)

    def slot(self, later, k):
        base = 0 if self.level == 0 else self.level + 1
        return jnp.where(later, self.levels + 1, 0) + base + k

    def block_of_mine(self, lists, frame, slab, k):
        other, later, exists = self.partner(frame)
        entry = lists[self.slot(later, k), frame * 2 + slab]
        return jnp.clip(entry - other * 4, 0, 3), exists

    def block_of_theirs(self, lists, frame, slab, k):
        other, later, exists = self.partner(frame)
        row = jnp.where(exists, other, frame) * 2 + slab
        entry = lists[self.slot(jnp.logical_not(later), k), row]
        return jnp.clip(entry - frame * 4, 0, 3), exists


def head_cols(head):
    return slice(head * DH, (head + 1) * DH)


def rows_of(slab, half):
    return slice(slab * half, (slab + 1) * half)


def each_core(body):
    core = lax.axis_index("space")
    for mine in range(2):
        pl.when(core == mine)(functools.partial(body, mine))


def pack_kernel(k, v, q, g, lists, k_own, v_own, qg_own, qg_send, lists_out, sems):
    def body(mine):
        moves = [(lists, lists_out)]
        for source, out in ((k, k_own), (v, v_own)):
            moves.append((source.at[:, head_cols(mine)], out))
        for head, out in ((mine, qg_own), (1 - mine, qg_send)):
            for source, cols in ((q, KEY), (g, VALUE)):
                moves.append((source.at[:, head_cols(head)], out.at[:, cols]))
        copies = [
            pltpu.make_async_copy(source, out, sems.at[n]) for n, (source, out) in enumerate(moves)
        ]
        for copy in copies:
            copy.start()
        for copy in copies:
            copy.wait()

    each_core(body)


def keys_kernel(own, came, keys):
    half = own.shape[0]

    def body(mine):
        keys[rows_of(mine, half), :] = own[...]
        keys[rows_of(1 - mine, half), :] = came[:, head_cols(mine)]

    each_core(body)


def values_kernel(keys, own, came, values, kv):
    half = own.shape[0]

    def body(mine):
        for slab, part in ((mine, own[...]), (1 - mine, came[:, head_cols(mine)])):
            rows = rows_of(slab, half)
            values[rows, :] = part
            kv[rows, VALUE] = part
            kv[rows, KEY] = keys[rows, :]

    each_core(body)


def select_kernel(far, block, lists, kv, *sends):
    frame = lax.axis_index("tm")
    for swap, send in zip(far, sends):
        for slab in range(2):
            b, _ = swap.block_of_theirs(lists, frame, slab, 0)
            row = pl.multiple_of(b * block, block)
            send[slab * block : (slab + 1) * block, :] = kv[pl.ds(row, block), :]


def forwards_first(frame):
    return lax.rem(frame, 2) == lax.rem(lax.shift_right_logical(frame, 1), 2)


def relay_kernel(y, z, out):
    first = forwards_first(lax.axis_index("tm"))

    @pl.when(first)
    def _():
        out[...] = z[...]

    @pl.when(jnp.logical_not(first))
    def _():
        out[...] = y[...]


class Piece:
    def __init__(self, k, v, row, size, exists=None, dk=None, dv=None, add=True):
        self.k_at, self.v_at, self.exists = k, v, exists
        self.rows, self.size = pl.ds(row, size), size
        self.dk, self.dv, self.add = dk, dv, add

    def store(self, at, value):
        ref, cols = at
        if self.add:
            ref[self.rows, cols] += value
        else:
            ref[self.rows, cols] = value.astype(ref.dtype)


def stack(parts):
    return parts[0] if len(parts) == 1 else jnp.concatenate(parts, axis=0)


def keys_of(group):
    return stack([p.k_at[0][p.rows, p.k_at[1]] for p in group])


def values_of(group):
    return stack([p.v_at[0][p.rows, p.v_at[1]] for p in group])


def by_piece(group, value):
    at = 0
    for piece in group:
        yield piece, value[at : at + piece.size, :]
        at += piece.size


def store_grads(group, value, name):
    for piece, part in by_piece(group, value):
        piece.store(getattr(piece, name), part)


def listed(swap, lists, frame, slab, block, k, v, count=1, **grads):
    pieces = []
    for n in range(count):
        b, exists = swap.block_of_mine(lists, frame, slab, n)
        pieces.append(Piece(k, v, pl.multiple_of(b * block, block), block, exists, **grads))
    return pieces


def arrived(swap, frame, slab, block, kv, **grads):
    _, _, exists = swap.partner(frame)
    return Piece((kv, KEY), (kv, VALUE), slab * block, block, exists, add=False, **grads)


def raised(group, s, base):
    parts = []
    for piece, part in by_piece(group, s):
        low = base if piece.exists is None else jnp.where(piece.exists, base, -NEG)
        parts.append(jnp.exp2(part * EXP_SCALE - low))
    return stack(parts)


def score_groups(q, groups, s_ref, peak):
    at = 0
    for group in groups:
        s = dot_nt(keys_of(group), q)
        s_ref[at : at + s.shape[0], :] = s
        at += s.shape[0]
        for piece, part in by_piece(group, s):
            top = jnp.max(part, axis=0, keepdims=True)
            if piece.exists is not None:
                top = jnp.where(piece.exists, top, NEG)
            peak = top if peak is None else jnp.maximum(peak, top)
    return peak


def group_scores(groups, s_ref):
    at = 0
    for group in groups:
        size = sum(piece.size for piece in group)
        yield group, s_ref[at : at + size, :]
        at += size


def forward_slab(q, groups, with_values, s_ref, old):
    peak = score_groups(q, groups, s_ref, None if old is None else old[0])
    total, acc = 0.0, 0.0
    if old is not None:
        shrink = jnp.exp2((old[0] - peak) * EXP_SCALE)
        total, acc = old[1] * shrink, old[2] * shrink
    for j, (group, s) in enumerate(group_scores(groups, s_ref)):
        e = raised(group, s, peak * EXP_SCALE)
        total = total + jnp.sum(e, axis=0, keepdims=True)
        if j < with_values:
            acc = acc + dot_tn(values_of(group), e.astype(BF16))
    return peak, total, acc


def backward_group(q, g, lse, row_dot, group, p=None):
    k = keys_of(group)
    if p is None:
        p = raised(group, dot_nt(k, q), lse)
    if group[0].dv is not None:
        store_grads(group, dot_nn(p.astype(BF16), g), "dv")
    ds = (p * (dot_nt(values_of(group), g) - row_dot)).astype(BF16)
    if group[0].dk is not None:
        store_grads(group, dot_nn(ds, q) * SCALE, "dk")
    return dot_tn(k, ds)


def join_kernel(own, came, out, turned):
    half = own.shape[0]

    def body(mine):
        for slab, source in ((mine, own), (1 - mine, came)):
            rows = rows_of(slab, half)
            out[rows, :] = source[...]
            turned[:, rows] = source[:, VALUE].T

    each_core(body)


ALL = slice(None)


def store_state(refs, rows, peak, total, acc):
    stat, acc_ref = refs
    stat[0:1, rows] = peak
    stat[1:2, rows] = total
    acc_ref[:, rows] = acc


def load_state(refs, rows):
    stat, acc_ref = refs
    return stat[0:1, rows], stat[1:2, rows], acc_ref[:, rows]


def own_groups(kv, half, **grads):
    return [
        [Piece((kv, KEY), (kv, VALUE), r, half, **grads)] for r in range(0, kv.shape[0], half)
    ]


def near_kernel(block, swap, lists, qg, kv, a_kv, stat, acc, s_ref):
    half = qg.shape[0] // 2
    frame = lax.axis_index("tm")
    for slab in range(2):
        rows = rows_of(slab, half)
        groups = own_groups(kv, half)
        groups.append(
            listed(swap, lists, frame, slab, block, (a_kv, KEY), (a_kv, VALUE), 2)
        )
        store_state((stat, acc), rows, *forward_slab(qg[rows, KEY], groups, 3, s_ref, None))


def middle_kernel(
    block, swaps, lists, qg, stat, acc, y_k, z_k, y_v, z_v, c_k, stat2, acc2, late, s_ref
):
    half = qg.shape[0] // 2
    frame = lax.axis_index("tm")
    z, y, relayed = swaps
    for slab in range(2):
        rows = rows_of(slab, half)
        at = (lists, frame, slab, block)
        group = listed(z, *at, (z_k, ALL), (z_v, ALL)) + listed(y, *at, (y_k, ALL), (y_v, ALL))
        more = listed(relayed, *at, (c_k, ALL), None, 2)
        old = load_state((stat, acc), rows)
        new = forward_slab(qg[rows, KEY], [group, more], 1, s_ref, old)
        store_state((stat2, acc2), rows, *new)
        late[slab] = s_ref[2 * block :, :]


def close_kernel(block, relayed, far, lists_any, qg, stat, acc, late_s, *refs):
    n = len(far)
    far_kv = refs[:n]
    lse_ref, part_ref, dc_v, p_ref, s_ref, grad, lists, sem = refs[n:]
    half = qg.shape[0] // 2
    frame = lax.axis_index("tm")
    copy = pltpu.make_async_copy(lists_any, lists, sem)
    copy.start()
    grad[...] = jnp.zeros_like(grad)
    for slab in range(2):
        rows = rows_of(slab, half)
        q = qg[rows, KEY]
        groups = [[arrived(swap, frame, slab, block, kv)] for swap, kv in zip(far, far_kv)]
        old = load_state((stat, acc), rows)
        peak, total, out = forward_slab(q, groups, n, s_ref, old)
        part_ref[:, rows] = out / total
        lse = peak * EXP_SCALE + jnp.log2(total)
        lse_ref[0:1, rows] = lse
    copy.wait()
    for slab in range(2):
        rows = rows_of(slab, half)
        group = listed(relayed, lists, frame, slab, block, None, None, 2, dv=(grad, ALL))
        p = raised(group, late_s[slab], lse_ref[0:1, rows])
        p_ref[slab] = p
        store_grads(group, dot_nn(p.astype(BF16), qg[rows, VALUE]), "dv")
    dc_v[...] = grad[...].astype(BF16)


def late_kernel(block, relayed, far, *refs):
    n = len(far)
    lists, qg, turned, lse_ref, part_ref, p_ref, c_k, c_v = refs[:8]
    far_kv = refs[8 : 8 + n]
    o_ref, dot_ref, dc_k, dq_ref = refs[8 + n : 12 + n]
    far_grad = refs[12 + n : 12 + 2 * n]
    grad = refs[12 + 2 * n]
    half = qg.shape[0] // 2
    frame = lax.axis_index("tm")
    grad[...] = jnp.zeros_like(grad)
    for slab in range(2):
        rows = rows_of(slab, half)
        q, g, lse = qg[rows, KEY], qg[rows, VALUE], lse_ref[0:1, rows]
        group = listed(
            relayed, lists, frame, slab, block, (c_k, ALL), (c_v, ALL), 2, dk=(grad, ALL)
        )
        p = p_ref[slab]
        o = (part_ref[:, rows] + dot_tn(values_of(group), p.astype(BF16))).astype(BF16)
        o_ref[:, rows] = o
        products = turned[:, rows].astype(F32) * o.astype(F32)
        row_dot = jnp.sum(products, axis=0, keepdims=True)
        dot_ref[0:1, rows] = row_dot
        dq = backward_group(q, g, lse, row_dot, group, p)
        for swap, kv, out in zip(far, far_kv, far_grad):
            group = [arrived(swap, frame, slab, block, kv, dk=(out, KEY), dv=(out, VALUE))]
            dq = dq + backward_group(q, g, lse, row_dot, group)
        dq_ref[:, rows] = dq
    dc_k[...] = grad[...].astype(BF16)


def first_kernel(block, swap, lists, qg, lse_ref, dot_ref, dq_old, a_kv, da, dq_ref, grad):
    half = qg.shape[0] // 2
    frame = lax.axis_index("tm")
    grad[...] = jnp.zeros_like(grad)
    for slab in range(2):
        rows = rows_of(slab, half)
        q, g, lse, row_dot = qg[rows, KEY], qg[rows, VALUE], lse_ref[0:1, rows], dot_ref[0:1, rows]
        group = listed(
            swap, lists, frame, slab, block, (a_kv, KEY), (a_kv, VALUE), 2,
            dk=(grad, KEY), dv=(grad, VALUE),
        )
        dq_ref[:, rows] = dq_old[:, rows] + backward_group(q, g, lse, row_dot, group)
    da[...] = grad[...].astype(BF16)


def second_kernel(
    block, swaps, lists, qg, lse_ref, dot_ref, dq_old, came, y_k, z_k, y_v, z_v, dz, dy, dq_ref
):
    half = qg.shape[0] // 2
    frame = lax.axis_index("tm")
    z, y = swaps
    relays = forwards_first(frame)
    more = came[...].astype(F32)
    for ref, takes in ((dz, relays), (dy, jnp.logical_not(relays))):
        ref[:, KEY] = jnp.zeros_like(more)
        ref[:, VALUE] = jnp.where(takes, more, 0.0)
    for slab in range(2):
        rows = rows_of(slab, half)
        q, g, lse, row_dot = qg[rows, KEY], qg[rows, VALUE], lse_ref[0:1, rows], dot_ref[0:1, rows]
        at = (lists, frame, slab, block)
        group = listed(z, *at, (z_k, ALL), (z_v, ALL), dk=(dz, KEY), dv=(dz, VALUE))
        group += listed(y, *at, (y_k, ALL), (y_v, ALL), dk=(dy, KEY), dv=(dy, VALUE))
        dq_ref[:, rows] = dq_old[:, rows] + backward_group(q, g, lse, row_dot, group)


def own_kernel(qg, lse_ref, dot_ref, dq_old, o, kv, placed, near, keep, send):
    half = qg.shape[0] // 2
    near[...] = placed[...]
    whole = []
    for slab in range(2):
        rows = rows_of(slab, half)
        q, g, lse, row_dot = qg[rows, KEY], qg[rows, VALUE], lse_ref[0:1, rows], dot_ref[0:1, rows]
        dq = dq_old[:, rows]
        for group in own_groups(kv, half, dk=(near, KEY), dv=(near, VALUE)):
            dq = dq + backward_group(q, g, lse, row_dot, group)
        whole.append((dq.T * SCALE).astype(BF16))

    def body(mine):
        for slab in range(2):
            out = keep if slab == mine else send
            out[:, KEY] = o[:, rows_of(slab, half)].T
            out[:, VALUE] = whole[slab]

    each_core(body)


def merge_kernel(dz, dy, came, z_out, y_out):
    first = forwards_first(lax.axis_index("tm"))
    more = came[...].astype(F32)
    z_out[:, KEY] = (dz[:, KEY] + jnp.where(first, more, 0.0)).astype(BF16)
    y_out[:, KEY] = (dy[:, KEY] + jnp.where(first, 0.0, more)).astype(BF16)
    z_out[:, VALUE] = dz[:, VALUE].astype(BF16)
    y_out[:, VALUE] = dy[:, VALUE].astype(BF16)


def place_kernel(block, far, *refs):
    lists, total = refs[0], refs[-1]
    frame = lax.axis_index("tm")
    total[...] = jnp.zeros_like(total)
    for swap, came in zip(far, refs[1:-1]):
        for slab in range(2):
            b, exists = swap.block_of_theirs(lists, frame, slab, 0)
            rows = pl.ds(pl.multiple_of(b * block, block), block)
            part = came[rows_of(slab, block), :].astype(F32)
            total[rows, :] += jnp.where(exists, part, 0.0)


def add_kernel(swaps, near, *refs):
    frame = lax.axis_index("tm")
    total = near[...]
    for swap, came in zip(swaps, refs[:-1]):
        _, _, exists = swap.partner(frame)
        total = total + jnp.where(exists, came[...].astype(F32), 0.0)
    refs[-1][...] = total


def gather_kernel(swap, near, came, keep, send):
    _, _, exists = swap.partner(lax.axis_index("tm"))
    half = near.shape[0] // 2

    def body(mine):
        for slab, out in ((1 - mine, send), (mine, keep)):
            rows = rows_of(slab, half)
            part = jnp.where(exists, came[rows, :].astype(F32), 0.0)
            out[...] = (near[rows, :] + part).astype(BF16)

    each_core(body)


def finish_kernel(keep, came, first, second):
    def body(mine):
        for head, source in ((mine, keep), (1 - mine, came)):
            first[:, head_cols(head)] = source[:, KEY]
            second[:, head_cols(head)] = source[:, VALUE]

    each_core(body)


def per_device(queries, key_rows, value_rows, out_grad, block_lists):
    s_dev, width = queries.shape
    count = lax.axis_size("tm")
    block = s_dev // 2
    pair = sds((s_dev, 2 * DH), BF16)
    single = sds((s_dev, DH), BF16)
    frame_two = sds((2 * s_dev, 2 * DH), BF16)
    frame_one = sds((2 * s_dev, DH), BF16)
    frame_sum = sds((2 * s_dev, 2 * DH), F32)
    stat_row = sds((8, 2 * s_dev), F32)
    turned_sum = sds((DH, 2 * s_dev), F32)
    turned_bf = sds((DH, 2 * s_dev), BF16)
    levels = count.bit_length() - 1
    near_swap, relayed = Swap(count, 0, False), Swap(count, 0, True)
    z_swap, y_swap = Swap(count, 1, False), Swap(count, 1, True)
    far = [Swap(count, level, second) for level in range(2, levels) for second in (False, True)]
    far = [swap for swap in far if swap.moves]
    n = len(far)
    grad_one = pltpu.VMEM((2 * s_dev, DH), F32)

    def across(value):
        return lax.ppermute(value, "space", [(0, 1), (1, 0)])

    def swapped(value, swap):
        return lax.ppermute(value, ("tm", "space"), swap.pairs)

    def scores(pieces):
        return pltpu.VMEM((pieces * block, s_dev), F32)


    k_came, v_came = across(key_rows), across(value_rows)
    sources = (key_rows, value_rows, queries, out_grad, block_lists.T)
    k_own, v_own, qg_own, qg_send, lists = call(
        pack_kernel,
        tuple(pltpu.with_memory_space_constraint(a, pltpu.HBM) for a in sources),
        [single, single, pair, pair, sds(sources[4].shape, jnp.int32)],
        scratch=[pltpu.SemaphoreType.DMA((7,))],
        source=HBM,
        scalars=HBM,
    )
    (keys,) = call(keys_kernel, (k_own, k_came), [frame_one])
    values, kv = call(values_kernel, (keys, v_own, v_came), [frame_one, frame_two])
    qg_send, _ = lax.optimization_barrier((qg_send, keys))
    y_k = swapped(keys, y_swap)
    z_k = swapped(keys, z_swap)
    a_kv = swapped(kv, near_swap)
    y_v = swapped(values, y_swap)
    z_v = swapped(values, z_swap)
    y_k, qg_came = lax.optimization_barrier((y_k, across(qg_send)))
    work = 4 * s_dev * s_dev * DH
    qg, turned = call(join_kernel, (qg_own, qg_came), [frame_two, turned_bf], flops=15 * work)
    kv, _ = lax.optimization_barrier((kv, turned))
    far_send = call(functools.partial(select_kernel, far, block), (lists, kv), [pair] * n)
    y_k, z_k, far_send = lax.optimization_barrier((y_k, z_k, far_send))
    (relay_k,) = call(relay_kernel, (y_k, z_k), [frame_one])
    relay_k, far_send = lax.optimization_barrier((relay_k, far_send))
    a_kv, _ = lax.optimization_barrier((a_kv, relay_k))
    c_k = swapped(relay_k, near_swap)
    far_kv = [swapped(value, swap) for value, swap in zip(far_send, far)]
    stat, acc = call(
        functools.partial(near_kernel, block, near_swap),
        (lists, qg, kv, a_kv),
        [stat_row, turned_sum],
        scratch=[scores(6)],
    )
    score_two = sds((2, s_dev, s_dev), F32)
    y_v, z_v, stat = lax.optimization_barrier((y_v, z_v, stat))
    (relay_v,) = call(relay_kernel, (y_v, z_v), [frame_one])
    relay_v, stat = lax.optimization_barrier((relay_v, stat))
    c_v = swapped(relay_v, near_swap)
    stat, acc, late_scores = call(
        functools.partial(middle_kernel, block, (z_swap, y_swap, relayed)),
        (lists, qg, stat, acc, y_k, z_k, y_v, z_v, c_k),
        [stat_row, turned_sum, score_two],
        scratch=[scores(4)],
    )
    acc, far_kv = lax.optimization_barrier((acc, far_kv))
    lse, part, dc_v, probs = call(
        functools.partial(close_kernel, block, relayed, far),
        (lists, qg, stat, acc, late_scores, *far_kv),
        [stat_row, turned_sum, frame_one, score_two],
        scratch=[
            scores(n),
            grad_one,
            pltpu.SMEM(lists.shape, jnp.int32),
            pltpu.SemaphoreType.DMA(()),
        ],
        scalars=pl.BlockSpec(memory_space=pl.ANY),
    )
    dc_v_came = swapped(dc_v, near_swap)
    o, row_dot, dc_k, dq, *far_grad = call(
        functools.partial(late_kernel, block, relayed, far),
        (lists, qg, turned, lse, part, probs, c_k, c_v, *far_kv),
        [turned_bf, stat_row, frame_one, turned_sum] + [pair] * n,
        scratch=[grad_one],
    )
    far_came = [swapped(value, swap) for value, swap in zip(far_grad, far)]
    dc_k_came = swapped(dc_k, near_swap)
    da, dq = call(
        functools.partial(first_kernel, block, near_swap),
        (lists, qg, lse, row_dot, dq, a_kv),
        [frame_two, turned_sum],
        scratch=[pltpu.VMEM((2 * s_dev, 2 * DH), F32)],
    )
    da, dc_k_came = lax.optimization_barrier((da, dc_k_came))
    da_came = swapped(da, near_swap)
    dz, dy, dq = call(
        functools.partial(second_kernel, block, (z_swap, y_swap)),
        (lists, qg, lse, row_dot, dq, dc_v_came, y_k, z_k, y_v, z_v),
        [frame_sum, frame_sum, turned_sum],
        flops=20 * work,
    )
    dz, dy = call(merge_kernel, (dz, dy, dc_k_came), [frame_two, frame_two])
    dy_came = swapped(dy, y_swap)
    dz_came = swapped(dz, z_swap)
    dq, dz, dy = lax.optimization_barrier((dq, dz, dy))
    far_came, dq = lax.optimization_barrier((far_came, dq))
    (placed,) = call(functools.partial(place_kernel, block, far), (lists, *far_came), [frame_sum])
    near, q_keep, q_send = call(
        own_kernel,
        (qg, lse, row_dot, dq, o, kv, placed),
        [frame_sum, pair, pair],
        flops=20 * work,
    )
    outputs = [sds((s_dev, width), BF16)] * 2
    attn_out, grad_q = call(finish_kernel, (q_keep, across(q_send)), outputs)
    near, attn_out, grad_q = lax.optimization_barrier((near, attn_out, grad_q))
    (near,) = call(
        functools.partial(add_kernel, (near_swap, y_swap)),
        (near, da_came, dy_came),
        [frame_sum],
        flops=20 * work,
    )
    k_keep, k_send = call(
        functools.partial(gather_kernel, z_swap), (near, dz_came), [pair, pair]
    )
    grad_k, grad_v = call(finish_kernel, (k_keep, across(k_send)), outputs)
    return attn_out, grad_q, grad_k, grad_v


def solution(mesh):
    rows = P(("groups", "tm", "space"), None)
    return jax.shard_map(
        per_device,
        mesh=mesh,
        in_specs=(rows, rows, rows, rows, P("groups", None)),
        out_specs=(rows, rows, rows, rows),
        check_vma=False,
    )
```

```python
import functools
import math

import jax
import jax.numpy as jnp
from jax import lax
from jax.experimental import pallas as pl
from jax.experimental.pallas import tpu as pltpu
from jax.sharding import PartitionSpec as P

DH = 128
F32 = jnp.float32
BF16 = jnp.bfloat16
VMEM = pl.BlockSpec(memory_space=pltpu.VMEM)
SMEM = pl.BlockSpec(memory_space=pltpu.SMEM)
HBM = pl.BlockSpec(memory_space=pltpu.HBM)
NEG = -1e30
SCALE = 1.0 / math.sqrt(DH)
EXP_SCALE = SCALE * math.log2(math.e)
KEY = slice(0, DH)
VALUE = slice(DH, 2 * DH)
sds = jax.ShapeDtypeStruct


def dot_nn(a, b):
    return lax.dot_general(a, b, (((1,), (0,)), ((), ())), preferred_element_type=F32)


def dot_nt(a, b):
    return lax.dot_general(a, b, (((1,), (1,)), ((), ())), preferred_element_type=F32)


def dot_tn(a, b):
    return lax.dot_general(a, b, (((0,), (0,)), ((), ())), preferred_element_type=F32)


def call(kernel, args, out_shape, scratch=(), source=VMEM, scalars=SMEM, flops=1024):
    return pl.pallas_call(
        kernel,
        out_shape=out_shape,
        in_specs=[scalars if a.dtype == jnp.int32 else source for a in args],
        out_specs=tuple(VMEM for _ in out_shape),
        scratch_shapes=list(scratch),
        compiler_params=pltpu.CompilerParams(vmem_limit_bytes=40 << 20),
        cost_estimate=pl.CostEstimate(flops=flops, bytes_accessed=1024, transcendentals=0),
    )(*args)


def swap_pairs(count, distance, second):
    pairs = []
    for frame in range(count):
        up = ((frame // distance) % 2 == 0) != second
        target = frame + distance if up else frame - distance
        for core in range(2):
            if 0 <= target < count:
                pairs.append((frame * 2 + core, target * 2 + core))
            else:
                pairs.append((frame * 2 + core, frame * 2 + 1 - core))
    return pairs


class Swap:
    def __init__(self, count, level, second):
        self.count, self.level, self.second = count, level, second
        self.levels = count.bit_length() - 1
        self.pairs = swap_pairs(count, 1 << level, second)
        self.moves = any(source // 2 != target // 2 for source, target in self.pairs)

    def partner(self, frame):
        odd = lax.rem(lax.shift_right_logical(frame, self.level), 2)
        later = odd == (1 if self.second else 0)
        other = jnp.where(later, frame + (1 << self.level), frame - (1 << self.level))
        return other, later, jnp.logical_and(other >= 0, other < self.count)

    def slot(self, later, k):
        base = 0 if self.level == 0 else self.level + 1
        return jnp.where(later, self.levels + 1, 0) + base + k

    def block_of_mine(self, lists, frame, slab, k):
        other, later, exists = self.partner(frame)
        entry = lists[self.slot(later, k), frame * 2 + slab]
        return jnp.clip(entry - other * 4, 0, 3), exists

    def block_of_theirs(self, lists, frame, slab, k):
        other, later, exists = self.partner(frame)
        row = jnp.where(exists, other, frame) * 2 + slab
        entry = lists[self.slot(jnp.logical_not(later), k), row]
        return jnp.clip(entry - frame * 4, 0, 3), exists


def head_cols(head):
    return slice(head * DH, (head + 1) * DH)


def rows_of(slab, half):
    return slice(slab * half, (slab + 1) * half)


def each_core(body):
    core = lax.axis_index("space")
    for mine in range(2):
        pl.when(core == mine)(functools.partial(body, mine))


def pack_kernel(k, v, q, g, lists, k_own, v_own, qg_own, qg_send, lists_out, sems):
    def body(mine):
        moves = [(lists, lists_out)]
        for source, out in ((k, k_own), (v, v_own)):
            moves.append((source.at[:, head_cols(mine)], out))
        for head, out in ((mine, qg_own), (1 - mine, qg_send)):
            for source, cols in ((q, KEY), (g, VALUE)):
                moves.append((source.at[:, head_cols(head)], out.at[:, cols]))
        copies = [
            pltpu.make_async_copy(source, out, sems.at[n]) for n, (source, out) in enumerate(moves)
        ]
        for copy in copies:
            copy.start()
        for copy in copies:
            copy.wait()

    each_core(body)


def keys_kernel(own, came, keys):
    half = own.shape[0]

    def body(mine):
        keys[rows_of(mine, half), :] = own[...]
        keys[rows_of(1 - mine, half), :] = came[:, head_cols(mine)]

    each_core(body)


def values_kernel(keys, own, came, values, kv):
    half = own.shape[0]

    def body(mine):
        for slab, part in ((mine, own[...]), (1 - mine, came[:, head_cols(mine)])):
            rows = rows_of(slab, half)
            values[rows, :] = part
            kv[rows, VALUE] = part
            kv[rows, KEY] = keys[rows, :]

    each_core(body)


def select_kernel(far, block, lists, kv, *sends):
    frame = lax.axis_index("tm")
    for swap, send in zip(far, sends):
        for slab in range(2):
            b, _ = swap.block_of_theirs(lists, frame, slab, 0)
            row = pl.multiple_of(b * block, block)
            send[slab * block : (slab + 1) * block, :] = kv[pl.ds(row, block), :]


def forwards_first(frame):
    return lax.rem(frame, 2) == lax.rem(lax.shift_right_logical(frame, 1), 2)


def relay_kernel(y, z, out):
    first = forwards_first(lax.axis_index("tm"))

    @pl.when(first)
    def _():
        out[...] = z[...]

    @pl.when(jnp.logical_not(first))
    def _():
        out[...] = y[...]


class Piece:
    def __init__(self, k, v, row, size, exists=None, dk=None, dv=None, add=True):
        self.k_at, self.v_at, self.exists = k, v, exists
        self.rows, self.size = pl.ds(row, size), size
        self.dk, self.dv, self.add = dk, dv, add

    def store(self, at, value):
        ref, cols = at
        if self.add:
            ref[self.rows, cols] += value
        else:
            ref[self.rows, cols] = value.astype(ref.dtype)


def stack(parts):
    return parts[0] if len(parts) == 1 else jnp.concatenate(parts, axis=0)


def keys_of(group):
    return stack([p.k_at[0][p.rows, p.k_at[1]] for p in group])


def values_of(group):
    return stack([p.v_at[0][p.rows, p.v_at[1]] for p in group])


def by_piece(group, value):
    at = 0
    for piece in group:
        yield piece, value[at : at + piece.size, :]
        at += piece.size


def store_grads(group, value, name):
    for piece, part in by_piece(group, value):
        piece.store(getattr(piece, name), part)


def listed(swap, lists, frame, slab, block, k, v, count=1, **grads):
    pieces = []
    for n in range(count):
        b, exists = swap.block_of_mine(lists, frame, slab, n)
        pieces.append(Piece(k, v, pl.multiple_of(b * block, block), block, exists, **grads))
    return pieces


def arrived(swap, frame, slab, block, kv, **grads):
    _, _, exists = swap.partner(frame)
    return Piece((kv, KEY), (kv, VALUE), slab * block, block, exists, add=False, **grads)


def raised(group, s, base):
    parts = []
    for piece, part in by_piece(group, s):
        low = base if piece.exists is None else jnp.where(piece.exists, base, -NEG)
        parts.append(jnp.exp2(part * EXP_SCALE - low))
    return stack(parts)


def score_groups(q, groups, s_ref, peak):
    at = 0
    for group in groups:
        s = dot_nt(keys_of(group), q)
        s_ref[at : at + s.shape[0], :] = s
        at += s.shape[0]
        for piece, part in by_piece(group, s):
            top = jnp.max(part, axis=0, keepdims=True)
            if piece.exists is not None:
                top = jnp.where(piece.exists, top, NEG)
            peak = top if peak is None else jnp.maximum(peak, top)
    return peak


def group_scores(groups, s_ref):
    at = 0
    for group in groups:
        size = sum(piece.size for piece in group)
        yield group, s_ref[at : at + size, :]
        at += size


def forward_slab(q, groups, with_values, s_ref, old):
    peak = score_groups(q, groups, s_ref, None if old is None else old[0])
    total, acc = 0.0, 0.0
    if old is not None:
        shrink = jnp.exp2((old[0] - peak) * EXP_SCALE)
        total, acc = old[1] * shrink, old[2] * shrink
    for j, (group, s) in enumerate(group_scores(groups, s_ref)):
        e = raised(group, s, peak * EXP_SCALE)
        total = total + jnp.sum(e, axis=0, keepdims=True)
        if j < with_values:
            acc = acc + dot_tn(values_of(group), e.astype(BF16))
    return peak, total, acc


def backward_group(q, g, lse, row_dot, group, p=None):
    k = keys_of(group)
    if p is None:
        p = raised(group, dot_nt(k, q), lse)
    if group[0].dv is not None:
        store_grads(group, dot_nn(p.astype(BF16), g), "dv")
    ds = (p * (dot_nt(values_of(group), g) - row_dot)).astype(BF16)
    if group[0].dk is not None:
        store_grads(group, dot_nn(ds, q) * SCALE, "dk")
    return dot_tn(k, ds)


def join_kernel(own, came, out, turned):
    half = own.shape[0]

    def body(mine):
        for slab, source in ((mine, own), (1 - mine, came)):
            rows = rows_of(slab, half)
            out[rows, :] = source[...]
            turned[:, rows] = source[:, VALUE].T

    each_core(body)


ALL = slice(None)


def store_state(refs, rows, peak, total, acc):
    stat, acc_ref = refs
    stat[0:1, rows] = peak
    stat[1:2, rows] = total
    acc_ref[:, rows] = acc


def load_state(refs, rows):
    stat, acc_ref = refs
    return stat[0:1, rows], stat[1:2, rows], acc_ref[:, rows]


def own_groups(kv, half, **grads):
    return [
        [Piece((kv, KEY), (kv, VALUE), r, half, **grads)] for r in range(0, kv.shape[0], half)
    ]


def near_kernel(block, swap, lists, qg, kv, a_kv, stat, acc, s_ref):
    half = qg.shape[0] // 2
    frame = lax.axis_index("tm")
    for slab in range(2):
        rows = rows_of(slab, half)
        groups = own_groups(kv, half)
        groups.append(
            listed(swap, lists, frame, slab, block, (a_kv, KEY), (a_kv, VALUE), 2)
        )
        store_state((stat, acc), rows, *forward_slab(qg[rows, KEY], groups, 3, s_ref, None))


def middle_kernel(
    block, swaps, lists, qg, stat, acc, y_k, z_k, y_v, z_v, c_k, stat2, acc2, late, s_ref
):
    half = qg.shape[0] // 2
    frame = lax.axis_index("tm")
    z, y, relayed = swaps
    for slab in range(2):
        rows = rows_of(slab, half)
        at = (lists, frame, slab, block)
        group = listed(z, *at, (z_k, ALL), (z_v, ALL)) + listed(y, *at, (y_k, ALL), (y_v, ALL))
        more = listed(relayed, *at, (c_k, ALL), None, 2)
        old = load_state((stat, acc), rows)
        new = forward_slab(qg[rows, KEY], [group, more], 1, s_ref, old)
        store_state((stat2, acc2), rows, *new)
        late[slab] = s_ref[2 * block :, :]


def close_kernel(block, relayed, far, lists_any, qg, stat, acc, late_s, *refs):
    n = len(far)
    far_kv = refs[:n]
    lse_ref, part_ref, dc_v, p_ref, s_ref, grad, lists, sem = refs[n:]
    half = qg.shape[0] // 2
    frame = lax.axis_index("tm")
    copy = pltpu.make_async_copy(lists_any, lists, sem)
    copy.start()
    grad[...] = jnp.zeros_like(grad)
    for slab in range(2):
        rows = rows_of(slab, half)
        q = qg[rows, KEY]
        groups = [[arrived(swap, frame, slab, block, kv)] for swap, kv in zip(far, far_kv)]
        old = load_state((stat, acc), rows)
        peak, total, out = forward_slab(q, groups, n, s_ref, old)
        part_ref[:, rows] = out / total
        lse = peak * EXP_SCALE + jnp.log2(total)
        lse_ref[0:1, rows] = lse
    copy.wait()
    for slab in range(2):
        rows = rows_of(slab, half)
        group = listed(relayed, lists, frame, slab, block, None, None, 2, dv=(grad, ALL))
        p = raised(group, late_s[slab], lse_ref[0:1, rows])
        p_ref[slab] = p
        store_grads(group, dot_nn(p.astype(BF16), qg[rows, VALUE]), "dv")
    dc_v[...] = grad[...].astype(BF16)


def late_kernel(block, relayed, far, *refs):
    n = len(far)
    lists, qg, turned, lse_ref, part_ref, p_ref, c_k, c_v = refs[:8]
    far_kv = refs[8 : 8 + n]
    o_ref, dot_ref, dc_k, dq_ref = refs[8 + n : 12 + n]
    far_grad = refs[12 + n : 12 + 2 * n]
    grad = refs[12 + 2 * n]
    half = qg.shape[0] // 2
    frame = lax.axis_index("tm")
    grad[...] = jnp.zeros_like(grad)
    for slab in range(2):
        rows = rows_of(slab, half)
        q, g, lse = qg[rows, KEY], qg[rows, VALUE], lse_ref[0:1, rows]
        group = listed(
            relayed, lists, frame, slab, block, (c_k, ALL), (c_v, ALL), 2, dk=(grad, ALL)
        )
        p = p_ref[slab]
        o = (part_ref[:, rows] + dot_tn(values_of(group), p.astype(BF16))).astype(BF16)
        o_ref[:, rows] = o
        products = turned[:, rows].astype(F32) * o.astype(F32)
        row_dot = jnp.sum(products, axis=0, keepdims=True)
        dot_ref[0:1, rows] = row_dot
        dq = backward_group(q, g, lse, row_dot, group, p)
        for swap, kv, out in zip(far, far_kv, far_grad):
            group = [arrived(swap, frame, slab, block, kv, dk=(out, KEY), dv=(out, VALUE))]
            dq = dq + backward_group(q, g, lse, row_dot, group)
        dq_ref[:, rows] = dq
    dc_k[...] = grad[...].astype(BF16)


def first_kernel(block, swap, lists, qg, lse_ref, dot_ref, dq_old, a_kv, da, dq_ref, grad):
    half = qg.shape[0] // 2
    frame = lax.axis_index("tm")
    grad[...] = jnp.zeros_like(grad)
    for slab in range(2):
        rows = rows_of(slab, half)
        q, g, lse, row_dot = qg[rows, KEY], qg[rows, VALUE], lse_ref[0:1, rows], dot_ref[0:1, rows]
        group = listed(
            swap, lists, frame, slab, block, (a_kv, KEY), (a_kv, VALUE), 2,
            dk=(grad, KEY), dv=(grad, VALUE),
        )
        dq_ref[:, rows] = dq_old[:, rows] + backward_group(q, g, lse, row_dot, group)
    da[...] = grad[...].astype(BF16)


def second_kernel(
    block, swaps, lists, qg, lse_ref, dot_ref, dq_old, came, y_k, z_k, y_v, z_v, dz, dy, dq_ref
):
    half = qg.shape[0] // 2
    frame = lax.axis_index("tm")
    z, y = swaps
    relays = forwards_first(frame)
    more = came[...].astype(F32)
    for ref, takes in ((dz, relays), (dy, jnp.logical_not(relays))):
        ref[:, KEY] = jnp.zeros_like(more)
        ref[:, VALUE] = jnp.where(takes, more, 0.0)
    for slab in range(2):
        rows = rows_of(slab, half)
        q, g, lse, row_dot = qg[rows, KEY], qg[rows, VALUE], lse_ref[0:1, rows], dot_ref[0:1, rows]
        at = (lists, frame, slab, block)
        group = listed(z, *at, (z_k, ALL), (z_v, ALL), dk=(dz, KEY), dv=(dz, VALUE))
        group += listed(y, *at, (y_k, ALL), (y_v, ALL), dk=(dy, KEY), dv=(dy, VALUE))
        dq_ref[:, rows] = dq_old[:, rows] + backward_group(q, g, lse, row_dot, group)


def own_kernel(qg, lse_ref, dot_ref, dq_old, o, kv, placed, near, keep, send):
    half = qg.shape[0] // 2
    near[...] = placed[...]
    whole = []
    for slab in range(2):
        rows = rows_of(slab, half)
        q, g, lse, row_dot = qg[rows, KEY], qg[rows, VALUE], lse_ref[0:1, rows], dot_ref[0:1, rows]
        dq = dq_old[:, rows]
        for group in own_groups(kv, half, dk=(near, KEY), dv=(near, VALUE)):
            dq = dq + backward_group(q, g, lse, row_dot, group)
        whole.append((dq.T * SCALE).astype(BF16))

    def body(mine):
        for slab in range(2):
            out = keep if slab == mine else send
            out[:, KEY] = o[:, rows_of(slab, half)].T
            out[:, VALUE] = whole[slab]

    each_core(body)


def merge_kernel(dz, dy, came, z_out, y_out):
    first = forwards_first(lax.axis_index("tm"))
    more = came[...].astype(F32)
    z_out[:, KEY] = (dz[:, KEY] + jnp.where(first, more, 0.0)).astype(BF16)
    y_out[:, KEY] = (dy[:, KEY] + jnp.where(first, 0.0, more)).astype(BF16)
    z_out[:, VALUE] = dz[:, VALUE].astype(BF16)
    y_out[:, VALUE] = dy[:, VALUE].astype(BF16)


def place_kernel(block, far, *refs):
    lists, total = refs[0], refs[-1]
    frame = lax.axis_index("tm")
    total[...] = jnp.zeros_like(total)
    for swap, came in zip(far, refs[1:-1]):
        for slab in range(2):
            b, exists = swap.block_of_theirs(lists, frame, slab, 0)
            rows = pl.ds(pl.multiple_of(b * block, block), block)
            part = came[rows_of(slab, block), :].astype(F32)
            total[rows, :] += jnp.where(exists, part, 0.0)


def add_kernel(swaps, near, *refs):
    frame = lax.axis_index("tm")
    total = near[...]
    for swap, came in zip(swaps, refs[:-1]):
        _, _, exists = swap.partner(frame)
        total = total + jnp.where(exists, came[...].astype(F32), 0.0)
    refs[-1][...] = total


def gather_kernel(swap, near, came, keep, send):
    _, _, exists = swap.partner(lax.axis_index("tm"))
    half = near.shape[0] // 2

    def body(mine):
        for slab, out in ((1 - mine, send), (mine, keep)):
            rows = rows_of(slab, half)
            part = jnp.where(exists, came[rows, :].astype(F32), 0.0)
            out[...] = (near[rows, :] + part).astype(BF16)

    each_core(body)


def finish_kernel(keep, came, first, second):
    def body(mine):
        for head, source in ((mine, keep), (1 - mine, came)):
            first[:, head_cols(head)] = source[:, KEY]
            second[:, head_cols(head)] = source[:, VALUE]

    each_core(body)


def per_device(queries, key_rows, value_rows, out_grad, block_lists):
    s_dev, width = queries.shape
    count = lax.axis_size("tm")
    block = s_dev // 2
    pair = sds((s_dev, 2 * DH), BF16)
    single = sds((s_dev, DH), BF16)
    frame_two = sds((2 * s_dev, 2 * DH), BF16)
    frame_one = sds((2 * s_dev, DH), BF16)
    frame_sum = sds((2 * s_dev, 2 * DH), F32)
    stat_row = sds((8, 2 * s_dev), F32)
    turned_sum = sds((DH, 2 * s_dev), F32)
    turned_bf = sds((DH, 2 * s_dev), BF16)
    levels = count.bit_length() - 1
    near_swap, relayed = Swap(count, 0, False), Swap(count, 0, True)
    z_swap, y_swap = Swap(count, 1, False), Swap(count, 1, True)
    far = [Swap(count, level, second) for level in range(2, levels) for second in (False, True)]
    far = [swap for swap in far if swap.moves]
    n = len(far)
    grad_one = pltpu.VMEM((2 * s_dev, DH), F32)

    def across(value):
        return lax.ppermute(value, "space", [(0, 1), (1, 0)])

    def swapped(value, swap):
        return lax.ppermute(value, ("tm", "space"), swap.pairs)

    def scores(pieces):
        return pltpu.VMEM((pieces * block, s_dev), F32)


    k_came, v_came = across(key_rows), across(value_rows)
    sources = (key_rows, value_rows, queries, out_grad, block_lists.T)
    k_own, v_own, qg_own, qg_send, lists = call(
        pack_kernel,
        tuple(pltpu.with_memory_space_constraint(a, pltpu.HBM) for a in sources),
        [single, single, pair, pair, sds(sources[4].shape, jnp.int32)],
        scratch=[pltpu.SemaphoreType.DMA((7,))],
        source=HBM,
        scalars=HBM,
    )
    (keys,) = call(keys_kernel, (k_own, k_came), [frame_one])
    values, kv = call(values_kernel, (keys, v_own, v_came), [frame_one, frame_two])
    qg_send, _ = lax.optimization_barrier((qg_send, keys))
    y_k = swapped(keys, y_swap)
    z_k = swapped(keys, z_swap)
    a_kv = swapped(kv, near_swap)
    y_v = swapped(values, y_swap)
    z_v = swapped(values, z_swap)
    y_k, qg_came = lax.optimization_barrier((y_k, across(qg_send)))
    work = 4 * s_dev * s_dev * DH
    qg, turned = call(join_kernel, (qg_own, qg_came), [frame_two, turned_bf], flops=15 * work)
    kv, _ = lax.optimization_barrier((kv, turned))
    far_send = call(functools.partial(select_kernel, far, block), (lists, kv), [pair] * n)
    y_k, z_k, far_send = lax.optimization_barrier((y_k, z_k, far_send))
    (relay_k,) = call(relay_kernel, (y_k, z_k), [frame_one])
    relay_k, far_send = lax.optimization_barrier((relay_k, far_send))
    a_kv, _ = lax.optimization_barrier((a_kv, relay_k))
    c_k = swapped(relay_k, near_swap)
    far_kv = [swapped(value, swap) for value, swap in zip(far_send, far)]
    stat, acc = call(
        functools.partial(near_kernel, block, near_swap),
        (lists, qg, kv, a_kv),
        [stat_row, turned_sum],
        scratch=[scores(6)],
    )
    score_two = sds((2, s_dev, s_dev), F32)
    y_v, z_v, stat = lax.optimization_barrier((y_v, z_v, stat))
    (relay_v,) = call(relay_kernel, (y_v, z_v), [frame_one])
    relay_v, stat = lax.optimization_barrier((relay_v, stat))
    c_v = swapped(relay_v, near_swap)
    stat, acc, late_scores = call(
        functools.partial(middle_kernel, block, (z_swap, y_swap, relayed)),
        (lists, qg, stat, acc, y_k, z_k, y_v, z_v, c_k),
        [stat_row, turned_sum, score_two],
        scratch=[scores(4)],
    )
    acc, far_kv = lax.optimization_barrier((acc, far_kv))
    lse, part, dc_v, probs = call(
        functools.partial(close_kernel, block, relayed, far),
        (lists, qg, stat, acc, late_scores, *far_kv),
        [stat_row, turned_sum, frame_one, score_two],
        scratch=[
            scores(n),
            grad_one,
            pltpu.SMEM(lists.shape, jnp.int32),
            pltpu.SemaphoreType.DMA(()),
        ],
        scalars=pl.BlockSpec(memory_space=pl.ANY),
    )
    dc_v_came = swapped(dc_v, near_swap)
    o, row_dot, dc_k, dq, *far_grad = call(
        functools.partial(late_kernel, block, relayed, far),
        (lists, qg, turned, lse, part, probs, c_k, c_v, *far_kv),
        [turned_bf, stat_row, frame_one, turned_sum] + [pair] * n,
        scratch=[grad_one],
    )
    far_came = [swapped(value, swap) for value, swap in zip(far_grad, far)]
    dc_k_came = swapped(dc_k, near_swap)
    da, dq = call(
        functools.partial(first_kernel, block, near_swap),
        (lists, qg, lse, row_dot, dq, a_kv),
        [frame_two, turned_sum],
        scratch=[pltpu.VMEM((2 * s_dev, 2 * DH), F32)],
    )
    da_came = swapped(da, near_swap)
    dz, dy, dq = call(
        functools.partial(second_kernel, block, (z_swap, y_swap)),
        (lists, qg, lse, row_dot, dq, dc_v_came, y_k, z_k, y_v, z_v),
        [frame_sum, frame_sum, turned_sum],
        flops=20 * work,
    )
    dz, dy = call(merge_kernel, (dz, dy, dc_k_came), [frame_two, frame_two])
    dy_came = swapped(dy, y_swap)
    dz_came = swapped(dz, z_swap)
    dq, dz, dy = lax.optimization_barrier((dq, dz, dy))
    far_came, dq = lax.optimization_barrier((far_came, dq))
    (placed,) = call(functools.partial(place_kernel, block, far), (lists, *far_came), [frame_sum])
    near, q_keep, q_send = call(
        own_kernel,
        (qg, lse, row_dot, dq, o, kv, placed),
        [frame_sum, pair, pair],
        flops=20 * work,
    )
    outputs = [sds((s_dev, width), BF16)] * 2
    attn_out, grad_q = call(finish_kernel, (q_keep, across(q_send)), outputs)
    near, attn_out, grad_q = lax.optimization_barrier((near, attn_out, grad_q))
    (near,) = call(
        functools.partial(add_kernel, (near_swap, y_swap)),
        (near, da_came, dy_came),
        [frame_sum],
        flops=20 * work,
    )
    k_keep, k_send = call(
        functools.partial(gather_kernel, z_swap), (near, dz_came), [pair, pair]
    )
    grad_k, grad_v = call(finish_kernel, (k_keep, across(k_send)), outputs)
    return attn_out, grad_q, grad_k, grad_v


def solution(mesh):
    rows = P(("groups", "tm", "space"), None)
    return jax.shard_map(
        per_device,
        mesh=mesh,
        in_specs=(rows, rows, rows, rows, P("groups", None)),
        out_specs=(rows, rows, rows, rows),
        check_vma=False,
    )
```

```python
import functools
import math

import jax
import jax.numpy as jnp
from jax import lax
from jax.experimental import pallas as pl
from jax.experimental.pallas import tpu as pltpu
from jax.sharding import PartitionSpec as P

DH = 128
F32 = jnp.float32
BF16 = jnp.bfloat16
VMEM = pl.BlockSpec(memory_space=pltpu.VMEM)
SMEM = pl.BlockSpec(memory_space=pltpu.SMEM)
HBM = pl.BlockSpec(memory_space=pltpu.HBM)
NEG = -1e30
SCALE = 1.0 / math.sqrt(DH)
EXP_SCALE = SCALE * math.log2(math.e)
KEY = slice(0, DH)
VALUE = slice(DH, 2 * DH)
sds = jax.ShapeDtypeStruct


def dot_nn(a, b):
    return lax.dot_general(a, b, (((1,), (0,)), ((), ())), preferred_element_type=F32)


def dot_nt(a, b):
    return lax.dot_general(a, b, (((1,), (1,)), ((), ())), preferred_element_type=F32)


def dot_tn(a, b):
    return lax.dot_general(a, b, (((0,), (0,)), ((), ())), preferred_element_type=F32)


def call(kernel, args, out_shape, scratch=(), source=VMEM, scalars=SMEM, flops=1024):
    return pl.pallas_call(
        kernel,
        out_shape=out_shape,
        in_specs=[scalars if a.dtype == jnp.int32 else source for a in args],
        out_specs=tuple(VMEM for _ in out_shape),
        scratch_shapes=list(scratch),
        compiler_params=pltpu.CompilerParams(vmem_limit_bytes=40 << 20),
        cost_estimate=pl.CostEstimate(flops=flops, bytes_accessed=1024, transcendentals=0),
    )(*args)


def swap_pairs(count, distance, second):
    pairs = []
    for frame in range(count):
        up = ((frame // distance) % 2 == 0) != second
        target = frame + distance if up else frame - distance
        for core in range(2):
            if 0 <= target < count:
                pairs.append((frame * 2 + core, target * 2 + core))
            else:
                pairs.append((frame * 2 + core, frame * 2 + 1 - core))
    return pairs


class Swap:
    def __init__(self, count, level, second):
        self.count, self.level, self.second = count, level, second
        self.levels = count.bit_length() - 1
        self.pairs = swap_pairs(count, 1 << level, second)
        self.moves = any(source // 2 != target // 2 for source, target in self.pairs)

    def partner(self, frame):
        odd = lax.rem(lax.shift_right_logical(frame, self.level), 2)
        later = odd == (1 if self.second else 0)
        other = jnp.where(later, frame + (1 << self.level), frame - (1 << self.level))
        return other, later, jnp.logical_and(other >= 0, other < self.count)

    def slot(self, later, k):
        base = 0 if self.level == 0 else self.level + 1
        return jnp.where(later, self.levels + 1, 0) + base + k

    def block_of_mine(self, lists, frame, slab, k):
        other, later, exists = self.partner(frame)
        entry = lists[self.slot(later, k), frame * 2 + slab]
        return jnp.clip(entry - other * 4, 0, 3), exists

    def block_of_theirs(self, lists, frame, slab, k):
        other, later, exists = self.partner(frame)
        row = jnp.where(exists, other, frame) * 2 + slab
        entry = lists[self.slot(jnp.logical_not(later), k), row]
        return jnp.clip(entry - frame * 4, 0, 3), exists


def head_cols(head):
    return slice(head * DH, (head + 1) * DH)


def rows_of(slab, half):
    return slice(slab * half, (slab + 1) * half)


def each_core(body):
    core = lax.axis_index("space")
    for mine in range(2):
        pl.when(core == mine)(functools.partial(body, mine))


def pack_kernel(k, v, q, g, lists, k_own, v_own, qg_own, qg_send, lists_out, sems):
    def body(mine):
        moves = [(lists, lists_out)]
        for source, out in ((k, k_own), (v, v_own)):
            moves.append((source.at[:, head_cols(mine)], out))
        for head, out in ((mine, qg_own), (1 - mine, qg_send)):
            for source, cols in ((q, KEY), (g, VALUE)):
                moves.append((source.at[:, head_cols(head)], out.at[:, cols]))
        copies = [
            pltpu.make_async_copy(source, out, sems.at[n]) for n, (source, out) in enumerate(moves)
        ]
        for copy in copies:
            copy.start()
        for copy in copies:
            copy.wait()

    each_core(body)


def keys_kernel(own, came, keys):
    half = own.shape[0]

    def body(mine):
        keys[rows_of(mine, half), :] = own[...]
        keys[rows_of(1 - mine, half), :] = came[:, head_cols(mine)]

    each_core(body)


def values_kernel(keys, own, came, values, kv):
    half = own.shape[0]

    def body(mine):
        for slab, part in ((mine, own[...]), (1 - mine, came[:, head_cols(mine)])):
            rows = rows_of(slab, half)
            values[rows, :] = part
            kv[rows, VALUE] = part
            kv[rows, KEY] = keys[rows, :]

    each_core(body)


def select_kernel(far, block, lists, kv, *sends):
    frame = lax.axis_index("tm")
    for swap, send in zip(far, sends):
        for slab in range(2):
            b, _ = swap.block_of_theirs(lists, frame, slab, 0)
            row = pl.multiple_of(b * block, block)
            send[slab * block : (slab + 1) * block, :] = kv[pl.ds(row, block), :]


def forwards_first(frame):
    return lax.rem(frame, 2) == lax.rem(lax.shift_right_logical(frame, 1), 2)


def relay_kernel(y, z, out):
    first = forwards_first(lax.axis_index("tm"))

    @pl.when(first)
    def _():
        out[...] = z[...]

    @pl.when(jnp.logical_not(first))
    def _():
        out[...] = y[...]


class Piece:
    def __init__(self, k, v, row, size, exists=None, dk=None, dv=None, add=True):
        self.k_at, self.v_at, self.exists = k, v, exists
        self.rows, self.size = pl.ds(row, size), size
        self.dk, self.dv, self.add = dk, dv, add

    def store(self, at, value):
        ref, cols = at
        if self.add:
            ref[self.rows, cols] += value
        else:
            ref[self.rows, cols] = value.astype(ref.dtype)


def stack(parts):
    return parts[0] if len(parts) == 1 else jnp.concatenate(parts, axis=0)


def keys_of(group):
    return stack([p.k_at[0][p.rows, p.k_at[1]] for p in group])


def values_of(group):
    return stack([p.v_at[0][p.rows, p.v_at[1]] for p in group])


def by_piece(group, value):
    at = 0
    for piece in group:
        yield piece, value[at : at + piece.size, :]
        at += piece.size


def store_grads(group, value, name):
    for piece, part in by_piece(group, value):
        piece.store(getattr(piece, name), part)


def listed(swap, lists, frame, slab, block, k, v, count=1, **grads):
    pieces = []
    for n in range(count):
        b, exists = swap.block_of_mine(lists, frame, slab, n)
        pieces.append(Piece(k, v, pl.multiple_of(b * block, block), block, exists, **grads))
    return pieces


def arrived(swap, frame, slab, block, kv, **grads):
    _, _, exists = swap.partner(frame)
    return Piece((kv, KEY), (kv, VALUE), slab * block, block, exists, add=False, **grads)


def raised(group, s, base):
    parts = []
    for piece, part in by_piece(group, s):
        low = base if piece.exists is None else jnp.where(piece.exists, base, -NEG)
        parts.append(jnp.exp2(part * EXP_SCALE - low))
    return stack(parts)


def score_groups(q, groups, s_ref, peak):
    at = 0
    for group in groups:
        s = dot_nt(keys_of(group), q)
        s_ref[at : at + s.shape[0], :] = s
        at += s.shape[0]
        for piece, part in by_piece(group, s):
            top = jnp.max(part, axis=0, keepdims=True)
            if piece.exists is not None:
                top = jnp.where(piece.exists, top, NEG)
            peak = top if peak is None else jnp.maximum(peak, top)
    return peak


def group_scores(groups, s_ref):
    at = 0
    for group in groups:
        size = sum(piece.size for piece in group)
        yield group, s_ref[at : at + size, :]
        at += size


def forward_slab(q, groups, with_values, s_ref, old):
    peak = score_groups(q, groups, s_ref, None if old is None else old[0])
    total, acc = 0.0, 0.0
    if old is not None:
        shrink = jnp.exp2((old[0] - peak) * EXP_SCALE)
        total, acc = old[1] * shrink, old[2] * shrink
    for j, (group, s) in enumerate(group_scores(groups, s_ref)):
        e = raised(group, s, peak * EXP_SCALE)
        total = total + jnp.sum(e, axis=0, keepdims=True)
        if j < with_values:
            acc = acc + dot_tn(values_of(group), e.astype(BF16))
    return peak, total, acc


def backward_group(q, g, lse, row_dot, group, p=None):
    k = keys_of(group)
    if p is None:
        p = raised(group, dot_nt(k, q), lse)
    if group[0].dv is not None:
        store_grads(group, dot_nn(p.astype(BF16), g), "dv")
    ds = (p * (dot_nt(values_of(group), g) - row_dot)).astype(BF16)
    if group[0].dk is not None:
        store_grads(group, dot_nn(ds, q) * SCALE, "dk")
    return dot_tn(k, ds)


def join_kernel(own, came, out, turned):
    half = own.shape[0]

    def body(mine):
        for slab, source in ((mine, own), (1 - mine, came)):
            rows = rows_of(slab, half)
            out[rows, :] = source[...]
            turned[:, rows] = source[:, VALUE].T

    each_core(body)


ALL = slice(None)


def store_state(refs, rows, peak, total, acc):
    stat, acc_ref = refs
    stat[0:1, rows] = peak
    stat[1:2, rows] = total
    acc_ref[:, rows] = acc


def load_state(refs, rows):
    stat, acc_ref = refs
    return stat[0:1, rows], stat[1:2, rows], acc_ref[:, rows]


def own_groups(kv, half, **grads):
    return [
        [Piece((kv, KEY), (kv, VALUE), r, half, **grads)] for r in range(0, kv.shape[0], half)
    ]


def near_kernel(block, swap, lists, qg, kv, a_kv, stat, acc, s_ref):
    half = qg.shape[0] // 2
    frame = lax.axis_index("tm")
    for slab in range(2):
        rows = rows_of(slab, half)
        groups = own_groups(kv, half)
        groups.append(
            listed(swap, lists, frame, slab, block, (a_kv, KEY), (a_kv, VALUE), 2)
        )
        store_state((stat, acc), rows, *forward_slab(qg[rows, KEY], groups, 3, s_ref, None))


def middle_kernel(
    block, swaps, lists, qg, stat, acc, y_k, z_k, y_v, z_v, c_k, stat2, acc2, late, s_ref
):
    half = qg.shape[0] // 2
    frame = lax.axis_index("tm")
    z, y, relayed = swaps
    for slab in range(2):
        rows = rows_of(slab, half)
        at = (lists, frame, slab, block)
        group = listed(z, *at, (z_k, ALL), (z_v, ALL)) + listed(y, *at, (y_k, ALL), (y_v, ALL))
        more = listed(relayed, *at, (c_k, ALL), None, 2)
        old = load_state((stat, acc), rows)
        new = forward_slab(qg[rows, KEY], [group, more], 1, s_ref, old)
        store_state((stat2, acc2), rows, *new)
        late[slab] = s_ref[2 * block :, :]


def close_kernel(block, relayed, far, lists_any, qg, stat, acc, late_s, *refs):
    n = len(far)
    far_kv = refs[:n]
    lse_ref, part_ref, dc_v, p_ref, s_ref, grad, lists, sem = refs[n:]
    half = qg.shape[0] // 2
    frame = lax.axis_index("tm")
    copy = pltpu.make_async_copy(lists_any, lists, sem)
    copy.start()
    grad[...] = jnp.zeros_like(grad)
    for slab in range(2):
        rows = rows_of(slab, half)
        q = qg[rows, KEY]
        groups = [[arrived(swap, frame, slab, block, kv)] for swap, kv in zip(far, far_kv)]
        old = load_state((stat, acc), rows)
        peak, total, out = forward_slab(q, groups, n, s_ref, old)
        part_ref[:, rows] = out / total
        lse = peak * EXP_SCALE + jnp.log2(total)
        lse_ref[0:1, rows] = lse
    copy.wait()
    for slab in range(2):
        rows = rows_of(slab, half)
        group = listed(relayed, lists, frame, slab, block, None, None, 2, dv=(grad, ALL))
        p = raised(group, late_s[slab], lse_ref[0:1, rows])
        p_ref[slab] = p
        store_grads(group, dot_nn(p.astype(BF16), qg[rows, VALUE]), "dv")
    dc_v[...] = grad[...].astype(BF16)


def late_kernel(block, relayed, far, *refs):
    n = len(far)
    lists, qg, turned, lse_ref, part_ref, p_ref, c_k, c_v = refs[:8]
    far_kv = refs[8 : 8 + n]
    o_ref, dot_ref, dc_k, dq_ref = refs[8 + n : 12 + n]
    far_grad = refs[12 + n : 12 + 2 * n]
    grad = refs[12 + 2 * n]
    half = qg.shape[0] // 2
    frame = lax.axis_index("tm")
    grad[...] = jnp.zeros_like(grad)
    for slab in range(2):
        rows = rows_of(slab, half)
        q, g, lse = qg[rows, KEY], qg[rows, VALUE], lse_ref[0:1, rows]
        group = listed(
            relayed, lists, frame, slab, block, (c_k, ALL), (c_v, ALL), 2, dk=(grad, ALL)
        )
        p = p_ref[slab]
        o = (part_ref[:, rows] + dot_tn(values_of(group), p.astype(BF16))).astype(BF16)
        o_ref[:, rows] = o
        products = turned[:, rows].astype(F32) * o.astype(F32)
        row_dot = jnp.sum(products, axis=0, keepdims=True)
        dot_ref[0:1, rows] = row_dot
        dq = backward_group(q, g, lse, row_dot, group, p)
        for swap, kv, out in zip(far, far_kv, far_grad):
            group = [arrived(swap, frame, slab, block, kv, dk=(out, KEY), dv=(out, VALUE))]
            dq = dq + backward_group(q, g, lse, row_dot, group)
        dq_ref[:, rows] = dq
    dc_k[...] = grad[...].astype(BF16)


def first_kernel(block, swap, lists, qg, lse_ref, dot_ref, dq_old, a_kv, da, dq_ref, grad):
    half = qg.shape[0] // 2
    frame = lax.axis_index("tm")
    grad[...] = jnp.zeros_like(grad)
    for slab in range(2):
        rows = rows_of(slab, half)
        q, g, lse, row_dot = qg[rows, KEY], qg[rows, VALUE], lse_ref[0:1, rows], dot_ref[0:1, rows]
        group = listed(
            swap, lists, frame, slab, block, (a_kv, KEY), (a_kv, VALUE), 2,
            dk=(grad, KEY), dv=(grad, VALUE),
        )
        dq_ref[:, rows] = dq_old[:, rows] + backward_group(q, g, lse, row_dot, group)
    da[...] = grad[...].astype(BF16)


def second_kernel(
    block, swaps, lists, qg, lse_ref, dot_ref, dq_old, came, y_k, z_k, y_v, z_v,
    dz_k, dy_k, dz_v, dy_v, dq_ref, z_sum, y_sum,
):
    half = qg.shape[0] // 2
    frame = lax.axis_index("tm")
    z, y = swaps
    relays = forwards_first(frame)
    more = came[...].astype(F32)
    for k, v, takes in ((dz_k, z_sum, relays), (dy_k, y_sum, jnp.logical_not(relays))):
        k[...] = jnp.zeros_like(more)
        v[...] = jnp.where(takes, more, 0.0)
    for slab in range(2):
        rows = rows_of(slab, half)
        q, g, lse, row_dot = qg[rows, KEY], qg[rows, VALUE], lse_ref[0:1, rows], dot_ref[0:1, rows]
        at = (lists, frame, slab, block)
        group = listed(z, *at, (z_k, ALL), (z_v, ALL), dk=(dz_k, ALL), dv=(z_sum, ALL))
        group += listed(y, *at, (y_k, ALL), (y_v, ALL), dk=(dy_k, ALL), dv=(y_sum, ALL))
        dq_ref[:, rows] = dq_old[:, rows] + backward_group(q, g, lse, row_dot, group)
    dz_v[...] = z_sum[...].astype(BF16)
    dy_v[...] = y_sum[...].astype(BF16)


def own_kernel(qg, lse_ref, dot_ref, dq_old, o, kv, placed, near, keep, send):
    half = qg.shape[0] // 2
    near[...] = placed[...]
    whole = []
    for slab in range(2):
        rows = rows_of(slab, half)
        q, g, lse, row_dot = qg[rows, KEY], qg[rows, VALUE], lse_ref[0:1, rows], dot_ref[0:1, rows]
        dq = dq_old[:, rows]
        for group in own_groups(kv, half, dk=(near, KEY), dv=(near, VALUE)):
            dq = dq + backward_group(q, g, lse, row_dot, group)
        whole.append((dq.T * SCALE).astype(BF16))

    def body(mine):
        for slab in range(2):
            out = keep if slab == mine else send
            out[:, KEY] = o[:, rows_of(slab, half)].T
            out[:, VALUE] = whole[slab]

    each_core(body)


def merge_kernel(dz, dy, came, z_out, y_out):
    first = forwards_first(lax.axis_index("tm"))
    more = came[...].astype(F32)
    z_out[...] = (dz[...] + jnp.where(first, more, 0.0)).astype(BF16)
    y_out[...] = (dy[...] + jnp.where(first, 0.0, more)).astype(BF16)


def place_kernel(block, swaps, far, *refs):
    lists, z_came, y_came, total = refs[0], refs[1], refs[2], refs[-1]
    frame = lax.axis_index("tm")
    values = 0.0
    for swap, came in zip(swaps, (z_came, y_came)):
        values = values + jnp.where(swap.partner(frame)[2], came[...].astype(F32), 0.0)
    total[:, KEY] = jnp.zeros_like(values)
    total[:, VALUE] = values
    for swap, came in zip(far, refs[3:-1]):
        for slab in range(2):
            b, exists = swap.block_of_theirs(lists, frame, slab, 0)
            rows = pl.ds(pl.multiple_of(b * block, block), block)
            part = came[rows_of(slab, block), :].astype(F32)
            total[rows, :] += jnp.where(exists, part, 0.0)


def add_kernel(swaps, near, da, dy, total):
    frame = lax.axis_index("tm")
    by_a, by_y = (swap.partner(frame)[2] for swap in swaps)
    total[:, VALUE] = near[:, VALUE] + jnp.where(by_a, da[:, VALUE].astype(F32), 0.0)
    keys = near[:, KEY] + jnp.where(by_a, da[:, KEY].astype(F32), 0.0)
    total[:, KEY] = keys + jnp.where(by_y, dy[...].astype(F32), 0.0)


def gather_kernel(swap, near, came, keep, send):
    _, _, exists = swap.partner(lax.axis_index("tm"))
    half = near.shape[0] // 2

    def body(mine):
        for slab, out in ((1 - mine, send), (mine, keep)):
            rows = rows_of(slab, half)
            part = jnp.where(exists, came[rows, :].astype(F32), 0.0)
            out[:, KEY] = (near[rows, KEY] + part).astype(BF16)
            out[:, VALUE] = near[rows, VALUE].astype(BF16)

    each_core(body)


def finish_kernel(keep, came, first, second):
    def body(mine):
        for head, source in ((mine, keep), (1 - mine, came)):
            first[:, head_cols(head)] = source[:, KEY]
            second[:, head_cols(head)] = source[:, VALUE]

    each_core(body)


def per_device(queries, key_rows, value_rows, out_grad, block_lists):
    s_dev, width = queries.shape
    count = lax.axis_size("tm")
    block = s_dev // 2
    pair = sds((s_dev, 2 * DH), BF16)
    single = sds((s_dev, DH), BF16)
    frame_two = sds((2 * s_dev, 2 * DH), BF16)
    frame_one = sds((2 * s_dev, DH), BF16)
    frame_sum = sds((2 * s_dev, 2 * DH), F32)
    stat_row = sds((8, 2 * s_dev), F32)
    turned_sum = sds((DH, 2 * s_dev), F32)
    turned_bf = sds((DH, 2 * s_dev), BF16)
    levels = count.bit_length() - 1
    near_swap, relayed = Swap(count, 0, False), Swap(count, 0, True)
    z_swap, y_swap = Swap(count, 1, False), Swap(count, 1, True)
    far = [Swap(count, level, second) for level in range(2, levels) for second in (False, True)]
    far = [swap for swap in far if swap.moves]
    n = len(far)
    grad_one = pltpu.VMEM((2 * s_dev, DH), F32)

    def across(value):
        return lax.ppermute(value, "space", [(0, 1), (1, 0)])

    def swapped(value, swap):
        return lax.ppermute(value, ("tm", "space"), swap.pairs)

    def scores(pieces):
        return pltpu.VMEM((pieces * block, s_dev), F32)


    k_came, v_came = across(key_rows), across(value_rows)
    sources = (key_rows, value_rows, queries, out_grad, block_lists.T)
    k_own, v_own, qg_own, qg_send, lists = call(
        pack_kernel,
        tuple(pltpu.with_memory_space_constraint(a, pltpu.HBM) for a in sources),
        [single, single, pair, pair, sds(sources[4].shape, jnp.int32)],
        scratch=[pltpu.SemaphoreType.DMA((7,))],
        source=HBM,
        scalars=HBM,
    )
    (keys,) = call(keys_kernel, (k_own, k_came), [frame_one])
    values, kv = call(values_kernel, (keys, v_own, v_came), [frame_one, frame_two])
    qg_send, _ = lax.optimization_barrier((qg_send, keys))
    y_k = swapped(keys, y_swap)
    z_k = swapped(keys, z_swap)
    a_kv = swapped(kv, near_swap)
    y_v = swapped(values, y_swap)
    z_v = swapped(values, z_swap)
    y_k, qg_came = lax.optimization_barrier((y_k, across(qg_send)))
    work = 4 * s_dev * s_dev * DH
    qg, turned = call(join_kernel, (qg_own, qg_came), [frame_two, turned_bf], flops=15 * work)
    kv, _ = lax.optimization_barrier((kv, turned))
    far_send = call(functools.partial(select_kernel, far, block), (lists, kv), [pair] * n)
    y_k, z_k, far_send = lax.optimization_barrier((y_k, z_k, far_send))
    (relay_k,) = call(relay_kernel, (y_k, z_k), [frame_one])
    relay_k, far_send = lax.optimization_barrier((relay_k, far_send))
    a_kv, _ = lax.optimization_barrier((a_kv, relay_k))
    c_k = swapped(relay_k, near_swap)
    far_kv = [swapped(value, swap) for value, swap in zip(far_send, far)]
    stat, acc = call(
        functools.partial(near_kernel, block, near_swap),
        (lists, qg, kv, a_kv),
        [stat_row, turned_sum],
        scratch=[scores(6)],
    )
    score_two = sds((2, s_dev, s_dev), F32)
    y_v, z_v, stat = lax.optimization_barrier((y_v, z_v, stat))
    (relay_v,) = call(relay_kernel, (y_v, z_v), [frame_one])
    relay_v, stat = lax.optimization_barrier((relay_v, stat))
    c_v = swapped(relay_v, near_swap)
    stat, acc, late_scores = call(
        functools.partial(middle_kernel, block, (z_swap, y_swap, relayed)),
        (lists, qg, stat, acc, y_k, z_k, y_v, z_v, c_k),
        [stat_row, turned_sum, score_two],
        scratch=[scores(4)],
    )
    acc, far_kv = lax.optimization_barrier((acc, far_kv))
    lse, part, dc_v, probs = call(
        functools.partial(close_kernel, block, relayed, far),
        (lists, qg, stat, acc, late_scores, *far_kv),
        [stat_row, turned_sum, frame_one, score_two],
        scratch=[
            scores(n),
            grad_one,
            pltpu.SMEM(lists.shape, jnp.int32),
            pltpu.SemaphoreType.DMA(()),
        ],
        scalars=pl.BlockSpec(memory_space=pl.ANY),
    )
    dc_v_came = swapped(dc_v, near_swap)
    o, row_dot, dc_k, dq, *far_grad = call(
        functools.partial(late_kernel, block, relayed, far),
        (lists, qg, turned, lse, part, probs, c_k, c_v, *far_kv),
        [turned_bf, stat_row, frame_one, turned_sum] + [pair] * n,
        scratch=[grad_one],
    )
    far_came = [swapped(value, swap) for value, swap in zip(far_grad, far)]
    dc_k_came = swapped(dc_k, near_swap)
    key_sum = sds((2 * s_dev, DH), F32)
    dz_k, dy_k, dz_v, dy_v, dq = call(
        functools.partial(second_kernel, block, (z_swap, y_swap)),
        (lists, qg, lse, row_dot, dq, dc_v_came, y_k, z_k, y_v, z_v),
        [key_sum, key_sum, frame_one, frame_one, turned_sum],
        scratch=[grad_one, grad_one],
        flops=20 * work,
    )
    dy_v_came = swapped(dy_v, y_swap)
    dz_v_came = swapped(dz_v, z_swap)
    da, dq = call(
        functools.partial(first_kernel, block, near_swap),
        (lists, qg, lse, row_dot, dq, a_kv),
        [frame_two, turned_sum],
        scratch=[pltpu.VMEM((2 * s_dev, 2 * DH), F32)],
    )
    da_came = swapped(da, near_swap)
    dz_k, dy_k = call(merge_kernel, (dz_k, dy_k, dc_k_came), [frame_one, frame_one])
    dy_k_came = swapped(dy_k, y_swap)
    dz_k_came = swapped(dz_k, z_swap)
    dq, dz_k, dy_k = lax.optimization_barrier((dq, dz_k, dy_k))
    far_came, dq = lax.optimization_barrier((far_came, dq))
    (placed,) = call(
        functools.partial(place_kernel, block, (z_swap, y_swap), far),
        (lists, dz_v_came, dy_v_came, *far_came),
        [frame_sum],
    )
    near, q_keep, q_send = call(
        own_kernel,
        (qg, lse, row_dot, dq, o, kv, placed),
        [frame_sum, pair, pair],
        flops=28 * work,
    )
    outputs = [sds((s_dev, width), BF16)] * 2
    attn_out, grad_q = call(finish_kernel, (q_keep, across(q_send)), outputs)
    (near,) = call(
        functools.partial(add_kernel, (near_swap, y_swap)),
        (near, da_came, dy_k_came),
        [frame_sum],
        flops=5 * work,
    )
    k_keep, k_send = call(
        functools.partial(gather_kernel, z_swap), (near, dz_k_came), [pair, pair]
    )
    grad_k, grad_v = call(finish_kernel, (k_keep, across(k_send)), outputs)
    return attn_out, grad_q, grad_k, grad_v


def solution(mesh):
    rows = P(("groups", "tm", "space"), None)
    return jax.shard_map(
        per_device,
        mesh=mesh,
        in_specs=(rows, rows, rows, rows, P("groups", None)),
        out_specs=(rows, rows, rows, rows),
        check_vma=False,
    )
```

```python
import functools
import math

import jax
import jax.numpy as jnp
from jax import lax
from jax.experimental import pallas as pl
from jax.experimental.pallas import tpu as pltpu
from jax.sharding import PartitionSpec as P

DH = 128
F32 = jnp.float32
BF16 = jnp.bfloat16
VMEM = pl.BlockSpec(memory_space=pltpu.VMEM)
SMEM = pl.BlockSpec(memory_space=pltpu.SMEM)
HBM = pl.BlockSpec(memory_space=pltpu.HBM)
NEG = -1e30
SCALE = 1.0 / math.sqrt(DH)
EXP_SCALE = SCALE * math.log2(math.e)
KEY = slice(0, DH)
VALUE = slice(DH, 2 * DH)
sds = jax.ShapeDtypeStruct


def dot_nn(a, b):
    return lax.dot_general(a, b, (((1,), (0,)), ((), ())), preferred_element_type=F32)


def dot_nt(a, b):
    return lax.dot_general(a, b, (((1,), (1,)), ((), ())), preferred_element_type=F32)


def dot_tn(a, b):
    return lax.dot_general(a, b, (((0,), (0,)), ((), ())), preferred_element_type=F32)


def call(kernel, args, out_shape, scratch=(), source=VMEM, scalars=SMEM, flops=1024):
    return pl.pallas_call(
        kernel,
        out_shape=out_shape,
        in_specs=[scalars if a.dtype == jnp.int32 else source for a in args],
        out_specs=tuple(VMEM for _ in out_shape),
        scratch_shapes=list(scratch),
        compiler_params=pltpu.CompilerParams(vmem_limit_bytes=40 << 20),
        cost_estimate=pl.CostEstimate(flops=flops, bytes_accessed=1024, transcendentals=0),
    )(*args)


def swap_pairs(count, distance, second):
    pairs = []
    for frame in range(count):
        up = ((frame // distance) % 2 == 0) != second
        target = frame + distance if up else frame - distance
        for core in range(2):
            if 0 <= target < count:
                pairs.append((frame * 2 + core, target * 2 + core))
            else:
                pairs.append((frame * 2 + core, frame * 2 + 1 - core))
    return pairs


class Swap:
    def __init__(self, count, level, second):
        self.count, self.level, self.second = count, level, second
        self.levels = count.bit_length() - 1
        self.pairs = swap_pairs(count, 1 << level, second)
        self.moves = any(source // 2 != target // 2 for source, target in self.pairs)

    def partner(self, frame):
        odd = lax.rem(lax.shift_right_logical(frame, self.level), 2)
        later = odd == (1 if self.second else 0)
        other = jnp.where(later, frame + (1 << self.level), frame - (1 << self.level))
        return other, later, jnp.logical_and(other >= 0, other < self.count)

    def slot(self, later, k):
        base = 0 if self.level == 0 else self.level + 1
        return jnp.where(later, self.levels + 1, 0) + base + k

    def block_of_mine(self, lists, frame, slab, k):
        other, later, exists = self.partner(frame)
        entry = lists[self.slot(later, k), frame * 2 + slab]
        return jnp.clip(entry - other * 4, 0, 3), exists

    def block_of_theirs(self, lists, frame, slab, k):
        other, later, exists = self.partner(frame)
        row = jnp.where(exists, other, frame) * 2 + slab
        entry = lists[self.slot(jnp.logical_not(later), k), row]
        return jnp.clip(entry - frame * 4, 0, 3), exists


def head_cols(head):
    return slice(head * DH, (head + 1) * DH)


def rows_of(slab, half):
    return slice(slab * half, (slab + 1) * half)


def each_core(body):
    core = lax.axis_index("space")
    for mine in range(2):
        pl.when(core == mine)(functools.partial(body, mine))


def pack_kernel(k, v, q, g, lists, k_own, v_own, qg_own, qg_send, lists_out, sems):
    def body(mine):
        moves = [(lists, lists_out)]
        for source, out in ((k, k_own), (v, v_own)):
            moves.append((source.at[:, head_cols(mine)], out))
        for head, out in ((mine, qg_own), (1 - mine, qg_send)):
            for source, cols in ((q, KEY), (g, VALUE)):
                moves.append((source.at[:, head_cols(head)], out.at[:, cols]))
        copies = [
            pltpu.make_async_copy(source, out, sems.at[n]) for n, (source, out) in enumerate(moves)
        ]
        for copy in copies:
            copy.start()
        for copy in copies:
            copy.wait()

    each_core(body)


def keys_kernel(own, came, keys):
    half = own.shape[0]

    def body(mine):
        keys[rows_of(mine, half), :] = own[...]
        keys[rows_of(1 - mine, half), :] = came[:, head_cols(mine)]

    each_core(body)


def values_kernel(keys, own, came, values, kv):
    half = own.shape[0]

    def body(mine):
        for slab, part in ((mine, own[...]), (1 - mine, came[:, head_cols(mine)])):
            rows = rows_of(slab, half)
            values[rows, :] = part
            kv[rows, VALUE] = part
            kv[rows, KEY] = keys[rows, :]

    each_core(body)


def select_kernel(far, block, lists, kv, *sends):
    frame = lax.axis_index("tm")
    for swap, send in zip(far, sends):
        for slab in range(2):
            b, _ = swap.block_of_theirs(lists, frame, slab, 0)
            row = pl.multiple_of(b * block, block)
            send[slab * block : (slab + 1) * block, :] = kv[pl.ds(row, block), :]


def forwards_first(frame):
    return lax.rem(frame, 2) == lax.rem(lax.shift_right_logical(frame, 1), 2)


def relay_kernel(y, z, out):
    first = forwards_first(lax.axis_index("tm"))

    @pl.when(first)
    def _():
        out[...] = z[...]

    @pl.when(jnp.logical_not(first))
    def _():
        out[...] = y[...]


class Piece:
    def __init__(self, k, v, row, size, exists=None, dk=None, dv=None, add=True):
        self.k_at, self.v_at, self.exists = k, v, exists
        self.rows, self.size = pl.ds(row, size), size
        self.dk, self.dv, self.add = dk, dv, add

    def store(self, at, value):
        ref, cols = at
        if self.add:
            ref[self.rows, cols] += value
        else:
            ref[self.rows, cols] = value.astype(ref.dtype)


def stack(parts):
    return parts[0] if len(parts) == 1 else jnp.concatenate(parts, axis=0)


def keys_of(group):
    return stack([p.k_at[0][p.rows, p.k_at[1]] for p in group])


def values_of(group):
    return stack([p.v_at[0][p.rows, p.v_at[1]] for p in group])


def by_piece(group, value):
    at = 0
    for piece in group:
        yield piece, value[at : at + piece.size, :]
        at += piece.size


def store_grads(group, value, name):
    for piece, part in by_piece(group, value):
        piece.store(getattr(piece, name), part)


def listed(swap, lists, frame, slab, block, k, v, count=1, **grads):
    pieces = []
    for n in range(count):
        b, exists = swap.block_of_mine(lists, frame, slab, n)
        pieces.append(Piece(k, v, pl.multiple_of(b * block, block), block, exists, **grads))
    return pieces


def arrived(swap, frame, slab, block, kv, **grads):
    _, _, exists = swap.partner(frame)
    return Piece((kv, KEY), (kv, VALUE), slab * block, block, exists, add=False, **grads)


def raised(group, s, base):
    parts = []
    for piece, part in by_piece(group, s):
        low = base if piece.exists is None else jnp.where(piece.exists, base, -NEG)
        parts.append(jnp.exp2(part * EXP_SCALE - low))
    return stack(parts)


def score_groups(q, groups, s_ref, peak):
    at = 0
    for group in groups:
        s = dot_nt(keys_of(group), q)
        s_ref[at : at + s.shape[0], :] = s
        at += s.shape[0]
        for piece, part in by_piece(group, s):
            top = jnp.max(part, axis=0, keepdims=True)
            if piece.exists is not None:
                top = jnp.where(piece.exists, top, NEG)
            peak = top if peak is None else jnp.maximum(peak, top)
    return peak


def group_scores(groups, s_ref):
    at = 0
    for group in groups:
        size = sum(piece.size for piece in group)
        yield group, s_ref[at : at + size, :]
        at += size


def forward_slab(q, groups, with_values, s_ref, old):
    peak = score_groups(q, groups, s_ref, None if old is None else old[0])
    total, acc = 0.0, 0.0
    if old is not None:
        shrink = jnp.exp2((old[0] - peak) * EXP_SCALE)
        total, acc = old[1] * shrink, old[2] * shrink
    for j, (group, s) in enumerate(group_scores(groups, s_ref)):
        e = raised(group, s, peak * EXP_SCALE)
        total = total + jnp.sum(e, axis=0, keepdims=True)
        if j < with_values:
            acc = acc + dot_tn(values_of(group), e.astype(BF16))
    return peak, total, acc


def backward_group(q, g, lse, row_dot, group, p=None):
    k = keys_of(group)
    if p is None:
        p = raised(group, dot_nt(k, q), lse)
    if group[0].dv is not None:
        store_grads(group, dot_nn(p.astype(BF16), g), "dv")
    ds = (p * (dot_nt(values_of(group), g) - row_dot)).astype(BF16)
    if group[0].dk is not None:
        store_grads(group, dot_nn(ds, q) * SCALE, "dk")
    return dot_tn(k, ds)


def join_kernel(own, came, out, turned):
    half = own.shape[0]

    def body(mine):
        for slab, source in ((mine, own), (1 - mine, came)):
            rows = rows_of(slab, half)
            out[rows, :] = source[...]
            turned[:, rows] = source[:, VALUE].T

    each_core(body)


ALL = slice(None)


def store_state(refs, rows, peak, total, acc):
    stat, acc_ref = refs
    stat[0:1, rows] = peak
    stat[1:2, rows] = total
    acc_ref[:, rows] = acc


def load_state(refs, rows):
    stat, acc_ref = refs
    return stat[0:1, rows], stat[1:2, rows], acc_ref[:, rows]


def own_groups(kv, half, **grads):
    return [
        [Piece((kv, KEY), (kv, VALUE), r, half, **grads)] for r in range(0, kv.shape[0], half)
    ]


def near_kernel(block, swap, lists, qg, kv, a_kv, stat, acc, s_ref):
    half = qg.shape[0] // 2
    frame = lax.axis_index("tm")
    for slab in range(2):
        rows = rows_of(slab, half)
        groups = own_groups(kv, half)
        groups.append(
            listed(swap, lists, frame, slab, block, (a_kv, KEY), (a_kv, VALUE), 2)
        )
        store_state((stat, acc), rows, *forward_slab(qg[rows, KEY], groups, 3, s_ref, None))


def middle_kernel(
    block, swaps, lists, qg, stat, acc, y_k, z_k, y_v, z_v, c_k, stat2, acc2, late, s_ref
):
    half = qg.shape[0] // 2
    frame = lax.axis_index("tm")
    z, y, relayed = swaps
    for slab in range(2):
        rows = rows_of(slab, half)
        at = (lists, frame, slab, block)
        group = listed(z, *at, (z_k, ALL), (z_v, ALL)) + listed(y, *at, (y_k, ALL), (y_v, ALL))
        more = listed(relayed, *at, (c_k, ALL), None, 2)
        old = load_state((stat, acc), rows)
        new = forward_slab(qg[rows, KEY], [group, more], 1, s_ref, old)
        store_state((stat2, acc2), rows, *new)
        late[slab] = s_ref[2 * block :, :]


def close_kernel(block, relayed, far, lists_any, qg, stat, acc, late_s, *refs):
    n = len(far)
    far_kv = refs[:n]
    lse_ref, part_ref, dc_v, p_ref, s_ref, grad, lists, sem = refs[n:]
    half = qg.shape[0] // 2
    frame = lax.axis_index("tm")
    copy = pltpu.make_async_copy(lists_any, lists, sem)
    copy.start()
    grad[...] = jnp.zeros_like(grad)
    for slab in range(2):
        rows = rows_of(slab, half)
        q = qg[rows, KEY]
        groups = [[arrived(swap, frame, slab, block, kv)] for swap, kv in zip(far, far_kv)]
        old = load_state((stat, acc), rows)
        peak, total, out = forward_slab(q, groups, n, s_ref, old)
        part_ref[:, rows] = out / total
        lse = peak * EXP_SCALE + jnp.log2(total)
        lse_ref[0:1, rows] = lse
    copy.wait()
    for slab in range(2):
        rows = rows_of(slab, half)
        group = listed(relayed, lists, frame, slab, block, None, None, 2, dv=(grad, ALL))
        p = raised(group, late_s[slab], lse_ref[0:1, rows])
        p_ref[slab] = p
        store_grads(group, dot_nn(p.astype(BF16), qg[rows, VALUE]), "dv")
    dc_v[...] = grad[...].astype(BF16)


def late_kernel(block, relayed, far, *refs):
    n = len(far)
    lists, qg, turned, lse_ref, part_ref, p_ref, c_k, c_v = refs[:8]
    far_kv = refs[8 : 8 + n]
    o_ref, dot_ref, dc_k, dq_ref = refs[8 + n : 12 + n]
    far_grad = refs[12 + n : 12 + 2 * n]
    grad = refs[12 + 2 * n]
    half = qg.shape[0] // 2
    frame = lax.axis_index("tm")
    grad[...] = jnp.zeros_like(grad)
    for slab in range(2):
        rows = rows_of(slab, half)
        q, g, lse = qg[rows, KEY], qg[rows, VALUE], lse_ref[0:1, rows]
        group = listed(
            relayed, lists, frame, slab, block, (c_k, ALL), (c_v, ALL), 2, dk=(grad, ALL)
        )
        p = p_ref[slab]
        o = (part_ref[:, rows] + dot_tn(values_of(group), p.astype(BF16))).astype(BF16)
        o_ref[:, rows] = o
        products = turned[:, rows].astype(F32) * o.astype(F32)
        row_dot = jnp.sum(products, axis=0, keepdims=True)
        dot_ref[0:1, rows] = row_dot
        dq = backward_group(q, g, lse, row_dot, group, p)
        for swap, kv, out in zip(far, far_kv, far_grad):
            group = [arrived(swap, frame, slab, block, kv, dk=(out, KEY), dv=(out, VALUE))]
            dq = dq + backward_group(q, g, lse, row_dot, group)
        dq_ref[:, rows] = dq
    dc_k[...] = grad[...].astype(BF16)


def first_kernel(block, swap, lists, qg, lse_ref, dot_ref, dq_old, a_kv, da, dq_ref, grad):
    half = qg.shape[0] // 2
    frame = lax.axis_index("tm")
    grad[...] = jnp.zeros_like(grad)
    for slab in range(2):
        rows = rows_of(slab, half)
        q, g, lse, row_dot = qg[rows, KEY], qg[rows, VALUE], lse_ref[0:1, rows], dot_ref[0:1, rows]
        group = listed(
            swap, lists, frame, slab, block, (a_kv, KEY), (a_kv, VALUE), 2,
            dk=(grad, KEY), dv=(grad, VALUE),
        )
        dq_ref[:, rows] = dq_old[:, rows] + backward_group(q, g, lse, row_dot, group)
    da[...] = grad[...].astype(BF16)


def second_kernel(
    block, swaps, lists, qg, lse_ref, dot_ref, dq_old, came, y_k, z_k, y_v, z_v,
    dz_k, dy_k, dz_v, dy_v, dq_ref, z_sum, y_sum,
):
    half = qg.shape[0] // 2
    frame = lax.axis_index("tm")
    z, y = swaps
    relays = forwards_first(frame)
    more = came[...].astype(F32)
    for k, v, takes in ((dz_k, z_sum, relays), (dy_k, y_sum, jnp.logical_not(relays))):
        k[...] = jnp.zeros_like(more)
        v[...] = jnp.where(takes, more, 0.0)
    for slab in range(2):
        rows = rows_of(slab, half)
        q, g, lse, row_dot = qg[rows, KEY], qg[rows, VALUE], lse_ref[0:1, rows], dot_ref[0:1, rows]
        at = (lists, frame, slab, block)
        group = listed(z, *at, (z_k, ALL), (z_v, ALL), dk=(dz_k, ALL), dv=(z_sum, ALL))
        group += listed(y, *at, (y_k, ALL), (y_v, ALL), dk=(dy_k, ALL), dv=(y_sum, ALL))
        dq_ref[:, rows] = dq_old[:, rows] + backward_group(q, g, lse, row_dot, group)
    dz_v[...] = z_sum[...].astype(BF16)
    dy_v[...] = y_sum[...].astype(BF16)


def own_kernel(qg, lse_ref, dot_ref, dq_old, o, kv, placed, near, keep, send):
    half = qg.shape[0] // 2
    near[...] = placed[...]
    whole = []
    for slab in range(2):
        rows = rows_of(slab, half)
        q, g, lse, row_dot = qg[rows, KEY], qg[rows, VALUE], lse_ref[0:1, rows], dot_ref[0:1, rows]
        dq = dq_old[:, rows]
        for group in own_groups(kv, half, dk=(near, KEY), dv=(near, VALUE)):
            dq = dq + backward_group(q, g, lse, row_dot, group)
        whole.append((dq.T * SCALE).astype(BF16))

    def body(mine):
        for slab in range(2):
            out = keep if slab == mine else send
            out[:, KEY] = o[:, rows_of(slab, half)].T
            out[:, VALUE] = whole[slab]

    each_core(body)


def merge_kernel(dz, dy, came, z_out, y_out):
    first = forwards_first(lax.axis_index("tm"))
    more = came[...].astype(F32)
    z_out[...] = (dz[...] + jnp.where(first, more, 0.0)).astype(BF16)
    y_out[...] = (dy[...] + jnp.where(first, 0.0, more)).astype(BF16)


def place_kernel(block, swaps, far, *refs):
    lists, z_came, y_came, total = refs[0], refs[1], refs[2], refs[-1]
    frame = lax.axis_index("tm")
    values = 0.0
    for swap, came in zip(swaps, (z_came, y_came)):
        values = values + jnp.where(swap.partner(frame)[2], came[...].astype(F32), 0.0)
    total[:, KEY] = jnp.zeros_like(values)
    total[:, VALUE] = values
    for swap, came in zip(far, refs[3:-1]):
        for slab in range(2):
            b, exists = swap.block_of_theirs(lists, frame, slab, 0)
            rows = pl.ds(pl.multiple_of(b * block, block), block)
            part = came[rows_of(slab, block), :].astype(F32)
            total[rows, :] += jnp.where(exists, part, 0.0)


def add_kernel(swaps, near, da, dy, total):
    frame = lax.axis_index("tm")
    by_a, by_y = (swap.partner(frame)[2] for swap in swaps)
    total[:, VALUE] = near[:, VALUE] + jnp.where(by_a, da[:, VALUE].astype(F32), 0.0)
    keys = near[:, KEY] + jnp.where(by_a, da[:, KEY].astype(F32), 0.0)
    total[:, KEY] = keys + jnp.where(by_y, dy[...].astype(F32), 0.0)


def gather_kernel(swap, near, came, keep, send):
    _, _, exists = swap.partner(lax.axis_index("tm"))
    half = near.shape[0] // 2

    def body(mine):
        for slab, out in ((1 - mine, send), (mine, keep)):
            rows = rows_of(slab, half)
            part = jnp.where(exists, came[rows, :].astype(F32), 0.0)
            out[:, KEY] = (near[rows, KEY] + part).astype(BF16)
            out[:, VALUE] = near[rows, VALUE].astype(BF16)

    each_core(body)


def finish_kernel(keep, came, first, second):
    def body(mine):
        for head, source in ((mine, keep), (1 - mine, came)):
            first[:, head_cols(head)] = source[:, KEY]
            second[:, head_cols(head)] = source[:, VALUE]

    each_core(body)


def per_device(queries, key_rows, value_rows, out_grad, block_lists):
    s_dev, width = queries.shape
    count = lax.axis_size("tm")
    block = s_dev // 2
    pair = sds((s_dev, 2 * DH), BF16)
    single = sds((s_dev, DH), BF16)
    frame_two = sds((2 * s_dev, 2 * DH), BF16)
    frame_one = sds((2 * s_dev, DH), BF16)
    frame_sum = sds((2 * s_dev, 2 * DH), F32)
    stat_row = sds((8, 2 * s_dev), F32)
    turned_sum = sds((DH, 2 * s_dev), F32)
    turned_bf = sds((DH, 2 * s_dev), BF16)
    levels = count.bit_length() - 1
    near_swap, relayed = Swap(count, 0, False), Swap(count, 0, True)
    z_swap, y_swap = Swap(count, 1, False), Swap(count, 1, True)
    far = [Swap(count, level, second) for level in range(2, levels) for second in (False, True)]
    far = [swap for swap in far if swap.moves]
    n = len(far)
    grad_one = pltpu.VMEM((2 * s_dev, DH), F32)

    def across(value):
        return lax.ppermute(value, "space", [(0, 1), (1, 0)])

    def swapped(value, swap):
        return lax.ppermute(value, ("tm", "space"), swap.pairs)

    def scores(pieces):
        return pltpu.VMEM((pieces * block, s_dev), F32)


    k_came, v_came = across(key_rows), across(value_rows)
    sources = (key_rows, value_rows, queries, out_grad, block_lists.T)
    k_own, v_own, qg_own, qg_send, lists = call(
        pack_kernel,
        tuple(pltpu.with_memory_space_constraint(a, pltpu.HBM) for a in sources),
        [single, single, pair, pair, sds(sources[4].shape, jnp.int32)],
        scratch=[pltpu.SemaphoreType.DMA((7,))],
        source=HBM,
        scalars=HBM,
    )
    (keys,) = call(keys_kernel, (k_own, k_came), [frame_one])
    values, kv = call(values_kernel, (keys, v_own, v_came), [frame_one, frame_two])
    qg_send, _ = lax.optimization_barrier((qg_send, keys))
    y_k = swapped(keys, y_swap)
    z_k = swapped(keys, z_swap)
    a_kv = swapped(kv, near_swap)
    y_v = swapped(values, y_swap)
    z_v = swapped(values, z_swap)
    y_k, qg_came = lax.optimization_barrier((y_k, across(qg_send)))
    work = 4 * s_dev * s_dev * DH
    qg, turned = call(join_kernel, (qg_own, qg_came), [frame_two, turned_bf], flops=15 * work)
    kv, _ = lax.optimization_barrier((kv, turned))
    far_send = call(functools.partial(select_kernel, far, block), (lists, kv), [pair] * n)
    y_k, z_k, far_send = lax.optimization_barrier((y_k, z_k, far_send))
    (relay_k,) = call(relay_kernel, (y_k, z_k), [frame_one])
    relay_k, far_send = lax.optimization_barrier((relay_k, far_send))
    a_kv, _ = lax.optimization_barrier((a_kv, relay_k))
    c_k = swapped(relay_k, near_swap)
    far_kv = [swapped(value, swap) for value, swap in zip(far_send, far)]
    stat, acc = call(
        functools.partial(near_kernel, block, near_swap),
        (lists, qg, kv, a_kv),
        [stat_row, turned_sum],
        scratch=[scores(6)],
    )
    score_two = sds((2, s_dev, s_dev), F32)
    y_v, z_v, stat = lax.optimization_barrier((y_v, z_v, stat))
    (relay_v,) = call(relay_kernel, (y_v, z_v), [frame_one])
    relay_v, stat = lax.optimization_barrier((relay_v, stat))
    c_v = swapped(relay_v, near_swap)
    stat, acc, late_scores = call(
        functools.partial(middle_kernel, block, (z_swap, y_swap, relayed)),
        (lists, qg, stat, acc, y_k, z_k, y_v, z_v, c_k),
        [stat_row, turned_sum, score_two],
        scratch=[scores(4)],
    )
    acc, far_kv = lax.optimization_barrier((acc, far_kv))
    lse, part, dc_v, probs = call(
        functools.partial(close_kernel, block, relayed, far),
        (lists, qg, stat, acc, late_scores, *far_kv),
        [stat_row, turned_sum, frame_one, score_two],
        scratch=[
            scores(n),
            grad_one,
            pltpu.SMEM(lists.shape, jnp.int32),
            pltpu.SemaphoreType.DMA(()),
        ],
        scalars=pl.BlockSpec(memory_space=pl.ANY),
    )
    dc_v_came = swapped(dc_v, near_swap)
    o, row_dot, dc_k, dq, *far_grad = call(
        functools.partial(late_kernel, block, relayed, far),
        (lists, qg, turned, lse, part, probs, c_k, c_v, *far_kv),
        [turned_bf, stat_row, frame_one, turned_sum] + [pair] * n,
        scratch=[grad_one],
    )
    far_came = [swapped(value, swap) for value, swap in zip(far_grad, far)]
    dc_k_came = swapped(dc_k, near_swap)
    key_sum = sds((2 * s_dev, DH), F32)
    dz_k, dy_k, dz_v, dy_v, dq = call(
        functools.partial(second_kernel, block, (z_swap, y_swap)),
        (lists, qg, lse, row_dot, dq, dc_v_came, y_k, z_k, y_v, z_v),
        [key_sum, key_sum, frame_one, frame_one, turned_sum],
        scratch=[grad_one, grad_one],
        flops=20 * work,
    )
    dy_v_came = swapped(dy_v, y_swap)
    dz_v_came = swapped(dz_v, z_swap)
    da, dq = call(
        functools.partial(first_kernel, block, near_swap),
        (lists, qg, lse, row_dot, dq, a_kv),
        [frame_two, turned_sum],
        scratch=[pltpu.VMEM((2 * s_dev, 2 * DH), F32)],
    )
    da_came = swapped(da, near_swap)
    dz_k, dy_k = call(merge_kernel, (dz_k, dy_k, dc_k_came), [frame_one, frame_one], flops=20 * work)
    dy_k_came = swapped(dy_k, y_swap)
    dz_k_came = swapped(dz_k, z_swap)
    dq, dz_k, dy_k = lax.optimization_barrier((dq, dz_k, dy_k))
    far_came, dq = lax.optimization_barrier((far_came, dq))
    (placed,) = call(
        functools.partial(place_kernel, block, (z_swap, y_swap), far),
        (lists, dz_v_came, dy_v_came, *far_came),
        [frame_sum],
    )
    near, q_keep, q_send = call(
        own_kernel,
        (qg, lse, row_dot, dq, o, kv, placed),
        [frame_sum, pair, pair],
        flops=28 * work,
    )
    outputs = [sds((s_dev, width), BF16)] * 2
    attn_out, grad_q = call(finish_kernel, (q_keep, across(q_send)), outputs)
    (near,) = call(
        functools.partial(add_kernel, (near_swap, y_swap)),
        (near, da_came, dy_k_came),
        [frame_sum],
        flops=5 * work,
    )
    k_keep, k_send = call(
        functools.partial(gather_kernel, z_swap), (near, dz_k_came), [pair, pair]
    )
    grad_k, grad_v = call(finish_kernel, (k_keep, across(k_send)), outputs)
    return attn_out, grad_q, grad_k, grad_v


def solution(mesh):
    rows = P(("groups", "tm", "space"), None)
    return jax.shard_map(
        per_device,
        mesh=mesh,
        in_specs=(rows, rows, rows, rows, P("groups", None)),
        out_specs=(rows, rows, rows, rows),
        check_vma=False,
    )
```

```python
import functools
import math

import jax
import jax.numpy as jnp
from jax import lax
from jax.experimental import pallas as pl
from jax.experimental.pallas import tpu as pltpu
from jax.sharding import PartitionSpec as P

DH = 128
F32 = jnp.float32
BF16 = jnp.bfloat16
VMEM = pl.BlockSpec(memory_space=pltpu.VMEM)
SMEM = pl.BlockSpec(memory_space=pltpu.SMEM)
HBM = pl.BlockSpec(memory_space=pltpu.HBM)
NEG = -1e30
SCALE = 1.0 / math.sqrt(DH)
EXP_SCALE = SCALE * math.log2(math.e)
KEY = slice(0, DH)
VALUE = slice(DH, 2 * DH)
sds = jax.ShapeDtypeStruct


def dot_nn(a, b):
    return lax.dot_general(a, b, (((1,), (0,)), ((), ())), preferred_element_type=F32)


def dot_nt(a, b):
    return lax.dot_general(a, b, (((1,), (1,)), ((), ())), preferred_element_type=F32)


def dot_tn(a, b):
    return lax.dot_general(a, b, (((0,), (0,)), ((), ())), preferred_element_type=F32)


def call(kernel, args, out_shape, scratch=(), source=VMEM, scalars=SMEM, flops=1024):
    return pl.pallas_call(
        kernel,
        out_shape=out_shape,
        in_specs=[scalars if a.dtype == jnp.int32 else source for a in args],
        out_specs=tuple(VMEM for _ in out_shape),
        scratch_shapes=list(scratch),
        compiler_params=pltpu.CompilerParams(vmem_limit_bytes=40 << 20),
        cost_estimate=pl.CostEstimate(flops=flops, bytes_accessed=1024, transcendentals=0),
    )(*args)


def swap_pairs(count, distance, second):
    pairs = []
    for frame in range(count):
        up = ((frame // distance) % 2 == 0) != second
        target = frame + distance if up else frame - distance
        for core in range(2):
            if 0 <= target < count:
                pairs.append((frame * 2 + core, target * 2 + core))
            else:
                pairs.append((frame * 2 + core, frame * 2 + 1 - core))
    return pairs


class Swap:
    def __init__(self, count, level, second):
        self.count, self.level, self.second = count, level, second
        self.levels = count.bit_length() - 1
        self.pairs = swap_pairs(count, 1 << level, second)
        self.moves = any(source // 2 != target // 2 for source, target in self.pairs)

    def partner(self, frame):
        odd = lax.rem(lax.shift_right_logical(frame, self.level), 2)
        later = odd == (1 if self.second else 0)
        other = jnp.where(later, frame + (1 << self.level), frame - (1 << self.level))
        return other, later, jnp.logical_and(other >= 0, other < self.count)

    def slot(self, later, k):
        base = 0 if self.level == 0 else self.level + 1
        return jnp.where(later, self.levels + 1, 0) + base + k

    def block_of_mine(self, lists, frame, slab, k):
        other, later, exists = self.partner(frame)
        entry = lists[self.slot(later, k), frame * 2 + slab]
        return jnp.clip(entry - other * 4, 0, 3), exists

    def block_of_theirs(self, lists, frame, slab, k):
        other, later, exists = self.partner(frame)
        row = jnp.where(exists, other, frame) * 2 + slab
        entry = lists[self.slot(jnp.logical_not(later), k), row]
        return jnp.clip(entry - frame * 4, 0, 3), exists


def head_cols(head):
    return slice(head * DH, (head + 1) * DH)


def rows_of(slab, half):
    return slice(slab * half, (slab + 1) * half)


def each_core(body):
    core = lax.axis_index("space")
    for mine in range(2):
        pl.when(core == mine)(functools.partial(body, mine))


def pack_kernel(k, v, q, g, lists, k_own, v_own, qg_own, qg_send, lists_out, sems):
    def body(mine):
        moves = [(lists, lists_out)]
        for source, out in ((k, k_own), (v, v_own)):
            moves.append((source.at[:, head_cols(mine)], out))
        for head, out in ((mine, qg_own), (1 - mine, qg_send)):
            for source, cols in ((q, KEY), (g, VALUE)):
                moves.append((source.at[:, head_cols(head)], out.at[:, cols]))
        copies = [
            pltpu.make_async_copy(source, out, sems.at[n]) for n, (source, out) in enumerate(moves)
        ]
        for copy in copies:
            copy.start()
        for copy in copies:
            copy.wait()

    each_core(body)


def keys_kernel(own, came, keys):
    half = own.shape[0]

    def body(mine):
        keys[rows_of(mine, half), :] = own[...]
        keys[rows_of(1 - mine, half), :] = came[:, head_cols(mine)]

    each_core(body)


def values_kernel(keys, own, came, values, kv):
    half = own.shape[0]

    def body(mine):
        for slab, part in ((mine, own[...]), (1 - mine, came[:, head_cols(mine)])):
            rows = rows_of(slab, half)
            values[rows, :] = part
            kv[rows, VALUE] = part
            kv[rows, KEY] = keys[rows, :]

    each_core(body)


def select_kernel(far, block, lists, kv, *sends):
    frame = lax.axis_index("tm")
    for swap, send in zip(far, sends):
        for slab in range(2):
            b, _ = swap.block_of_theirs(lists, frame, slab, 0)
            row = pl.multiple_of(b * block, block)
            send[slab * block : (slab + 1) * block, :] = kv[pl.ds(row, block), :]


def forwards_first(frame):
    return lax.rem(frame, 2) == lax.rem(lax.shift_right_logical(frame, 1), 2)


def relay_kernel(y, z, out):
    first = forwards_first(lax.axis_index("tm"))

    @pl.when(first)
    def _():
        out[...] = z[...]

    @pl.when(jnp.logical_not(first))
    def _():
        out[...] = y[...]


class Piece:
    def __init__(self, k, v, row, size, exists=None, dk=None, dv=None, add=True):
        self.k_at, self.v_at, self.exists = k, v, exists
        self.rows, self.size = pl.ds(row, size), size
        self.dk, self.dv, self.add = dk, dv, add

    def store(self, at, value):
        ref, cols = at
        if self.add:
            ref[self.rows, cols] += value
        else:
            ref[self.rows, cols] = value.astype(ref.dtype)


def stack(parts):
    return parts[0] if len(parts) == 1 else jnp.concatenate(parts, axis=0)


def keys_of(group):
    return stack([p.k_at[0][p.rows, p.k_at[1]] for p in group])


def values_of(group):
    return stack([p.v_at[0][p.rows, p.v_at[1]] for p in group])


def by_piece(group, value):
    at = 0
    for piece in group:
        yield piece, value[at : at + piece.size, :]
        at += piece.size


def store_grads(group, value, name):
    for piece, part in by_piece(group, value):
        piece.store(getattr(piece, name), part)


def listed(swap, lists, frame, slab, block, k, v, count=1, **grads):
    pieces = []
    for n in range(count):
        b, exists = swap.block_of_mine(lists, frame, slab, n)
        pieces.append(Piece(k, v, pl.multiple_of(b * block, block), block, exists, **grads))
    return pieces


def arrived(swap, frame, slab, block, kv, **grads):
    _, _, exists = swap.partner(frame)
    return Piece((kv, KEY), (kv, VALUE), slab * block, block, exists, add=False, **grads)


def raised(group, s, base):
    parts = []
    for piece, part in by_piece(group, s):
        low = base if piece.exists is None else jnp.where(piece.exists, base, -NEG)
        parts.append(jnp.exp2(part * EXP_SCALE - low))
    return stack(parts)


def score_groups(q, groups, s_ref, peak):
    at = 0
    for group in groups:
        s = dot_nt(keys_of(group), q)
        s_ref[at : at + s.shape[0], :] = s
        at += s.shape[0]
        for piece, part in by_piece(group, s):
            top = jnp.max(part, axis=0, keepdims=True)
            if piece.exists is not None:
                top = jnp.where(piece.exists, top, NEG)
            peak = top if peak is None else jnp.maximum(peak, top)
    return peak


def group_scores(groups, s_ref):
    at = 0
    for group in groups:
        size = sum(piece.size for piece in group)
        yield group, s_ref[at : at + size, :]
        at += size


def forward_slab(q, groups, with_values, s_ref, old):
    peak = score_groups(q, groups, s_ref, None if old is None else old[0])
    total, acc = 0.0, 0.0
    if old is not None:
        shrink = jnp.exp2((old[0] - peak) * EXP_SCALE)
        total, acc = old[1] * shrink, old[2] * shrink
    for j, (group, s) in enumerate(group_scores(groups, s_ref)):
        e = raised(group, s, peak * EXP_SCALE)
        total = total + jnp.sum(e, axis=0, keepdims=True)
        if j < with_values:
            acc = acc + dot_tn(values_of(group), e.astype(BF16))
    return peak, total, acc


def backward_group(q, g, lse, row_dot, group, p=None):
    k = keys_of(group)
    if p is None:
        p = raised(group, dot_nt(k, q), lse)
    if group[0].dv is not None:
        store_grads(group, dot_nn(p.astype(BF16), g), "dv")
    ds = (p * (dot_nt(values_of(group), g) - row_dot)).astype(BF16)
    if group[0].dk is not None:
        store_grads(group, dot_nn(ds, q) * SCALE, "dk")
    return dot_tn(k, ds)


def join_kernel(own, came, out, turned):
    half = own.shape[0]

    def body(mine):
        for slab, source in ((mine, own), (1 - mine, came)):
            rows = rows_of(slab, half)
            out[rows, :] = source[...]
            turned[:, rows] = source[:, VALUE].T

    each_core(body)


ALL = slice(None)


def store_state(refs, rows, peak, total, acc):
    stat, acc_ref = refs
    stat[0:1, rows] = peak
    stat[1:2, rows] = total
    acc_ref[:, rows] = acc


def load_state(refs, rows):
    stat, acc_ref = refs
    return stat[0:1, rows], stat[1:2, rows], acc_ref[:, rows]


def own_groups(kv, half, **grads):
    return [
        [Piece((kv, KEY), (kv, VALUE), r, half, **grads)] for r in range(0, kv.shape[0], half)
    ]


def near_kernel(block, swap, lists, qg, kv, a_kv, stat, acc, s_ref):
    half = qg.shape[0] // 2
    frame = lax.axis_index("tm")
    for slab in range(2):
        rows = rows_of(slab, half)
        groups = own_groups(kv, half)
        groups.append(
            listed(swap, lists, frame, slab, block, (a_kv, KEY), (a_kv, VALUE), 2)
        )
        store_state((stat, acc), rows, *forward_slab(qg[rows, KEY], groups, 3, s_ref, None))


def middle_kernel(
    block, swaps, lists, qg, stat, acc, y_k, z_k, y_v, z_v, c_k, stat2, acc2, late, s_ref
):
    half = qg.shape[0] // 2
    frame = lax.axis_index("tm")
    z, y, relayed = swaps
    for slab in range(2):
        rows = rows_of(slab, half)
        at = (lists, frame, slab, block)
        group = listed(z, *at, (z_k, ALL), (z_v, ALL)) + listed(y, *at, (y_k, ALL), (y_v, ALL))
        more = listed(relayed, *at, (c_k, ALL), None, 2)
        old = load_state((stat, acc), rows)
        new = forward_slab(qg[rows, KEY], [group, more], 1, s_ref, old)
        store_state((stat2, acc2), rows, *new)
        late[slab] = s_ref[2 * block :, :]


def close_kernel(block, relayed, far, lists_any, qg, stat, acc, late_s, *refs):
    n = len(far)
    far_kv = refs[:n]
    lse_ref, part_ref, dc_v, p_ref, s_ref, grad, lists, sem = refs[n:]
    half = qg.shape[0] // 2
    frame = lax.axis_index("tm")
    copy = pltpu.make_async_copy(lists_any, lists, sem)
    copy.start()
    grad[...] = jnp.zeros_like(grad)
    for slab in range(2):
        rows = rows_of(slab, half)
        q = qg[rows, KEY]
        groups = [[arrived(swap, frame, slab, block, kv)] for swap, kv in zip(far, far_kv)]
        old = load_state((stat, acc), rows)
        peak, total, out = forward_slab(q, groups, n, s_ref, old)
        part_ref[:, rows] = out / total
        lse = peak * EXP_SCALE + jnp.log2(total)
        lse_ref[0:1, rows] = lse
    copy.wait()
    for slab in range(2):
        rows = rows_of(slab, half)
        group = listed(relayed, lists, frame, slab, block, None, None, 2, dv=(grad, ALL))
        p = raised(group, late_s[slab], lse_ref[0:1, rows])
        p_ref[slab] = p
        store_grads(group, dot_nn(p.astype(BF16), qg[rows, VALUE]), "dv")
    dc_v[...] = grad[...].astype(BF16)


def late_kernel(block, relayed, far, *refs):
    n = len(far)
    lists_any, qg, turned, lse_ref, part_ref, p_ref, c_k, c_v = refs[:8]
    far_kv = refs[8 : 8 + n]
    o_ref, dot_ref, dc_k, dq_ref = refs[8 + n : 12 + n]
    far_grad = refs[12 + n : 12 + 2 * n]
    grad, lists, sem = refs[12 + 2 * n :]
    copy = pltpu.make_async_copy(lists_any, lists, sem)
    copy.start()
    half = qg.shape[0] // 2
    frame = lax.axis_index("tm")
    grad[...] = jnp.zeros_like(grad)
    copy.wait()
    for slab in range(2):
        rows = rows_of(slab, half)
        q, g, lse = qg[rows, KEY], qg[rows, VALUE], lse_ref[0:1, rows]
        group = listed(
            relayed, lists, frame, slab, block, (c_k, ALL), (c_v, ALL), 2, dk=(grad, ALL)
        )
        p = p_ref[slab]
        o = (part_ref[:, rows] + dot_tn(values_of(group), p.astype(BF16))).astype(BF16)
        o_ref[:, rows] = o
        products = turned[:, rows].astype(F32) * o.astype(F32)
        row_dot = jnp.sum(products, axis=0, keepdims=True)
        dot_ref[0:1, rows] = row_dot
        dq = backward_group(q, g, lse, row_dot, group, p)
        for swap, kv, out in zip(far, far_kv, far_grad):
            group = [arrived(swap, frame, slab, block, kv, dk=(out, KEY), dv=(out, VALUE))]
            dq = dq + backward_group(q, g, lse, row_dot, group)
        dq_ref[:, rows] = dq
    dc_k[...] = grad[...].astype(BF16)


def first_kernel(block, swap, lists, qg, lse_ref, dot_ref, dq_old, a_kv, da, dq_ref, grad):
    half = qg.shape[0] // 2
    frame = lax.axis_index("tm")
    grad[...] = jnp.zeros_like(grad)
    for slab in range(2):
        rows = rows_of(slab, half)
        q, g, lse, row_dot = qg[rows, KEY], qg[rows, VALUE], lse_ref[0:1, rows], dot_ref[0:1, rows]
        group = listed(
            swap, lists, frame, slab, block, (a_kv, KEY), (a_kv, VALUE), 2,
            dk=(grad, KEY), dv=(grad, VALUE),
        )
        dq_ref[:, rows] = dq_old[:, rows] + backward_group(q, g, lse, row_dot, group)
    da[...] = grad[...].astype(BF16)


def second_kernel(
    block, swaps, lists, qg, lse_ref, dot_ref, dq_old, came, y_k, z_k, y_v, z_v,
    dz_k, dy_k, dz_v, dy_v, dq_ref, z_sum, y_sum,
):
    half = qg.shape[0] // 2
    frame = lax.axis_index("tm")
    z, y = swaps
    relays = forwards_first(frame)
    more = came[...].astype(F32)
    for k, v, takes in ((dz_k, z_sum, relays), (dy_k, y_sum, jnp.logical_not(relays))):
        k[...] = jnp.zeros_like(more)
        v[...] = jnp.where(takes, more, 0.0)
    for slab in range(2):
        rows = rows_of(slab, half)
        q, g, lse, row_dot = qg[rows, KEY], qg[rows, VALUE], lse_ref[0:1, rows], dot_ref[0:1, rows]
        at = (lists, frame, slab, block)
        group = listed(z, *at, (z_k, ALL), (z_v, ALL), dk=(dz_k, ALL), dv=(z_sum, ALL))
        group += listed(y, *at, (y_k, ALL), (y_v, ALL), dk=(dy_k, ALL), dv=(y_sum, ALL))
        dq_ref[:, rows] = dq_old[:, rows] + backward_group(q, g, lse, row_dot, group)
    dz_v[...] = z_sum[...].astype(BF16)
    dy_v[...] = y_sum[...].astype(BF16)


def own_kernel(qg, lse_ref, dot_ref, dq_old, o, kv, placed, near, keep, send):
    half = qg.shape[0] // 2
    near[...] = placed[...]
    whole = []
    for slab in range(2):
        rows = rows_of(slab, half)
        q, g, lse, row_dot = qg[rows, KEY], qg[rows, VALUE], lse_ref[0:1, rows], dot_ref[0:1, rows]
        dq = dq_old[:, rows]
        for group in own_groups(kv, half, dk=(near, KEY), dv=(near, VALUE)):
            dq = dq + backward_group(q, g, lse, row_dot, group)
        whole.append((dq.T * SCALE).astype(BF16))

    def body(mine):
        for slab in range(2):
            out = keep if slab == mine else send
            out[:, KEY] = o[:, rows_of(slab, half)].T
            out[:, VALUE] = whole[slab]

    each_core(body)


def merge_kernel(dz, dy, came, z_out, y_out):
    first = forwards_first(lax.axis_index("tm"))
    more = came[...].astype(F32)
    z_out[...] = (dz[...] + jnp.where(first, more, 0.0)).astype(BF16)
    y_out[...] = (dy[...] + jnp.where(first, 0.0, more)).astype(BF16)


def place_kernel(block, swaps, far, *refs):
    lists, z_came, y_came, total = refs[0], refs[1], refs[2], refs[-1]
    frame = lax.axis_index("tm")
    values = 0.0
    for swap, came in zip(swaps, (z_came, y_came)):
        values = values + jnp.where(swap.partner(frame)[2], came[...].astype(F32), 0.0)
    total[:, KEY] = jnp.zeros_like(values)
    total[:, VALUE] = values
    for swap, came in zip(far, refs[3:-1]):
        for slab in range(2):
            b, exists = swap.block_of_theirs(lists, frame, slab, 0)
            rows = pl.ds(pl.multiple_of(b * block, block), block)
            part = came[rows_of(slab, block), :].astype(F32)
            total[rows, :] += jnp.where(exists, part, 0.0)


def add_kernel(swaps, near, da, dy, total):
    frame = lax.axis_index("tm")
    by_a, by_y = (swap.partner(frame)[2] for swap in swaps)
    total[:, VALUE] = near[:, VALUE] + jnp.where(by_a, da[:, VALUE].astype(F32), 0.0)
    keys = near[:, KEY] + jnp.where(by_a, da[:, KEY].astype(F32), 0.0)
    total[:, KEY] = keys + jnp.where(by_y, dy[...].astype(F32), 0.0)


def gather_kernel(swap, near, came, keep, send):
    _, _, exists = swap.partner(lax.axis_index("tm"))
    half = near.shape[0] // 2

    def body(mine):
        for slab, out in ((1 - mine, send), (mine, keep)):
            rows = rows_of(slab, half)
            part = jnp.where(exists, came[rows, :].astype(F32), 0.0)
            out[:, KEY] = (near[rows, KEY] + part).astype(BF16)
            out[:, VALUE] = near[rows, VALUE].astype(BF16)

    each_core(body)


def finish_kernel(keep, came, first, second):
    def body(mine):
        for head, source in ((mine, keep), (1 - mine, came)):
            first[:, head_cols(head)] = source[:, KEY]
            second[:, head_cols(head)] = source[:, VALUE]

    each_core(body)


def per_device(queries, key_rows, value_rows, out_grad, block_lists):
    s_dev, width = queries.shape
    count = lax.axis_size("tm")
    block = s_dev // 2
    pair = sds((s_dev, 2 * DH), BF16)
    single = sds((s_dev, DH), BF16)
    frame_two = sds((2 * s_dev, 2 * DH), BF16)
    frame_one = sds((2 * s_dev, DH), BF16)
    frame_sum = sds((2 * s_dev, 2 * DH), F32)
    stat_row = sds((8, 2 * s_dev), F32)
    turned_sum = sds((DH, 2 * s_dev), F32)
    turned_bf = sds((DH, 2 * s_dev), BF16)
    levels = count.bit_length() - 1
    near_swap, relayed = Swap(count, 0, False), Swap(count, 0, True)
    z_swap, y_swap = Swap(count, 1, False), Swap(count, 1, True)
    far = [Swap(count, level, second) for level in range(2, levels) for second in (False, True)]
    far = [swap for swap in far if swap.moves]
    n = len(far)
    grad_one = pltpu.VMEM((2 * s_dev, DH), F32)

    def across(value):
        return lax.ppermute(value, "space", [(0, 1), (1, 0)])

    def swapped(value, swap):
        return lax.ppermute(value, ("tm", "space"), swap.pairs)

    def scores(pieces):
        return pltpu.VMEM((pieces * block, s_dev), F32)


    k_came, v_came = across(key_rows), across(value_rows)
    sources = (key_rows, value_rows, queries, out_grad, block_lists.T)
    k_own, v_own, qg_own, qg_send, lists = call(
        pack_kernel,
        tuple(pltpu.with_memory_space_constraint(a, pltpu.HBM) for a in sources),
        [single, single, pair, pair, sds(sources[4].shape, jnp.int32)],
        scratch=[pltpu.SemaphoreType.DMA((7,))],
        source=HBM,
        scalars=HBM,
    )
    (keys,) = call(keys_kernel, (k_own, k_came), [frame_one])
    values, kv = call(values_kernel, (keys, v_own, v_came), [frame_one, frame_two])
    qg_send, _ = lax.optimization_barrier((qg_send, keys))
    y_k = swapped(keys, y_swap)
    z_k = swapped(keys, z_swap)
    a_kv = swapped(kv, near_swap)
    y_v = swapped(values, y_swap)
    z_v = swapped(values, z_swap)
    y_k, qg_came = lax.optimization_barrier((y_k, across(qg_send)))
    work = 4 * s_dev * s_dev * DH
    qg, turned = call(join_kernel, (qg_own, qg_came), [frame_two, turned_bf], flops=15 * work)
    kv, _ = lax.optimization_barrier((kv, turned))
    far_send = call(functools.partial(select_kernel, far, block), (lists, kv), [pair] * n)
    y_k, z_k, far_send = lax.optimization_barrier((y_k, z_k, far_send))
    (relay_k,) = call(relay_kernel, (y_k, z_k), [frame_one])
    relay_k, far_send = lax.optimization_barrier((relay_k, far_send))
    a_kv, _ = lax.optimization_barrier((a_kv, relay_k))
    c_k = swapped(relay_k, near_swap)
    far_kv = [swapped(value, swap) for value, swap in zip(far_send, far)]
    stat, acc = call(
        functools.partial(near_kernel, block, near_swap),
        (lists, qg, kv, a_kv),
        [stat_row, turned_sum],
        scratch=[scores(6)],
    )
    score_two = sds((2, s_dev, s_dev), F32)
    y_v, z_v, stat = lax.optimization_barrier((y_v, z_v, stat))
    (relay_v,) = call(relay_kernel, (y_v, z_v), [frame_one])
    relay_v, stat = lax.optimization_barrier((relay_v, stat))
    c_v = swapped(relay_v, near_swap)
    stat, acc, late_scores = call(
        functools.partial(middle_kernel, block, (z_swap, y_swap, relayed)),
        (lists, qg, stat, acc, y_k, z_k, y_v, z_v, c_k),
        [stat_row, turned_sum, score_two],
        scratch=[scores(4)],
    )
    acc, far_kv = lax.optimization_barrier((acc, far_kv))
    lse, part, dc_v, probs = call(
        functools.partial(close_kernel, block, relayed, far),
        (lists, qg, stat, acc, late_scores, *far_kv),
        [stat_row, turned_sum, frame_one, score_two],
        scratch=[
            scores(n),
            grad_one,
            pltpu.SMEM(lists.shape, jnp.int32),
            pltpu.SemaphoreType.DMA(()),
        ],
        scalars=pl.BlockSpec(memory_space=pl.ANY),
    )
    dc_v_came = swapped(dc_v, near_swap)
    o, row_dot, dc_k, dq, *far_grad = call(
        functools.partial(late_kernel, block, relayed, far),
        (lists, qg, turned, lse, part, probs, c_k, c_v, *far_kv),
        [turned_bf, stat_row, frame_one, turned_sum] + [pair] * n,
        scratch=[
            grad_one,
            pltpu.SMEM(lists.shape, jnp.int32),
            pltpu.SemaphoreType.DMA(()),
        ],
        scalars=pl.BlockSpec(memory_space=pl.ANY),
    )
    far_came = [swapped(value, swap) for value, swap in zip(far_grad, far)]
    dc_k_came = swapped(dc_k, near_swap)
    key_sum = sds((2 * s_dev, DH), F32)
    dz_k, dy_k, dz_v, dy_v, dq = call(
        functools.partial(second_kernel, block, (z_swap, y_swap)),
        (lists, qg, lse, row_dot, dq, dc_v_came, y_k, z_k, y_v, z_v),
        [key_sum, key_sum, frame_one, frame_one, turned_sum],
        scratch=[grad_one, grad_one],
        flops=20 * work,
    )
    dy_v_came = swapped(dy_v, y_swap)
    dz_v_came = swapped(dz_v, z_swap)
    da, dq = call(
        functools.partial(first_kernel, block, near_swap),
        (lists, qg, lse, row_dot, dq, a_kv),
        [frame_two, turned_sum],
        scratch=[pltpu.VMEM((2 * s_dev, 2 * DH), F32)],
    )
    da_came = swapped(da, near_swap)
    dz_k, dy_k = call(merge_kernel, (dz_k, dy_k, dc_k_came), [frame_one, frame_one])
    dy_k_came = swapped(dy_k, y_swap)
    dz_k_came = swapped(dz_k, z_swap)
    dq, dz_k, dy_k = lax.optimization_barrier((dq, dz_k, dy_k))
    far_came, dq = lax.optimization_barrier((far_came, dq))
    (placed,) = call(
        functools.partial(place_kernel, block, (z_swap, y_swap), far),
        (lists, dz_v_came, dy_v_came, *far_came),
        [frame_sum],
    )
    near, q_keep, q_send = call(
        own_kernel,
        (qg, lse, row_dot, dq, o, kv, placed),
        [frame_sum, pair, pair],
        flops=28 * work,
    )
    outputs = [sds((s_dev, width), BF16)] * 2
    attn_out, grad_q = call(finish_kernel, (q_keep, across(q_send)), outputs)
    (near,) = call(
        functools.partial(add_kernel, (near_swap, y_swap)),
        (near, da_came, dy_k_came),
        [frame_sum],
        flops=5 * work,
    )
    k_keep, k_send = call(
        functools.partial(gather_kernel, z_swap), (near, dz_k_came), [pair, pair]
    )
    grad_k, grad_v = call(finish_kernel, (k_keep, across(k_send)), outputs)
    return attn_out, grad_q, grad_k, grad_v


def solution(mesh):
    rows = P(("groups", "tm", "space"), None)
    return jax.shard_map(
        per_device,
        mesh=mesh,
        in_specs=(rows, rows, rows, rows, P("groups", None)),
        out_specs=(rows, rows, rows, rows),
        check_vma=False,
    )
```
